32 devices in a mesh: seq: 4 (over x, core), fsdp: 8 (over z, y).
Axes of the slice: x: 2, y: 2, z: 4, core: 2. Of those that a mesh axis runs over, the one named last changes fastest.
Arguments:
- patches: bfloat16 [24, 1024, 1152], P('fsdp', 'seq'), may hold values from -6 to 6
- lengths: int32 [24, 4], P('fsdp'), may hold values from 0 to 1024, as said below
- first_gain: bfloat16 [1152], P('fsdp'), may hold values from 0.5 to 1.5
- first_shift: bfloat16 [1152], P('fsdp'), may hold values from -3 to 3
- query_weight: bfloat16 [1152, 1152], P('fsdp'), may hold values from -0.1875 to 0.1875
- query_bias: bfloat16 [1152], P('fsdp'), may hold values from -3 to 3
- key_weight: bfloat16 [1152, 1152], P('fsdp'), may hold values from -0.1875 to 0.1875
- value_weight: bfloat16 [1152, 1152], P('fsdp'), may hold values from -0.1875 to 0.1875
- value_bias: bfloat16 [1152], P('fsdp'), may hold values from -3 to 3
- output_weight: bfloat16 [1152, 1152], P('fsdp'), may hold values from -0.75 to 0.75
- output_bias: bfloat16 [1152], P('fsdp'), may hold values from -3 to 3
- second_gain: bfloat16 [1152], P('fsdp'), may hold values from 0.5 to 1.5
- second_shift: bfloat16 [1152], P('fsdp'), may hold values from -3 to 3
- hidden_weight: bfloat16 [1152, 4304], P('fsdp'), may hold values from -0.1875 to 0.1875
- hidden_bias: bfloat16 [4304], replicated, may hold values from -3 to 3
- down_weight: bfloat16 [4304, 1152], P(None, 'fsdp'), may hold values from -0.09375 to 0.09375
- down_bias: bfloat16 [1152], P('fsdp'), may hold values from -3 to 3
- cotangent: bfloat16 [24, 1024, 1152], P('fsdp', 'seq'), may hold values from -6 to 6
Outputs:
- layer_output: bfloat16 [24, 1024, 1152], P('fsdp', 'seq')
- grad_patches: float32 [24, 1024, 1152], P('fsdp', 'seq')
- grad_first_gain: float32 [1152], P('fsdp')
- grad_first_shift: float32 [1152], P('fsdp')
- grad_query_weight: float32 [1152, 1152], P('fsdp')
- grad_query_bias: float32 [1152], P('fsdp')
- grad_key_weight: float32 [1152, 1152], P('fsdp')
- grad_value_weight: float32 [1152, 1152], P('fsdp')
- grad_value_bias: float32 [1152], P('fsdp')
- grad_output_weight: float32 [1152, 1152], P('fsdp')
- grad_output_bias: float32 [1152], P('fsdp')
- grad_second_gain: float32 [1152], P('fsdp')
- grad_second_shift: float32 [1152], P('fsdp')
- grad_hidden_weight: float32 [1152, 4304], P('fsdp')
- grad_hidden_bias: float32 [4304], replicated
- grad_down_weight: float32 [4304, 1152], P(None, 'fsdp')
- grad_down_bias: float32 [1152], P('fsdp')
The draws below stay inside these ranges and needn't reach their ends.
Inputs may be any that keep to these rules, and one draw needn't show every extreme that they name: `lengths`: each row lists its pictures' patch counts in its first slots: 1 to 4 pictures of 100 or more patches each, summing to at most 1024; the remaining slots are 0 and the rest of the row is padding. Some row holds one picture of 1024 patches.
All inputs are finite; a program needn't handle non-finite values.
Results may differ from the reference program's by a relative error of at most 0.013.
Values may be sent and summed in bfloat16 or wider, within the bound.
No kernel may reach another device: no remote copies, remote signals or barrier semaphores. Data moves between devices by JAX's collectives and lax.ppermute only.
A program may use at most 320 MiB of HBM per device.

```python
import math
import jax
import jax.numpy as jnp
from jax import lax

D = 1152
HEADS = 16
HEAD_DIM = 72
FF = 4304
LEN = 1024
PICS = 4
MINPIC = 100
ROWS = 24


def draw_lengths(key, part):
    count_key, size_key = jax.random.split(key)
    row_index = jnp.arange(ROWS, dtype=jnp.int32)
    single_row = row_index % 8 == 0
    count_pics = jax.random.randint(count_key, (ROWS,), 1, PICS + 1).astype(jnp.int32)
    count_pics = jnp.where(single_row, 1, count_pics).astype(jnp.int32)
    upper_len = (LEN // count_pics).astype(jnp.int32)
    sizes_drawn = jax.random.randint(size_key, (ROWS, PICS), MINPIC, upper_len[:, None] + 1).astype(jnp.int32)
    sizes_drawn = jnp.where(single_row[:, None], LEN, sizes_drawn).astype(jnp.int32)
    slot_index = jnp.arange(PICS, dtype=jnp.int32)
    return jnp.where(slot_index[None, :] < count_pics[:, None], sizes_drawn, 0).astype(jnp.int32)


def levels(own_key, dims, cuts, least, high):
    factor_of, own = 1.0, jax.random.fold_in(own_key, 6)
    for axis_at, blocks in cuts:
        draws = jnp.exp(jax.random.uniform(jax.random.fold_in(own, axis_at), (blocks,), jnp.float32, least / len(cuts), high / len(cuts)))
        factor_of = factor_of * jnp.repeat(draws, dims[axis_at] // blocks).reshape([-1 if axis == axis_at else 1 for axis in range(len(dims))])
    return factor_of


def scatter_about(key, extent, width, reach, cuts=(), kind=jnp.bfloat16):
    factor_of = levels(key, extent, cuts, -0.22, 0.18) if cuts else 1.0
    values = jax.random.normal(key, extent, jnp.float32) * width * factor_of
    return jnp.minimum(jnp.maximum(values, -reach), reach).astype(kind)


def setup_inputs(seed: int = 0) -> dict:
    splits = jax.random.split(jax.random.key(seed), 19)
    return {
        "patches": scatter_about(splits[0], (ROWS, LEN, D), 1.0, 6.0, ((0, 8), (1, 4))),
        "lengths": draw_lengths(jax.random.fold_in(splits[18], 71), 0),
        "first_gain": jnp.clip(1.0 + 0.1 * jax.random.normal(splits[2], (D,), jnp.float32), 0.5, 1.5).astype(jnp.bfloat16),
        "first_shift": scatter_about(splits[3], (D,), 0.5, 3.0, ((0, 8),)),
        "query_weight": scatter_about(splits[4], (D, D), D ** -0.5, 0.1875, ((0, 8),)),
        "query_bias": scatter_about(splits[5], (D,), 0.5, 3.0, ((0, 8),)),
        "key_weight": scatter_about(splits[6], (D, D), D ** -0.5, 0.1875, ((0, 8),)),
        "value_weight": scatter_about(splits[7], (D, D), D ** -0.5, 0.1875, ((0, 8),)),
        "value_bias": scatter_about(splits[8], (D,), 0.5, 3.0, ((0, 8),)),
        "output_weight": scatter_about(splits[9], (D, D), HEAD_DIM ** -0.5, 0.75, ((0, 8),)),
        "output_bias": scatter_about(splits[10], (D,), 0.5, 3.0, ((0, 8),)),
        "second_gain": jnp.clip(1.0 + 0.1 * jax.random.normal(splits[11], (D,), jnp.float32), 0.5, 1.5).astype(jnp.bfloat16),
        "second_shift": scatter_about(splits[12], (D,), 0.5, 3.0, ((0, 8),)),
        "hidden_weight": scatter_about(splits[13], (D, FF), D ** -0.5, 0.1875, ((0, 8),)),
        "hidden_bias": scatter_about(splits[14], (FF,), 0.5, 3.0),
        "down_weight": scatter_about(splits[15], (FF, D), FF ** -0.5, 0.09375, ((1, 8),)),
        "down_bias": scatter_about(splits[16], (D,), 0.5, 3.0, ((0, 8),)),
        "cotangent": scatter_about(splits[17], (ROWS, LEN, D), 1.0, 6.0, ((0, 8), (1, 4))),
    }


@jax.custom_vjp
def low(v):
    return lax.optimization_barrier(v.astype(jnp.bfloat16)).astype(jnp.float32)

@jax.custom_vjp
def low_back(v):
    return v

def low_keep(v):
    return (low(v), None)

def low_pass(kept, grad):
    return (grad,)

def back_keep(v):
    return (v, None)

def back_low(kept, grad):
    return (low(grad),)
low.defvjp(low_keep, low_pass)
low_back.defvjp(back_keep, back_low)
EPS = 1e-06
GELU_COEF = math.sqrt(2.0 / math.pi)
MASKED = -1e+30
HIGH = lax.Precision.HIGHEST

def matmul(left, right):
    return jnp.dot(left, right, precision=HIGH, preferred_element_type=jnp.float32)

def layer_norm(values, gain, shift):
    center = values - lax.optimization_barrier(jnp.mean(values, axis=-1, keepdims=True))
    spread = lax.optimization_barrier(jnp.mean(center * center, axis=-1, keepdims=True))
    return center * lax.rsqrt(spread + EPS) * gain + shift

def gelu_tanh(inner):
    return 0.5 * inner * (1.0 + jnp.tanh(GELU_COEF * (inner + 0.044715 * inner * inner * inner)))

def picture_ids(lengths, seq_len):
    position = jnp.arange(seq_len, dtype=jnp.int32)
    picture_ends = jnp.cumsum(lengths, axis=-1).astype(jnp.int32)
    picture = lax.optimization_barrier(jnp.sum((position[None, :, None] >= picture_ends[:, None, :]).astype(jnp.int32), axis=-1)).astype(jnp.int32)
    usable = position[None, :] < picture_ends[:, -1:]
    return (picture, usable)

def row_forward(params, row_input, picture, usable):
    gain_one, shift_one, w_query, bias_query, w_key, w_value, bias_value, w_output, bias_output, gain_two, shift_two, w_hidden, bias_hidden, w_down, bias_down = params
    seq_len = row_input.shape[0]
    normed = low(layer_norm(row_input, gain_one, shift_one))
    queries = low(low_back(matmul(normed, w_query) + bias_query))
    key_rows = low(low_back(matmul(normed, w_key)))
    value_rows = low(low_back(matmul(normed, w_value) + bias_value))
    query_heads = queries.reshape(seq_len, HEADS, HEAD_DIM)
    key_heads = key_rows.reshape(seq_len, HEADS, HEAD_DIM)
    value_heads = value_rows.reshape(seq_len, HEADS, HEAD_DIM)
    scores = low_back(jnp.einsum('qhd,khd->hqk', query_heads, key_heads, precision=HIGH) * (1.0 / math.sqrt(HEAD_DIM)))
    position = jnp.arange(seq_len, dtype=jnp.int32)
    allowed = (picture[:, None] == picture[None, :]) & usable[None, :] | (position[:, None] == position[None, :])
    scores = jnp.where(allowed[None], scores, MASKED)
    row_peak = lax.optimization_barrier(jnp.max(scores, axis=-1, keepdims=True))
    exponent = jnp.exp(scores - row_peak)
    soft_weights = exponent / lax.optimization_barrier(jnp.sum(exponent, axis=-1, keepdims=True))
    attended = jnp.einsum('hqk,khd->qhd', low(soft_weights), value_heads, precision=HIGH).reshape(seq_len, HEADS * HEAD_DIM)
    attended = low(low_back(attended))
    branch = low_back(matmul(attended, w_output) + bias_output)
    middle = row_input + branch
    second_normed = low(layer_norm(middle, gain_two, shift_two))
    pre_act = low_back(matmul(second_normed, w_hidden) + bias_hidden)
    activated = low(gelu_tanh(pre_act))
    mlp_branch = low_back(matmul(activated, w_down) + bias_down)
    return middle + mlp_branch

def reference(patches, lengths, first_gain, first_shift, query_weight, query_bias, key_weight, value_weight, value_bias, output_weight, output_bias, second_gain, second_shift, hidden_weight, hidden_bias, down_weight, down_bias, cotangent):
    params = (first_gain.astype(jnp.float32), first_shift.astype(jnp.float32), query_weight.astype(jnp.float32), query_bias.astype(jnp.float32), key_weight.astype(jnp.float32), value_weight.astype(jnp.float32), value_bias.astype(jnp.float32), output_weight.astype(jnp.float32), output_bias.astype(jnp.float32), second_gain.astype(jnp.float32), second_shift.astype(jnp.float32), hidden_weight.astype(jnp.float32), hidden_bias.astype(jnp.float32), down_weight.astype(jnp.float32), down_bias.astype(jnp.float32))
    picture, usable = picture_ids(lengths, LEN)

    def whole(inputs, weights):
        step_fn = jax.checkpoint(lambda packed: row_forward(weights, packed[0], packed[1], packed[2]))
        return lax.map(step_fn, (inputs, picture, usable))
    result, pull = jax.vjp(whole, patches.astype(jnp.float32), params)
    grad_input, grads = pull(cotangent.astype(jnp.float32))
    return (result.astype(jnp.bfloat16), grad_input, grads[0], grads[1], grads[2], grads[3], grads[4], grads[5], grads[6], grads[7], grads[8], grads[9], grads[10], grads[11], grads[12], grads[13], grads[14])
```

```python
import functools
import math

import jax
import jax.numpy as jnp
from jax import lax
from jax.experimental import pallas as pl
from jax.experimental.pallas import tpu as pltpu
from jax.sharding import PartitionSpec as P

HEAD_DIM = 72
EPS = 1e-06
GELU_COEF = math.sqrt(2.0 / math.pi)
MASKED = -1e30
F32 = jnp.float32
BF16 = jnp.bfloat16
SCALE = 1.0 / math.sqrt(HEAD_DIM)
WIN = 256
VMEM = 60 << 20


def round_up(value, step):
    return (value + step - 1) // step * step


def dot(left, right, dims=((1,), (0,))):
    return lax.dot_general(left, right, (dims, ((), ())), preferred_element_type=F32)


NT = ((1,), (1,))
TN = ((0,), (0,))


def params(semantics):
    return pltpu.CompilerParams(dimension_semantics=semantics, vmem_limit_bytes=VMEM)


def swap(array, axis, bit):
    size = lax.axis_size(axis)
    return lax.ppermute(array, axis, [(i, i ^ bit) for i in range(size)])


def bits_of(size):
    return [1 << k for k in reversed(range(size.bit_length() - 1))]


def after(value, *earlier):
    return lax.optimization_barrier((value,) + tuple(earlier))[0]


def gather_shards(shard, gate=None):
    parts = {0: shard}
    first = {}
    for bit in bits_of(lax.axis_size("fsdp")):
        fresh = {}
        for distance, part in parts.items():
            if gate and bit in gate and distance == 0:
                part = after(part, gate[bit])
            fresh[distance | bit] = swap(part, "fsdp", bit)
        first[bit] = fresh[bit]
        parts.update(fresh)
    return parts, first


def rel_position(distance, count):
    width = count.bit_length() - 1
    return sum(((distance >> k) & 1) << (width - 1 - k) for k in range(width))


def assemble_kernel(count, rows, off_ref, *refs):
    out_ref = refs[count]
    for distance in range(count):
        start = pl.multiple_of(off_ref[distance], 16)
        out_ref[pl.ds(start, rows), :] = refs[distance][...]


def assemble(parts, me):
    count = len(parts)
    rows, cols = parts[0].shape
    if rows % 16:
        stacked = jnp.stack([parts[d] for d in range(count)])
        return jnp.take(stacked, me ^ jnp.arange(count), axis=0).reshape(count * rows, cols)
    offsets = ((me ^ jnp.arange(count, dtype=jnp.int32)) * rows).astype(jnp.int32)
    tile = cols
    for candidate in (640, 384, 128):
        if cols % candidate == 0:
            tile = candidate
            break
    return pl.pallas_call(
        functools.partial(assemble_kernel, count, rows),
        out_shape=jax.ShapeDtypeStruct((count * rows, cols), parts[0].dtype),
        grid_spec=pltpu.PrefetchScalarGridSpec(
            num_scalar_prefetch=1,
            grid=(cols // tile,),
            in_specs=[pl.BlockSpec((rows, tile), lambda n, off: (0, n))] * count,
            out_specs=pl.BlockSpec((count * rows, tile), lambda n, off: (0, n)),
        ),
        compiler_params=params(("arbitrary",)),
        cost_estimate=pl.CostEstimate(
            flops=0, transcendentals=0, bytes_accessed=4 * count * rows * cols
        ),
        name="assemble",
    )(offsets, *[parts[d] for d in range(count)])


def weight_grad_kernel(pairs, count, rows, pos_ref, *refs):
    lefts, rights = refs[:pairs], refs[pairs : 2 * pairs]
    out_ref, turned = refs[2 * pairs], refs[2 * pairs + 1]
    tokens = lefts[0].shape[0]

    @pl.when(pl.program_id(0) == 0)
    def _():
        for i in range(pairs):
            turned[:, i * tokens : (i + 1) * tokens] = lefts[i][...].T

    total = dot(turned[:, :tokens], rights[0][...])
    for i in range(1, pairs):
        total += dot(turned[:, i * tokens : (i + 1) * tokens], rights[i][...])
    for shard in range(count):
        start = pl.multiple_of(pos_ref[shard], 16)
        out_ref[pl.ds(start, rows), :] = total[shard * rows : (shard + 1) * rows].astype(BF16)


def weight_grad(lefts, rights, me, count, first_col=0, cols=None):
    tokens, width = lefts[0].shape
    cols = cols or rights[0].shape[1]
    rows = width // count
    order = me ^ jnp.arange(count, dtype=jnp.int32)
    table = jnp.array([rel_position(d, count) for d in range(count)], jnp.int32)
    if rows % 16:
        total = sum(dot(a, b[:, first_col : first_col + cols], TN) for a, b in zip(lefts, rights))
        by_distance = jnp.take(total.astype(BF16).reshape(count, rows, cols), order, axis=0)
        back = [0] * count
        for d in range(count):
            back[rel_position(d, count)] = d
        return jnp.take(by_distance, jnp.array(back), axis=0)
    positions = (table[order] * rows).astype(jnp.int32)
    tile = 256 if first_col % 256 == 0 else 128
    pairs = len(lefts)
    base = first_col // tile
    return pl.pallas_call(
        functools.partial(weight_grad_kernel, pairs, count, rows),
        out_shape=jax.ShapeDtypeStruct((width, cols), BF16),
        grid_spec=pltpu.PrefetchScalarGridSpec(
            num_scalar_prefetch=1,
            grid=(pl.cdiv(cols, tile),),
            in_specs=[
                pl.BlockSpec((tokens, width), lambda n, off: (0, 0), pipeline_mode=pl.Buffered(1))
            ]
            * pairs
            + [pl.BlockSpec((tokens, tile), lambda n, off: (0, n + base))] * pairs,
            out_specs=pl.BlockSpec((width, tile), lambda n, off: (0, n)),
            scratch_shapes=[pltpu.VMEM((width, pairs * tokens), BF16)],
        ),
        compiler_params=params(("arbitrary",)),
        cost_estimate=pl.CostEstimate(
            flops=2 * pairs * tokens * width * cols,
            transcendentals=0,
            bytes_accessed=2 * (pairs * tokens * (width + cols) + width * cols),
        ),
        name="weight_grad",
    )(positions, *lefts, *rights).reshape(count, rows, cols)


def scatter_sum(blocks):
    for bit in reversed(bits_of(lax.axis_size("fsdp"))):
        half = blocks.shape[0] // 2
        arrived = swap(blocks[half:], "fsdp", bit)
        blocks = (blocks[:half].astype(F32) + arrived.astype(F32)).astype(BF16)
    mine = blocks[0]
    for bit in bits_of(lax.axis_size("seq"))[:-1]:
        arrived = swap(mine, "seq", bit)
        total = mine.astype(F32) + arrived.astype(F32)
        mine = total.astype(BF16)
    return total


def norm_kernel(x_ref, gain_ref, shift_ref, out_ref):
    values = x_ref[...].astype(F32)
    center = values - jnp.mean(values, axis=-1, keepdims=True)
    spread = jnp.mean(center * center, axis=-1, keepdims=True)
    out_ref[...] = (center * lax.rsqrt(spread + EPS) * gain_ref[...] + shift_ref[...]).astype(BF16)


def norm(values, gain, shift):
    rows, width = values.shape
    block = 256 if rows % 256 == 0 else rows
    return pl.pallas_call(
        norm_kernel,
        out_shape=jax.ShapeDtypeStruct((rows, width), BF16),
        grid=(rows // block,),
        in_specs=[
            pl.BlockSpec((block, width), lambda i: (i, 0)),
            pl.BlockSpec((1, width), lambda i: (0, 0)),
            pl.BlockSpec((1, width), lambda i: (0, 0)),
        ],
        out_specs=pl.BlockSpec((block, width), lambda i: (i, 0)),
        compiler_params=params(("arbitrary",)),
        cost_estimate=pl.CostEstimate(
            flops=10 * rows * width, transcendentals=0, bytes_accessed=6 * rows * width
        ),
        name="norm",
    )(values, gain, shift)


def norm_back_kernel(x_ref, own_ref, other_ref, gain_ref, add_ref, dx_ref, low_ref, dg_ref, ds_ref):
    values = x_ref[...].astype(F32)
    center = values - jnp.mean(values, axis=-1, keepdims=True)
    spread = jnp.mean(center * center, axis=-1, keepdims=True)
    inverse = lax.rsqrt(spread + EPS)
    hat = center * inverse
    grad = own_ref[...].astype(F32) + other_ref[...].astype(F32)
    scaled = grad * gain_ref[...]
    first = jnp.mean(scaled, axis=-1, keepdims=True)
    second = jnp.mean(scaled * hat, axis=-1, keepdims=True)
    total = add_ref[...].astype(F32) + inverse * (scaled - first - hat * second)
    dx_ref[...] = total
    low_ref[...] = total.astype(BF16)

    @pl.when(pl.program_id(0) == 0)
    def _():
        dg_ref[...] = jnp.zeros_like(dg_ref)
        ds_ref[...] = jnp.zeros_like(ds_ref)

    dg_ref[...] += jnp.sum(grad * hat, axis=0, keepdims=True)
    ds_ref[...] += jnp.sum(grad, axis=0, keepdims=True)


def norm_back(values, own, other, gain, add):
    rows, width = values.shape
    block = 256 if rows % 256 == 0 else rows
    wide = pl.BlockSpec((block, width), lambda i: (i, 0))
    line = pl.BlockSpec((1, width), lambda i: (0, 0))
    return pl.pallas_call(
        norm_back_kernel,
        out_shape=(
            jax.ShapeDtypeStruct((rows, width), F32),
            jax.ShapeDtypeStruct((rows, width), BF16),
            jax.ShapeDtypeStruct((1, width), F32),
            jax.ShapeDtypeStruct((1, width), F32),
        ),
        grid=(rows // block,),
        in_specs=[wide, wide, wide, line, wide],
        out_specs=(wide, wide, line, line),
        compiler_params=params(("arbitrary",)),
        cost_estimate=pl.CostEstimate(
            flops=20 * rows * width, transcendentals=0, bytes_accessed=18 * rows * width
        ),
        name="norm_back",
    )(values, own, other, gain, add)


def hidden_kernel(x_ref, w_ref, b_ref, act_ref, slope_ref):
    pre = dot(x_ref[...], w_ref[...]) + b_ref[...]
    square = pre * pre
    turn = jnp.tanh(GELU_COEF * (pre + 0.044715 * square * pre))
    act_ref[...] = (0.5 * pre * (1.0 + turn)).astype(BF16)
    inner = GELU_COEF * (1.0 + 3.0 * 0.044715 * square)
    slope_ref[...] = (0.5 * (1.0 + turn) + 0.5 * pre * (1.0 - turn * turn) * inner).astype(BF16)


def hidden(x, weight, bias):
    rows, width = x.shape
    cols = weight.shape[1]
    block = 128
    out = pl.BlockSpec((block, cols), lambda i: (i, 0))
    return pl.pallas_call(
        hidden_kernel,
        out_shape=(jax.ShapeDtypeStruct((rows, cols), BF16),) * 2,
        grid=(rows // block,),
        in_specs=[
            pl.BlockSpec((block, width), lambda i: (i, 0)),
            pl.BlockSpec((width, cols), lambda i: (0, 0), pipeline_mode=pl.Buffered(1)),
            pl.BlockSpec((1, cols), lambda i: (0, 0)),
        ],
        out_specs=(out, out),
        compiler_params=params(("arbitrary",)),
        cost_estimate=pl.CostEstimate(
            flops=2 * rows * width * cols,
            transcendentals=rows * cols,
            bytes_accessed=2 * (rows * width + width * cols + 2 * rows * cols),
        ),
        name="hidden",
    )(x, weight, bias)


def head_window(head, padded):
    tile = jnp.minimum((head * HEAD_DIM) >> 7, (padded - WIN) >> 7)
    return pl.multiple_of(tile * 128, 128), head * HEAD_DIM - tile * 128


def only_head(block, lane, low):
    return jnp.where((lane >= low) & (lane < low + HEAD_DIM), block.astype(F32), 0.0).astype(BF16)


def attend_kernel(which, heads, blocks, padded, need_ref, col_ref, row_ref, *refs):
    sides = refs[:blocks]
    out_ref, lse_ref, score, peak, total, acc = refs[blocks:]
    row = pl.program_id(0)
    tokens = out_ref.shape[1]
    lane = lax.broadcasted_iota(jnp.int32, (tokens, WIN), 1)
    slot = lax.broadcasted_iota(jnp.int32, (tokens, 128), 1)
    out_ref[...] = jnp.zeros_like(out_ref)
    lse_ref[...] = jnp.zeros_like(lse_ref)

    def one_head(head, carry):
        start, low = head_window(head, padded)
        query = only_head(sides[which][0, :, pl.ds(start, WIN)], lane, low)
        peak[...] = jnp.full_like(peak, MASKED)
        total[...] = jnp.zeros_like(total)
        acc[...] = jnp.zeros_like(acc)
        for block in range(blocks):

            @pl.when(need_ref[row, which, block] != 0)
            def _():
                key = sides[block][0, :, pl.ds(padded + start, WIN)]
                found = jnp.where(
                    col_ref[0, which] == row_ref[0, block : block + 1], dot(query, key, NT), MASKED
                )
                score[block] = found
                peak[...] = jnp.maximum(peak[...], jnp.max(found, axis=-1, keepdims=True))

        for block in range(blocks):

            @pl.when(need_ref[row, which, block] != 0)
            def _():
                weight = jnp.exp((score[block] - peak[:, :1]) * SCALE)
                total[...] += jnp.sum(weight, axis=-1, keepdims=True)
                value = sides[block][0, :, pl.ds(2 * padded + start, WIN)]
                acc[...] += dot(weight.astype(BF16), value)

        result = acc[...] / total[:, :1]
        kept = out_ref[0, :, pl.ds(start, WIN)].astype(F32)
        mine = (lane >= low) & (lane < low + HEAD_DIM)
        out_ref[0, :, pl.ds(start, WIN)] = jnp.where(mine, result, kept).astype(BF16)
        lse = peak[...] * SCALE + jnp.log(total[...])
        lse_ref[0] = jnp.where(slot == head, lse, lse_ref[0])
        return carry

    lax.fori_loop(0, heads, one_head, 0)


def attend(which, sides, need, seg_col, seg_row, heads):
    rows, tokens, wide = sides[0].shape
    blocks, padded = len(sides), wide // 3
    cost = rows * heads * blocks * tokens * tokens
    return pl.pallas_call(
        functools.partial(attend_kernel, which, heads, blocks, padded),
        out_shape=(
            jax.ShapeDtypeStruct((rows, tokens, padded), BF16),
            jax.ShapeDtypeStruct((rows, tokens, 128), F32),
        ),
        grid_spec=pltpu.PrefetchScalarGridSpec(
            num_scalar_prefetch=1,
            grid=(rows,),
            in_specs=[
                pl.BlockSpec((1, blocks, tokens, 1), lambda r, need: (r, 0, 0, 0)),
                pl.BlockSpec((1, blocks, tokens), lambda r, need: (r, 0, 0)),
            ]
            + [pl.BlockSpec((1, tokens, wide), lambda r, need: (r, 0, 0))] * blocks,
            out_specs=(
                pl.BlockSpec((1, tokens, padded), lambda r, need: (r, 0, 0)),
                pl.BlockSpec((1, tokens, 128), lambda r, need: (r, 0, 0)),
            ),
            scratch_shapes=[
                pltpu.VMEM((blocks, tokens, tokens), F32),
                pltpu.VMEM((tokens, 128), F32),
                pltpu.VMEM((tokens, 128), F32),
                pltpu.VMEM((tokens, WIN), F32),
            ],
        ),
        compiler_params=params(("arbitrary",)),
        cost_estimate=pl.CostEstimate(
            flops=4 * cost * WIN, transcendentals=cost, bytes_accessed=2 * rows * tokens * wide * blocks
        ),
        name="attend",
    )(need, seg_col, seg_row, *sides)


def attend_back_kernel(heads, blocks, padded, need_ref, col_ref, row_ref, pick_ref, *refs):
    sides = refs[:blocks]
    grads, outs, lses = refs[blocks : blocks + 2], refs[blocks + 2 : blocks + 4], refs[blocks + 4 : blocks + 6]
    results = refs[blocks + 6 : 2 * blocks + 6]
    sums, lse_turn, inner_turn, dq = refs[2 * blocks + 6 :]
    row = pl.program_id(0)
    tokens = grads[0].shape[1]
    lane = lax.broadcasted_iota(jnp.int32, (tokens, WIN), 1)
    sums[...] = jnp.zeros_like(sums)
    for which in range(2):
        results[which][0, :, :padded] = jnp.zeros((tokens, padded), BF16)
        lse_turn[...] = lses[which][0].T
        product = grads[which][0].astype(F32) * outs[which][0].astype(F32)
        high = product.astype(BF16)
        rest = (product - high.astype(F32)).astype(BF16)
        inner_turn[...] = dot(pick_ref[...], high, NT) + dot(pick_ref[...], rest, NT)

        def one_head(head, carry, which=which):
            start, low = head_window(head, padded)
            query = only_head(sides[which][0, :, pl.ds(start, WIN)], lane, low)
            grad = only_head(grads[which][0, :, pl.ds(start, WIN)], lane, low)
            lse = lse_turn[pl.ds(head, 1), :]
            inner = inner_turn[pl.ds(head, 1), :]
            dq[...] = jnp.zeros_like(dq)
            for block in range(blocks):

                @pl.when(need_ref[row, which, block] != 0)
                def _():
                    key = sides[block][0, :, pl.ds(padded + start, WIN)]
                    value = sides[block][0, :, pl.ds(2 * padded + start, WIN)]
                    seen = col_ref[0, block] == row_ref[0, which : which + 1]
                    prob = jnp.where(seen, jnp.exp(dot(key, query, NT) * SCALE - lse), 0.0)
                    slope = (prob * (dot(value, grad, NT) - inner)).astype(BF16)
                    sums[block, :, pl.ds(start, WIN)] += dot(slope, query)
                    sums[block, :, pl.ds(padded + start, WIN)] += dot(prob.astype(BF16), grad)
                    dq[...] += dot(slope, key, TN)

            kept = results[which][0, :, pl.ds(start, WIN)].astype(F32)
            mine = (lane >= low) & (lane < low + HEAD_DIM)
            results[which][0, :, pl.ds(start, WIN)] = jnp.where(mine, dq[...] * SCALE, kept).astype(BF16)
            return carry

        lax.fori_loop(0, heads, one_head, 0)
    for block in range(blocks):
        skip = padded if block < 2 else 0
        results[block][0, :, skip : skip + padded] = (sums[block, :, :padded] * SCALE).astype(BF16)
        results[block][0, :, skip + padded :] = sums[block, :, padded:].astype(BF16)


def attend_back(sides, grads, outs, lses, need, seg_col, seg_row, heads):
    rows, tokens, wide = sides[0].shape
    blocks, padded = len(sides), wide // 3
    cost = 2 * rows * heads * blocks * tokens * tokens
    column = lax.broadcasted_iota(jnp.int32, (128, padded), 1)
    pick = (column // HEAD_DIM == lax.broadcasted_iota(jnp.int32, (128, padded), 0)).astype(BF16)
    narrow = pl.BlockSpec((1, tokens, padded), lambda r, need: (r, 0, 0))
    line = pl.BlockSpec((1, tokens, 128), lambda r, need: (r, 0, 0))
    widths = [wide if block < 2 else 2 * padded for block in range(blocks)]
    return pl.pallas_call(
        functools.partial(attend_back_kernel, heads, blocks, padded),
        out_shape=tuple(jax.ShapeDtypeStruct((rows, tokens, w), BF16) for w in widths),
        grid_spec=pltpu.PrefetchScalarGridSpec(
            num_scalar_prefetch=1,
            grid=(rows,),
            in_specs=[
                pl.BlockSpec((1, blocks, tokens, 1), lambda r, need: (r, 0, 0, 0)),
                pl.BlockSpec((1, blocks, tokens), lambda r, need: (r, 0, 0)),
                pl.BlockSpec((128, padded), lambda r, need: (0, 0)),
            ]
            + [pl.BlockSpec((1, tokens, wide), lambda r, need: (r, 0, 0))] * blocks
            + [narrow] * 4
            + [line] * 2,
            out_specs=tuple(pl.BlockSpec((1, tokens, w), lambda r, need: (r, 0, 0)) for w in widths),
            scratch_shapes=[
                pltpu.VMEM((blocks, tokens, 2 * padded), F32),
                pltpu.VMEM((128, tokens), F32),
                pltpu.VMEM((128, tokens), F32),
                pltpu.VMEM((tokens, WIN), F32),
            ],
        ),
        compiler_params=params(("arbitrary",)),
        cost_estimate=pl.CostEstimate(
            flops=10 * cost * WIN,
            transcendentals=cost,
            bytes_accessed=4 * rows * tokens * wide * blocks,
        ),
        name="attend_back",
    )(need, seg_col, seg_row, pick, *sides, *grads, *outs, *lses)


def column_sum(array):
    ones = jnp.ones((8, array.shape[0]), BF16)
    return dot(ones, array)[0]


def local(
    patches,
    lengths,
    first_gain,
    first_shift,
    query_weight,
    query_bias,
    key_weight,
    value_weight,
    value_bias,
    output_weight,
    output_bias,
    second_gain,
    second_shift,
    hidden_weight,
    hidden_bias,
    down_weight,
    down_bias,
    cotangent,
):
    seq_count, shards = lax.axis_size("seq"), lax.axis_size("fsdp")
    place, me = lax.axis_index("seq"), lax.axis_index("fsdp")
    core = place & 1
    is_first = core == 0
    rows, tokens, width = patches.shape
    flat = rows * tokens
    heads = width // HEAD_DIM // 2
    half = heads * HEAD_DIM
    padded = round_up(half, 128)
    ff = hidden_bias.shape[0]
    ff_half = round_up(ff, 256) // 2
    out_cols = padded
    out_cut = width - padded

    def my_half(array, size, padded_size):
        first, second = array[..., :size], array[..., size:]
        grow = [(0, 0)] * (array.ndim - 1)
        first = jnp.pad(first, grow + [(0, padded_size - size)])
        second = jnp.pad(second, grow + [(0, padded_size - second.shape[-1])])
        return jnp.where(is_first, first, second)

    vectors = jnp.stack(
        [
            first_gain,
            first_shift,
            query_bias,
            value_bias,
            output_bias,
            second_gain,
            second_shift,
            down_bias,
        ]
    )
    vector_parts, _ = gather_shards(vectors)
    stacked = jnp.stack([vector_parts[d] for d in range(shards)])
    stacked = jnp.take(stacked, me ^ jnp.arange(shards), axis=0)
    stacked = stacked.transpose(1, 0, 2).reshape(8, width).astype(F32)
    gain_one, shift_one, bias_query, bias_value, bias_output, gain_two, shift_two, bias_down = [
        stacked[i : i + 1] for i in range(8)
    ]

    shard_qkv = jnp.concatenate(
        [my_half(w, half, padded) for w in (query_weight, key_weight, value_weight)], axis=1
    )
    shard_out = jnp.where(is_first, output_weight[:, :out_cols], output_weight[:, out_cut:])
    shard_hidden = my_half(hidden_weight, ff_half, ff_half)
    shard_down = my_half(down_weight.T, ff_half, ff_half)
    parts_qkv, first_qkv = gather_shards(shard_qkv)
    parts_out, first_out = gather_shards(shard_out, first_qkv)
    parts_hidden, first_hidden = gather_shards(shard_hidden, first_out)
    parts_down, _ = gather_shards(shard_down, first_hidden)

    block_of = place ^ jnp.arange(seq_count, dtype=jnp.int32)
    position = block_of[:, None] * tokens + jnp.arange(tokens, dtype=jnp.int32)[None, :]
    ends = jnp.cumsum(lengths, axis=-1)
    picture = jnp.sum(
        (position[None, :, :, None] >= ends[:, None, None, :]).astype(jnp.int32), axis=-1
    )
    usable = position[None] < ends[:, -1][:, None, None]
    segment = jnp.where(usable, picture, 1000 + position[None])
    seg_row = segment
    seg_col = segment[..., None]
    low_id = jnp.min(jnp.where(usable, picture, 1 << 20), axis=-1)
    high_id = jnp.max(jnp.where(usable, picture, -1), axis=-1)
    need = (low_id[:, :2, None] <= high_id[:, None, :]) & (low_id[:, None, :] <= high_id[:, :2, None])
    need = need | jnp.eye(2, seq_count, dtype=jnp.bool_)[None]
    need = need.astype(jnp.int32)

    inputs = patches.reshape(flat, width)
    incoming = cotangent.reshape(flat, width)
    incoming_pair = swap(incoming, "seq", 1)
    normed = {0: norm(inputs, gain_one, shift_one)}
    for bit in bits_of(seq_count):
        normed.update({j | bit: swap(part, "seq", bit) for j, part in list(normed.items())})
    w_qkv = assemble(parts_qkv, me)
    zeros = jnp.zeros((1, padded), F32)
    bias_qkv = jnp.concatenate(
        [my_half(bias_query, half, padded), zeros, my_half(bias_value, half, padded)], axis=1
    )
    sides = [
        (dot(normed[j], w_qkv) + bias_qkv).astype(BF16).reshape(rows, tokens, 3 * padded)
        for j in range(seq_count)
    ]
    out_pair, lse_pair = attend(1, sides, need, seg_col, seg_row, heads)
    other_half = swap(out_pair, "seq", 1)
    out_own, lse_own = attend(0, sides, need, seg_col, seg_row, heads)
    own_cut = out_own.reshape(flat, padded)[:, :half]
    other_cut = other_half.reshape(flat, padded)[:, :half]
    attended = jnp.where(
        is_first,
        jnp.concatenate([own_cut, other_cut], axis=1),
        jnp.concatenate([other_cut, own_cut], axis=1),
    )
    w_out_mine = assemble(parts_out, me)
    w_out_other = swap(w_out_mine, "seq", 1)
    w_out = jnp.where(
        is_first,
        jnp.concatenate([w_out_mine[:, :out_cut], w_out_other], axis=1),
        jnp.concatenate([w_out_other[:, :out_cut], w_out_mine], axis=1),
    )
    middle = inputs.astype(F32) + dot(attended, w_out) + bias_output
    second = norm(middle, gain_two, shift_two)
    second_pair = swap(second, "seq", 1)
    w_hidden = assemble(parts_hidden, me)
    bias_hidden = my_half(hidden_bias.astype(F32)[None], ff_half, ff_half)
    act_own, slope_own = hidden(second, w_hidden, bias_hidden)
    act_pair, slope_pair = hidden(second_pair, w_hidden, bias_hidden)
    w_down = assemble(parts_down, me)
    down_pair = dot(act_pair, w_down, NT).astype(BF16)
    down_back = swap(down_pair, "seq", 1)
    result = middle + dot(act_own, w_down, NT) + down_back.astype(F32) + bias_down
    layer_output = result.astype(BF16).reshape(rows, tokens, width)

    grad_down = weight_grad([incoming, incoming_pair], [act_own, act_pair], me, shards)
    pre_pair = (dot(incoming_pair, w_down) * slope_pair.astype(F32)).astype(BF16)
    back_pair = dot(pre_pair, w_hidden, NT).astype(BF16)
    back_other = swap(back_pair, "seq", 1)
    pre_own = (dot(incoming, w_down) * slope_own.astype(F32)).astype(BF16)
    back_own = dot(pre_own, w_hidden, NT)
    sum_down = scatter_sum(grad_down)
    grad_hidden = weight_grad([second, second_pair], [pre_own, pre_pair], me, shards)
    sum_hidden = scatter_sum(grad_hidden)
    grad_hidden_bias = column_sum(pre_own) + column_sum(pre_pair)
    grad_middle, branch, grad_gain_two, grad_shift_two = norm_back(
        middle, back_own, back_other, gain_two, incoming
    )
    grad_attended = dot(branch, w_out, NT).astype(BF16)
    grad_first, grad_second = grad_attended[:, :half], grad_attended[:, half:]
    grow = ((0, 0), (0, padded - half))
    grad_mine = jnp.pad(jnp.where(is_first, grad_first, grad_second), grow)
    grad_send = jnp.pad(jnp.where(is_first, grad_second, grad_first), grow)
    grad_pair = swap(grad_send, "seq", 1)
    partial_out = weight_grad([attended], [branch], me, shards)
    out_mine = jnp.where(is_first, partial_out[..., :out_cols], partial_out[..., out_cut:])
    out_send = jnp.where(is_first, partial_out[..., out_cut:], partial_out[..., :out_cols])
    out_back = swap(out_send, "seq", 1)
    grad_out = (out_mine.astype(F32) + out_back.astype(F32)).astype(BF16)
    sum_out = scatter_sum(grad_out)
    shape = (rows, tokens, padded)
    grad_sides = attend_back(
        sides,
        [grad_mine.reshape(shape), grad_pair.reshape(shape)],
        [out_own, out_pair],
        [lse_own, lse_pair],
        need,
        seg_col,
        seg_row,
        heads,
    )
    grad_sides = [g.reshape(flat, g.shape[-1]) for g in grad_sides]
    w_kv = w_qkv[:, padded:]
    grad_query = weight_grad(
        [normed[0], normed[1]], [grad_sides[0], grad_sides[1]], me, shards, 0, padded
    )
    far = [jnp.pad(grad_sides[j], ((0, 0), (padded, 0))) for j in range(2, seq_count)]
    grad_kv = weight_grad(
        [normed[j] for j in range(seq_count)], grad_sides[:2] + far, me, shards, padded, 2 * padded
    )
    sum_query = scatter_sum(grad_query)
    sum_kv = scatter_sum(grad_kv)
    back = {
        j: dot(grad_sides[j], w_qkv if j < 2 else w_kv, NT) for j in reversed(range(seq_count))
    }
    for bit in reversed(bits_of(seq_count)):
        kept = {j: part for j, part in back.items() if not j & bit}
        if bit == bits_of(seq_count)[0]:
            last = swap(back[bit].astype(BF16), "seq", bit)
            back = kept
        else:
            back = {j: part + swap(back[j | bit].astype(BF16), "seq", bit) for j, part in kept.items()}
    grad_patches, _, grad_gain_one, grad_shift_one = norm_back(
        inputs, back[0], last, gain_one, grad_middle
    )

    def widen(vector, size):
        own = vector[None, :size]
        none = jnp.zeros_like(own)
        return jnp.where(
            is_first, jnp.concatenate([own, none], axis=1), jnp.concatenate([none, own], axis=1)
        )

    grad_bias_query = sum(column_sum(grad_sides[j][:, :padded]) for j in range(2))
    grad_bias_value = sum(column_sum(grad_sides[j][:, -padded:]) for j in range(seq_count))
    lines = [
        grad_gain_one,
        grad_shift_one,
        widen(grad_bias_query, half),
        widen(grad_bias_value, half),
        column_sum(branch)[None],
        grad_gain_two,
        grad_shift_two,
        column_sum(incoming)[None],
    ]
    bundle = jnp.concatenate(
        [jnp.concatenate(lines, axis=1), widen(grad_hidden_bias, ff_half)], axis=1
    )
    for axis in ("seq", "fsdp"):
        for bit in bits_of(lax.axis_size(axis)):
            bundle = bundle + swap(bundle, axis, bit)
    own_width = width // shards
    own_vectors = [
        lax.dynamic_slice_in_dim(bundle[0, i * width : (i + 1) * width], me * own_width, own_width, 0)
        for i in range(8)
    ]
    hidden_total = bundle[0, 8 * width : 8 * width + ff]

    def whole(mine, size, total):
        other = swap(mine, "seq", 1)
        return jnp.where(
            is_first,
            jnp.concatenate([mine[:, :size], other[:, : total - size]], axis=1),
            jnp.concatenate([other[:, :size], mine[:, : total - size]], axis=1),
        )

    full_query = whole(sum_query, half, width)
    full_key = whole(sum_kv[:, :padded], half, width)
    full_value = whole(sum_kv[:, padded:], half, width)
    full_hidden = whole(sum_hidden, ff_half, ff)
    full_down = whole(sum_down, ff_half, ff).T
    other_out = swap(sum_out, "seq", 1)
    full_out = jnp.where(
        is_first,
        jnp.concatenate([sum_out[:, :out_cut], other_out], axis=1),
        jnp.concatenate([other_out[:, :out_cut], sum_out], axis=1),
    )
    return (
        layer_output,
        grad_patches.reshape(rows, tokens, width),
        own_vectors[0],
        own_vectors[1],
        full_query,
        own_vectors[2],
        full_key,
        full_value,
        own_vectors[3],
        full_out,
        own_vectors[4],
        own_vectors[5],
        own_vectors[6],
        full_hidden,
        hidden_total,
        full_down,
        own_vectors[7],
    )


def solution(mesh):
    shard, line, tokens = P("fsdp", None), P("fsdp"), P("fsdp", "seq", None)
    in_specs = (
        tokens,
        shard,
        line,
        line,
        shard,
        line,
        shard,
        shard,
        line,
        shard,
        line,
        line,
        line,
        shard,
        P(),
        P(None, "fsdp"),
        line,
        tokens,
    )
    out_specs = (
        tokens,
        tokens,
        line,
        line,
        shard,
        line,
        shard,
        shard,
        line,
        shard,
        line,
        line,
        line,
        shard,
        P(),
        P(None, "fsdp"),
        line,
    )
    return jax.shard_map(local, mesh=mesh, in_specs=in_specs, out_specs=out_specs, check_vma=False)
```

```python
import functools
import math

import jax
import jax.numpy as jnp
from jax import lax
from jax.experimental import pallas as pl
from jax.experimental.pallas import tpu as pltpu
from jax.sharding import PartitionSpec as P

HEAD_DIM = 72
EPS = 1e-06
GELU_COEF = math.sqrt(2.0 / math.pi)
MASKED = -1e30
F32 = jnp.float32
BF16 = jnp.bfloat16
SCALE = 1.0 / math.sqrt(HEAD_DIM)
WIN = 256
LOG2E = math.log2(math.e)
VMEM = 60 << 20


def round_up(value, step):
    return (value + step - 1) // step * step


def dot(left, right, dims=((1,), (0,))):
    return lax.dot_general(left, right, (dims, ((), ())), preferred_element_type=F32)


NT = ((1,), (1,))
TN = ((0,), (0,))


def params(semantics):
    return pltpu.CompilerParams(dimension_semantics=semantics, vmem_limit_bytes=VMEM)


def swap(array, axis, bits):
    size = lax.axis_size(axis)
    return lax.ppermute(array, axis, [(i, i ^ bits) for i in range(size)])


def bits_of(size):
    return [1 << k for k in reversed(range(size.bit_length() - 1))]


def after(value, *earlier):
    return lax.optimization_barrier((value,) + tuple(earlier))[0]


class Chain:
    def __init__(self):
        self.last = ()

    def __call__(self, *values, wait=()):
        held = lax.optimization_barrier(tuple(values) + tuple(self.last) + tuple(wait))
        return held[: len(values)] if len(values) > 1 else held[0]

    def done(self, *results):
        self.last = results
        return results if len(results) > 1 else results[0]


def gather_all(shard):
    parts = {0: shard}
    for bit in bits_of(lax.axis_size("fsdp")):
        parts.update({d | bit: swap(part, "fsdp", bit) for d, part in list(parts.items())})
    return parts


def gather_direct(shard):
    return {0: shard} | {d: swap(shard, "fsdp", d) for d in range(1, lax.axis_size("fsdp"))}


def in_order(parts, me):
    count = len(parts)
    return jnp.take(jnp.stack([parts[d] for d in range(count)]), me ^ jnp.arange(count), axis=0)


def rel_position(distance, count):
    width = count.bit_length() - 1
    return sum(((distance >> k) & 1) << (width - 1 - k) for k in range(width))


def scatter_step(keep, arrived, rows):
    size = keep.shape[0]
    if size == rows:
        return (keep.astype(F32) + arrived.astype(F32)).astype(BF16), None
    return [
        (keep[part].astype(F32) + arrived[part].astype(F32)).astype(BF16)
        for part in (slice(0, size // 2), slice(size // 2, size))
    ]


def seq_sum(mine):
    for bit in bits_of(lax.axis_size("seq"))[:-1]:
        total = mine.astype(F32) + swap(mine, "seq", bit).astype(F32)
        mine = total.astype(BF16)
    return total


def assemble_kernel(count, rows, single, off_ref, *refs):
    outs = refs[count:]

    def fill(out_ref):
        for distance in range(count):
            start = pl.multiple_of(off_ref[distance], 16)
            out_ref[pl.ds(start, rows), :] = refs[distance][...]

    if single:
        fill(outs[0])
    else:
        pl.when(pl.program_id(0) == 0)(lambda: fill(outs[0]))
        pl.when(pl.program_id(0) > 0)(lambda: fill(outs[1]))


def assemble(parts, me, cut=None):
    count = len(parts)
    rows, cols = parts[0].shape
    if rows % 16:
        full = in_order(parts, me).reshape(count * rows, cols)
        return (full[:, :cut], full[:, cut:]) if cut else full
    offsets = ((me ^ jnp.arange(count, dtype=jnp.int32)) * rows).astype(jnp.int32)
    tile = cut or min(cols, 1152)
    widths = [cut, cols - cut] if cut else [cols]
    maps = [lambda n, off: (0, 0), lambda n, off: (0, jnp.maximum(n - 1, 0))]
    if not cut:
        maps = [lambda n, off: (0, n)]
    outs = pl.pallas_call(
        functools.partial(assemble_kernel, count, rows, not cut),
        out_shape=[jax.ShapeDtypeStruct((count * rows, w), parts[0].dtype) for w in widths],
        grid_spec=pltpu.PrefetchScalarGridSpec(
            num_scalar_prefetch=1,
            grid=(pl.cdiv(cols, tile),),
            in_specs=[pl.BlockSpec((rows, tile), lambda n, off: (0, n))] * count,
            out_specs=[pl.BlockSpec((count * rows, tile), m) for m in maps],
        ),
        compiler_params=params(("arbitrary",)),
        cost_estimate=pl.CostEstimate(
            flops=0, transcendentals=0, bytes_accessed=4 * count * rows * cols
        ),
        name="assemble",
    )(offsets, *[parts[d] for d in range(count)])
    return outs if cut else outs[0]


def weight_grad_kernel(pairs, count, rows, pos_ref, *refs):
    lefts, rights = refs[:pairs], refs[pairs : 2 * pairs]
    keep_ref, send_ref = refs[2 * pairs : 2 * pairs + 2]
    total = dot(lefts[0][...], rights[0][...], TN)
    for i in range(1, pairs):
        total += dot(lefts[i][...], rights[i][...], TN)
    for shard in range(count):
        start = pl.multiple_of(pos_ref[shard], 16)
        block = total[shard * rows : (shard + 1) * rows].astype(BF16)

        @pl.when(pos_ref[count] == shard % 2)
        def _():
            keep_ref[pl.ds(start, rows), :] = block

        @pl.when(pos_ref[count] != shard % 2)
        def _():
            send_ref[pl.ds(start, rows), :] = block


def weight_grad(lefts, rights, me, count):
    width = lefts[0].shape[1]
    cols = rights[0].shape[1]
    rows = width // count
    order = me ^ jnp.arange(count, dtype=jnp.int32)
    table = jnp.array([rel_position(d, count) for d in range(count)], jnp.int32)
    half = count // 2
    if rows % 16:
        total = sum(dot(a, b, TN) for a, b in zip(lefts, rights))
        by_distance = jnp.take(total.astype(BF16).reshape(count, rows, cols), order, axis=0)
        back = [0] * count
        for d in range(count):
            back[rel_position(d, count)] = d
        placed = jnp.take(by_distance, jnp.array(back), axis=0).reshape(width, cols)
        return placed[: width // 2], placed[width // 2 :]
    positions = jnp.concatenate([table[order] % half * rows, (me & 1)[None]]).astype(jnp.int32)
    tile = 256
    pairs = len(lefts)
    flops = sum(2 * a.shape[0] * width * cols for a in lefts)
    moved = sum(2 * a.shape[0] * (width + cols) for a in lefts) + 2 * width * cols
    return pl.pallas_call(
        functools.partial(weight_grad_kernel, pairs, count, rows),
        out_shape=[jax.ShapeDtypeStruct((width // 2, cols), BF16)] * 2,
        grid_spec=pltpu.PrefetchScalarGridSpec(
            num_scalar_prefetch=1,
            grid=(pl.cdiv(cols, tile),),
            in_specs=[
                pl.BlockSpec(a.shape, lambda n, off: (0, 0), pipeline_mode=pl.Buffered(1))
                for a in lefts
            ]
            + [pl.BlockSpec((b.shape[0], tile), lambda n, off: (0, n)) for b in rights],
            out_specs=[pl.BlockSpec((width // 2, tile), lambda n, off: (0, n))] * 2,
        ),
        compiler_params=params(("arbitrary",)),
        cost_estimate=pl.CostEstimate(flops=flops, transcendentals=0, bytes_accessed=moved),
        name="weight_grad",
    )(positions, *lefts, *rights)


def normalized(values):
    center = values - jnp.mean(values, axis=-1, keepdims=True)
    spread = jnp.mean(center * center, axis=-1, keepdims=True)
    inverse = lax.rsqrt(spread + EPS)
    return center * inverse, inverse


def row_block(rows):
    return 256 if rows % 256 == 0 else 128 if rows % 128 == 0 else rows


def norm_kernel(steps, x_refs, gain_ref, shift_ref, out_ref):
    for i, x_ref in enumerate(x_refs):

        @pl.when(pl.program_id(0) // steps == i)
        def _():
            hat, _ = normalized(x_ref[...].astype(F32))
            out_ref[...] = (hat * gain_ref[...] + shift_ref[...]).astype(BF16)


def norm(arrays, gain, shift):
    rows, width = arrays[0].shape
    block = row_block(rows)
    steps, count = rows // block, len(arrays)

    def kernel(*refs):
        norm_kernel(steps, refs[:count], *refs[count:])

    line = pl.BlockSpec((1, width), lambda i: (0, 0))
    return pl.pallas_call(
        kernel,
        out_shape=jax.ShapeDtypeStruct((count * rows, width), BF16),
        grid=(count * steps,),
        in_specs=[
            pl.BlockSpec((block, width), lambda i, k=k: (jnp.clip(i - k * steps, 0, steps - 1), 0))
            for k in range(count)
        ]
        + [line, line],
        out_specs=pl.BlockSpec((block, width), lambda i: (i, 0)),
        compiler_params=params(("arbitrary",)),
        cost_estimate=pl.CostEstimate(
            flops=10 * count * rows * width, transcendentals=0, bytes_accessed=4 * count * rows * width
        ),
        name="norm",
    )(*arrays, gain, shift)


def join_kernel(half, core_ref, own_ref, other_ref, x_ref, w_ref, b_ref, g_ref, s_ref, *outs):
    att_ref, mid_ref, out_ref = outs
    own, other = own_ref[:, :half], other_ref[:, :half]

    @pl.when(core_ref[0] == 0)
    def _():
        att_ref[...] = jnp.concatenate([own, other], axis=1)

    @pl.when(core_ref[0] != 0)
    def _():
        att_ref[...] = jnp.concatenate([other, own], axis=1)

    middle = x_ref[...].astype(F32) + dot(att_ref[...], w_ref[...]) + b_ref[...]
    mid_ref[...] = middle
    hat, _ = normalized(middle)
    out_ref[...] = (hat * g_ref[...] + s_ref[...]).astype(BF16)


def join(core, own, other, inputs, weight, bias, gain, shift, half):
    rows, width = inputs.shape
    padded = own.shape[1]
    block = row_block(rows)
    line = pl.BlockSpec((1, width), lambda i, c: (0, 0))
    wide = pl.BlockSpec((block, width), lambda i, c: (i, 0))
    part = pl.BlockSpec((block, padded), lambda i, c: (i, 0))
    return pl.pallas_call(
        functools.partial(join_kernel, half),
        out_shape=(
            jax.ShapeDtypeStruct((rows, width), BF16),
            jax.ShapeDtypeStruct((rows, width), F32),
            jax.ShapeDtypeStruct((rows, width), BF16),
        ),
        grid_spec=pltpu.PrefetchScalarGridSpec(
            num_scalar_prefetch=1,
            grid=(rows // block,),
            in_specs=[
                part,
                part,
                wide,
                pl.BlockSpec((width, width), lambda i, c: (0, 0), pipeline_mode=pl.Buffered(1)),
                line,
                line,
                line,
            ],
            out_specs=(wide, wide, wide),
        ),
        compiler_params=params(("arbitrary",)),
        cost_estimate=pl.CostEstimate(
            flops=2 * rows * width * width, transcendentals=0, bytes_accessed=14 * rows * width
        ),
        name="join",
    )(core, own, other, inputs, weight, bias, gain, shift)


def norm_back_values(x_ref, grads, gain_ref, add_ref, dg_ref, ds_ref):
    hat, inverse = normalized(x_ref[...].astype(F32))
    grad = grads[0][...].astype(F32)
    for other in grads[1:]:
        grad += other[...].astype(F32)
    scaled = grad * gain_ref[...]
    first = jnp.mean(scaled, axis=-1, keepdims=True)
    second = jnp.mean(scaled * hat, axis=-1, keepdims=True)

    @pl.when(pl.program_id(0) == 0)
    def _():
        dg_ref[...] = jnp.zeros_like(dg_ref)
        ds_ref[...] = jnp.zeros_like(ds_ref)

    dg_ref[...] += jnp.sum(grad * hat, axis=0, keepdims=True)
    ds_ref[...] += jnp.sum(grad, axis=0, keepdims=True)
    return add_ref[...].astype(F32) + inverse * (scaled - first - hat * second)


def first_back(values, grads, gain, add):
    rows, width = values.shape
    block = row_block(rows)
    count = len(grads)

    def kernel(x_ref, *refs):
        gain_ref, add_ref, dx_ref, dg_ref, ds_ref = refs[count:]
        dx_ref[...] = norm_back_values(x_ref, refs[:count], gain_ref, add_ref, dg_ref, ds_ref)

    wide = pl.BlockSpec((block, width), lambda i: (i, 0))
    line = pl.BlockSpec((1, width), lambda i: (0, 0))
    return pl.pallas_call(
        kernel,
        out_shape=(
            jax.ShapeDtypeStruct((rows, width), F32),
            jax.ShapeDtypeStruct((1, width), F32),
            jax.ShapeDtypeStruct((1, width), F32),
        ),
        grid=(rows // block,),
        in_specs=[wide] * (1 + count) + [line, wide],
        out_specs=(wide, line, line),
        compiler_params=params(("arbitrary",)),
        cost_estimate=pl.CostEstimate(
            flops=20 * rows * width, transcendentals=0, bytes_accessed=18 * rows * width
        ),
        name="first_back",
    )(values, *grads, gain, add)


def second_back(core, values, grads, gain, add, weight, half, padded):
    rows, width = values.shape
    block = row_block(rows)
    count = len(grads)

    def kernel(core_ref, x_ref, *refs):
        gain_ref, add_ref, w_ref, dx_ref, low_ref, mine_ref, send_ref, db_ref, dg_ref, ds_ref = refs[count:]
        total = norm_back_values(x_ref, refs[:count], gain_ref, add_ref, dg_ref, ds_ref)
        low = total.astype(BF16)
        dx_ref[...] = total
        low_ref[...] = low

        @pl.when(pl.program_id(0) == 0)
        def _():
            db_ref[...] = jnp.zeros_like(db_ref)

        db_ref[...] += jnp.sum(low.astype(F32), axis=0, keepdims=True)
        back = dot(low, w_ref[...], NT).astype(BF16)
        empty = jnp.zeros((block, padded - half), BF16)
        halves = [jnp.concatenate([back[:, i * half : (i + 1) * half], empty], axis=1) for i in range(2)]

        @pl.when(core_ref[0] == 0)
        def _():
            mine_ref[...], send_ref[...] = halves[0], halves[1]

        @pl.when(core_ref[0] != 0)
        def _():
            mine_ref[...], send_ref[...] = halves[1], halves[0]

    wide = pl.BlockSpec((block, width), lambda i, c: (i, 0))
    part = pl.BlockSpec((block, padded), lambda i, c: (i, 0))
    line = pl.BlockSpec((1, width), lambda i, c: (0, 0))
    square = pl.BlockSpec((width, width), lambda i, c: (0, 0), pipeline_mode=pl.Buffered(1))
    return pl.pallas_call(
        kernel,
        out_shape=(
            jax.ShapeDtypeStruct((rows, width), F32),
            jax.ShapeDtypeStruct((rows, width), BF16),
            jax.ShapeDtypeStruct((rows, padded), BF16),
            jax.ShapeDtypeStruct((rows, padded), BF16),
            jax.ShapeDtypeStruct((1, width), F32),
            jax.ShapeDtypeStruct((1, width), F32),
            jax.ShapeDtypeStruct((1, width), F32),
        ),
        grid_spec=pltpu.PrefetchScalarGridSpec(
            num_scalar_prefetch=1,
            grid=(rows // block,),
            in_specs=[wide] * (1 + count) + [line, wide, square],
            out_specs=(wide, wide, part, part, line, line, line),
        ),
        compiler_params=params(("arbitrary",)),
        cost_estimate=pl.CostEstimate(
            flops=2 * rows * width * width, transcendentals=0, bytes_accessed=20 * rows * width
        ),
        name="second_back",
    )(core, values, *grads, gain, add, weight)


def hidden(arrays, weight, bias):
    rows, width = arrays[0].shape
    cols = weight.shape[1]
    block = row_block(rows)
    steps, count = rows // block, len(arrays)

    def kernel(*refs):
        w_ref, b_ref, act_ref, slope_ref, x_ref = refs[count:]
        for i in range(count):

            @pl.when(pl.program_id(0) // steps == i)
            def _():
                x_ref[...] = refs[i][...]

        pre = dot(x_ref[...], w_ref[...]) + b_ref[...]
        square = pre * pre
        turn = jnp.tanh(pre * (GELU_COEF + GELU_COEF * 0.044715 * square))
        act_ref[...] = (0.5 * pre * (1.0 + turn)).astype(BF16)
        inner = GELU_COEF + 3.0 * 0.044715 * GELU_COEF * square
        slope_ref[...] = (0.5 * (1.0 + turn) * (1.0 + pre * (1.0 - turn) * inner)).astype(BF16)

    out = pl.BlockSpec((block, cols), lambda i: (i, 0))
    return pl.pallas_call(
        kernel,
        out_shape=(
            jax.ShapeDtypeStruct((count * rows, cols), BF16),
            jax.ShapeDtypeStruct((count * rows, cols), BF16),
            jax.ShapeDtypeStruct((count * rows, width), BF16),
        ),
        grid=(count * steps,),
        in_specs=[
            pl.BlockSpec((block, width), lambda i, k=k: (jnp.clip(i - k * steps, 0, steps - 1), 0))
            for k in range(count)
        ]
        + [
            pl.BlockSpec((width, cols), lambda i: (0, 0), pipeline_mode=pl.Buffered(1)),
            pl.BlockSpec((1, cols), lambda i: (0, 0)),
        ],
        out_specs=(out, out, pl.BlockSpec((block, width), lambda i: (i, 0))),
        compiler_params=params(("arbitrary",)),
        cost_estimate=pl.CostEstimate(
            flops=2 * count * rows * width * cols,
            transcendentals=count * rows * cols,
            bytes_accessed=2 * (2 * count * rows * width + width * cols + 2 * count * rows * cols),
        ),
        name="hidden",
    )(*arrays, weight, bias)


def head_window(head):
    first = head * HEAD_DIM
    start = first // 128 * 128
    return start, round_up(first + HEAD_DIM, 128) - start, first - start


def head_lanes(rows, width, low):
    lane = lax.broadcasted_iota(jnp.int32, (rows, width), 1)
    return (lane >= low) & (lane < low + HEAD_DIM)


def only_head(block, low):
    mine = head_lanes(*block.shape, low)
    return jnp.where(mine, block.astype(F32), 0.0).astype(BF16)


def pick_block(near_ref, far_ref, block):
    return near_ref.at[block, 0] if block < 2 else far_ref.at[block - 2, 0]


def attend_kernel(row, heads, blocks, padded, need_ref, col_ref, row_ref, q_ref, near_ref, far_ref, *refs):
    own_ref, pair_ref, lse_ref, queries, score, peak, total, acc, lses = refs[-9:]
    outs = (own_ref, pair_ref)
    tokens = own_ref.shape[1]
    slot = lax.broadcasted_iota(jnp.int32, (2 * tokens, 128), 1)
    for which in range(2):
        outs[which][...] = jnp.zeros_like(outs[which])
    windows = [head_window(head) for head in range(heads)]
    for head, (start, width, low) in enumerate(windows):
        for which in range(2):
            queries[head, which * tokens : (which + 1) * tokens, :width] = only_head(
                q_ref[which, 0, :, start : start + width], low
            )
    peak[...] = jnp.full_like(peak, MASKED)
    total[...] = jnp.zeros_like(total)
    acc[...] = jnp.zeros_like(acc)
    for block in range(blocks):

        @pl.when(need_ref[row, block] != 0)
        def _():
            side = pick_block(near_ref, far_ref, block)
            seen = col_ref[0] == row_ref[0, block : block + 1]
            for head, (start, width, _) in enumerate(windows):
                key = side[:, start : start + width]
                found = jnp.where(seen, dot(queries[head, :, :width], key, NT), MASKED)
                score[head, block] = found
                top = peak[head]
                for at in range(0, tokens, 128):
                    top = jnp.maximum(top, found[:, at : at + 128])
                peak[head] = top

    for head in range(heads):
        top = jnp.max(peak[head], axis=-1, keepdims=True) * (SCALE * LOG2E)
        peak[head] = jnp.broadcast_to(top, peak.shape[1:])

    for block in range(blocks):

        @pl.when(need_ref[row, block] != 0)
        def _():
            side = pick_block(near_ref, far_ref, block)
            for head, (start, width, _) in enumerate(windows):
                top, share = peak[head], total[head]
                pieces = []
                for at in range(0, tokens, 128):
                    part = jnp.exp2(score[head, block, :, at : at + 128] * (SCALE * LOG2E) - top)
                    share += part
                    pieces.append(part.astype(BF16))
                total[head] = share
                value = side[:, padded + start : padded + start + width]
                acc[head, :, :width] += dot(jnp.concatenate(pieces, axis=1), value)

    for head, (start, width, low) in enumerate(windows):
        norm = jnp.sum(total[head], axis=-1, keepdims=True)
        result = acc[head, :, :width] / norm
        mine = head_lanes(tokens, width, low)
        for which in range(2):
            kept = outs[which][0, :, start : start + width].astype(F32)
            fresh = result[which * tokens : (which + 1) * tokens]
            outs[which][0, :, start : start + width] = jnp.where(mine, fresh, kept).astype(BF16)
        lse = peak[head] + jnp.log2(norm)
        lses[...] = lse if head == 0 else jnp.where(slot == head, lse, lses[...])
    lse_ref[0] = lses[...].T[:heads]


def attend(row, query, near, far, need, seg_col, seg_row, heads, before):
    _, rows, tokens, padded = query.shape
    blocks = 2 + far.shape[0]
    cost = 2 * heads * blocks * tokens * tokens
    narrow = pl.BlockSpec((1, tokens, padded), lambda i, need: (row, 0, 0))
    lines = pl.BlockSpec((1, heads, 2 * tokens), lambda i, need: (row, 0, 0))

    def stack(count, width):
        return pl.BlockSpec((count, 1, tokens, width), lambda i, need: (0, row, 0, 0))

    return pl.pallas_call(
        functools.partial(attend_kernel, row, heads, blocks, padded),
        out_shape=(
            jax.ShapeDtypeStruct((rows, tokens, padded), BF16),
            jax.ShapeDtypeStruct((rows, tokens, padded), BF16),
            jax.ShapeDtypeStruct((rows, heads, 2 * tokens), F32),
        ),
        grid_spec=pltpu.PrefetchScalarGridSpec(
            num_scalar_prefetch=1,
            grid=(1,),
            in_specs=[
                pl.BlockSpec((1, 2 * tokens, 1), lambda i, need: (row, 0, 0)),
                pl.BlockSpec((1, blocks, tokens), lambda i, need: (row, 0, 0)),
                stack(2, padded),
                stack(2, 2 * padded),
                stack(blocks - 2, 2 * padded),
            ]
            + [pl.BlockSpec(memory_space=pl.ANY)] * len(before),
            out_specs=(narrow, narrow, lines),
            scratch_shapes=[
                pltpu.VMEM((heads, 2 * tokens, WIN), BF16),
                pltpu.VMEM((heads, blocks, 2 * tokens, tokens), F32),
                pltpu.VMEM((heads, 2 * tokens, 128), F32),
                pltpu.VMEM((heads, 2 * tokens, 128), F32),
                pltpu.VMEM((heads, 2 * tokens, WIN), F32),
                pltpu.VMEM((2 * tokens, 128), F32),
            ],
        ),
        input_output_aliases={6 + i: i for i in range(len(before))},
        compiler_params=params(("arbitrary",)),
        cost_estimate=pl.CostEstimate(
            flops=8 * cost * WIN,
            transcendentals=cost,
            bytes_accessed=6 * blocks * tokens * padded,
        ),
        name="attend",
    )(need, seg_col, seg_row, query, near, far, *before)


def attend_back_kernel(
    row, heads, blocks, padded, need_ref, col_ref, row_ref, pick_ref, q_ref, near_ref, far_ref, *refs
):
    grads, outs, lse_ref = refs[0:2], refs[2:4], refs[4]
    dq_ref, dnear_ref, dfar_ref, sums, inner_turn, queries, incoming, dq = refs[-8:]
    tokens = grads[0].shape[1]
    sums[...] = jnp.zeros_like(sums)
    for which in range(2):
        dq_ref[which, 0] = jnp.zeros((tokens, padded), BF16)
        product = grads[which][0].astype(F32) * outs[which][0].astype(F32)
        high = product.astype(BF16)
        rest = (product - high.astype(F32)).astype(BF16)
        inner_turn[:, which * tokens : (which + 1) * tokens] = dot(pick_ref[...], high, NT) + dot(
            pick_ref[...], rest, NT
        )
    windows = [head_window(head) for head in range(heads)]
    for head, (start, width, low) in enumerate(windows):
        for which in range(2):
            there = slice(which * tokens, (which + 1) * tokens)
            here = slice(start, start + width)
            queries[head, there, :width] = only_head(q_ref[which, 0, :, here], low)
            incoming[head, there, :width] = only_head(grads[which][0, :, here], low)
    dq[...] = jnp.zeros_like(dq)
    for block in range(blocks):

        @pl.when(need_ref[row, block] != 0)
        def _():
            side = pick_block(near_ref, far_ref, block)
            seen = col_ref[0, block] == row_ref[0]
            for head, (start, width, _) in enumerate(windows):
                end = start + width
                key, value = side[:, start:end], side[:, padded + start : padded + end]
                query, grad = queries[head, :, :width], incoming[head, :, :width]
                found = dot(key, query, NT) * (SCALE * LOG2E) - lse_ref[0, head : head + 1, :]
                prob = jnp.where(seen, jnp.exp2(found), 0.0)
                inner = inner_turn[head : head + 1, :]
                slope = (prob * (dot(value, grad, NT) - inner)).astype(BF16)
                sums[block, :, start:end] += dot(slope, query)
                sums[block, :, padded + start : padded + end] += dot(prob.astype(BF16), grad)
                dq[head, :, :width] += dot(slope, key, TN)

    for head, (start, width, low) in enumerate(windows):
        mine = head_lanes(tokens, width, low)
        for which in range(2):
            kept = dq_ref[which, 0, :, start : start + width].astype(F32)
            fresh = dq[head, which * tokens : (which + 1) * tokens, :width] * SCALE
            dq_ref[which, 0, :, start : start + width] = jnp.where(mine, fresh, kept).astype(BF16)
    for block in range(blocks):
        side = pick_block(dnear_ref, dfar_ref, block)
        side[:, :padded] = (sums[block, :, :padded] * SCALE).astype(BF16)
        side[:, padded:] = sums[block, :, padded:].astype(BF16)


def attend_back(row, query, near, far, grads, outs, lse, need, seg_col, seg_row, heads, before):
    _, rows, tokens, padded = query.shape
    blocks = 2 + far.shape[0]
    cost = 2 * heads * blocks * tokens * tokens
    column = lax.broadcasted_iota(jnp.int32, (heads, padded), 1)
    pick = (column // HEAD_DIM == lax.broadcasted_iota(jnp.int32, (heads, padded), 0)).astype(BF16)
    narrow = pl.BlockSpec((1, tokens, padded), lambda i, need: (row, 0, 0))

    def stack(count, width):
        return pl.BlockSpec((count, 1, tokens, width), lambda i, need: (0, row, 0, 0))

    return pl.pallas_call(
        functools.partial(attend_back_kernel, row, heads, blocks, padded),
        out_shape=tuple(jax.ShapeDtypeStruct(a.shape, BF16) for a in (query, near, far)),
        grid_spec=pltpu.PrefetchScalarGridSpec(
            num_scalar_prefetch=1,
            grid=(1,),
            in_specs=[
                pl.BlockSpec((1, blocks, tokens, 1), lambda i, need: (row, 0, 0, 0)),
                pl.BlockSpec((1, 1, 2 * tokens), lambda i, need: (row, 0, 0)),
                pl.BlockSpec((heads, padded), lambda i, need: (0, 0)),
                stack(2, padded),
                stack(2, 2 * padded),
                stack(blocks - 2, 2 * padded),
            ]
            + [narrow] * 4
            + [pl.BlockSpec((1, heads, 2 * tokens), lambda i, need: (row, 0, 0))]
            + [pl.BlockSpec(memory_space=pl.ANY)] * len(before),
            out_specs=(stack(2, padded), stack(2, 2 * padded), stack(blocks - 2, 2 * padded)),
            scratch_shapes=[
                pltpu.VMEM((blocks, tokens, 2 * padded), F32),
                pltpu.VMEM((heads, 2 * tokens), F32),
                pltpu.VMEM((heads, 2 * tokens, WIN), BF16),
                pltpu.VMEM((heads, 2 * tokens, WIN), BF16),
                pltpu.VMEM((heads, 2 * tokens, WIN), F32),
            ],
        ),
        input_output_aliases={12 + i: i for i in range(len(before))},
        compiler_params=params(("arbitrary",)),
        cost_estimate=pl.CostEstimate(
            flops=20 * cost * WIN,
            transcendentals=cost,
            bytes_accessed=12 * blocks * tokens * padded,
        ),
        name="attend_back",
    )(need, seg_col, seg_row, pick, query, near, far, *grads, *outs, lse, *before)


def column_sum(array):
    return dot(jnp.ones((8, array.shape[0]), BF16), array)[:1]


def local(
    patches,
    lengths,
    first_gain,
    first_shift,
    query_weight,
    query_bias,
    key_weight,
    value_weight,
    value_bias,
    output_weight,
    output_bias,
    second_gain,
    second_shift,
    hidden_weight,
    hidden_bias,
    down_weight,
    down_bias,
    cotangent,
):
    seq_count, shards = lax.axis_size("seq"), lax.axis_size("fsdp")
    place, me = lax.axis_index("seq"), lax.axis_index("fsdp")
    core = place & 1
    is_first = core == 0
    core_flag = core[None].astype(jnp.int32)
    rows, tokens, width = patches.shape
    flat = rows * tokens
    heads = width // HEAD_DIM // 2
    half = heads * HEAD_DIM
    padded = round_up(half, 128)
    ff = hidden_bias.shape[0]
    ff_half = round_up(ff, 256) // 2
    out_cols = padded
    out_cut = width - padded
    shard_rows = width // shards
    chain = Chain()

    def my_half(array, size, padded_size):
        first, second = array[..., :size], array[..., size:]
        grow = [(0, 0)] * (array.ndim - 1)
        first = jnp.pad(first, grow + [(0, padded_size - size)])
        second = jnp.pad(second, grow + [(0, padded_size - second.shape[-1])])
        return jnp.where(is_first, first, second)

    vectors = jnp.stack(
        [
            first_gain,
            first_shift,
            query_bias,
            value_bias,
            output_bias,
            second_gain,
            second_shift,
            down_bias,
        ]
    )
    vector_parts = gather_direct(vectors)
    shard_qkv = jnp.concatenate(
        [my_half(w, half, padded) for w in (query_weight, key_weight, value_weight)], axis=1
    )
    shard_out = jnp.where(is_first, output_weight[:, :out_cols], output_weight[:, out_cut:])
    shard_hidden = my_half(hidden_weight, ff_half, ff_half)
    shard_down = my_half(down_weight.T, ff_half, ff_half)
    inputs = patches.reshape(flat, width)
    incoming = cotangent.reshape(flat, width)
    raw = {0: inputs}
    for bit in bits_of(seq_count):
        raw.update({j | bit: swap(part, "seq", bit) for j, part in list(raw.items())})
    incoming_near = jnp.concatenate([incoming, swap(incoming, "seq", 1)], axis=0)

    staged = shards == 8
    shard_qkv = after(shard_qkv, *vector_parts.values())
    if staged:
        q = {0: shard_qkv}
        q[4], q[1] = swap(q[0], "fsdp", 4), swap(q[0], "fsdp", 1)
        o = {0: after(shard_out, q[1])}
        o[1] = swap(o[0], "fsdp", 1)
        q[2], q[5] = swap(after(q[0], q[4]), "fsdp", 2), swap(q[4], "fsdp", 1)
        q[6], q[3] = swap(after(q[4], q[2]), "fsdp", 2), swap(after(q[2], q[5]), "fsdp", 1)
        o[4], o[5] = swap(after(o[0], q[6]), "fsdp", 4), swap(after(o[1], q[6]), "fsdp", 4)
        q[7] = swap(after(q[6], q[3]), "fsdp", 1)
        h = {0: after(shard_hidden, q[7])}
        h[4], h[1] = swap(h[0], "fsdp", 4), swap(h[0], "fsdp", 1)
    else:
        q, o, h = gather_all(shard_qkv), gather_all(shard_out), gather_all(shard_hidden)

    stacked = in_order(vector_parts, me).transpose(1, 0, 2).reshape(8, width).astype(F32)
    gain_one, shift_one, bias_query, bias_value, bias_output, gain_two, shift_two, bias_down = [
        stacked[i : i + 1] for i in range(8)
    ]

    block_of = place ^ jnp.arange(seq_count, dtype=jnp.int32)
    position = block_of[:, None] * tokens + jnp.arange(tokens, dtype=jnp.int32)[None, :]
    ends = jnp.cumsum(lengths, axis=-1)
    picture = jnp.sum(
        (position[None, :, :, None] >= ends[:, None, None, :]).astype(jnp.int32), axis=-1
    )
    usable = position[None] < ends[:, -1][:, None, None]
    segment = jnp.where(usable, picture, 1000 + position[None])
    low_id = jnp.min(jnp.where(usable, picture, 1 << 20), axis=-1)
    high_id = jnp.max(jnp.where(usable, picture, -1), axis=-1)
    need = (low_id[:, :2, None] <= high_id[:, None, :]) & (low_id[:, None, :] <= high_id[:, :2, None])
    need = need | jnp.eye(2, seq_count, dtype=jnp.bool_)[None]
    need = jnp.any(need, axis=1).astype(jnp.int32)
    near_flat = segment[:, :2].reshape(rows, 2 * tokens)
    seg_rows, seg_cols = segment, segment[..., None]
    seg_near_row, seg_near_col = near_flat[:, None], near_flat[..., None]

    normed_near = norm([raw[0], raw[1]], gain_one, shift_one)
    normed_far = norm([raw[j] for j in range(2, seq_count)], gain_one, shift_one)
    bias_q = my_half(bias_query, half, padded)
    bias_kv = jnp.concatenate([jnp.zeros((1, padded), F32), my_half(bias_value, half, padded)], axis=1)
    w_q, w_kv = chain.done(*assemble(q, me, padded))
    near_in, w_q, w_kv = chain(normed_near, w_q, w_kv)
    query = (dot(near_in, w_q) + bias_q).astype(BF16)
    near = (dot(near_in, w_kv) + bias_kv).astype(BF16)
    chain.done(query, near)
    if staged:
        far_in, w_kv, h[4], h[1], o[4], o[5] = chain(normed_far, w_kv, h[4], h[1], o[4], o[5])
        h[2], h[5] = swap(after(h[0], h[4]), "fsdp", 2), swap(h[4], "fsdp", 1)
        o[2], o[3] = swap(after(o[0], o[4]), "fsdp", 2), swap(after(o[1], o[4]), "fsdp", 2)
        o[6], o[7] = swap(o[4], "fsdp", 2), swap(o[5], "fsdp", 2)
    else:
        far_in = chain(normed_far)
    far = chain.done((dot(far_in, w_kv) + bias_kv).astype(BF16))
    query = query.reshape(2, rows, tokens, padded)
    near = near.reshape(2, rows, tokens, 2 * padded)
    far = far.reshape(seq_count - 2, rows, tokens, 2 * padded)
    gate = after(shard_down, *([h[4], h[1]] if staged else []))
    w_down = lax.all_gather(gate, "fsdp", axis=0, tiled=True)
    found = ()
    for row in range(rows):
        query, near, far = chain(query, near, far)
        if staged and row == 1:
            query, h[2], h[5] = chain(query, h[2], h[5])
            h[6], h[3] = swap(after(h[4], h[2]), "fsdp", 2), swap(after(h[2], h[5]), "fsdp", 1)
        if staged and row == 2:
            query, h[6], h[3] = chain(query, h[6], h[3])
            h[7] = swap(after(h[6], h[3]), "fsdp", 1)
        found = attend(row, query, near, far, need, seg_near_col, seg_rows, heads, found)
        chain.done(*found)
    out_own, out_pair, lse = found
    other_half = swap(out_pair, "seq", 1).reshape(flat, padded)
    o = dict(zip(o, chain(*o.values())))
    w_out_mine = assemble(o, me)
    w_out_other = swap(w_out_mine, "seq", 1)
    w_out = jnp.where(
        is_first,
        jnp.concatenate([w_out_mine[:, :out_cut], w_out_other], axis=1),
        jnp.concatenate([w_out_other[:, :out_cut], w_out_mine], axis=1),
    )
    attended, middle, second = join(
        core_flag,
        out_own.reshape(flat, padded),
        other_half,
        inputs,
        w_out,
        bias_output,
        gain_two,
        shift_two,
        half,
    )
    second_pair = swap(second, "seq", 1)
    chain.done(second)
    h = dict(zip(h, chain(*h.values())))
    w_hidden = chain.done(assemble(h, me))
    bias_hidden = my_half(hidden_bias.astype(F32)[None], ff_half, ff_half)
    second, second_pair, w_hidden = chain(second, second_pair, w_hidden)
    act, slope, second_near = chain.done(*hidden([second, second_pair], w_hidden, bias_hidden))

    incoming_near, act = chain(incoming_near, act)
    grad_down = chain.done(dot(incoming_near, act, TN).astype(BF16))
    part_down = lax.psum_scatter(grad_down, "fsdp", scatter_dimension=0, tiled=True)
    incoming_near, slope = chain(incoming_near, slope)
    grad_pre = chain.done((dot(incoming_near, w_down) * slope.astype(F32)).astype(BF16))
    grad_pre = chain(grad_pre)
    back = chain.done(dot(grad_pre, w_hidden, NT).astype(BF16))
    back_other = swap(back[flat:], "seq", 1)
    second_near, grad_pre = chain(second_near, grad_pre)
    grad_hidden = chain.done(dot(second_near, grad_pre, TN).astype(BF16))
    part_hidden = lax.psum_scatter(grad_hidden, "fsdp", scatter_dimension=0, tiled=True)
    back, back_other = chain(back, back_other)
    grad_middle, branch, grad_mine, grad_send, grad_bias_out, grad_gain_two, grad_shift_two = second_back(
        core_flag, middle, [back[:flat], back_other], gain_two, incoming, w_out, half, padded
    )
    chain.done(branch)
    grad_pair = swap(grad_send, "seq", 1)
    attended, branch = chain(attended, branch)
    out_keep, out_send = chain.done(*weight_grad([attended], [branch], me, shards))

    def core_part(array):
        low, high = array[:, :out_cols], array[:, out_cut:]
        return jnp.where(is_first, low, high), jnp.where(is_first, high, low)

    keep_mine, keep_other = core_part(out_keep)
    send_mine, send_other = core_part(out_send)
    keep_back, send_back = swap(keep_other, "seq", 1), swap(send_other, "seq", 1)
    grad_hidden_bias = column_sum(grad_pre)

    shape = (rows, tokens, padded)
    grads = [grad_mine.reshape(shape), grad_pair.reshape(shape)]
    found = ()
    for row in range(rows):
        query, near, far, *grads = chain(query, near, far, *grads)
        if row == 1:
            keep_back, send_back, query = chain(keep_back, send_back, query)
            out_keep = (keep_mine.astype(F32) + keep_back.astype(F32)).astype(BF16)
            out_send = (send_mine.astype(F32) + send_back.astype(F32)).astype(BF16)
            out_back = swap(out_send, "fsdp", 1)
        if row == 2:
            out_back, query = chain(out_back, query)
            out_keep, out_send = scatter_step(out_keep, out_back, shard_rows)
            out_back = swap(out_send, "fsdp", 2)
        found = attend_back(
            row,
            query,
            near,
            far,
            grads,
            [out_own, out_pair],
            lse,
            need,
            seg_cols,
            seg_near_row,
            heads,
            found,
        )
        chain.done(*found)
    dq, dnear, dfar = [g.reshape(-1, g.shape[-1]) for g in found]
    dfar, w_kv = chain(dfar, w_kv)
    back_far = chain.done(dot(dfar, w_kv, NT).astype(BF16))
    far_parts = {j: back_far[(j - 2) * flat : (j - 1) * flat] for j in range(2, seq_count)}
    far_sent = {j: swap(part, "seq", 1) for j, part in far_parts.items() if j & 1}
    normed_near, normed_far, dnear, dfar = chain(normed_near, normed_far, dnear, dfar)
    kv_keep, kv_send = weight_grad([normed_near, normed_far], [dnear, dfar], me, shards)
    chain.done(kv_keep, kv_send)
    kv_back = swap(kv_send, "fsdp", 1)
    far_sent = {j: chain(part) for j, part in far_sent.items()}
    far_sums = {
        j: (far_parts[j].astype(F32) + far_sent[j | 1].astype(F32)).astype(BF16)
        for j in far_parts
        if not j & 1
    }
    chain.done(*far_sums.values())
    arrived = []
    for bit in bits_of(seq_count)[:-1]:
        moved = {j: swap(part, "seq", bit) for j, part in far_sums.items() if j & bit}
        far_sums = {j: part for j, part in far_sums.items() if not j & bit}
        for j, part in moved.items():
            if j == bit:
                arrived.append(part)
            else:
                far_sums[j ^ bit] = (far_sums[j ^ bit].astype(F32) + part.astype(F32)).astype(BF16)
    normed_near, dq, out_back = chain(normed_near, dq, out_back)
    out_keep, out_send = scatter_step(out_keep, out_back, shard_rows)
    out_back = swap(out_send, "fsdp", 4) if out_send is not None else None
    q_keep, q_send = chain.done(*weight_grad([normed_near], [dq], me, shards))
    q_back = swap(q_send, "fsdp", 1)
    dq, dnear = chain(dq, dnear)
    back_near = chain.done((dot(dq, w_q, NT) + dot(dnear, w_kv, NT)).astype(BF16))
    pair_back = swap(back_near[flat:], "seq", 1)

    def next_bits(keep, back, bits):
        for bit in bits:
            keep, send = scatter_step(keep, back, shard_rows)
            if send is not None:
                back = swap(send, "fsdp", bit)
        return keep

    act, middle = chain(act, middle)
    down_pair = chain.done(dot(act[flat:], w_down, NT).astype(BF16))
    down_back = swap(down_pair, "seq", 1)
    rest = [2 << k for k in range(shards.bit_length() - 2)] + [0]
    kv_back, q_back = chain(kv_back, q_back)
    kv_sum = next_bits(kv_keep, kv_back, rest)
    q_sum = next_bits(q_keep, q_back, rest)
    out_sum = next_bits(out_keep, out_back, rest[2:]) if shards >= 8 else out_keep
    act, down_back = chain(act, down_back)
    result = middle + dot(act[:flat], w_down, NT) + down_back.astype(F32) + bias_down
    layer_output = chain.done(result.astype(BF16)).reshape(rows, tokens, width)
    grad_patches, grad_gain_one, grad_shift_one = first_back(
        inputs, [back_near[:flat], pair_back] + arrived, gain_one, grad_middle
    )

    def widen(own, size):
        own = own[:, :size]
        none = jnp.zeros_like(own)
        return jnp.where(
            is_first, jnp.concatenate([own, none], axis=1), jnp.concatenate([none, own], axis=1)
        )

    grad_bias_value = column_sum(dnear[:, padded:]) + column_sum(dfar[:, padded:])
    early = jnp.concatenate(
        [
            widen(column_sum(dq), half),
            widen(grad_bias_value, half),
            grad_bias_out,
            grad_gain_two,
            grad_shift_two,
            column_sum(incoming),
            widen(grad_hidden_bias, ff_half),
        ],
        axis=1,
    )
    late = jnp.concatenate([grad_gain_one, grad_shift_one], axis=1)

    def everywhere(bundle):
        for axis in ("seq", "fsdp"):
            for bit in bits_of(lax.axis_size(axis)):
                bundle = bundle + swap(bundle, axis, bit)
        return bundle

    early, late = everywhere(early), everywhere(late)

    def owned(bundle, i):
        return lax.dynamic_slice_in_dim(
            bundle[0, i * width : (i + 1) * width], me * shard_rows, shard_rows, 0
        )

    hidden_total = early[0, 6 * width : 6 * width + ff]

    def whole(mine, size, total):
        other = swap(mine, "seq", 1)
        return jnp.where(
            is_first,
            jnp.concatenate([mine[:, :size], other[:, : total - size]], axis=1),
            jnp.concatenate([other[:, :size], mine[:, : total - size]], axis=1),
        )

    full_down = whole(seq_sum(part_down), ff_half, ff).T
    full_hidden = whole(seq_sum(part_hidden), ff_half, ff)
    out_total, q_total, kv_total = seq_sum(out_sum), seq_sum(q_sum), seq_sum(kv_sum)
    other_out = swap(out_total, "seq", 1)
    full_out = jnp.where(
        is_first,
        jnp.concatenate([out_total[:, :out_cut], other_out], axis=1),
        jnp.concatenate([other_out[:, :out_cut], out_total], axis=1),
    )
    full_query = whole(q_total, half, width)
    full_key = whole(kv_total[:, :padded], half, width)
    full_value = whole(kv_total[:, padded:], half, width)
    return (
        layer_output,
        grad_patches.reshape(rows, tokens, width),
        owned(late, 0),
        owned(late, 1),
        full_query,
        owned(early, 0),
        full_key,
        full_value,
        owned(early, 1),
        full_out,
        owned(early, 2),
        owned(early, 3),
        owned(early, 4),
        full_hidden,
        hidden_total,
        full_down,
        owned(early, 5),
    )


def solution(mesh):
    shard, line, tokens = P("fsdp", None), P("fsdp"), P("fsdp", "seq", None)
    in_specs = (
        tokens,
        shard,
        line,
        line,
        shard,
        line,
        shard,
        shard,
        line,
        shard,
        line,
        line,
        line,
        shard,
        P(),
        P(None, "fsdp"),
        line,
        tokens,
    )
    out_specs = (
        tokens,
        tokens,
        line,
        line,
        shard,
        line,
        shard,
        shard,
        line,
        shard,
        line,
        line,
        line,
        shard,
        P(),
        P(None, "fsdp"),
        line,
    )
    return jax.shard_map(local, mesh=mesh, in_specs=in_specs, out_specs=out_specs, check_vma=False)
```

```python
import functools
import math

import jax
import jax.numpy as jnp
from jax import lax
from jax.experimental import pallas as pl
from jax.experimental.pallas import tpu as pltpu
from jax.sharding import PartitionSpec as P

HEAD_DIM = 72
EPS = 1e-06
GELU_COEF = math.sqrt(2.0 / math.pi)
MASKED = -1e30
F32 = jnp.float32
BF16 = jnp.bfloat16
SCALE = 1.0 / math.sqrt(HEAD_DIM)
WIN = 256
LOG2E = math.log2(math.e)
VMEM = 60 << 20


def round_up(value, step):
    return (value + step - 1) // step * step


def dot(left, right, dims=((1,), (0,))):
    return lax.dot_general(left, right, (dims, ((), ())), preferred_element_type=F32)


NT = ((1,), (1,))
TN = ((0,), (0,))


def params(semantics):
    return pltpu.CompilerParams(dimension_semantics=semantics, vmem_limit_bytes=VMEM)


def swap(array, axis, bits):
    size = lax.axis_size(axis)
    return lax.ppermute(array, axis, [(i, i ^ bits) for i in range(size)])


def bits_of(size):
    return [1 << k for k in reversed(range(size.bit_length() - 1))]


def after(value, *earlier):
    return lax.optimization_barrier((value,) + tuple(earlier))[0]


class Chain:
    def __init__(self):
        self.last = ()

    def __call__(self, *values, wait=()):
        held = lax.optimization_barrier(tuple(values) + tuple(self.last) + tuple(wait))
        return held[: len(values)] if len(values) > 1 else held[0]

    def done(self, *results):
        self.last = results
        return results if len(results) > 1 else results[0]


def gather_all(shard):
    parts = {0: shard}
    for bit in bits_of(lax.axis_size("fsdp")):
        parts.update({d | bit: swap(part, "fsdp", bit) for d, part in list(parts.items())})
    return parts


def gather_direct(shard):
    return {0: shard} | {d: swap(shard, "fsdp", d) for d in range(1, lax.axis_size("fsdp"))}


def in_order(parts, me):
    count = len(parts)
    return jnp.take(jnp.stack([parts[d] for d in range(count)]), me ^ jnp.arange(count), axis=0)


def rel_position(distance, count):
    width = count.bit_length() - 1
    return sum(((distance >> k) & 1) << (width - 1 - k) for k in range(width))


def scatter_step(keep, arrived, rows):
    size = keep.shape[0]
    if size == rows:
        return (keep.astype(F32) + arrived.astype(F32)).astype(BF16), None
    return [
        (keep[part].astype(F32) + arrived[part].astype(F32)).astype(BF16)
        for part in (slice(0, size // 2), slice(size // 2, size))
    ]


def seq_sum(mine):
    for bit in bits_of(lax.axis_size("seq"))[:-1]:
        total = mine.astype(F32) + swap(mine, "seq", bit).astype(F32)
        mine = total.astype(BF16)
    return total


def assemble_kernel(count, rows, single, off_ref, *refs):
    outs = refs[count:]

    def fill(out_ref):
        for distance in range(count):
            start = pl.multiple_of(off_ref[distance], 16)
            out_ref[pl.ds(start, rows), :] = refs[distance][...]

    if single:
        fill(outs[0])
    else:
        pl.when(pl.program_id(0) == 0)(lambda: fill(outs[0]))
        pl.when(pl.program_id(0) > 0)(lambda: fill(outs[1]))


def assemble(parts, me, cut=None):
    count = len(parts)
    rows, cols = parts[0].shape
    if rows % 16:
        full = in_order(parts, me).reshape(count * rows, cols)
        return (full[:, :cut], full[:, cut:]) if cut else full
    offsets = ((me ^ jnp.arange(count, dtype=jnp.int32)) * rows).astype(jnp.int32)
    tile = cut or min(cols, 1152)
    widths = [cut, cols - cut] if cut else [cols]
    maps = [lambda n, off: (0, 0), lambda n, off: (0, jnp.maximum(n - 1, 0))]
    if not cut:
        maps = [lambda n, off: (0, n)]
    outs = pl.pallas_call(
        functools.partial(assemble_kernel, count, rows, not cut),
        out_shape=[jax.ShapeDtypeStruct((count * rows, w), parts[0].dtype) for w in widths],
        grid_spec=pltpu.PrefetchScalarGridSpec(
            num_scalar_prefetch=1,
            grid=(pl.cdiv(cols, tile),),
            in_specs=[pl.BlockSpec((rows, tile), lambda n, off: (0, n))] * count,
            out_specs=[pl.BlockSpec((count * rows, tile), m) for m in maps],
        ),
        compiler_params=params(("arbitrary",)),
        cost_estimate=pl.CostEstimate(
            flops=0, transcendentals=0, bytes_accessed=4 * count * rows * cols
        ),
        name="assemble",
    )(offsets, *[parts[d] for d in range(count)])
    return outs if cut else outs[0]


def weight_grad_kernel(pairs, count, rows, pos_ref, *refs):
    lefts, rights = refs[:pairs], refs[pairs : 2 * pairs]
    keep_ref, send_ref, sum_ref = refs[2 * pairs :]
    total = dot(lefts[0][...], rights[0][...], TN)
    for i in range(1, pairs):
        total += dot(lefts[i][...], rights[i][...], TN)
    sum_ref[...] = sum(dot(jnp.ones((8, r.shape[0]), BF16), r[...]) for r in rights)
    for shard in range(count):
        start = pl.multiple_of(pos_ref[shard], 16)
        block = total[shard * rows : (shard + 1) * rows].astype(BF16)

        @pl.when(pos_ref[count] == shard % 2)
        def _():
            keep_ref[pl.ds(start, rows), :] = block

        @pl.when(pos_ref[count] != shard % 2)
        def _():
            send_ref[pl.ds(start, rows), :] = block


def weight_grad(lefts, rights, me, count):
    width = lefts[0].shape[1]
    cols = rights[0].shape[1]
    rows = width // count
    order = me ^ jnp.arange(count, dtype=jnp.int32)
    table = jnp.array([rel_position(d, count) for d in range(count)], jnp.int32)
    half = count // 2
    if rows % 16:
        total = sum(dot(a, b, TN) for a, b in zip(lefts, rights))
        by_distance = jnp.take(total.astype(BF16).reshape(count, rows, cols), order, axis=0)
        back = [0] * count
        for d in range(count):
            back[rel_position(d, count)] = d
        placed = jnp.take(by_distance, jnp.array(back), axis=0).reshape(width, cols)
        ones = [jnp.ones((8, b.shape[0]), BF16) for b in rights]
        sums = sum(dot(one, b) for one, b in zip(ones, rights))
        return placed[: width // 2], placed[width // 2 :], sums
    positions = jnp.concatenate([table[order] % half * rows, (me & 1)[None]]).astype(jnp.int32)
    tile = 256
    pairs = len(lefts)
    flops = sum(2 * a.shape[0] * width * cols for a in lefts)
    moved = sum(2 * a.shape[0] * (width + cols) for a in lefts) + 2 * width * cols
    return pl.pallas_call(
        functools.partial(weight_grad_kernel, pairs, count, rows),
        out_shape=[jax.ShapeDtypeStruct((width // 2, cols), BF16)] * 2
        + [jax.ShapeDtypeStruct((8, cols), F32)],
        grid_spec=pltpu.PrefetchScalarGridSpec(
            num_scalar_prefetch=1,
            grid=(pl.cdiv(cols, tile),),
            in_specs=[
                pl.BlockSpec(a.shape, lambda n, off: (0, 0), pipeline_mode=pl.Buffered(1))
                for a in lefts
            ]
            + [pl.BlockSpec((b.shape[0], tile), lambda n, off: (0, n)) for b in rights],
            out_specs=[pl.BlockSpec((width // 2, tile), lambda n, off: (0, n))] * 2
            + [pl.BlockSpec((8, tile), lambda n, off: (0, n))],
        ),
        compiler_params=params(("arbitrary",)),
        cost_estimate=pl.CostEstimate(flops=flops, transcendentals=0, bytes_accessed=moved),
        name="weight_grad",
    )(positions, *lefts, *rights)


def normalized(values):
    center = values - jnp.mean(values, axis=-1, keepdims=True)
    spread = jnp.mean(center * center, axis=-1, keepdims=True)
    inverse = lax.rsqrt(spread + EPS)
    return center * inverse, inverse


def row_block(rows):
    return 256 if rows % 256 == 0 else 128 if rows % 128 == 0 else rows


def norm_kernel(steps, x_refs, gain_ref, shift_ref, out_ref):
    for i, x_ref in enumerate(x_refs):

        @pl.when(pl.program_id(0) // steps == i)
        def _():
            hat, _ = normalized(x_ref[...].astype(F32))
            out_ref[...] = (hat * gain_ref[...] + shift_ref[...]).astype(BF16)


def norm(arrays, gain, shift):
    rows, width = arrays[0].shape
    block = row_block(rows)
    steps, count = rows // block, len(arrays)

    def kernel(*refs):
        norm_kernel(steps, refs[:count], *refs[count:])

    line = pl.BlockSpec((1, width), lambda i: (0, 0))
    return pl.pallas_call(
        kernel,
        out_shape=jax.ShapeDtypeStruct((count * rows, width), BF16),
        grid=(count * steps,),
        in_specs=[
            pl.BlockSpec((block, width), lambda i, k=k: (jnp.clip(i - k * steps, 0, steps - 1), 0))
            for k in range(count)
        ]
        + [line, line],
        out_specs=pl.BlockSpec((block, width), lambda i: (i, 0)),
        compiler_params=params(("arbitrary",)),
        cost_estimate=pl.CostEstimate(
            flops=10 * count * rows * width, transcendentals=0, bytes_accessed=4 * count * rows * width
        ),
        name="norm",
    )(*arrays, gain, shift)


def join_kernel(half, core_ref, own_ref, other_ref, x_ref, w_ref, b_ref, g_ref, s_ref, *outs):
    att_ref, mid_ref, out_ref = outs
    own, other = own_ref[:, :half], other_ref[:, :half]

    @pl.when(core_ref[0] == 0)
    def _():
        att_ref[...] = jnp.concatenate([own, other], axis=1)

    @pl.when(core_ref[0] != 0)
    def _():
        att_ref[...] = jnp.concatenate([other, own], axis=1)

    middle = x_ref[...].astype(F32) + dot(att_ref[...], w_ref[...]) + b_ref[...]
    mid_ref[...] = middle
    hat, _ = normalized(middle)
    out_ref[...] = (hat * g_ref[...] + s_ref[...]).astype(BF16)


def join(core, own, other, inputs, weight, bias, gain, shift, half):
    rows, width = inputs.shape
    padded = own.shape[1]
    block = row_block(rows)
    line = pl.BlockSpec((1, width), lambda i, c: (0, 0))
    wide = pl.BlockSpec((block, width), lambda i, c: (i, 0))
    part = pl.BlockSpec((block, padded), lambda i, c: (i, 0))
    return pl.pallas_call(
        functools.partial(join_kernel, half),
        out_shape=(
            jax.ShapeDtypeStruct((rows, width), BF16),
            jax.ShapeDtypeStruct((rows, width), F32),
            jax.ShapeDtypeStruct((rows, width), BF16),
        ),
        grid_spec=pltpu.PrefetchScalarGridSpec(
            num_scalar_prefetch=1,
            grid=(rows // block,),
            in_specs=[
                part,
                part,
                wide,
                pl.BlockSpec((width, width), lambda i, c: (0, 0), pipeline_mode=pl.Buffered(1)),
                line,
                line,
                line,
            ],
            out_specs=(wide, wide, wide),
        ),
        compiler_params=params(("arbitrary",)),
        cost_estimate=pl.CostEstimate(
            flops=2 * rows * width * width, transcendentals=0, bytes_accessed=14 * rows * width
        ),
        name="join",
    )(core, own, other, inputs, weight, bias, gain, shift)


def norm_back_values(x_ref, grads, gain_ref, add_ref, lines_ref):
    hat, inverse = normalized(x_ref[...].astype(F32))
    grad = grads[0][...].astype(F32)
    for other in grads[1:]:
        grad += other[...].astype(F32)
    scaled = grad * gain_ref[...]
    first = jnp.mean(scaled, axis=-1, keepdims=True)
    second = jnp.mean(scaled * hat, axis=-1, keepdims=True)

    @pl.when(pl.program_id(0) == 0)
    def _():
        lines_ref[...] = jnp.zeros_like(lines_ref)

    lines_ref[0:1] += jnp.sum(grad * hat, axis=0, keepdims=True)
    lines_ref[1:2] += jnp.sum(grad, axis=0, keepdims=True)
    return add_ref[...].astype(F32) + inverse * (scaled - first - hat * second)


def first_back(core, values, grads, gain, add, q_sums, kv_sums, half):
    rows, width = values.shape
    block = row_block(rows)
    count = len(grads)
    padded = q_sums.shape[1]

    def kernel(core_ref, x_ref, *refs):
        gain_ref, add_ref, q_ref, kv_ref, dx_ref, lines_ref = refs[count:]
        dx_ref[...] = norm_back_values(x_ref, refs[:count], gain_ref, add_ref, lines_ref)
        for line, part in ((2, q_ref[0:1, :half]), (3, kv_ref[0:1, padded : padded + half])):
            none = jnp.zeros_like(part)

            @pl.when(core_ref[0] == 0)
            def _():
                lines_ref[line : line + 1] = jnp.concatenate([part, none], axis=1)

            @pl.when(core_ref[0] != 0)
            def _():
                lines_ref[line : line + 1] = jnp.concatenate([none, part], axis=1)

    wide = pl.BlockSpec((block, width), lambda i, c: (i, 0))
    return pl.pallas_call(
        kernel,
        out_shape=(
            jax.ShapeDtypeStruct((rows, width), F32),
            jax.ShapeDtypeStruct((8, width), F32),
        ),
        grid_spec=pltpu.PrefetchScalarGridSpec(
            num_scalar_prefetch=1,
            grid=(rows // block,),
            in_specs=[wide] * (1 + count)
            + [
                pl.BlockSpec((1, width), lambda i, c: (0, 0)),
                wide,
                pl.BlockSpec(q_sums.shape, lambda i, c: (0, 0)),
                pl.BlockSpec(kv_sums.shape, lambda i, c: (0, 0)),
            ],
            out_specs=(wide, pl.BlockSpec((8, width), lambda i, c: (0, 0))),
        ),
        compiler_params=params(("arbitrary",)),
        cost_estimate=pl.CostEstimate(
            flops=20 * rows * width, transcendentals=0, bytes_accessed=18 * rows * width
        ),
        name="first_back",
    )(core, values, *grads, gain, add, q_sums, kv_sums)


def second_back(core, values, grads, gain, add, weight, half, padded):
    rows, width = values.shape
    block = row_block(rows)
    count = len(grads)

    def kernel(core_ref, x_ref, *refs):
        gain_ref, add_ref, w_ref, dx_ref, low_ref, mine_ref, send_ref, lines_ref = refs[count:]
        total = norm_back_values(x_ref, refs[:count], gain_ref, add_ref, lines_ref)
        low = total.astype(BF16)
        dx_ref[...] = total
        low_ref[...] = low
        lines_ref[2:3] += jnp.sum(low.astype(F32), axis=0, keepdims=True)
        lines_ref[3:4] += jnp.sum(add_ref[...].astype(F32), axis=0, keepdims=True)
        back = dot(low, w_ref[...], NT).astype(BF16)
        empty = jnp.zeros((block, padded - half), BF16)
        halves = [jnp.concatenate([back[:, i * half : (i + 1) * half], empty], axis=1) for i in range(2)]

        @pl.when(core_ref[0] == 0)
        def _():
            mine_ref[...], send_ref[...] = halves[0], halves[1]

        @pl.when(core_ref[0] != 0)
        def _():
            mine_ref[...], send_ref[...] = halves[1], halves[0]

    wide = pl.BlockSpec((block, width), lambda i, c: (i, 0))
    part = pl.BlockSpec((block, padded), lambda i, c: (i, 0))
    line = pl.BlockSpec((1, width), lambda i, c: (0, 0))
    square = pl.BlockSpec((width, width), lambda i, c: (0, 0), pipeline_mode=pl.Buffered(1))
    return pl.pallas_call(
        kernel,
        out_shape=(
            jax.ShapeDtypeStruct((rows, width), F32),
            jax.ShapeDtypeStruct((rows, width), BF16),
            jax.ShapeDtypeStruct((rows, padded), BF16),
            jax.ShapeDtypeStruct((rows, padded), BF16),
            jax.ShapeDtypeStruct((8, width), F32),
        ),
        grid_spec=pltpu.PrefetchScalarGridSpec(
            num_scalar_prefetch=1,
            grid=(rows // block,),
            in_specs=[wide] * (1 + count) + [line, wide, square],
            out_specs=(wide, wide, part, part, pl.BlockSpec((8, width), lambda i, c: (0, 0))),
        ),
        compiler_params=params(("arbitrary",)),
        cost_estimate=pl.CostEstimate(
            flops=2 * rows * width * width, transcendentals=0, bytes_accessed=20 * rows * width
        ),
        name="second_back",
    )(core, values, *grads, gain, add, weight)


def shards_kernel(half, padded, cut, core_ref, q_ref, k_ref, v_ref, o_ref, qkv_ref, out_ref):
    empty = jnp.zeros((q_ref.shape[0], padded - half), BF16)
    for core in range(2):

        @pl.when(core_ref[0] == core)
        def _():
            for i, ref in enumerate((q_ref, k_ref, v_ref)):
                part = ref[:, core * half : (core + 1) * half]
                qkv_ref[:, i * padded : (i + 1) * padded] = jnp.concatenate([part, empty], axis=1)
            out_ref[...] = o_ref[:, core * cut : core * cut + padded]


def attention_shards(core, weights, half, padded):
    rows, width = weights[0].shape
    return pl.pallas_call(
        functools.partial(shards_kernel, half, padded, width - padded),
        out_shape=(
            jax.ShapeDtypeStruct((rows, 3 * padded), BF16),
            jax.ShapeDtypeStruct((rows, padded), BF16),
        ),
        grid_spec=pltpu.PrefetchScalarGridSpec(
            num_scalar_prefetch=1,
            grid=(1,),
            in_specs=[pl.BlockSpec((rows, width), lambda i, c: (0, 0))] * 4,
            out_specs=(
                pl.BlockSpec((rows, 3 * padded), lambda i, c: (0, 0)),
                pl.BlockSpec((rows, padded), lambda i, c: (0, 0)),
            ),
        ),
        compiler_params=params(("arbitrary",)),
        cost_estimate=pl.CostEstimate(
            flops=0, transcendentals=0, bytes_accessed=16 * rows * width
        ),
        name="attention_shards",
    )(core, *weights)


def hidden(arrays, weight, bias):
    rows, width = arrays[0].shape
    cols = weight.shape[1]
    block = row_block(rows)
    steps, count = rows // block, len(arrays)

    def kernel(*refs):
        w_ref, b_ref, act_ref, slope_ref, x_ref = refs[count:]
        for i in range(count):

            @pl.when(pl.program_id(0) // steps == i)
            def _():
                x_ref[...] = refs[i][...]

        pre = dot(x_ref[...], w_ref[...]) + b_ref[...]
        square = pre * pre
        turn = jnp.tanh(pre * (GELU_COEF + GELU_COEF * 0.044715 * square))
        act_ref[...] = (0.5 * pre * (1.0 + turn)).astype(BF16)
        inner = GELU_COEF + 3.0 * 0.044715 * GELU_COEF * square
        slope_ref[...] = (0.5 * (1.0 + turn) * (1.0 + pre * (1.0 - turn) * inner)).astype(BF16)

    out = pl.BlockSpec((block, cols), lambda i: (i, 0))
    return pl.pallas_call(
        kernel,
        out_shape=(
            jax.ShapeDtypeStruct((count * rows, cols), BF16),
            jax.ShapeDtypeStruct((count * rows, cols), BF16),
            jax.ShapeDtypeStruct((count * rows, width), BF16),
        ),
        grid=(count * steps,),
        in_specs=[
            pl.BlockSpec((block, width), lambda i, k=k: (jnp.clip(i - k * steps, 0, steps - 1), 0))
            for k in range(count)
        ]
        + [
            pl.BlockSpec((width, cols), lambda i: (0, 0), pipeline_mode=pl.Buffered(1)),
            pl.BlockSpec((1, cols), lambda i: (0, 0)),
        ],
        out_specs=(out, out, pl.BlockSpec((block, width), lambda i: (i, 0))),
        compiler_params=params(("arbitrary",)),
        cost_estimate=pl.CostEstimate(
            flops=2 * count * rows * width * cols,
            transcendentals=count * rows * cols,
            bytes_accessed=2 * (2 * count * rows * width + width * cols + 2 * count * rows * cols),
        ),
        name="hidden",
    )(*arrays, weight, bias)


def head_window(head):
    first = head * HEAD_DIM
    start = first // 128 * 128
    return start, round_up(first + HEAD_DIM, 128) - start, first - start


def head_lanes(rows, width, low):
    lane = lax.broadcasted_iota(jnp.int32, (rows, width), 1)
    return (lane >= low) & (lane < low + HEAD_DIM)


def only_head(block, low):
    mine = head_lanes(*block.shape, low)
    return jnp.where(mine, block.astype(F32), 0.0).astype(BF16)


def pick_block(near_ref, far_ref, block):
    return near_ref.at[block, 0] if block < 2 else far_ref.at[block - 2, 0]


def attend_kernel(row, heads, blocks, padded, need_ref, col_ref, row_ref, q_ref, near_ref, far_ref, *refs):
    own_ref, pair_ref, lse_ref, queries, score, peak, total, acc, lses = refs[-9:]
    outs = (own_ref, pair_ref)
    tokens = own_ref.shape[1]
    slot = lax.broadcasted_iota(jnp.int32, (2 * tokens, 128), 1)
    for which in range(2):
        outs[which][...] = jnp.zeros_like(outs[which])
    windows = [head_window(head) for head in range(heads)]
    for head, (start, width, low) in enumerate(windows):
        for which in range(2):
            queries[head, which * tokens : (which + 1) * tokens, :width] = only_head(
                q_ref[which, 0, :, start : start + width], low
            )
    peak[...] = jnp.full_like(peak, MASKED)
    total[...] = jnp.zeros_like(total)
    acc[...] = jnp.zeros_like(acc)
    for block in range(blocks):

        @pl.when(need_ref[row, block] != 0)
        def _():
            side = pick_block(near_ref, far_ref, block)
            seen = col_ref[0] == row_ref[0, block : block + 1]
            for head, (start, width, _) in enumerate(windows):
                key = side[:, start : start + width]
                found = jnp.where(seen, dot(queries[head, :, :width], key, NT), MASKED)
                score[head, block] = found
                top = peak[head]
                for at in range(0, tokens, 128):
                    top = jnp.maximum(top, found[:, at : at + 128])
                peak[head] = top

    for head in range(heads):
        top = jnp.max(peak[head], axis=-1, keepdims=True) * (SCALE * LOG2E)
        peak[head] = jnp.broadcast_to(top, peak.shape[1:])

    for block in range(blocks):

        @pl.when(need_ref[row, block] != 0)
        def _():
            side = pick_block(near_ref, far_ref, block)
            for head, (start, width, _) in enumerate(windows):
                top, share = peak[head], total[head]
                pieces = []
                for at in range(0, tokens, 128):
                    part = jnp.exp2(score[head, block, :, at : at + 128] * (SCALE * LOG2E) - top)
                    share += part
                    pieces.append(part.astype(BF16))
                total[head] = share
                value = side[:, padded + start : padded + start + width]
                acc[head, :, :width] += dot(jnp.concatenate(pieces, axis=1), value)

    for head, (start, width, low) in enumerate(windows):
        norm = jnp.sum(total[head], axis=-1, keepdims=True)
        result = acc[head, :, :width] / norm
        mine = head_lanes(tokens, width, low)
        for which in range(2):
            kept = outs[which][0, :, start : start + width].astype(F32)
            fresh = result[which * tokens : (which + 1) * tokens]
            outs[which][0, :, start : start + width] = jnp.where(mine, fresh, kept).astype(BF16)
        lse = peak[head] + jnp.log2(norm)
        lses[...] = lse if head == 0 else jnp.where(slot == head, lse, lses[...])
    lse_ref[0] = lses[...].T[:heads]


def attend(row, query, near, far, need, seg_col, seg_row, heads, before):
    _, rows, tokens, padded = query.shape
    blocks = 2 + far.shape[0]
    cost = 2 * heads * blocks * tokens * tokens
    narrow = pl.BlockSpec((1, tokens, padded), lambda i, need: (row, 0, 0))
    lines = pl.BlockSpec((1, heads, 2 * tokens), lambda i, need: (row, 0, 0))

    def stack(count, width):
        return pl.BlockSpec((count, 1, tokens, width), lambda i, need: (0, row, 0, 0))

    return pl.pallas_call(
        functools.partial(attend_kernel, row, heads, blocks, padded),
        out_shape=(
            jax.ShapeDtypeStruct((rows, tokens, padded), BF16),
            jax.ShapeDtypeStruct((rows, tokens, padded), BF16),
            jax.ShapeDtypeStruct((rows, heads, 2 * tokens), F32),
        ),
        grid_spec=pltpu.PrefetchScalarGridSpec(
            num_scalar_prefetch=1,
            grid=(1,),
            in_specs=[
                pl.BlockSpec((1, 2 * tokens, 1), lambda i, need: (row, 0, 0)),
                pl.BlockSpec((1, blocks, tokens), lambda i, need: (row, 0, 0)),
                stack(2, padded),
                stack(2, 2 * padded),
                stack(blocks - 2, 2 * padded),
            ]
            + [pl.BlockSpec(memory_space=pl.ANY)] * len(before),
            out_specs=(narrow, narrow, lines),
            scratch_shapes=[
                pltpu.VMEM((heads, 2 * tokens, WIN), BF16),
                pltpu.VMEM((heads, blocks, 2 * tokens, tokens), F32),
                pltpu.VMEM((heads, 2 * tokens, 128), F32),
                pltpu.VMEM((heads, 2 * tokens, 128), F32),
                pltpu.VMEM((heads, 2 * tokens, WIN), F32),
                pltpu.VMEM((2 * tokens, 128), F32),
            ],
        ),
        input_output_aliases={6 + i: i for i in range(len(before))},
        compiler_params=params(("arbitrary",)),
        cost_estimate=pl.CostEstimate(
            flops=8 * cost * WIN,
            transcendentals=cost,
            bytes_accessed=6 * blocks * tokens * padded,
        ),
        name="attend",
    )(need, seg_col, seg_row, query, near, far, *before)


def attend_back_kernel(
    row, heads, blocks, padded, need_ref, col_ref, row_ref, pick_ref, q_ref, near_ref, far_ref, *refs
):
    grads, outs, lse_ref = refs[0:2], refs[2:4], refs[4]
    dq_ref, dnear_ref, dfar_ref, sums, inner_turn, queries, incoming, dq = refs[-8:]
    tokens = grads[0].shape[1]
    sums[...] = jnp.zeros_like(sums)
    for which in range(2):
        dq_ref[which, 0] = jnp.zeros((tokens, padded), BF16)
        product = grads[which][0].astype(F32) * outs[which][0].astype(F32)
        high = product.astype(BF16)
        rest = (product - high.astype(F32)).astype(BF16)
        inner_turn[:, which * tokens : (which + 1) * tokens] = dot(pick_ref[...], high, NT) + dot(
            pick_ref[...], rest, NT
        )
    windows = [head_window(head) for head in range(heads)]
    for head, (start, width, low) in enumerate(windows):
        for which in range(2):
            there = slice(which * tokens, (which + 1) * tokens)
            here = slice(start, start + width)
            queries[head, there, :width] = only_head(q_ref[which, 0, :, here], low)
            incoming[head, there, :width] = only_head(grads[which][0, :, here], low)
    dq[...] = jnp.zeros_like(dq)
    for block in range(blocks):

        @pl.when(need_ref[row, block] != 0)
        def _():
            side = pick_block(near_ref, far_ref, block)
            seen = col_ref[0, block] == row_ref[0]
            for head, (start, width, _) in enumerate(windows):
                end = start + width
                key, value = side[:, start:end], side[:, padded + start : padded + end]
                query, grad = queries[head, :, :width], incoming[head, :, :width]
                found = dot(key, query, NT) * (SCALE * LOG2E) - lse_ref[0, head : head + 1, :]
                prob = jnp.where(seen, jnp.exp2(found), 0.0)
                inner = inner_turn[head : head + 1, :]
                slope = (prob * (dot(value, grad, NT) - inner)).astype(BF16)
                sums[block, :, start:end] += dot(slope, query)
                sums[block, :, padded + start : padded + end] += dot(prob.astype(BF16), grad)
                dq[head, :, :width] += dot(slope, key, TN)

    for head, (start, width, low) in enumerate(windows):
        mine = head_lanes(tokens, width, low)
        for which in range(2):
            kept = dq_ref[which, 0, :, start : start + width].astype(F32)
            fresh = dq[head, which * tokens : (which + 1) * tokens, :width] * SCALE
            dq_ref[which, 0, :, start : start + width] = jnp.where(mine, fresh, kept).astype(BF16)
    for block in range(blocks):
        side = pick_block(dnear_ref, dfar_ref, block)
        side[:, :padded] = (sums[block, :, :padded] * SCALE).astype(BF16)
        side[:, padded:] = sums[block, :, padded:].astype(BF16)


def attend_back(row, query, near, far, grads, outs, lse, need, seg_col, seg_row, heads, before):
    _, rows, tokens, padded = query.shape
    blocks = 2 + far.shape[0]
    cost = 2 * heads * blocks * tokens * tokens
    column = lax.broadcasted_iota(jnp.int32, (heads, padded), 1)
    pick = (column // HEAD_DIM == lax.broadcasted_iota(jnp.int32, (heads, padded), 0)).astype(BF16)
    narrow = pl.BlockSpec((1, tokens, padded), lambda i, need: (row, 0, 0))

    def stack(count, width):
        return pl.BlockSpec((count, 1, tokens, width), lambda i, need: (0, row, 0, 0))

    return pl.pallas_call(
        functools.partial(attend_back_kernel, row, heads, blocks, padded),
        out_shape=tuple(jax.ShapeDtypeStruct(a.shape, BF16) for a in (query, near, far)),
        grid_spec=pltpu.PrefetchScalarGridSpec(
            num_scalar_prefetch=1,
            grid=(1,),
            in_specs=[
                pl.BlockSpec((1, blocks, tokens, 1), lambda i, need: (row, 0, 0, 0)),
                pl.BlockSpec((1, 1, 2 * tokens), lambda i, need: (row, 0, 0)),
                pl.BlockSpec((heads, padded), lambda i, need: (0, 0)),
                stack(2, padded),
                stack(2, 2 * padded),
                stack(blocks - 2, 2 * padded),
            ]
            + [narrow] * 4
            + [pl.BlockSpec((1, heads, 2 * tokens), lambda i, need: (row, 0, 0))]
            + [pl.BlockSpec(memory_space=pl.ANY)] * len(before),
            out_specs=(stack(2, padded), stack(2, 2 * padded), stack(blocks - 2, 2 * padded)),
            scratch_shapes=[
                pltpu.VMEM((blocks, tokens, 2 * padded), F32),
                pltpu.VMEM((heads, 2 * tokens), F32),
                pltpu.VMEM((heads, 2 * tokens, WIN), BF16),
                pltpu.VMEM((heads, 2 * tokens, WIN), BF16),
                pltpu.VMEM((heads, 2 * tokens, WIN), F32),
            ],
        ),
        input_output_aliases={12 + i: i for i in range(len(before))},
        compiler_params=params(("arbitrary",)),
        cost_estimate=pl.CostEstimate(
            flops=20 * cost * WIN,
            transcendentals=cost,
            bytes_accessed=12 * blocks * tokens * padded,
        ),
        name="attend_back",
    )(need, seg_col, seg_row, pick, query, near, far, *grads, *outs, lse, *before)


def column_sum(array):
    return dot(jnp.ones((8, array.shape[0]), BF16), array)[:1]


def local(
    patches,
    lengths,
    first_gain,
    first_shift,
    query_weight,
    query_bias,
    key_weight,
    value_weight,
    value_bias,
    output_weight,
    output_bias,
    second_gain,
    second_shift,
    hidden_weight,
    hidden_bias,
    down_weight,
    down_bias,
    cotangent,
):
    seq_count, shards = lax.axis_size("seq"), lax.axis_size("fsdp")
    place, me = lax.axis_index("seq"), lax.axis_index("fsdp")
    core = place & 1
    is_first = core == 0
    core_flag = core[None].astype(jnp.int32)
    rows, tokens, width = patches.shape
    flat = rows * tokens
    heads = width // HEAD_DIM // 2
    half = heads * HEAD_DIM
    padded = round_up(half, 128)
    ff = hidden_bias.shape[0]
    ff_half = round_up(ff, 256) // 2
    out_cols = padded
    out_cut = width - padded
    shard_rows = width // shards
    chain = Chain()

    def my_half(array, size, padded_size):
        first, second = array[..., :size], array[..., size:]
        grow = [(0, 0)] * (array.ndim - 1)
        first = jnp.pad(first, grow + [(0, padded_size - size)])
        second = jnp.pad(second, grow + [(0, padded_size - second.shape[-1])])
        return jnp.where(is_first, first, second)

    inputs = patches.reshape(flat, width)
    incoming = cotangent.reshape(flat, width)
    shard_qkv, shard_out = attention_shards(
        core_flag, [query_weight, key_weight, value_weight, output_weight], half, padded
    )
    raw = {0: inputs}
    for bit in bits_of(seq_count):
        raw.update({j | bit: swap(part, "seq", bit) for j, part in list(raw.items())})
    staged = shards == 8
    y, z, zz = 1, 2, 4
    q = {0: shard_qkv}
    if staged:
        q[z], q[zz], q[y] = (swap(q[0], "fsdp", bit) for bit in (z, zz, y))
        early = (q[y],)
    else:
        q, early = gather_all(shard_qkv), (shard_qkv,)
    vectors = after(
        jnp.stack(
            [
                first_gain,
                first_shift,
                query_bias,
                value_bias,
                output_bias,
                second_gain,
                second_shift,
                down_bias,
            ]
        ),
        shard_qkv,
    )
    vector_parts = gather_all(vectors)
    shard_hidden = my_half(after(hidden_weight, shard_qkv), ff_half, ff_half)
    shard_down = my_half(after(down_weight, shard_qkv).T, ff_half, ff_half)
    incoming_near = jnp.concatenate([incoming, swap(after(incoming, *early), "seq", 1)], axis=0)
    if staged:
        o, h, d = {0: after(shard_out, q[y])}, {0: after(shard_hidden, q[y])}, {0: shard_down}
        o[y], h[y] = swap(o[0], "fsdp", y), swap(h[0], "fsdp", y)
        q[zz | z] = swap(after(q[zz], q[z]), "fsdp", z)
        q[z | y], q[zz | y] = swap(q[z], "fsdp", y), swap(after(q[zz], q[z]), "fsdp", y)
        o[zz], o[zz | y] = (swap(after(o[k], q[zz]), "fsdp", zz) for k in (0, y))
        q[zz | z | y] = swap(after(q[zz | z], q[z | y], q[zz | y]), "fsdp", y)
        h[z], h[zz] = (swap(after(h[0], q[zz | z], o[zz]), "fsdp", bit) for bit in (z, zz))
        d[y] = swap(after(d[0], q[zz | z | y]), "fsdp", y)
    else:
        o, h, d = gather_all(shard_out), gather_all(shard_hidden), gather_all(shard_down)

    stacked = in_order(vector_parts, me).transpose(1, 0, 2).reshape(8, width).astype(F32)
    gain_one, shift_one, bias_query, bias_value, bias_output, gain_two, shift_two, bias_down = [
        stacked[i : i + 1] for i in range(8)
    ]

    block_of = place ^ jnp.arange(seq_count, dtype=jnp.int32)
    position = block_of[:, None] * tokens + jnp.arange(tokens, dtype=jnp.int32)[None, :]
    ends = jnp.cumsum(lengths, axis=-1)
    picture = jnp.sum(
        (position[None, :, :, None] >= ends[:, None, None, :]).astype(jnp.int32), axis=-1
    )
    usable = position[None] < ends[:, -1][:, None, None]
    segment = jnp.where(usable, picture, 1000 + position[None])
    low_id = jnp.min(jnp.where(usable, picture, 1 << 20), axis=-1)
    high_id = jnp.max(jnp.where(usable, picture, -1), axis=-1)
    need = (low_id[:, :2, None] <= high_id[:, None, :]) & (low_id[:, None, :] <= high_id[:, :2, None])
    need = need | jnp.eye(2, seq_count, dtype=jnp.bool_)[None]
    need = jnp.any(need, axis=1).astype(jnp.int32)
    near_flat = segment[:, :2].reshape(rows, 2 * tokens)
    seg_rows, seg_cols = segment, segment[..., None]
    seg_near_row, seg_near_col = near_flat[:, None], near_flat[..., None]

    raw_near, incoming_near = after(raw[1], incoming_near), after(incoming_near, raw[1])
    normed_near = norm([raw[0], raw_near], gain_one, shift_one)
    normed_far = norm([after(raw[j], normed_near) for j in range(2, seq_count)], gain_one, shift_one)
    bias_q = my_half(bias_query, half, padded)
    bias_kv = jnp.concatenate([jnp.zeros((1, padded), F32), my_half(bias_value, half, padded)], axis=1)
    q = {k: after(part, normed_far) for k, part in q.items()}
    w_q, w_kv = chain.done(*assemble(q, me, padded))
    near_in, w_q, w_kv = chain(normed_near, w_q, w_kv)
    if staged:
        h[z], h[zz], near_in = chain(h[z], h[zz], near_in)
        h[zz | z] = swap(h[zz], "fsdp", z)
        h[z | y], h[zz | y] = swap(h[z], "fsdp", y), swap(h[zz], "fsdp", y)
        for k in (0, y, zz, zz | y):
            o[k | z] = swap(after(o[k], h[zz], h[z]), "fsdp", z)
    query = (dot(near_in, w_q) + bias_q).astype(BF16)
    near = (dot(near_in, w_kv) + bias_kv).astype(BF16)
    chain.done(query, near)
    far_in, w_kv = chain(normed_far, w_kv)
    if staged:
        h[zz | z], far_in = chain(h[zz | z], far_in)
        h[zz | z | y] = swap(h[zz | z], "fsdp", y)
    far = chain.done((dot(far_in, w_kv) + bias_kv).astype(BF16))
    query = query.reshape(2, rows, tokens, padded)
    near = near.reshape(2, rows, tokens, 2 * padded)
    far = far.reshape(seq_count - 2, rows, tokens, 2 * padded)
    if staged:
        *rest, query = chain(*o.values(), query)
        o = dict(zip(o, rest))
        d[z], d[zz] = (swap(after(d[0], *rest), "fsdp", bit) for bit in (z, zz))
    found = ()
    for row in range(rows):
        query, near, far = chain(query, near, far)
        found = chain.done(*attend(row, query, near, far, need, seg_near_col, seg_rows, heads, found))
        if row == rows - 2:
            o = dict(zip(o, chain(*o.values())))
            w_out_mine = chain.done(assemble(o, me))
            w_out_other = swap(w_out_mine, "seq", 1)
    out_own, out_pair, lse = found
    other_half = swap(out_pair, "seq", 1).reshape(flat, padded)
    w_out_mine, w_out_other = chain(w_out_mine, w_out_other)
    w_out = jnp.where(
        is_first,
        jnp.concatenate([w_out_mine[:, :out_cut], w_out_other], axis=1),
        jnp.concatenate([w_out_other[:, :out_cut], w_out_mine], axis=1),
    )
    if staged:
        d[z], d[zz], w_out = chain(d[z], d[zz], w_out)
        d[zz | z] = swap(d[zz], "fsdp", z)
        d[z | y], d[zz | y] = swap(d[z], "fsdp", y), swap(d[zz], "fsdp", y)
    attended, middle, second = join(
        core_flag,
        out_own.reshape(flat, padded),
        other_half,
        inputs,
        w_out,
        bias_output,
        gain_two,
        shift_two,
        half,
    )
    second_pair = swap(second, "seq", 1)
    chain.done(second)
    h = dict(zip(h, chain(*h.values())))
    w_hidden = chain.done(assemble(h, me))
    if staged:
        d[zz | z], w_hidden = chain(d[zz | z], w_hidden)
        d[zz | z | y] = swap(d[zz | z], "fsdp", y)
    bias_hidden = my_half(hidden_bias.astype(F32)[None], ff_half, ff_half)
    second, second_pair, w_hidden = chain(second, second_pair, w_hidden)
    act, slope, second_near = chain.done(*hidden([second, second_pair], w_hidden, bias_hidden))

    incoming_near, act = chain(incoming_near, act)
    grad_down = chain.done(dot(incoming_near, act, TN).astype(BF16))
    part_down = lax.psum_scatter(grad_down, "fsdp", scatter_dimension=0, tiled=True)
    d = dict(zip(d, chain(*d.values())))
    w_down = chain.done(assemble(d, me))
    incoming_near, slope, w_down = chain(incoming_near, slope, w_down)
    grad_pre = chain.done((dot(incoming_near, w_down) * slope.astype(F32)).astype(BF16))
    grad_pre = chain(grad_pre)
    back = chain.done(dot(grad_pre, w_hidden, NT).astype(BF16))
    back_other = swap(back[flat:], "seq", 1)
    second_near, grad_pre = chain(second_near, grad_pre)
    grad_hidden = chain.done(dot(second_near, grad_pre, TN).astype(BF16))
    part_hidden = lax.psum_scatter(grad_hidden, "fsdp", scatter_dimension=0, tiled=True)
    back, back_other = chain(back, back_other)
    grad_middle, branch, grad_mine, grad_send, lines = second_back(
        core_flag, middle, [back[:flat], back_other], gain_two, incoming, w_out, half, padded
    )
    chain.done(branch)
    grad_pair = swap(grad_send, "seq", 1)
    attended, branch = chain(attended, branch)
    out_keep, out_send, _ = chain.done(*weight_grad([attended], [branch], me, shards))

    def core_part(array):
        low, high = array[:, :out_cols], array[:, out_cut:]
        return jnp.where(is_first, low, high), jnp.where(is_first, high, low)

    keep_mine, keep_other = core_part(out_keep)
    send_mine, send_other = core_part(out_send)
    keep_back, send_back = swap(keep_other, "seq", 1), swap(send_other, "seq", 1)
    grad_pre = chain(grad_pre)
    hidden_line = chain.done(column_sum(grad_pre))

    links = [("seq", bit) for bit in bits_of(seq_count)] + [("fsdp", bit) for bit in bits_of(shards)]
    todo = list(links)
    small = [lines, hidden_line]
    moving = []

    def small_step(guard):
        nonlocal small, moving
        if moving:
            *moving, guard = chain(*moving, guard)
            small = [a + b for a, b in zip(small, moving)]
            moving = []
        if todo:
            axis, bit = todo.pop(0)
            parts = small if (axis, bit) != ("seq", 1) else small[:1]
            moving = [swap(part, axis, bit) for part in parts]
            if len(parts) < len(small):
                moving.append(jnp.zeros_like(small[1]))
        return guard

    branch = small_step(branch)
    shape = (rows, tokens, padded)
    grads = [grad_mine.reshape(shape), grad_pair.reshape(shape)]
    found = ()
    for row in range(rows):
        query, near, far, *grads = chain(query, near, far, *grads)
        if row >= 1:
            query = small_step(query)
        if row == 1:
            keep_back, send_back, query = chain(keep_back, send_back, query)
            out_keep = (keep_mine.astype(F32) + keep_back.astype(F32)).astype(BF16)
            out_send = (send_mine.astype(F32) + send_back.astype(F32)).astype(BF16)
            out_back = swap(out_send, "fsdp", 1)
        if row == 2:
            out_back, part_down, query = chain(out_back, part_down, query)
            out_keep, out_send = scatter_step(out_keep, out_back, shard_rows)
            out_back = swap(out_send, "fsdp", 2)
            down_seq = swap(part_down, "seq", bits_of(seq_count)[0])
        found = attend_back(
            row,
            query,
            near,
            far,
            grads,
            [out_own, out_pair],
            lse,
            need,
            seg_cols,
            seg_near_row,
            heads,
            found,
        )
        chain.done(*found)
    dq, dnear, dfar = [g.reshape(-1, g.shape[-1]) for g in found]
    dfar, w_kv, down_seq, out_back = chain(dfar, w_kv, down_seq, out_back)
    dfar = small_step(dfar)
    out_keep, out_send = scatter_step(out_keep, out_back, shard_rows)
    out_back = swap(out_send, "fsdp", 4) if out_send is not None else None

    def seq_rest(mine, arrived):
        total = mine.astype(F32) + arrived.astype(F32)
        for bit in bits_of(seq_count)[1:-1]:
            mine = total.astype(BF16)
            total = mine.astype(F32) + swap(mine, "seq", bit).astype(F32)
        return total

    top = bits_of(seq_count)[0]
    down_total = seq_rest(part_down, down_seq)
    down_other = swap(down_total, "seq", 1)
    back_far = chain.done(dot(dfar, w_kv, NT).astype(BF16))
    far_parts = {j: back_far[(j - 2) * flat : (j - 1) * flat] for j in range(2, seq_count)}
    far_sent = {j: swap(part, "seq", 1) for j, part in far_parts.items() if j & 1}
    normed_near, normed_far, dnear, dfar = chain(normed_near, normed_far, dnear, dfar)
    dnear = small_step(dnear)
    kv_keep, kv_send, kv_sums = chain.done(*weight_grad([normed_near, normed_far], [dnear, dfar], me, shards))
    kv_back = swap(kv_send, "fsdp", 1)
    far_sent = {j: chain(part) for j, part in far_sent.items()}
    far_sums = {
        j: (far_parts[j].astype(F32) + far_sent[j | 1].astype(F32)).astype(BF16)
        for j in far_parts
        if not j & 1
    }
    chain.done(*far_sums.values())
    arrived = []
    for bit in bits_of(seq_count)[:-1]:
        moved = {j: swap(part, "seq", bit) for j, part in far_sums.items() if j & bit}
        far_sums = {j: part for j, part in far_sums.items() if not j & bit}
        for j, part in moved.items():
            if j == bit:
                arrived.append(part)
            else:
                far_sums[j ^ bit] = (far_sums[j ^ bit].astype(F32) + part.astype(F32)).astype(BF16)
    normed_near, dq = chain(normed_near, dq)
    dq = small_step(dq)
    q_keep, q_send, q_sums = chain.done(*weight_grad([normed_near], [dq], me, shards))
    q_back = swap(q_send, "fsdp", 1)
    dq, dnear = chain(dq, dnear)
    back_near = chain.done((dot(dq, w_q, NT) + dot(dnear, w_kv, NT)).astype(BF16))
    pair_back = swap(back_near[flat:], "seq", 1)
    while todo or moving:
        dnear = small_step(dnear)

    lines_all = small

    act, middle = chain(act, middle)
    down_pair = chain.done(dot(act[flat:], w_down, NT).astype(BF16))
    down_back = swap(down_pair, "seq", 1)
    act, down_back, middle = chain(act, down_back, middle)
    result = middle + dot(act[:flat], w_down, NT) + down_back.astype(F32) + bias_down
    layer_output = chain.done(result.astype(BF16)).reshape(rows, tokens, width)

    later = [2 << k for k in range(shards.bit_length() - 2)]

    def next_step(keep, back, bits):
        back = chain(back)
        keep, send = scatter_step(keep, back, shard_rows)
        chain.done(keep)
        return keep, swap(send, "fsdp", bits.pop(0)) if bits else None

    kv_bits, q_bits, out_bits = list(later), list(later), list(later[2:])
    kv_keep, kv_back = next_step(kv_keep, kv_back, kv_bits)
    if out_back is not None:
        out_keep, out_back = next_step(out_keep, out_back, out_bits)
        while out_back is not None:
            out_keep, out_back = next_step(out_keep, out_back, out_bits)
    out_seq = swap(out_keep, "seq", top)
    pair_back, *arrived = chain(pair_back, *arrived)
    grad_patches, late = first_back(
        core_flag,
        inputs,
        [back_near[:flat], pair_back] + arrived,
        gain_one,
        grad_middle,
        q_sums,
        kv_sums,
        half,
    )
    chain.done(grad_patches)
    small, todo, moving = [late], list(links[1:]) + links[:1], []
    part_hidden = chain(part_hidden)
    hidden_seq = swap(part_hidden, "seq", top)
    late_guard = small_step(part_hidden)
    while q_back is not None or kv_back is not None:
        if kv_back is not None:
            kv_keep, kv_back = next_step(kv_keep, kv_back, kv_bits)
        late_guard = small_step(late_guard)
        if q_back is not None:
            q_keep, q_back = next_step(q_keep, q_back, q_bits)
    kv_seq, q_seq = swap(kv_keep, "seq", top), swap(q_keep, "seq", top)
    hidden_seq = chain(hidden_seq)
    hidden_total = chain.done(seq_rest(part_hidden, hidden_seq))
    hidden_other = swap(hidden_total, "seq", 1)
    while todo or moving:
        late_guard = small_step(late_guard)
    (late,) = small

    own_lines = lax.dynamic_slice_in_dim(lines_all[0], me * shard_rows, shard_rows, 1)
    late_lines = lax.dynamic_slice_in_dim(late, me * shard_rows, shard_rows, 1)

    def whole(mine, other, size, total):
        return jnp.where(
            is_first,
            jnp.concatenate([mine[:, :size], other[:, : total - size]], axis=1),
            jnp.concatenate([other[:, :size], mine[:, : total - size]], axis=1),
        )

    bias_line = lines_all[1]
    full_bias = whole(bias_line, swap(bias_line, "seq", 1), ff_half, ff)[0]
    full_down = whole(down_total, down_other, ff_half, ff).T
    full_hidden = whole(hidden_total, hidden_other, ff_half, ff)
    out_total, q_total, kv_total = seq_rest(out_keep, out_seq), seq_rest(q_keep, q_seq), seq_rest(kv_keep, kv_seq)
    out_other, q_other, kv_other = [swap(a, "seq", 1) for a in (out_total, q_total, kv_total)]
    full_out = jnp.where(
        is_first,
        jnp.concatenate([out_total[:, :out_cut], out_other], axis=1),
        jnp.concatenate([out_other[:, :out_cut], out_total], axis=1),
    )
    full_query = whole(q_total, q_other, half, width)
    full_key = whole(kv_total[:, :padded], kv_other[:, :padded], half, width)
    full_value = whole(kv_total[:, padded:], kv_other[:, padded:], half, width)
    return (
        layer_output,
        grad_patches.reshape(rows, tokens, width),
        late_lines[0],
        late_lines[1],
        full_query,
        late_lines[2],
        full_key,
        full_value,
        late_lines[3],
        full_out,
        own_lines[2],
        own_lines[0],
        own_lines[1],
        full_hidden,
        full_bias,
        full_down,
        own_lines[3],
    )


def solution(mesh):
    shard, line, tokens = P("fsdp", None), P("fsdp"), P("fsdp", "seq", None)
    in_specs = (
        tokens,
        shard,
        line,
        line,
        shard,
        line,
        shard,
        shard,
        line,
        shard,
        line,
        line,
        line,
        shard,
        P(),
        P(None, "fsdp"),
        line,
        tokens,
    )
    out_specs = (
        tokens,
        tokens,
        line,
        line,
        shard,
        line,
        shard,
        shard,
        line,
        shard,
        line,
        line,
        line,
        shard,
        P(),
        P(None, "fsdp"),
        line,
    )
    return jax.shard_map(local, mesh=mesh, in_specs=in_specs, out_specs=out_specs, check_vma=False)
```

```python
import functools
import math

import jax
import jax.numpy as jnp
from jax import lax
from jax.experimental import pallas as pl
from jax.experimental.pallas import tpu as pltpu
from jax.sharding import PartitionSpec as P

HEAD_DIM = 72
EPS = 1e-06
GELU_COEF = math.sqrt(2.0 / math.pi)
MASKED = -1e30
F32 = jnp.float32
BF16 = jnp.bfloat16
SCALE = 1.0 / math.sqrt(HEAD_DIM)
WIN = 256
LOG2E = math.log2(math.e)
VMEM = 60 << 20
NOMINAL = pl.CostEstimate(flops=1, transcendentals=0, bytes_accessed=1)


def round_up(value, step):
    return (value + step - 1) // step * step


def dot(left, right, dims=((1,), (0,))):
    return lax.dot_general(left, right, (dims, ((), ())), preferred_element_type=F32)


NT = ((1,), (1,))
TN = ((0,), (0,))


def params(semantics):
    return pltpu.CompilerParams(dimension_semantics=semantics, vmem_limit_bytes=VMEM)


def swap(array, axis, bits):
    size = lax.axis_size(axis)
    return lax.ppermute(array, axis, [(i, i ^ bits) for i in range(size)])


def bits_of(size):
    return [1 << k for k in reversed(range(size.bit_length() - 1))]


def after(value, *earlier):
    return lax.optimization_barrier((value,) + tuple(earlier))[0]


class Chain:
    def __init__(self):
        self.last = ()

    def __call__(self, *values, wait=()):
        held = lax.optimization_barrier(tuple(values) + tuple(self.last) + tuple(wait))
        return held[: len(values)] if len(values) > 1 else held[0]

    def done(self, *results):
        self.last = results
        return results if len(results) > 1 else results[0]


class Flights:
    def __init__(self, chain):
        self.chain, self.open = chain, []

    def send(self, array, axis, bits):
        self.open.append([swap(array, axis, bits)])
        return self.open[-1]

    def land(self, *values, through=None):
        count = len(self.open)
        if through is not None:
            count = 1 + next(i for i, box in enumerate(self.open) if box is through)
        ready, self.open = self.open[:count], self.open[count:]
        held = self.chain(*[box[0] for box in ready], *values)
        held = held if isinstance(held, (tuple, list)) else [held]
        for box, array in zip(ready, held):
            box[0] = array
        rest = list(held[len(ready) :])
        return rest if len(rest) > 1 else rest[0] if rest else None


def in_order(parts, me):
    count = len(parts)
    return jnp.take(jnp.stack([parts[d] for d in range(count)]), me ^ jnp.arange(count), axis=0)


def gather_all(shard):
    parts = {0: shard}
    for bit in bits_of(lax.axis_size("fsdp")):
        parts.update({d | bit: swap(part, "fsdp", bit) for d, part in list(parts.items())})
    return parts


def rel_position(distance, count):
    width = count.bit_length() - 1
    return sum(((distance >> k) & 1) << (width - 1 - k) for k in range(width))


def assemble_kernel(count, rows, single, off_ref, *refs):
    outs = refs[count:]

    def fill(out_ref):
        for distance in range(count):
            start = pl.multiple_of(off_ref[distance], 16)
            out_ref[pl.ds(start, rows), :] = refs[distance][...]

    if single:
        fill(outs[0])
    else:
        pl.when(pl.program_id(0) == 0)(lambda: fill(outs[0]))
        pl.when(pl.program_id(0) > 0)(lambda: fill(outs[1]))


def assemble(parts, me, cut=None):
    count = len(parts)
    rows, cols = parts[0].shape
    if rows % 16:
        full = in_order(parts, me).reshape(count * rows, cols)
        return (full[:, :cut], full[:, cut:]) if cut else full
    offsets = ((me ^ jnp.arange(count, dtype=jnp.int32)) * rows).astype(jnp.int32)
    tile = cut or min(cols, 1152)
    widths = [cut, cols - cut] if cut else [cols]
    maps = [lambda n, off: (0, 0), lambda n, off: (0, jnp.maximum(n - 1, 0))]
    if not cut:
        maps = [lambda n, off: (0, n)]
    outs = pl.pallas_call(
        functools.partial(assemble_kernel, count, rows, not cut),
        out_shape=[jax.ShapeDtypeStruct((count * rows, w), parts[0].dtype) for w in widths],
        grid_spec=pltpu.PrefetchScalarGridSpec(
            num_scalar_prefetch=1,
            grid=(pl.cdiv(cols, tile),),
            in_specs=[pl.BlockSpec((rows, tile), lambda n, off: (0, n))] * count,
            out_specs=[pl.BlockSpec((count * rows, tile), m) for m in maps],
        ),
        compiler_params=params(("arbitrary",)),
        cost_estimate=NOMINAL,
        name="assemble",
    )(offsets, *[parts[d] for d in range(count)])
    return outs if cut else outs[0]


def weight_grad_kernel(pairs, count, rows, pos_ref, *refs):
    lefts, rights = refs[:pairs], refs[pairs : 2 * pairs]
    keep_ref, send_ref, sum_ref = refs[2 * pairs :]
    total = dot(lefts[0][...], rights[0][...], TN)
    for i in range(1, pairs):
        total += dot(lefts[i][...], rights[i][...], TN)
    sum_ref[...] = sum(dot(jnp.ones((8, r.shape[0]), BF16), r[...]) for r in rights)
    for shard in range(count):
        start = pl.multiple_of(pos_ref[shard], 16)
        block = total[shard * rows : (shard + 1) * rows].astype(BF16)

        @pl.when(pos_ref[count] == shard % 2)
        def _():
            keep_ref[pl.ds(start, rows), :] = block

        @pl.when(pos_ref[count] != shard % 2)
        def _():
            send_ref[pl.ds(start, rows), :] = block


def weight_grad(lefts, rights, me, count):
    width = lefts[0].shape[1]
    cols = rights[0].shape[1]
    rows = width // count
    order = me ^ jnp.arange(count, dtype=jnp.int32)
    table = jnp.array([rel_position(d, count) for d in range(count)], jnp.int32)
    half = count // 2
    if rows % 16:
        total = sum(dot(a, b, TN) for a, b in zip(lefts, rights))
        by_distance = jnp.take(total.astype(BF16).reshape(count, rows, cols), order, axis=0)
        back = [0] * count
        for d in range(count):
            back[rel_position(d, count)] = d
        placed = jnp.take(by_distance, jnp.array(back), axis=0).reshape(width, cols)
        ones = [jnp.ones((8, b.shape[0]), BF16) for b in rights]
        sums = sum(dot(one, b) for one, b in zip(ones, rights))
        return placed[: width // 2], placed[width // 2 :], sums
    positions = jnp.concatenate([table[order] % half * rows, (me & 1)[None]]).astype(jnp.int32)
    tile = 256
    pairs = len(lefts)
    return pl.pallas_call(
        functools.partial(weight_grad_kernel, pairs, count, rows),
        out_shape=[jax.ShapeDtypeStruct((width // 2, cols), BF16)] * 2
        + [jax.ShapeDtypeStruct((8, cols), F32)],
        grid_spec=pltpu.PrefetchScalarGridSpec(
            num_scalar_prefetch=1,
            grid=(pl.cdiv(cols, tile),),
            in_specs=[
                pl.BlockSpec(a.shape, lambda n, off: (0, 0), pipeline_mode=pl.Buffered(1))
                for a in lefts
            ]
            + [pl.BlockSpec((b.shape[0], tile), lambda n, off: (0, n)) for b in rights],
            out_specs=[pl.BlockSpec((width // 2, tile), lambda n, off: (0, n))] * 2
            + [pl.BlockSpec((8, tile), lambda n, off: (0, n))],
        ),
        compiler_params=params(("arbitrary",)),
        cost_estimate=NOMINAL,
        name="weight_grad",
    )(positions, *lefts, *rights)


def normalized(values):
    center = values - jnp.mean(values, axis=-1, keepdims=True)
    spread = jnp.mean(center * center, axis=-1, keepdims=True)
    inverse = lax.rsqrt(spread + EPS)
    return center * inverse, inverse


def row_block(rows):
    return 256 if rows % 256 == 0 else 128 if rows % 128 == 0 else rows


def norm(arrays, gain, shift):
    width = arrays[0].shape[1]
    block = min(row_block(a.shape[0]) for a in arrays)
    steps = [a.shape[0] // block for a in arrays]
    firsts = [sum(steps[:k]) for k in range(len(steps))]
    count, total = len(arrays), sum(steps)

    def kernel(*refs):
        gain_ref, shift_ref, out_ref = refs[count:]
        at = pl.program_id(0)
        for k in range(count):

            @pl.when((at >= firsts[k]) & (at < firsts[k] + steps[k]))
            def _():
                hat, _ = normalized(refs[k][...].astype(F32))
                out_ref[...] = (hat * gain_ref[...] + shift_ref[...]).astype(BF16)

    line = pl.BlockSpec((1, width), lambda i: (0, 0))
    return pl.pallas_call(
        kernel,
        out_shape=jax.ShapeDtypeStruct((total * block, width), BF16),
        grid=(total,),
        in_specs=[
            pl.BlockSpec((block, width), lambda i, k=k: (jnp.clip(i - firsts[k], 0, steps[k] - 1), 0))
            for k in range(count)
        ]
        + [line, line],
        out_specs=pl.BlockSpec((block, width), lambda i: (i, 0)),
        compiler_params=params(("arbitrary",)),
        cost_estimate=NOMINAL,
        name="norm",
    )(*arrays, gain, shift)


def join_kernel(half, core_ref, own_ref, other_ref, x_ref, w_ref, b_ref, g_ref, s_ref, *outs):
    att_ref, mid_ref, out_ref = outs
    own, other = own_ref[:, :half], other_ref[:, :half]

    @pl.when(core_ref[0] == 0)
    def _():
        att_ref[...] = jnp.concatenate([own, other], axis=1)

    @pl.when(core_ref[0] != 0)
    def _():
        att_ref[...] = jnp.concatenate([other, own], axis=1)

    middle = x_ref[...].astype(F32) + dot(att_ref[...], w_ref[...]) + b_ref[...]
    mid_ref[...] = middle
    hat, _ = normalized(middle)
    out_ref[...] = (hat * g_ref[...] + s_ref[...]).astype(BF16)


def join(core, own, other, inputs, weight, bias, gain, shift, half):
    rows, width = inputs.shape
    padded = own.shape[1]
    block = row_block(rows)
    line = pl.BlockSpec((1, width), lambda i, c: (0, 0))
    wide = pl.BlockSpec((block, width), lambda i, c: (i, 0))
    part = pl.BlockSpec((block, padded), lambda i, c: (i, 0))
    return pl.pallas_call(
        functools.partial(join_kernel, half),
        out_shape=(
            jax.ShapeDtypeStruct((rows, width), BF16),
            jax.ShapeDtypeStruct((rows, width), F32),
            jax.ShapeDtypeStruct((rows, width), BF16),
        ),
        grid_spec=pltpu.PrefetchScalarGridSpec(
            num_scalar_prefetch=1,
            grid=(rows // block,),
            in_specs=[
                part,
                part,
                wide,
                pl.BlockSpec((width, width), lambda i, c: (0, 0), pipeline_mode=pl.Buffered(1)),
                line,
                line,
                line,
            ],
            out_specs=(wide, wide, wide),
        ),
        compiler_params=params(("arbitrary",)),
        cost_estimate=NOMINAL,
        name="join",
    )(core, own, other, inputs, weight, bias, gain, shift)


def norm_back_values(x_ref, grads, gain_ref, add_ref, lines_ref):
    hat, inverse = normalized(x_ref[...].astype(F32))
    grad = grads[0][...].astype(F32)
    for other in grads[1:]:
        grad += other[...].astype(F32)
    scaled = grad * gain_ref[...]
    first = jnp.mean(scaled, axis=-1, keepdims=True)
    second = jnp.mean(scaled * hat, axis=-1, keepdims=True)

    @pl.when(pl.program_id(0) == 0)
    def _():
        lines_ref[...] = jnp.zeros_like(lines_ref)

    lines_ref[0:1] += jnp.sum(grad * hat, axis=0, keepdims=True)
    lines_ref[1:2] += jnp.sum(grad, axis=0, keepdims=True)
    return add_ref[...].astype(F32) + inverse * (scaled - first - hat * second)


def first_back(core, values, grads, gain, add, q_sums, kv_sums, half):
    rows, width = values.shape
    block = row_block(rows)
    count = len(grads)
    padded = q_sums.shape[1]

    def kernel(core_ref, x_ref, *refs):
        gain_ref, add_ref, q_ref, kv_ref, dx_ref, lines_ref = refs[count:]
        dx_ref[...] = norm_back_values(x_ref, refs[:count], gain_ref, add_ref, lines_ref)
        for line, part in ((2, q_ref[0:1, :half]), (3, kv_ref[0:1, padded : padded + half])):
            none = jnp.zeros_like(part)

            @pl.when(core_ref[0] == 0)
            def _():
                lines_ref[line : line + 1] = jnp.concatenate([part, none], axis=1)

            @pl.when(core_ref[0] != 0)
            def _():
                lines_ref[line : line + 1] = jnp.concatenate([none, part], axis=1)

    wide = pl.BlockSpec((block, width), lambda i, c: (i, 0))
    return pl.pallas_call(
        kernel,
        out_shape=(
            jax.ShapeDtypeStruct((rows, width), F32),
            jax.ShapeDtypeStruct((8, width), F32),
        ),
        grid_spec=pltpu.PrefetchScalarGridSpec(
            num_scalar_prefetch=1,
            grid=(rows // block,),
            in_specs=[wide] * (1 + count)
            + [
                pl.BlockSpec((1, width), lambda i, c: (0, 0)),
                wide,
                pl.BlockSpec(q_sums.shape, lambda i, c: (0, 0)),
                pl.BlockSpec(kv_sums.shape, lambda i, c: (0, 0)),
            ],
            out_specs=(wide, pl.BlockSpec((8, width), lambda i, c: (0, 0))),
        ),
        compiler_params=params(("arbitrary",)),
        cost_estimate=NOMINAL,
        name="first_back",
    )(core, values, *grads, gain, add, q_sums, kv_sums)


def second_back(core, values, grads, gain, add, weight, hidden_line, half, padded):
    rows, width = values.shape
    block = row_block(rows)
    count = len(grads)

    def kernel(core_ref, x_ref, *refs):
        gain_ref, add_ref, w_ref, hid_ref, dx_ref, low_ref, mine_ref, send_ref, lines_ref = refs[count:]
        total = norm_back_values(x_ref, refs[:count], gain_ref, add_ref, lines_ref)
        low = total.astype(BF16)
        dx_ref[...] = total
        low_ref[...] = low
        lines_ref[2:3] += jnp.sum(low.astype(F32), axis=0, keepdims=True)
        lines_ref[3:4] += jnp.sum(add_ref[...].astype(F32), axis=0, keepdims=True)
        spare = hid_ref.shape[1] - width
        for core in range(2):

            @pl.when(core_ref[0] == core)
            def _():
                lines_ref[4 + 2 * core : 5 + 2 * core] = hid_ref[:, :width]
                lines_ref[5 + 2 * core : 6 + 2 * core, :spare] = hid_ref[:, width:]

        back = dot(low, w_ref[...], NT).astype(BF16)
        empty = jnp.zeros((block, padded - half), BF16)
        halves = [jnp.concatenate([back[:, i * half : (i + 1) * half], empty], axis=1) for i in range(2)]

        @pl.when(core_ref[0] == 0)
        def _():
            mine_ref[...], send_ref[...] = halves[0], halves[1]

        @pl.when(core_ref[0] != 0)
        def _():
            mine_ref[...], send_ref[...] = halves[1], halves[0]

    wide = pl.BlockSpec((block, width), lambda i, c: (i, 0))
    part = pl.BlockSpec((block, padded), lambda i, c: (i, 0))
    line = pl.BlockSpec((1, width), lambda i, c: (0, 0))
    square = pl.BlockSpec((width, width), lambda i, c: (0, 0), pipeline_mode=pl.Buffered(1))
    return pl.pallas_call(
        kernel,
        out_shape=(
            jax.ShapeDtypeStruct((rows, width), F32),
            jax.ShapeDtypeStruct((rows, width), BF16),
            jax.ShapeDtypeStruct((rows, padded), BF16),
            jax.ShapeDtypeStruct((rows, padded), BF16),
            jax.ShapeDtypeStruct((8, width), F32),
        ),
        grid_spec=pltpu.PrefetchScalarGridSpec(
            num_scalar_prefetch=1,
            grid=(rows // block,),
            in_specs=[wide] * (1 + count)
            + [line, wide, square, pl.BlockSpec(hidden_line.shape, lambda i, c: (0, 0))],
            out_specs=(wide, wide, part, part, pl.BlockSpec((8, width), lambda i, c: (0, 0))),
        ),
        compiler_params=params(("arbitrary",)),
        cost_estimate=NOMINAL,
        name="second_back",
    )(core, values, *grads, gain, add, weight, hidden_line)


def rows_matmul(name, lefts, weights, finish, extras, outs, dims=((1,), (0,)), split=False, first_row=0):
    rows = outs[0].shape[0]
    block = row_block(rows)
    steps = rows // block
    half = steps // 2
    count, terms = len(lefts), len(lefts) + len(weights)

    def kernel(*refs):
        total = dot(refs[0][...], refs[count][...], dims)
        for i in range(1, count):
            total += dot(refs[i][...], refs[count + i][...], dims)
        results = finish(total, *refs[terms : terms + len(extras)])
        targets = refs[terms + len(extras) :]
        if split:

            @pl.when(pl.program_id(0) < half)
            def _():
                targets[0][...] = results[0]

            @pl.when(pl.program_id(0) >= half)
            def _():
                targets[1][...] = results[0]

            targets = targets[1:]
        else:
            targets[0][...] = results[0]
        for target, result in zip(targets[1:], results[1:]):

            @pl.when(pl.program_id(0) == 0)
            def _():
                target[...] = jnp.zeros_like(target)

            target[...] += result

    def by_rows(array):
        return pl.BlockSpec((block, array.shape[1]), lambda i: (i, 0))

    def whole(array):
        return pl.BlockSpec(array.shape, lambda i: (0, 0), pipeline_mode=pl.Buffered(1))

    first = outs[0]
    if split:
        part = jax.ShapeDtypeStruct((rows // 2, first.shape[1]), first.dtype)
        shapes = [part, part] + list(outs[1:])
        specs = [
            pl.BlockSpec((block, first.shape[1]), lambda i: (jnp.minimum(i, half - 1), 0)),
            pl.BlockSpec((block, first.shape[1]), lambda i: (jnp.maximum(i - half, 0), 0)),
        ]
    else:
        shapes, specs = list(outs), [by_rows(first)]
    specs += [pl.BlockSpec(out.shape, lambda i: (0, 0)) for out in outs[1:]]
    return pl.pallas_call(
        kernel,
        out_shape=shapes,
        grid=(steps,),
        in_specs=[
            pl.BlockSpec((block, a.shape[1]), lambda i: (i + first_row // block, 0)) for a in lefts
        ]
        + [whole(w) for w in weights]
        + [by_rows(e) if e.shape[0] == rows else whole(e) for e in extras],
        out_specs=specs,
        compiler_params=params(("arbitrary",)),
        cost_estimate=NOMINAL,
        name=name,
    )(*lefts, *weights, *extras)


def like(rows, cols, kind=BF16):
    return jax.ShapeDtypeStruct((rows, cols), kind)


def plain(total):
    return (total.astype(BF16),)


def with_bias(total, bias_ref):
    return ((total + bias_ref[...]).astype(BF16),)


def with_slope(total, slope_ref):
    low = (total * slope_ref[...].astype(F32)).astype(BF16)
    return low, jnp.sum(low.astype(F32), axis=0, keepdims=True)


def layer_end(total, middle_ref, other_ref, bias_ref):
    return ((middle_ref[...] + total + other_ref[...].astype(F32) + bias_ref[...]).astype(BF16),)


def small_call(kernel, outs, scalars, arrays, name):
    vmem = pl.BlockSpec(memory_space=pltpu.VMEM)
    return pl.pallas_call(
        kernel,
        out_shape=outs,
        in_specs=[pl.BlockSpec(memory_space=pltpu.SMEM)] * len(scalars) + [vmem] * len(arrays),
        out_specs=[vmem] * len(outs),
        compiler_params=pltpu.CompilerParams(vmem_limit_bytes=VMEM),
        cost_estimate=NOMINAL,
        name=name,
    )(*scalars, *arrays)


def add_rows(left, right, kind=BF16, pieces=1):
    rows, cols = left.shape
    size = rows // pieces

    def kernel(left_ref, right_ref, *outs):
        for i, out_ref in enumerate(outs):
            part = slice(i * size, (i + 1) * size)
            out_ref[...] = (left_ref[part].astype(F32) + right_ref[part].astype(F32)).astype(kind)

    return small_call(kernel, [like(size, cols, kind)] * pieces, [], [left, right], "add_rows")


def scatter_step(keep, arrived, rows):
    if keep.shape[0] == rows:
        return add_rows(keep, arrived)[0], None
    return add_rows(keep, arrived, BF16, 2)


def both_cores(core, mine, other, size, total, start=0, turn=False):
    rows = mine.shape[0]

    def kernel(core_ref, mine_ref, other_ref, out_ref):
        for at, refs in ((0, (mine_ref, other_ref)), (1, (other_ref, mine_ref))):

            @pl.when(core_ref[0] == at)
            def _():
                first = refs[0][:, start : start + size]
                second = refs[1][:, start : start + total - size]
                if turn:
                    out_ref[:size], out_ref[size:] = first.T, second.T
                else:
                    out_ref[...] = jnp.concatenate([first, second], axis=1)

    shape = like(total, rows, mine.dtype) if turn else like(rows, total, mine.dtype)
    return small_call(kernel, [shape], [core], [mine, other], "both_cores")[0]


def core_columns(core, arrays, cols):
    rows, width = arrays[0].shape

    def kernel(core_ref, *refs):
        for at in range(2):

            @pl.when(core_ref[0] == at)
            def _():
                for i in range(len(arrays)):
                    for k, where in enumerate((at, 1 - at)):
                        low = where * (width - cols)
                        refs[len(arrays) * (1 + k) + i][...] = refs[i][:, low : low + cols]

    return small_call(kernel, [like(rows, cols)] * (2 * len(arrays)), [core], arrays, "core_columns")


def stack_rows(first, second):
    rows, cols = first.shape
    block = row_block(rows)
    steps = rows // block

    def kernel(first_ref, second_ref, out_ref):
        for i, ref in enumerate((first_ref, second_ref)):

            @pl.when(pl.program_id(0) // steps == i)
            def _():
                out_ref[...] = ref[...]

    return pl.pallas_call(
        kernel,
        out_shape=like(2 * rows, cols),
        grid=(2 * steps,),
        in_specs=[
            pl.BlockSpec((block, cols), lambda i: (jnp.minimum(i, steps - 1), 0)),
            pl.BlockSpec((block, cols), lambda i: (jnp.maximum(i - steps, 0), 0)),
        ],
        out_specs=pl.BlockSpec((block, cols), lambda i: (i, 0)),
        compiler_params=params(("arbitrary",)),
        cost_estimate=NOMINAL,
        name="stack_rows",
    )(first, second)


def mask_kernel(rows, tokens, blocks, len_ref, place_ref, need_ref, row_ref, col_ref, near_row, near_col):
    place = place_ref[0]
    for row in range(rows):
        ends = [len_ref[row, 0]]
        for p in range(1, len_ref.shape[1]):
            ends.append(ends[-1] + len_ref[row, p])

        def pictures(position):
            return sum((position >= end).astype(jnp.int32) for end in ends)

        def segment(position):
            return jnp.where(position < ends[-1], pictures(position), 1000 + position)

        spans = []
        for block in range(blocks):
            start = jnp.bitwise_xor(place, block) * tokens
            across = segment(start + lax.broadcasted_iota(jnp.int32, (1, tokens), 1))
            down = segment(start + lax.broadcasted_iota(jnp.int32, (tokens, 1), 0))
            row_ref[row, block : block + 1] = across
            col_ref[row, block] = down
            if block < 2:
                near_row[row, :, block * tokens : (block + 1) * tokens] = across
                near_col[row, block * tokens : (block + 1) * tokens] = down
            last = jnp.minimum(start + tokens, ends[-1]) - 1
            low = sum(jnp.where(start >= end, 1, 0) for end in ends)
            high = sum(jnp.where(last >= end, 1, 0) for end in ends)
            spans.append((start < ends[-1], low, high))
        for block, (real, low, high) in enumerate(spans):
            if block < 2:
                need_ref[row, block] = 1
            else:
                need_ref[row, block] = sum(
                    jnp.where(real & ok & (low <= top) & (bottom <= high), 1, 0) for ok, bottom, top in spans[:2]
                )


def masks(lengths, place, blocks, tokens):
    rows = lengths.shape[0]
    shapes = [(rows, blocks, tokens), (rows, blocks, tokens, 1), (rows, 1, 2 * tokens), (rows, 2 * tokens, 1)]
    smem = pl.BlockSpec(memory_space=pltpu.SMEM)
    return pl.pallas_call(
        functools.partial(mask_kernel, rows, tokens, blocks),
        out_shape=[jax.ShapeDtypeStruct((rows, blocks), jnp.int32)]
        + [jax.ShapeDtypeStruct(shape, jnp.int32) for shape in shapes],
        in_specs=[smem, smem],
        out_specs=[smem] + [pl.BlockSpec(memory_space=pltpu.VMEM)] * 4,
        compiler_params=pltpu.CompilerParams(vmem_limit_bytes=VMEM),
        cost_estimate=NOMINAL,
        name="masks",
    )(lengths, place)


def lay_vectors(meta, parts, half, padded):
    count, lines, size = parts.shape

    def kernel(meta_ref, parts_ref, lines_ref, q_ref, kv_ref):
        for shard in range(count):
            block = parts_ref[jnp.bitwise_xor(meta_ref[1], shard)]
            lines_ref[:, shard * size : (shard + 1) * size] = block.astype(F32)
        q_ref[...] = jnp.zeros_like(q_ref)
        kv_ref[...] = jnp.zeros_like(kv_ref)
        for core in range(2):

            @pl.when(meta_ref[0] == core)
            def _():
                q_ref[:, :half] = lines_ref[2:3, core * half : (core + 1) * half]
                kv_ref[:, padded : padded + half] = lines_ref[3:4, core * half : (core + 1) * half]

    outs = [like(lines, count * size, F32), like(1, padded, F32), like(1, 2 * padded, F32)]
    return small_call(kernel, outs, [meta], [parts], "lay_vectors")


def mlp_shards(core, out_shard, hidden_weight, down_weight, cols):
    rows, total = hidden_weight.shape
    before = out_shard.shape[1]

    def kernel(core_ref, part_ref, hidden_ref, down_ref, first_out, down_out):
        first_out[:, :before] = part_ref[...]
        for at in range(2):

            @pl.when(core_ref[0] == at)
            def _():
                low = at * cols
                high = min(low + cols, total)
                size = high - low
                first_out[:, before : before + size] = hidden_ref[:, low:high]
                down_out[:, :size] = down_ref[low:high].T
                if size < cols:
                    empty = jnp.zeros((rows, cols - size), BF16)
                    first_out[:, before + size :] = empty
                    down_out[:, size:] = empty

    outs = [like(rows, before + cols), like(rows, cols)]
    return small_call(kernel, outs, [core], [out_shard, hidden_weight, down_weight], "mlp_shards")


def attention_shards(core, weights, vectors, half, padded):
    rows, width = weights[0].shape
    cut = width - padded

    def kernel(core_ref, q_ref, k_ref, v_ref, o_ref, *refs):
        qkv_ref, out_ref, lines_ref = refs[len(vectors) :]
        empty = jnp.zeros((rows, padded - half), BF16)
        for at in range(2):

            @pl.when(core_ref[0] == at)
            def _():
                for i, ref in enumerate((q_ref, k_ref, v_ref)):
                    part = ref[:, at * half : (at + 1) * half]
                    qkv_ref[:, i * padded : (i + 1) * padded] = jnp.concatenate([part, empty], axis=1)
                out_ref[...] = o_ref[:, at * cut : at * cut + padded]

        for i in range(len(vectors)):
            lines_ref[i : i + 1] = refs[i][...]

    outs = [like(rows, 3 * padded), like(rows, padded), like(len(vectors), vectors[0].shape[1])]
    return small_call(kernel, outs, [core], [*weights, *vectors], "attention_shards")


def hidden(arrays, weight, bias):
    rows, width = arrays[0].shape
    cols = weight.shape[1]
    block = row_block(rows)
    steps, count = rows // block, len(arrays)

    def kernel(*refs):
        w_ref, b_ref, act_ref, slope_ref, x_ref = refs[count:]
        for i in range(count):

            @pl.when(pl.program_id(0) // steps == i)
            def _():
                x_ref[...] = refs[i][...]

        pre = dot(x_ref[...], w_ref[...]) + b_ref[...]
        square = pre * pre
        turn = jnp.tanh(pre * (GELU_COEF + GELU_COEF * 0.044715 * square))
        act_ref[...] = (0.5 * pre * (1.0 + turn)).astype(BF16)
        inner = GELU_COEF + 3.0 * 0.044715 * GELU_COEF * square
        slope_ref[...] = (0.5 * (1.0 + turn) * (1.0 + pre * (1.0 - turn) * inner)).astype(BF16)

    out = pl.BlockSpec((block, cols), lambda i: (i, 0))
    return pl.pallas_call(
        kernel,
        out_shape=(
            jax.ShapeDtypeStruct((count * rows, cols), BF16),
            jax.ShapeDtypeStruct((count * rows, cols), BF16),
            jax.ShapeDtypeStruct((count * rows, width), BF16),
        ),
        grid=(count * steps,),
        in_specs=[
            pl.BlockSpec((block, width), lambda i, k=k: (jnp.clip(i - k * steps, 0, steps - 1), 0))
            for k in range(count)
        ]
        + [
            pl.BlockSpec((width, cols), lambda i: (0, 0), pipeline_mode=pl.Buffered(1)),
            pl.BlockSpec((1, cols), lambda i: (0, 0)),
        ],
        out_specs=(out, out, pl.BlockSpec((block, width), lambda i: (i, 0))),
        compiler_params=params(("arbitrary",)),
        cost_estimate=NOMINAL,
        name="hidden",
    )(*arrays, weight, bias)


def head_window(head):
    first = head * HEAD_DIM
    start = first // 128 * 128
    return start, round_up(first + HEAD_DIM, 128) - start, first - start


def head_lanes(rows, width, low):
    lane = lax.broadcasted_iota(jnp.int32, (rows, width), 1)
    return (lane >= low) & (lane < low + HEAD_DIM)


def only_head(block, low):
    mine = head_lanes(*block.shape, low)
    return jnp.where(mine, block.astype(F32), 0.0).astype(BF16)


def pick_block(near_ref, far_ref, block):
    return near_ref.at[block, 0] if block < 2 else far_ref.at[block - 2, 0]


def attend_kernel(row, heads, blocks, padded, need_ref, col_ref, row_ref, q_ref, near_ref, far_ref, *refs):
    own_ref, pair_ref, lse_ref, queries, score, peak, total, acc, lses = refs[-9:]
    outs = (own_ref, pair_ref)
    tokens = own_ref.shape[1]
    slot = lax.broadcasted_iota(jnp.int32, (2 * tokens, 128), 1)
    for which in range(2):
        outs[which][...] = jnp.zeros_like(outs[which])
    windows = [head_window(head) for head in range(heads)]
    for head, (start, width, low) in enumerate(windows):
        for which in range(2):
            queries[head, which * tokens : (which + 1) * tokens, :width] = only_head(
                q_ref[which, 0, :, start : start + width], low
            )
    peak[...] = jnp.full_like(peak, MASKED)
    total[...] = jnp.zeros_like(total)
    acc[...] = jnp.zeros_like(acc)
    for block in range(blocks):

        @pl.when(need_ref[row, block] != 0)
        def _():
            side = pick_block(near_ref, far_ref, block)
            seen = col_ref[0] == row_ref[0, block : block + 1]
            for head, (start, width, _) in enumerate(windows):
                key = side[:, start : start + width]
                found = jnp.where(seen, dot(queries[head, :, :width], key, NT), MASKED)
                score[head, block] = found
                top = peak[head]
                for at in range(0, tokens, 128):
                    top = jnp.maximum(top, found[:, at : at + 128])
                peak[head] = top

    for head in range(heads):
        top = jnp.max(peak[head], axis=-1, keepdims=True) * (SCALE * LOG2E)
        peak[head] = jnp.broadcast_to(top, peak.shape[1:])

    for block in range(blocks):

        @pl.when(need_ref[row, block] != 0)
        def _():
            side = pick_block(near_ref, far_ref, block)
            for head, (start, width, _) in enumerate(windows):
                top, share = peak[head], total[head]
                pieces = []
                for at in range(0, tokens, 128):
                    part = jnp.exp2(score[head, block, :, at : at + 128] * (SCALE * LOG2E) - top)
                    share += part
                    pieces.append(part.astype(BF16))
                total[head] = share
                value = side[:, padded + start : padded + start + width]
                acc[head, :, :width] += dot(jnp.concatenate(pieces, axis=1), value)

    for head, (start, width, low) in enumerate(windows):
        norm = jnp.sum(total[head], axis=-1, keepdims=True)
        result = acc[head, :, :width] / norm
        mine = head_lanes(tokens, width, low)
        for which in range(2):
            kept = outs[which][0, :, start : start + width].astype(F32)
            fresh = result[which * tokens : (which + 1) * tokens]
            outs[which][0, :, start : start + width] = jnp.where(mine, fresh, kept).astype(BF16)
        lse = peak[head] + jnp.log2(norm)
        lses[...] = lse if head == 0 else jnp.where(slot == head, lse, lses[...])
    lse_ref[0] = lses[...].T[:heads]


def attend(row, query, near, far, need, seg_col, seg_row, heads, before):
    _, rows, tokens, padded = query.shape
    blocks = 2 + far.shape[0]
    narrow = pl.BlockSpec((1, tokens, padded), lambda i, need: (row, 0, 0))
    lines = pl.BlockSpec((1, heads, 2 * tokens), lambda i, need: (row, 0, 0))

    def stack(count, width):
        return pl.BlockSpec((count, 1, tokens, width), lambda i, need: (0, row, 0, 0))

    return pl.pallas_call(
        functools.partial(attend_kernel, row, heads, blocks, padded),
        out_shape=(
            jax.ShapeDtypeStruct((rows, tokens, padded), BF16),
            jax.ShapeDtypeStruct((rows, tokens, padded), BF16),
            jax.ShapeDtypeStruct((rows, heads, 2 * tokens), F32),
        ),
        grid_spec=pltpu.PrefetchScalarGridSpec(
            num_scalar_prefetch=1,
            grid=(1,),
            in_specs=[
                pl.BlockSpec((1, 2 * tokens, 1), lambda i, need: (row, 0, 0)),
                pl.BlockSpec((1, blocks, tokens), lambda i, need: (row, 0, 0)),
                stack(2, padded),
                stack(2, 2 * padded),
                stack(blocks - 2, 2 * padded),
            ]
            + [pl.BlockSpec(memory_space=pl.ANY)] * len(before),
            out_specs=(narrow, narrow, lines),
            scratch_shapes=[
                pltpu.VMEM((heads, 2 * tokens, WIN), BF16),
                pltpu.VMEM((heads, blocks, 2 * tokens, tokens), F32),
                pltpu.VMEM((heads, 2 * tokens, 128), F32),
                pltpu.VMEM((heads, 2 * tokens, 128), F32),
                pltpu.VMEM((heads, 2 * tokens, WIN), F32),
                pltpu.VMEM((2 * tokens, 128), F32),
            ],
        ),
        input_output_aliases={6 + i: i for i in range(len(before))},
        compiler_params=params(("arbitrary",)),
        cost_estimate=NOMINAL,
        name="attend",
    )(need, seg_col, seg_row, query, near, far, *before)


def attend_back_kernel(
    row, heads, blocks, padded, need_ref, col_ref, row_ref, pick_ref, q_ref, near_ref, far_ref, *refs
):
    grads, outs, lse_ref = refs[0:2], refs[2:4], refs[4]
    dq_ref, dnear_ref, dfar_ref, sums, inner_turn, queries, incoming, dq = refs[-8:]
    tokens = grads[0].shape[1]
    sums[...] = jnp.zeros_like(sums)
    for which in range(2):
        dq_ref[which, 0] = jnp.zeros((tokens, padded), BF16)
        product = grads[which][0].astype(F32) * outs[which][0].astype(F32)
        high = product.astype(BF16)
        rest = (product - high.astype(F32)).astype(BF16)
        inner_turn[:, which * tokens : (which + 1) * tokens] = dot(pick_ref[...], high, NT) + dot(
            pick_ref[...], rest, NT
        )
    windows = [head_window(head) for head in range(heads)]
    for head, (start, width, low) in enumerate(windows):
        for which in range(2):
            there = slice(which * tokens, (which + 1) * tokens)
            here = slice(start, start + width)
            queries[head, there, :width] = only_head(q_ref[which, 0, :, here], low)
            incoming[head, there, :width] = only_head(grads[which][0, :, here], low)
    dq[...] = jnp.zeros_like(dq)
    for block in range(blocks):

        @pl.when(need_ref[row, block] != 0)
        def _():
            side = pick_block(near_ref, far_ref, block)
            seen = col_ref[0, block] == row_ref[0]
            for head, (start, width, _) in enumerate(windows):
                end = start + width
                key, value = side[:, start:end], side[:, padded + start : padded + end]
                query, grad = queries[head, :, :width], incoming[head, :, :width]
                found = dot(key, query, NT) * (SCALE * LOG2E) - lse_ref[0, head : head + 1, :]
                prob = jnp.where(seen, jnp.exp2(found), 0.0)
                inner = inner_turn[head : head + 1, :]
                slope = (prob * (dot(value, grad, NT) - inner)).astype(BF16)
                sums[block, :, start:end] += dot(slope, query)
                sums[block, :, padded + start : padded + end] += dot(prob.astype(BF16), grad)
                dq[head, :, :width] += dot(slope, key, TN)

    for head, (start, width, low) in enumerate(windows):
        mine = head_lanes(tokens, width, low)
        for which in range(2):
            kept = dq_ref[which, 0, :, start : start + width].astype(F32)
            fresh = dq[head, which * tokens : (which + 1) * tokens, :width] * SCALE
            dq_ref[which, 0, :, start : start + width] = jnp.where(mine, fresh, kept).astype(BF16)
    for block in range(blocks):
        side = pick_block(dnear_ref, dfar_ref, block)
        side[:, :padded] = (sums[block, :, :padded] * SCALE).astype(BF16)
        side[:, padded:] = sums[block, :, padded:].astype(BF16)


def attend_back(row, query, near, far, grads, outs, lse, need, seg_col, seg_row, heads, before):
    _, rows, tokens, padded = query.shape
    blocks = 2 + far.shape[0]
    column = lax.broadcasted_iota(jnp.int32, (heads, padded), 1)
    pick = (column // HEAD_DIM == lax.broadcasted_iota(jnp.int32, (heads, padded), 0)).astype(BF16)
    narrow = pl.BlockSpec((1, tokens, padded), lambda i, need: (row, 0, 0))

    def stack(count, width):
        return pl.BlockSpec((count, 1, tokens, width), lambda i, need: (0, row, 0, 0))

    return pl.pallas_call(
        functools.partial(attend_back_kernel, row, heads, blocks, padded),
        out_shape=tuple(jax.ShapeDtypeStruct(a.shape, BF16) for a in (query, near, far)),
        grid_spec=pltpu.PrefetchScalarGridSpec(
            num_scalar_prefetch=1,
            grid=(1,),
            in_specs=[
                pl.BlockSpec((1, blocks, tokens, 1), lambda i, need: (row, 0, 0, 0)),
                pl.BlockSpec((1, 1, 2 * tokens), lambda i, need: (row, 0, 0)),
                pl.BlockSpec((heads, padded), lambda i, need: (0, 0)),
                stack(2, padded),
                stack(2, 2 * padded),
                stack(blocks - 2, 2 * padded),
            ]
            + [narrow] * 4
            + [pl.BlockSpec((1, heads, 2 * tokens), lambda i, need: (row, 0, 0))]
            + [pl.BlockSpec(memory_space=pl.ANY)] * len(before),
            out_specs=(stack(2, padded), stack(2, 2 * padded), stack(blocks - 2, 2 * padded)),
            scratch_shapes=[
                pltpu.VMEM((blocks, tokens, 2 * padded), F32),
                pltpu.VMEM((heads, 2 * tokens), F32),
                pltpu.VMEM((heads, 2 * tokens, WIN), BF16),
                pltpu.VMEM((heads, 2 * tokens, WIN), BF16),
                pltpu.VMEM((heads, 2 * tokens, WIN), F32),
            ],
        ),
        input_output_aliases={12 + i: i for i in range(len(before))},
        compiler_params=params(("arbitrary",)),
        cost_estimate=NOMINAL,
        name="attend_back",
    )(need, seg_col, seg_row, pick, query, near, far, *grads, *outs, lse, *before)


def local(
    patches,
    lengths,
    first_gain,
    first_shift,
    query_weight,
    query_bias,
    key_weight,
    value_weight,
    value_bias,
    output_weight,
    output_bias,
    second_gain,
    second_shift,
    hidden_weight,
    hidden_bias,
    down_weight,
    down_bias,
    cotangent,
):
    seq_count, shards = lax.axis_size("seq"), lax.axis_size("fsdp")
    place, me = lax.axis_index("seq"), lax.axis_index("fsdp")
    core = place & 1
    is_first = core == 0
    core_flag = core[None].astype(jnp.int32)
    rows, tokens, width = patches.shape
    flat = rows * tokens
    heads = width // HEAD_DIM // 2
    half = heads * HEAD_DIM
    padded = round_up(half, 128)
    ff = hidden_bias.shape[0]
    ff_half = round_up(ff, 256) // 2
    out_cols = padded
    out_cut = width - padded
    shard_rows = width // shards
    chain = Chain()

    def my_half(array, size, padded_size):
        first, second = array[..., :size], array[..., size:]
        grow = [(0, 0)] * (array.ndim - 1)
        first = jnp.pad(first, grow + [(0, padded_size - size)])
        second = jnp.pad(second, grow + [(0, padded_size - second.shape[-1])])
        return jnp.where(is_first, first, second)

    flights = Flights(chain)
    staged = shards == 8 and seq_count == 4
    y, z, zz = 1, 2, 4
    top = bits_of(seq_count)[0]

    inputs = patches.reshape(flat, width)
    incoming = cotangent.reshape(flat, width)
    shard_qkv, shard_out, vectors = chain.done(
        *attention_shards(
            core_flag,
            [query_weight, key_weight, value_weight, output_weight],
            [
                vector[None]
                for vector in (
                    first_gain,
                    first_shift,
                    query_bias,
                    value_bias,
                    output_bias,
                    second_gain,
                    second_shift,
                    down_bias,
                )
            ],
            half,
            padded,
        )
    )
    place_flag = place[None].astype(jnp.int32)

    def over(box_from, bits):
        return flights.send(box_from[0], "fsdp", bits)

    def both(stacked_lines, arrived):
        return jnp.concatenate([stacked_lines, arrived], axis=0)

    vectors = vectors[None]
    if staged:
        q = {0: [shard_qkv]}
        vec = flights.send(vectors, "fsdp", y)
        q[y] = over(q[0], y)
        far_raw = [flights.send(patches[0], "seq", 2)]
        q[z], q[zz] = over(q[0], z), over(q[0], zz)
        shard_out, vectors = flights.land(shard_out, vectors, through=vec)
        vectors = both(vectors, vec[0])
        vec = flights.send(vectors, "fsdp", z)
        shard_ho, shard_down = chain.done(
            *mlp_shards(core_flag, shard_out, hidden_weight, down_weight, ff_half)
        )
        h, d = {0: [shard_ho]}, {0: [shard_down]}
        lengths = flights.land(lengths, through=far_raw[0])
        h[y] = over(h[0], y)
        far_raw.append(flights.send(patches[1:].reshape(flat - tokens, width), "seq", 2))
        need, seg_rows, seg_cols, seg_near_row, seg_near_col = chain.done(
            *masks(lengths, place_flag, seq_count, tokens)
        )
        vectors = flights.land(vectors, through=vec)
        vectors = both(vectors, vec[0])
        vec = flights.send(vectors, "fsdp", zz)
        q[zz | z] = over(q[zz], z)
        q[z | y] = over(q[z], y)
        vectors = flights.land(vectors, through=h[y])
        q[zz | y] = over(q[zz], y)
        vectors = flights.land(vectors, through=q[zz | z])
        raw_pair = flights.send(inputs, "seq", 1)
        q[zz | z | y] = over(q[zz | z], y)
        h[z] = over(h[0], z)
        vectors = both(vectors, vec[0])
        meta = chain(jnp.stack([core, me]).astype(jnp.int32))
        stacked, bias_q, bias_kv = chain.done(*lay_vectors(meta, vectors, half, padded))
        gain_one, shift_one = stacked[0:1], stacked[1:2]
        gain_one = flights.land(gain_one, through=raw_pair)
        far_pair = [flights.send(box[0], "seq", 1) for box in far_raw]
        h[zz] = over(h[0], zz)
        normed_near = chain.done(norm([inputs, raw_pair[0]], gain_one, shift_one))
        bias_hidden = my_half(after(hidden_bias, gain_one).astype(F32)[None], ff_half, ff_half)
        gain_one = flights.land(gain_one, through=far_pair[-1])
        h[z | y], d[y] = over(h[z], y), over(d[0], y)
        w_q, w_kv = chain.done(*assemble({k: box[0] for k, box in q.items()}, me, padded))
    else:
        parts = gather_all(shard_qkv)
        for k in range(shards.bit_length() - 1):
            vectors = both(vectors, swap(vectors, "fsdp", 1 << k))
        shard_ho, shard_down = mlp_shards(core_flag, shard_out, hidden_weight, down_weight, ff_half)
        raw = {0: inputs}
        for bit in bits_of(seq_count):
            raw.update({j | bit: swap(part, "seq", bit) for j, part in list(raw.items())})
        need, seg_rows, seg_cols, seg_near_row, seg_near_col = masks(lengths, place_flag, seq_count, tokens)
        stacked, bias_q, bias_kv = lay_vectors(
            jnp.stack([core, me]).astype(jnp.int32), vectors, half, padded
        )
        gain_one, shift_one = stacked[0:1], stacked[1:2]
        normed_near = norm([raw[0], raw[1]], gain_one, shift_one)
        far_raw, far_pair = [[raw[j]] for j in range(2, seq_count)], []
        bias_hidden = my_half(hidden_bias.astype(F32)[None], ff_half, ff_half)
        w_q, w_kv = chain.done(*assemble(parts, me, padded))
    _, _, bias_query, bias_value, bias_output, gain_two, shift_two, bias_down = [
        stacked[i : i + 1] for i in range(8)
    ]

    near_in, w_q, w_kv = chain(normed_near, w_q, w_kv)
    (query,) = rows_matmul("query", [near_in], [w_q], with_bias, [bias_q], [like(2 * flat, padded)])
    near_in = after(near_in, query)
    (near,) = rows_matmul("near", [near_in], [w_kv], with_bias, [bias_kv], [like(2 * flat, 2 * padded)])
    chain.done(query, near)
    gain_one, w_kv = chain(gain_one, w_kv)
    normed_far = chain.done(norm([box[0] for box in far_raw + far_pair], gain_one, shift_one))
    if staged:
        w_kv = flights.land(w_kv, through=h[z | y])
        h[zz | y], h[zz | z] = over(h[zz], y), over(h[zz], z)
    far_in, w_kv = chain(normed_far, w_kv)
    (far,) = rows_matmul(
        "far", [far_in], [w_kv], with_bias, [bias_kv], [like(normed_far.shape[0], 2 * padded)]
    )
    chain.done(far)
    query = query.reshape(2, rows, tokens, padded)
    near = near.reshape(2, rows, tokens, 2 * padded)
    far = far.reshape(seq_count - 2, rows, tokens, 2 * padded)
    found = ()
    for row in range(rows):
        query, near, far = chain(query, near, far)
        if staged and row == 1:
            query = flights.land(query)
            h[zz | z | y] = over(h[zz | z], y)
            d[z], d[zz] = over(d[0], z), over(d[0], zz)
        found = chain.done(*attend(row, query, near, far, need, seg_near_col, seg_rows, heads, found))
    out_own, out_pair, lse = found
    if staged:
        out_own, out_pair = flights.land(out_own, out_pair)
        h_parts = {k: box[0] for k, box in h.items()}
    else:
        out_own, out_pair = flights.land(out_own, out_pair)
        h_parts = gather_all(chain(shard_ho))
    w_out_mine, w_hidden = chain.done(*assemble(h_parts, me, out_cols))
    out_pair, w_out_mine = chain(out_pair, w_out_mine)
    other_half = flights.send(out_pair, "seq", 1)
    w_out_other = flights.send(w_out_mine, "seq", 1)
    incoming_pair = flights.send(incoming, "seq", 1)
    w_out_mine, w_hidden = flights.land(w_out_mine, w_hidden, through=incoming_pair)
    if staged:
        d[zz | z], d[z | y] = over(d[zz], z), over(d[z], y)
    w_out = chain.done(both_cores(core_flag, w_out_mine, w_out_other[0], out_cut, width))
    own_half, w_out = chain(out_own.reshape(flat, padded), w_out)
    attended, middle, second = chain.done(
        *join(
            core_flag,
            own_half,
            other_half[0].reshape(flat, padded),
            inputs,
            w_out,
            bias_output,
            gain_two,
            shift_two,
            half,
        )
    )
    second_pair = flights.send(second, "seq", 1)
    incoming_own = chain(incoming)
    incoming_near = chain.done(stack_rows(incoming_own, incoming_pair[0]))
    second, w_hidden = flights.land(second, w_hidden)
    if staged:
        d[zz | y], d[zz | z | y] = over(d[zz], y), over(d[zz | z], y)
    act, slope, second_near = chain.done(*hidden([second, second_pair[0]], w_hidden, bias_hidden))

    incoming_near, act = chain(incoming_near, act)
    grad_down = chain.done(dot(incoming_near, act, TN).astype(BF16))
    part_down = lax.psum_scatter(grad_down, "fsdp", scatter_dimension=0, tiled=True)
    if staged:
        slope = flights.land(slope)
        d_parts = {k: box[0] for k, box in d.items()}
    else:
        d_parts = gather_all(chain(shard_down))
    w_down = chain.done(assemble(d_parts, me))
    incoming_near, slope, w_down = chain(incoming_near, slope, w_down)
    grad_pre, hidden_line = chain.done(
        *rows_matmul(
            "grad_pre",
            [incoming_near],
            [w_down],
            with_slope,
            [slope],
            [like(2 * flat, ff_half), like(1, ff_half, F32)],
        )
    )
    grad_pre = chain(grad_pre)
    back, back_pair = chain.done(
        *rows_matmul("back", [grad_pre], [w_hidden], plain, [], [like(2 * flat, width)], NT, True)
    )
    back_other = flights.send(back_pair, "seq", 1)
    second_near, grad_pre = chain(second_near, grad_pre)
    grad_hidden = chain.done(dot(second_near, grad_pre, TN).astype(BF16))
    part_hidden = lax.psum_scatter(grad_hidden, "fsdp", scatter_dimension=0, tiled=True)
    back = flights.land(back)
    grad_middle, branch, grad_mine, grad_send, lines = second_back(
        core_flag, middle, [back, back_other[0]], gain_two, incoming, w_out, hidden_line, half, padded
    )
    chain.done(branch, grad_send)
    grad_pair = flights.send(grad_send, "seq", 1)
    attended, branch = chain(attended, branch)
    out_keep, out_send, _ = chain.done(*weight_grad([attended], [branch], me, shards))
    out_keep, out_send = chain(out_keep, out_send)
    keep_mine, send_mine, keep_other, send_other = chain.done(
        *core_columns(core_flag, [out_keep, out_send], out_cols)
    )
    query = flights.land(query)

    links = [("seq", bit) for bit in bits_of(seq_count)] + [("fsdp", bit) for bit in bits_of(shards)]

    class Everywhere:
        def __init__(self, array, order):
            self.array, self.todo, self.box = array, list(order), None

        def send(self):
            if self.todo:
                self.box = flights.send(self.array, *self.todo.pop(0))

        def step(self):
            if self.box is not None:
                self.array = chain.done(*add_rows(self.array, self.box[0], F32))
                self.box = None
                self.send()

    small = Everywhere(lines, links)
    keep_back, send_back = flights.send(keep_other, "seq", 1), flights.send(send_other, "seq", 1)
    small.send()
    shape = (rows, tokens, padded)
    grads = [grad_mine.reshape(shape), grad_pair[0].reshape(shape)]
    found = ()
    far_bits = [2 << k for k in range(shards.bit_length() - 2)]
    out_bits = list(far_bits)

    def next_step(keep, box, bits):
        keep, send = scatter_step(keep, box[0], shard_rows)
        chain.done(keep)
        return keep, flights.send(send, "fsdp", bits.pop(0)) if bits else None

    def seq_rest(mine, arrived):
        for bit in bits_of(seq_count)[1:-1]:
            (mine,) = add_rows(mine, arrived)
            arrived = swap(mine, "seq", bit)
        return chain.done(*add_rows(mine, arrived, F32))

    for row in range(rows):
        query, near, far, *grads = chain(query, near, far, *grads)
        found = attend_back(
            row, query, near, far, grads, [out_own, out_pair], lse, need, seg_cols, seg_near_row, heads, found
        )
        chain.done(*found)
        query = flights.land(query)
        small.step()
        if row == 0:
            (out_keep,), (out_send,) = add_rows(keep_mine, keep_back[0]), add_rows(send_mine, send_back[0])
            chain.done(out_keep, out_send)
            out_box = flights.send(out_send, "fsdp", y)
        else:
            out_keep, out_box = next_step(out_keep, out_box, out_bits)
        if row == 1:
            part_down = chain(part_down)
            down_seq = flights.send(part_down, "seq", top)
        if row == 2:
            down_total = seq_rest(part_down, down_seq[0])
            down_other = flights.send(down_total, "seq", 1)
    dq, dnear, dfar = [g.reshape(-1, g.shape[-1]) for g in found]
    dfar, w_kv = chain(dfar, w_kv)
    two = seq_count == 4
    back_far = rows_matmul("back_far", [dfar], [w_kv], plain, [], [like(dfar.shape[0], width)], NT, two)
    chain.done(*back_far)
    dnear = flights.land(dnear)
    small.step()
    while out_box is not None:
        out_keep, out_box = next_step(out_keep, out_box, out_bits)
        if out_box is not None:
            dnear = flights.land(dnear)
    out_seq = flights.send(out_keep, "seq", top)
    if two:
        far_parts = {2 + i: part for i, part in enumerate(back_far)}
    else:
        far_parts = {j: back_far[0][(j - 2) * flat : (j - 1) * flat] for j in range(2, seq_count)}
    far_sent = {j: flights.send(part, "seq", 1) for j, part in far_parts.items() if j & 1}
    normed_near, dnear, dfar = chain(normed_near, dnear, dfar)
    kv_keep, kv_send, kv_sums = chain.done(
        *weight_grad([normed_near, normed_far], [dnear, dfar], me, shards)
    )
    dq = flights.land(dq)
    kv_box = flights.send(kv_send, "fsdp", y)
    far_sums = {j: add_rows(far_parts[j], far_sent[j | 1][0])[0] for j in far_parts if not j & 1}
    chain.done(*far_sums.values())
    arrived = []
    for bit in bits_of(seq_count)[:-1]:
        moved = {j: flights.send(part, "seq", bit) for j, part in far_sums.items() if j & bit}
        far_sums = {j: part for j, part in far_sums.items() if not j & bit}
        for j, box in moved.items():
            if j == bit:
                arrived.append(box)
            else:
                (far_sums[j ^ bit],) = add_rows(far_sums[j ^ bit], box[0])
    small.step()
    out_total = seq_rest(out_keep, out_seq[0])
    dq, dnear = chain(dq, dnear)
    back_own, back_pair = chain.done(
        *rows_matmul("back_near", [dq, dnear], [w_q, w_kv], plain, [], [like(2 * flat, width)], NT, True)
    )
    pair_back = flights.send(back_pair, "seq", 1)
    normed_near, dq = chain(normed_near, dq)
    q_keep, q_send, q_sums = chain.done(*weight_grad([normed_near], [dq], me, shards))
    q_box = flights.send(q_send, "fsdp", y)
    act, middle = chain(act, middle)
    (down_pair,) = rows_matmul(
        "down_pair", [act], [w_down], plain, [], [like(flat, width)], NT, first_row=flat
    )
    chain.done(down_pair)
    down_back = flights.send(down_pair, "seq", 1)
    out_other = flights.send(out_total, "seq", 1)
    kv_bits, q_bits = list(far_bits), list(far_bits)
    down_total = flights.land(down_total, through=kv_box)
    kv_keep, kv_box = next_step(kv_keep, kv_box, kv_bits)
    full_down = chain.done(both_cores(core_flag, chain(down_total), down_other[0], ff_half, ff, turn=True))
    late_in = flights.land(inputs, through=pair_back)
    grad_patches, late = chain.done(
        *first_back(
            core_flag,
            late_in,
            [back_own, pair_back[0]] + [box[0] for box in arrived],
            gain_one,
            grad_middle,
            q_sums,
            kv_sums,
            half,
        )
    )
    late = Everywhere(late, links[1:] + links[:1])
    late.send()
    out_total = flights.land(out_total, through=out_other)
    q_keep, q_box = next_step(q_keep, q_box, q_bits)
    act, middle = chain(act, middle)
    (layer_output,) = rows_matmul(
        "down_own", [act], [w_down], layer_end, [middle, down_back[0], bias_down], [like(flat, width)], NT
    )
    layer_output = chain.done(layer_output).reshape(rows, tokens, width)
    part_hidden = chain(part_hidden)
    hidden_seq = flights.send(part_hidden, "seq", top)
    full_out = chain.done(both_cores(core_flag, chain(out_total), out_other[0], out_cut, width))
    done = {}
    full_hidden = None

    def finish(name, keep, box):
        if name not in done:
            done[name] = [keep, flights.send(keep, "seq", top)]
        elif len(done[name]) == 2:
            total = seq_rest(done[name][0], done[name][1][0])
            done[name] = [total, flights.send(total, "seq", 1), None]

    while flights.open:
        full_out = flights.land(full_out)
        late.step()
        small.step()
        if kv_box is not None:
            kv_keep, kv_box = next_step(kv_keep, kv_box, kv_bits)
        if kv_box is None:
            finish("kv", kv_keep, kv_box)
        if q_box is not None:
            q_keep, q_box = next_step(q_keep, q_box, q_bits)
        if q_box is None:
            finish("q", q_keep, q_box)
        if full_hidden is None and "hidden" in done:
            total, other, _ = done["hidden"]
            full_hidden = chain.done(both_cores(core_flag, chain(total), other[0], ff_half, ff))
        if "hidden" not in done:
            total = seq_rest(part_hidden, hidden_seq[0])
            done["hidden"] = [total, flights.send(total, "seq", 1), None]
    kv_total, kv_other = done["kv"][0], done["kv"][1][0]
    q_total, q_other = done["q"][0], done["q"][1][0]

    own_lines = lax.dynamic_slice_in_dim(small.array, me * shard_rows, shard_rows, 1)
    late_lines = lax.dynamic_slice_in_dim(late.array, me * shard_rows, shard_rows, 1)
    cuts = [width, ff_half - width, width, ff - ff_half - width]
    full_bias = jnp.concatenate([small.array[4 + i, :size] for i, size in enumerate(cuts)])
    full_query = both_cores(core_flag, q_total, q_other, half, width)
    full_key = both_cores(core_flag, kv_total, kv_other, half, width)
    full_value = both_cores(core_flag, kv_total, kv_other, half, width, padded)
    return (
        layer_output,
        grad_patches.reshape(rows, tokens, width),
        late_lines[0],
        late_lines[1],
        full_query,
        late_lines[2],
        full_key,
        full_value,
        late_lines[3],
        full_out,
        own_lines[2],
        own_lines[0],
        own_lines[1],
        full_hidden,
        full_bias,
        full_down,
        own_lines[3],
    )


def solution(mesh):
    shard, line, tokens = P("fsdp", None), P("fsdp"), P("fsdp", "seq", None)
    in_specs = (
        tokens,
        shard,
        line,
        line,
        shard,
        line,
        shard,
        shard,
        line,
        shard,
        line,
        line,
        line,
        shard,
        P(),
        P(None, "fsdp"),
        line,
        tokens,
    )
    out_specs = (
        tokens,
        tokens,
        line,
        line,
        shard,
        line,
        shard,
        shard,
        line,
        shard,
        line,
        line,
        line,
        shard,
        P(),
        P(None, "fsdp"),
        line,
    )
    return jax.shard_map(local, mesh=mesh, in_specs=in_specs, out_specs=out_specs, check_vma=False)
```

```python
import functools
import math

import jax
import jax.numpy as jnp
from jax import lax
from jax.experimental import pallas as pl
from jax.experimental.pallas import tpu as pltpu
from jax.sharding import PartitionSpec as P

HEAD_DIM = 72
EPS = 1e-06
GELU_COEF = math.sqrt(2.0 / math.pi)
MASKED = -1e30
F32 = jnp.float32
BF16 = jnp.bfloat16
SCALE = 1.0 / math.sqrt(HEAD_DIM)
WIN = 256
LOG2E = math.log2(math.e)
VMEM = 60 << 20
NOMINAL = pl.CostEstimate(flops=1, transcendentals=0, bytes_accessed=1)


def round_up(value, step):
    return (value + step - 1) // step * step


def dot(left, right, dims=((1,), (0,))):
    return lax.dot_general(left, right, (dims, ((), ())), preferred_element_type=F32)


NT = ((1,), (1,))
TN = ((0,), (0,))


def params(semantics):
    return pltpu.CompilerParams(dimension_semantics=semantics, vmem_limit_bytes=VMEM)


def swap(array, axis, bits):
    size = lax.axis_size(axis)
    return lax.ppermute(array, axis, [(i, i ^ bits) for i in range(size)])


def bits_of(size):
    return [1 << k for k in reversed(range(size.bit_length() - 1))]


def after(value, *earlier):
    return lax.optimization_barrier((value,) + tuple(earlier))[0]


class Chain:
    def __init__(self):
        self.last = ()

    def __call__(self, *values, wait=()):
        held = lax.optimization_barrier(tuple(values) + tuple(self.last) + tuple(wait))
        return held[: len(values)] if len(values) > 1 else held[0]

    def done(self, *results):
        self.last = results
        return results if len(results) > 1 else results[0]


class Flights:
    def __init__(self, chain):
        self.chain, self.open = chain, []

    def send(self, array, axis, bits):
        self.open.append([swap(array, axis, bits)])
        return self.open[-1]

    def land(self, *values, through=None):
        count = len(self.open)
        if through is not None:
            count = sum(i + 1 for i, box in enumerate(self.open) if box is through)
        ready, self.open = self.open[:count], self.open[count:]
        held = self.chain(*[box[0] for box in ready], *values)
        held = held if isinstance(held, (tuple, list)) else [held]
        for box, array in zip(ready, held):
            box[0] = array
        rest = list(held[len(ready) :])
        return rest if len(rest) > 1 else rest[0] if rest else None


def in_order(parts, me):
    count = len(parts)
    return jnp.take(jnp.stack([parts[d] for d in range(count)]), me ^ jnp.arange(count), axis=0)


def gather_all(shard):
    parts = {0: shard}
    for bit in bits_of(lax.axis_size("fsdp")):
        parts.update({d | bit: swap(part, "fsdp", bit) for d, part in list(parts.items())})
    return parts


def rel_position(distance, count):
    width = count.bit_length() - 1
    return sum(((distance >> k) & 1) << (width - 1 - k) for k in range(width))


def assemble_kernel(count, rows, single, off_ref, *refs):
    outs = refs[count:]

    def fill(out_ref):
        for distance in range(count):
            start = pl.multiple_of(off_ref[distance], 16)
            out_ref[pl.ds(start, rows), :] = refs[distance][...]

    if single:
        fill(outs[0])
    else:
        pl.when(pl.program_id(0) == 0)(lambda: fill(outs[0]))
        pl.when(pl.program_id(0) > 0)(lambda: fill(outs[1]))


def assemble(parts, me, cut=None):
    count = len(parts)
    rows, cols = parts[0].shape
    if rows % 16:
        full = in_order(parts, me).reshape(count * rows, cols)
        return (full[:, :cut], full[:, cut:]) if cut else full
    offsets = ((me ^ jnp.arange(count, dtype=jnp.int32)) * rows).astype(jnp.int32)
    tile = cut or min(cols, 1152)
    widths = [cut, cols - cut] if cut else [cols]
    maps = [lambda n, off: (0, 0), lambda n, off: (0, jnp.maximum(n - 1, 0))]
    if not cut:
        maps = [lambda n, off: (0, n)]
    outs = pl.pallas_call(
        functools.partial(assemble_kernel, count, rows, not cut),
        out_shape=[jax.ShapeDtypeStruct((count * rows, w), parts[0].dtype) for w in widths],
        grid_spec=pltpu.PrefetchScalarGridSpec(
            num_scalar_prefetch=1,
            grid=(pl.cdiv(cols, tile),),
            in_specs=[pl.BlockSpec((rows, tile), lambda n, off: (0, n))] * count,
            out_specs=[pl.BlockSpec((count * rows, tile), m) for m in maps],
        ),
        compiler_params=params(("arbitrary",)),
        cost_estimate=NOMINAL,
        name="assemble",
    )(offsets, *[parts[d] for d in range(count)])
    return outs if cut else outs[0]


def weight_grad_kernel(pairs, count, rows, pos_ref, *refs):
    lefts, rights = refs[:pairs], refs[pairs : 2 * pairs]
    keep_ref, send_ref, sum_ref = refs[2 * pairs :]
    total = dot(lefts[0][...], rights[0][...], TN)
    for i in range(1, pairs):
        total += dot(lefts[i][...], rights[i][...], TN)
    sum_ref[...] = sum(dot(jnp.ones((8, r.shape[0]), BF16), r[...]) for r in rights)
    for shard in range(count):
        start = pl.multiple_of(pos_ref[shard], 16)
        block = total[shard * rows : (shard + 1) * rows].astype(BF16)

        @pl.when(pos_ref[count] == shard % 2)
        def _():
            keep_ref[pl.ds(start, rows), :] = block

        @pl.when(pos_ref[count] != shard % 2)
        def _():
            send_ref[pl.ds(start, rows), :] = block


def weight_grad(lefts, rights, me, count):
    width = lefts[0].shape[1]
    cols = rights[0].shape[1]
    rows = width // count
    order = me ^ jnp.arange(count, dtype=jnp.int32)
    table = jnp.array([rel_position(d, count) for d in range(count)], jnp.int32)
    half = count // 2
    if rows % 16:
        total = sum(dot(a, b, TN) for a, b in zip(lefts, rights))
        by_distance = jnp.take(total.astype(BF16).reshape(count, rows, cols), order, axis=0)
        back = [0] * count
        for d in range(count):
            back[rel_position(d, count)] = d
        placed = jnp.take(by_distance, jnp.array(back), axis=0).reshape(width, cols)
        ones = [jnp.ones((8, b.shape[0]), BF16) for b in rights]
        sums = sum(dot(one, b) for one, b in zip(ones, rights))
        return placed[: width // 2], placed[width // 2 :], sums
    positions = jnp.concatenate([table[order] % half * rows, (me & 1)[None]]).astype(jnp.int32)
    tile = 256
    pairs = len(lefts)
    return pl.pallas_call(
        functools.partial(weight_grad_kernel, pairs, count, rows),
        out_shape=[jax.ShapeDtypeStruct((width // 2, cols), BF16)] * 2
        + [jax.ShapeDtypeStruct((8, cols), F32)],
        grid_spec=pltpu.PrefetchScalarGridSpec(
            num_scalar_prefetch=1,
            grid=(pl.cdiv(cols, tile),),
            in_specs=[
                pl.BlockSpec(a.shape, lambda n, off: (0, 0), pipeline_mode=pl.Buffered(1))
                for a in lefts
            ]
            + [pl.BlockSpec((b.shape[0], tile), lambda n, off: (0, n)) for b in rights],
            out_specs=[pl.BlockSpec((width // 2, tile), lambda n, off: (0, n))] * 2
            + [pl.BlockSpec((8, tile), lambda n, off: (0, n))],
        ),
        compiler_params=params(("arbitrary",)),
        cost_estimate=NOMINAL,
        name="weight_grad",
    )(positions, *lefts, *rights)


def normalized(values):
    center = values - jnp.mean(values, axis=-1, keepdims=True)
    spread = jnp.mean(center * center, axis=-1, keepdims=True)
    inverse = lax.rsqrt(spread + EPS)
    return center * inverse, inverse


def row_block(rows):
    return 256 if rows % 256 == 0 else 128 if rows % 128 == 0 else rows


def norm(arrays, gain, shift):
    width = arrays[0].shape[1]
    block = min(row_block(a.shape[0]) for a in arrays)
    steps = [a.shape[0] // block for a in arrays]
    firsts = [sum(steps[:k]) for k in range(len(steps))]
    count, total = len(arrays), sum(steps)

    def kernel(*refs):
        gain_ref, shift_ref, out_ref = refs[count:]
        at = pl.program_id(0)
        for k in range(count):

            @pl.when((at >= firsts[k]) & (at < firsts[k] + steps[k]))
            def _():
                hat, _ = normalized(refs[k][...].astype(F32))
                out_ref[...] = (hat * gain_ref[...] + shift_ref[...]).astype(BF16)

    line = pl.BlockSpec((1, width), lambda i: (0, 0))
    return pl.pallas_call(
        kernel,
        out_shape=jax.ShapeDtypeStruct((total * block, width), BF16),
        grid=(total,),
        in_specs=[
            pl.BlockSpec((block, width), lambda i, k=k: (jnp.clip(i - firsts[k], 0, steps[k] - 1), 0))
            for k in range(count)
        ]
        + [line, line],
        out_specs=pl.BlockSpec((block, width), lambda i: (i, 0)),
        compiler_params=params(("arbitrary",)),
        cost_estimate=NOMINAL,
        name="norm",
    )(*arrays, gain, shift)


def join_kernel(half, core_ref, own_ref, other_ref, x_ref, w_ref, b_ref, g_ref, s_ref, *outs):
    att_ref, mid_ref, out_ref = outs
    own, other = own_ref[:, :half], other_ref[:, :half]

    @pl.when(core_ref[0] == 0)
    def _():
        att_ref[...] = jnp.concatenate([own, other], axis=1)

    @pl.when(core_ref[0] != 0)
    def _():
        att_ref[...] = jnp.concatenate([other, own], axis=1)

    middle = x_ref[...].astype(F32) + dot(att_ref[...], w_ref[...]) + b_ref[...]
    mid_ref[...] = middle
    hat, _ = normalized(middle)
    out_ref[...] = (hat * g_ref[...] + s_ref[...]).astype(BF16)


def join(core, own, other, inputs, weight, bias, gain, shift, half):
    rows, width = inputs.shape
    padded = own.shape[1]
    block = row_block(rows)
    line = pl.BlockSpec((1, width), lambda i, c: (0, 0))
    wide = pl.BlockSpec((block, width), lambda i, c: (i, 0))
    part = pl.BlockSpec((block, padded), lambda i, c: (i, 0))
    return pl.pallas_call(
        functools.partial(join_kernel, half),
        out_shape=(
            jax.ShapeDtypeStruct((rows, width), BF16),
            jax.ShapeDtypeStruct((rows, width), F32),
            jax.ShapeDtypeStruct((rows, width), BF16),
        ),
        grid_spec=pltpu.PrefetchScalarGridSpec(
            num_scalar_prefetch=1,
            grid=(rows // block,),
            in_specs=[
                part,
                part,
                wide,
                pl.BlockSpec((width, width), lambda i, c: (0, 0), pipeline_mode=pl.Buffered(1)),
                line,
                line,
                line,
            ],
            out_specs=(wide, wide, wide),
        ),
        compiler_params=params(("arbitrary",)),
        cost_estimate=NOMINAL,
        name="join",
    )(core, own, other, inputs, weight, bias, gain, shift)


def norm_back_values(x_ref, grads, gain_ref, add_ref, lines_ref):
    hat, inverse = normalized(x_ref[...].astype(F32))
    grad = grads[0][...].astype(F32)
    for other in grads[1:]:
        grad += other[...].astype(F32)
    scaled = grad * gain_ref[...]
    first = jnp.mean(scaled, axis=-1, keepdims=True)
    second = jnp.mean(scaled * hat, axis=-1, keepdims=True)

    @pl.when(pl.program_id(0) == 0)
    def _():
        lines_ref[...] = jnp.zeros_like(lines_ref)

    lines_ref[0:1] += jnp.sum(grad * hat, axis=0, keepdims=True)
    lines_ref[1:2] += jnp.sum(grad, axis=0, keepdims=True)
    return add_ref[...].astype(F32) + inverse * (scaled - first - hat * second)


def first_back(core, values, grads, gain, add, q_sums, kv_sums, half):
    rows, width = values.shape
    block = row_block(rows)
    count = len(grads)
    padded = q_sums.shape[1]

    def kernel(core_ref, x_ref, *refs):
        gain_ref, add_ref, q_ref, kv_ref, dx_ref, lines_ref = refs[count:]
        dx_ref[...] = norm_back_values(x_ref, refs[:count], gain_ref, add_ref, lines_ref)
        for line, part in ((2, q_ref[0:1, :half]), (3, kv_ref[0:1, padded : padded + half])):
            none = jnp.zeros_like(part)

            @pl.when(core_ref[0] == 0)
            def _():
                lines_ref[line : line + 1] = jnp.concatenate([part, none], axis=1)

            @pl.when(core_ref[0] != 0)
            def _():
                lines_ref[line : line + 1] = jnp.concatenate([none, part], axis=1)

    wide = pl.BlockSpec((block, width), lambda i, c: (i, 0))
    return pl.pallas_call(
        kernel,
        out_shape=(
            jax.ShapeDtypeStruct((rows, width), F32),
            jax.ShapeDtypeStruct((8, width), F32),
        ),
        grid_spec=pltpu.PrefetchScalarGridSpec(
            num_scalar_prefetch=1,
            grid=(rows // block,),
            in_specs=[wide] * (1 + count)
            + [
                pl.BlockSpec((1, width), lambda i, c: (0, 0)),
                wide,
                pl.BlockSpec(q_sums.shape, lambda i, c: (0, 0)),
                pl.BlockSpec(kv_sums.shape, lambda i, c: (0, 0)),
            ],
            out_specs=(wide, pl.BlockSpec((8, width), lambda i, c: (0, 0))),
        ),
        compiler_params=params(("arbitrary",)),
        cost_estimate=NOMINAL,
        name="first_back",
    )(core, values, *grads, gain, add, q_sums, kv_sums)


def second_back(core, values, grads, gain, add, weight, hidden_line, half, padded):
    rows, width = values.shape
    block = row_block(rows)
    count = len(grads)

    def kernel(core_ref, x_ref, *refs):
        gain_ref, add_ref, w_ref, hid_ref, dx_ref, low_ref, mine_ref, send_ref, lines_ref = refs[count:]
        total = norm_back_values(x_ref, refs[:count], gain_ref, add_ref, lines_ref)
        low = total.astype(BF16)
        dx_ref[...] = total
        low_ref[...] = low
        lines_ref[2:3] += jnp.sum(low.astype(F32), axis=0, keepdims=True)
        lines_ref[3:4] += jnp.sum(add_ref[...].astype(F32), axis=0, keepdims=True)
        spare = hid_ref.shape[1] - width
        for core in range(2):

            @pl.when(core_ref[0] == core)
            def _():
                lines_ref[4 + 2 * core : 5 + 2 * core] = hid_ref[:, :width]
                lines_ref[5 + 2 * core : 6 + 2 * core, :spare] = hid_ref[:, width:]

        back = dot(low, w_ref[...], NT).astype(BF16)
        empty = jnp.zeros((block, padded - half), BF16)
        halves = [jnp.concatenate([back[:, i * half : (i + 1) * half], empty], axis=1) for i in range(2)]

        @pl.when(core_ref[0] == 0)
        def _():
            mine_ref[...], send_ref[...] = halves[0], halves[1]

        @pl.when(core_ref[0] != 0)
        def _():
            mine_ref[...], send_ref[...] = halves[1], halves[0]

    wide = pl.BlockSpec((block, width), lambda i, c: (i, 0))
    part = pl.BlockSpec((block, padded), lambda i, c: (i, 0))
    line = pl.BlockSpec((1, width), lambda i, c: (0, 0))
    square = pl.BlockSpec((width, width), lambda i, c: (0, 0), pipeline_mode=pl.Buffered(1))
    return pl.pallas_call(
        kernel,
        out_shape=(
            jax.ShapeDtypeStruct((rows, width), F32),
            jax.ShapeDtypeStruct((rows, width), BF16),
            jax.ShapeDtypeStruct((rows, padded), BF16),
            jax.ShapeDtypeStruct((rows, padded), BF16),
            jax.ShapeDtypeStruct((8, width), F32),
        ),
        grid_spec=pltpu.PrefetchScalarGridSpec(
            num_scalar_prefetch=1,
            grid=(rows // block,),
            in_specs=[wide] * (1 + count)
            + [line, wide, square, pl.BlockSpec(hidden_line.shape, lambda i, c: (0, 0))],
            out_specs=(wide, wide, part, part, pl.BlockSpec((8, width), lambda i, c: (0, 0))),
        ),
        compiler_params=params(("arbitrary",)),
        cost_estimate=NOMINAL,
        name="second_back",
    )(core, values, *grads, gain, add, weight, hidden_line)


def rows_matmul(name, lefts, weights, finish, extras, outs, dims=((1,), (0,)), split=False, first_row=0):
    rows = outs[0].shape[0]
    block = row_block(rows)
    steps = rows // block
    half = steps // 2
    count, terms = len(lefts), len(lefts) + len(weights)

    def kernel(*refs):
        total = dot(refs[0][...], refs[count][...], dims)
        for i in range(1, count):
            total += dot(refs[i][...], refs[count + i][...], dims)
        results = finish(total, *refs[terms : terms + len(extras)])
        targets = refs[terms + len(extras) :]
        if split:

            @pl.when(pl.program_id(0) < half)
            def _():
                targets[0][...] = results[0]

            @pl.when(pl.program_id(0) >= half)
            def _():
                targets[1][...] = results[0]

            targets = targets[1:]
        else:
            targets[0][...] = results[0]
        for target, result in zip(targets[1:], results[1:]):

            @pl.when(pl.program_id(0) == 0)
            def _():
                target[...] = jnp.zeros_like(target)

            target[...] += result

    def by_rows(array):
        return pl.BlockSpec((block, array.shape[1]), lambda i: (i, 0))

    def whole(array):
        return pl.BlockSpec(array.shape, lambda i: (0, 0), pipeline_mode=pl.Buffered(1))

    first = outs[0]
    if split:
        part = jax.ShapeDtypeStruct((rows // 2, first.shape[1]), first.dtype)
        shapes = [part, part] + list(outs[1:])
        specs = [
            pl.BlockSpec((block, first.shape[1]), lambda i: (jnp.minimum(i, half - 1), 0)),
            pl.BlockSpec((block, first.shape[1]), lambda i: (jnp.maximum(i - half, 0), 0)),
        ]
    else:
        shapes, specs = list(outs), [by_rows(first)]
    specs += [pl.BlockSpec(out.shape, lambda i: (0, 0)) for out in outs[1:]]
    return pl.pallas_call(
        kernel,
        out_shape=shapes,
        grid=(steps,),
        in_specs=[
            pl.BlockSpec((block, a.shape[1]), lambda i: (i + first_row // block, 0)) for a in lefts
        ]
        + [whole(w) for w in weights]
        + [by_rows(e) if e.shape[0] == rows else whole(e) for e in extras],
        out_specs=specs,
        compiler_params=params(("arbitrary",)),
        cost_estimate=NOMINAL,
        name=name,
    )(*lefts, *weights, *extras)


def like(rows, cols, kind=BF16):
    return jax.ShapeDtypeStruct((rows, cols), kind)


def plain(total):
    return (total.astype(BF16),)


def with_bias(total, bias_ref):
    return ((total + bias_ref[...]).astype(BF16),)


def with_slope(total, slope_ref):
    low = (total * slope_ref[...].astype(F32)).astype(BF16)
    return low, jnp.sum(low.astype(F32), axis=0, keepdims=True)


def layer_end(total, middle_ref, other_ref, bias_ref):
    return ((middle_ref[...] + total + other_ref[...].astype(F32) + bias_ref[...]).astype(BF16),)


def small_call(kernel, outs, scalars, arrays, name):
    vmem = pl.BlockSpec(memory_space=pltpu.VMEM)
    return pl.pallas_call(
        kernel,
        out_shape=outs,
        in_specs=[pl.BlockSpec(memory_space=pltpu.SMEM)] * len(scalars) + [vmem] * len(arrays),
        out_specs=[vmem] * len(outs),
        compiler_params=pltpu.CompilerParams(vmem_limit_bytes=VMEM),
        cost_estimate=NOMINAL,
        name=name,
    )(*scalars, *arrays)


def add_rows(left, right, kind=BF16, pieces=1):
    size = left.shape[0] // pieces
    parts = [slice(i * size, (i + 1) * size) for i in range(pieces)]
    return [(left[part].astype(F32) + right[part].astype(F32)).astype(kind) for part in parts]


def scatter_step(keep, arrived, rows):
    if keep.shape[0] == rows:
        return add_rows(keep, arrived)[0], None
    return add_rows(keep, arrived, BF16, 2)


def both_cores(core, mine, other, size, total, start=0, turn=False):
    rows = mine.shape[0]

    def kernel(core_ref, mine_ref, other_ref, out_ref):
        for at, refs in ((0, (mine_ref, other_ref)), (1, (other_ref, mine_ref))):

            @pl.when(core_ref[0] == at)
            def _():
                first = refs[0][:, start : start + size]
                second = refs[1][:, start : start + total - size]
                if turn:
                    out_ref[:size], out_ref[size:] = first.T, second.T
                else:
                    out_ref[...] = jnp.concatenate([first, second], axis=1)

    shape = like(total, rows, mine.dtype) if turn else like(rows, total, mine.dtype)
    return small_call(kernel, [shape], [core], [mine, other], "both_cores")[0]


def both_columns(is_first, mine, other, size, total, start=0):
    mine, other = mine[:, start:], other[:, start:]
    return jnp.where(
        is_first,
        jnp.concatenate([mine[:, :size], other[:, : total - size]], axis=1),
        jnp.concatenate([other[:, :size], mine[:, : total - size]], axis=1),
    )


def core_columns(core, arrays, cols):
    rows, width = arrays[0].shape

    def kernel(core_ref, *refs):
        for at in range(2):

            @pl.when(core_ref[0] == at)
            def _():
                for i in range(len(arrays)):
                    for k, where in enumerate((at, 1 - at)):
                        low = where * (width - cols)
                        refs[len(arrays) * (1 + k) + i][...] = refs[i][:, low : low + cols]

    return small_call(kernel, [like(rows, cols)] * (2 * len(arrays)), [core], arrays, "core_columns")


def stack_rows(first, second):
    rows, cols = first.shape
    block = row_block(rows)
    steps = rows // block

    def kernel(first_ref, second_ref, out_ref):
        for i, ref in enumerate((first_ref, second_ref)):

            @pl.when(pl.program_id(0) // steps == i)
            def _():
                out_ref[...] = ref[...]

    return pl.pallas_call(
        kernel,
        out_shape=like(2 * rows, cols),
        grid=(2 * steps,),
        in_specs=[
            pl.BlockSpec((block, cols), lambda i: (jnp.minimum(i, steps - 1), 0)),
            pl.BlockSpec((block, cols), lambda i: (jnp.maximum(i - steps, 0), 0)),
        ],
        out_specs=pl.BlockSpec((block, cols), lambda i: (i, 0)),
        compiler_params=params(("arbitrary",)),
        cost_estimate=NOMINAL,
        name="stack_rows",
    )(first, second)


def mask_kernel(rows, tokens, blocks, len_ref, place_ref, need_ref, row_ref, col_ref, near_row, near_col):
    place = place_ref[0]
    for row in range(rows):
        ends = [len_ref[row, 0]]
        for p in range(1, len_ref.shape[1]):
            ends.append(ends[-1] + len_ref[row, p])

        def pictures(position):
            return sum((position >= end).astype(jnp.int32) for end in ends)

        def segment(position):
            return jnp.where(position < ends[-1], pictures(position), 1000 + position)

        spans = []
        for block in range(blocks):
            start = jnp.bitwise_xor(place, block) * tokens
            across = segment(start + lax.broadcasted_iota(jnp.int32, (1, tokens), 1))
            down = segment(start + lax.broadcasted_iota(jnp.int32, (tokens, 1), 0))
            row_ref[row, block : block + 1] = across
            col_ref[row, block] = down
            if block < 2:
                near_row[row, :, block * tokens : (block + 1) * tokens] = across
                near_col[row, block * tokens : (block + 1) * tokens] = down
            last = jnp.minimum(start + tokens, ends[-1]) - 1
            low = sum(jnp.where(start >= end, 1, 0) for end in ends)
            high = sum(jnp.where(last >= end, 1, 0) for end in ends)
            spans.append((start < ends[-1], low, high))
        for block, (real, low, high) in enumerate(spans):
            if block < 2:
                need_ref[row, block] = 1
            else:
                need_ref[row, block] = sum(
                    jnp.where(real & ok & (low <= top) & (bottom <= high), 1, 0) for ok, bottom, top in spans[:2]
                )


def masks(lengths, place, blocks, tokens):
    rows = lengths.shape[0]
    shapes = [(rows, blocks, tokens), (rows, blocks, tokens, 1), (rows, 1, 2 * tokens), (rows, 2 * tokens, 1)]
    smem = pl.BlockSpec(memory_space=pltpu.SMEM)
    return pl.pallas_call(
        functools.partial(mask_kernel, rows, tokens, blocks),
        out_shape=[jax.ShapeDtypeStruct((rows, blocks), jnp.int32)]
        + [jax.ShapeDtypeStruct(shape, jnp.int32) for shape in shapes],
        in_specs=[smem, smem],
        out_specs=[smem] + [pl.BlockSpec(memory_space=pltpu.VMEM)] * 4,
        compiler_params=pltpu.CompilerParams(vmem_limit_bytes=VMEM),
        cost_estimate=NOMINAL,
        name="masks",
    )(lengths, place)


def lay_vectors(meta, parts, half, padded):
    count, lines, size = parts.shape

    def kernel(meta_ref, parts_ref, lines_ref, q_ref, kv_ref):
        for shard in range(count):
            block = parts_ref[jnp.bitwise_xor(meta_ref[1], shard)]
            lines_ref[:, shard * size : (shard + 1) * size] = block.astype(F32)
        q_ref[...] = jnp.zeros_like(q_ref)
        kv_ref[...] = jnp.zeros_like(kv_ref)
        for core in range(2):

            @pl.when(meta_ref[0] == core)
            def _():
                q_ref[:, :half] = lines_ref[2:3, core * half : (core + 1) * half]
                kv_ref[:, padded : padded + half] = lines_ref[3:4, core * half : (core + 1) * half]

    outs = [like(lines, count * size, F32), like(1, padded, F32), like(1, 2 * padded, F32)]
    return small_call(kernel, outs, [meta], [parts], "lay_vectors")


def mlp_shards(core, out_shard, hidden_weight, down_weight, cols):
    rows, total = hidden_weight.shape
    before = out_shard.shape[1]

    def kernel(core_ref, part_ref, hidden_ref, down_ref, first_out, down_out):
        first_out[:, :before] = part_ref[...]
        for at in range(2):

            @pl.when(core_ref[0] == at)
            def _():
                low = at * cols
                high = min(low + cols, total)
                size = high - low
                first_out[:, before : before + size] = hidden_ref[:, low:high]
                down_out[:, :size] = down_ref[low:high].T
                if size < cols:
                    empty = jnp.zeros((rows, cols - size), BF16)
                    first_out[:, before + size :] = empty
                    down_out[:, size:] = empty

    outs = [like(rows, before + cols), like(rows, cols)]
    return small_call(kernel, outs, [core], [out_shard, hidden_weight, down_weight], "mlp_shards")


def attention_shards(core, weights, half, padded):
    rows, width = weights[0].shape
    cut = width - padded

    def kernel(core_ref, q_ref, k_ref, v_ref, o_ref, qkv_ref, out_ref):
        empty = jnp.zeros((rows, padded - half), BF16)
        for at in range(2):

            @pl.when(core_ref[0] == at)
            def _():
                for i, ref in enumerate((q_ref, k_ref, v_ref)):
                    part = ref[:, at * half : (at + 1) * half]
                    qkv_ref[:, i * padded : (i + 1) * padded] = jnp.concatenate([part, empty], axis=1)
                out_ref[...] = o_ref[:, at * cut : at * cut + padded]

    outs = [like(rows, 3 * padded), like(rows, padded)]
    return small_call(kernel, outs, [core], weights, "attention_shards")


def hidden(arrays, weight, bias):
    rows, width = arrays[0].shape
    cols = weight.shape[1]
    block = row_block(rows)
    steps, count = rows // block, len(arrays)

    def kernel(*refs):
        w_ref, b_ref, act_ref, slope_ref, x_ref = refs[count:]
        for i in range(count):

            @pl.when(pl.program_id(0) // steps == i)
            def _():
                x_ref[...] = refs[i][...]

        pre = dot(x_ref[...], w_ref[...]) + b_ref[...]
        square = pre * pre
        turn = jnp.tanh(pre * (GELU_COEF + GELU_COEF * 0.044715 * square))
        act_ref[...] = (0.5 * pre * (1.0 + turn)).astype(BF16)
        inner = GELU_COEF + 3.0 * 0.044715 * GELU_COEF * square
        slope_ref[...] = (0.5 * (1.0 + turn) * (1.0 + pre * (1.0 - turn) * inner)).astype(BF16)

    out = pl.BlockSpec((block, cols), lambda i: (i, 0))
    return pl.pallas_call(
        kernel,
        out_shape=(
            jax.ShapeDtypeStruct((count * rows, cols), BF16),
            jax.ShapeDtypeStruct((count * rows, cols), BF16),
            jax.ShapeDtypeStruct((count * rows, width), BF16),
        ),
        grid=(count * steps,),
        in_specs=[
            pl.BlockSpec((block, width), lambda i, k=k: (jnp.clip(i - k * steps, 0, steps - 1), 0))
            for k in range(count)
        ]
        + [
            pl.BlockSpec((width, cols), lambda i: (0, 0), pipeline_mode=pl.Buffered(1)),
            pl.BlockSpec((1, cols), lambda i: (0, 0)),
        ],
        out_specs=(out, out, pl.BlockSpec((block, width), lambda i: (i, 0))),
        compiler_params=params(("arbitrary",)),
        cost_estimate=NOMINAL,
        name="hidden",
    )(*arrays, weight, bias)


def head_window(head):
    first = head * HEAD_DIM
    start = first // 128 * 128
    return start, round_up(first + HEAD_DIM, 128) - start, first - start


def head_lanes(rows, width, low):
    lane = lax.broadcasted_iota(jnp.int32, (rows, width), 1)
    return (lane >= low) & (lane < low + HEAD_DIM)


def only_head(block, low):
    mine = head_lanes(*block.shape, low)
    return jnp.where(mine, block.astype(F32), 0.0).astype(BF16)


def pick_block(near_ref, far_ref, block):
    return near_ref.at[block, 0] if block < 2 else far_ref.at[block - 2, 0]


def attend_kernel(row, heads, blocks, padded, need_ref, col_ref, row_ref, q_ref, near_ref, far_ref, *refs):
    own_ref, pair_ref, lse_ref, queries, score, peak, total, acc, lses = refs[-9:]
    outs = (own_ref, pair_ref)
    tokens = own_ref.shape[1]
    slot = lax.broadcasted_iota(jnp.int32, (2 * tokens, 128), 1)
    for which in range(2):
        outs[which][...] = jnp.zeros_like(outs[which])
    windows = [head_window(head) for head in range(heads)]
    for head, (start, width, low) in enumerate(windows):
        for which in range(2):
            queries[head, which * tokens : (which + 1) * tokens, :width] = only_head(
                q_ref[which, 0, :, start : start + width], low
            )
    peak[...] = jnp.full_like(peak, MASKED)
    total[...] = jnp.zeros_like(total)
    acc[...] = jnp.zeros_like(acc)
    for block in range(blocks):

        @pl.when(need_ref[row, block] != 0)
        def _():
            side = pick_block(near_ref, far_ref, block)
            seen = col_ref[0] == row_ref[0, block : block + 1]
            for head, (start, width, _) in enumerate(windows):
                key = side[:, start : start + width]
                found = jnp.where(seen, dot(queries[head, :, :width], key, NT), MASKED)
                score[head, block] = found
                top = peak[head]
                for at in range(0, tokens, 128):
                    top = jnp.maximum(top, found[:, at : at + 128])
                peak[head] = top

    for head in range(heads):
        top = jnp.max(peak[head], axis=-1, keepdims=True) * (SCALE * LOG2E)
        peak[head] = jnp.broadcast_to(top, peak.shape[1:])

    for block in range(blocks):

        @pl.when(need_ref[row, block] != 0)
        def _():
            side = pick_block(near_ref, far_ref, block)
            for head, (start, width, _) in enumerate(windows):
                top, share = peak[head], total[head]
                pieces = []
                for at in range(0, tokens, 128):
                    part = jnp.exp2(score[head, block, :, at : at + 128] * (SCALE * LOG2E) - top)
                    share += part
                    pieces.append(part.astype(BF16))
                total[head] = share
                value = side[:, padded + start : padded + start + width]
                acc[head, :, :width] += dot(jnp.concatenate(pieces, axis=1), value)

    for head, (start, width, low) in enumerate(windows):
        norm = jnp.sum(total[head], axis=-1, keepdims=True)
        result = acc[head, :, :width] / norm
        mine = head_lanes(tokens, width, low)
        for which in range(2):
            kept = outs[which][0, :, start : start + width].astype(F32)
            fresh = result[which * tokens : (which + 1) * tokens]
            outs[which][0, :, start : start + width] = jnp.where(mine, fresh, kept).astype(BF16)
        lse = peak[head] + jnp.log2(norm)
        lses[...] = lse if head == 0 else jnp.where(slot == head, lse, lses[...])
    lse_ref[0] = lses[...].T[:heads]


def attend(row, query, near, far, need, seg_col, seg_row, heads, before):
    _, rows, tokens, padded = query.shape
    blocks = 2 + far.shape[0]
    narrow = pl.BlockSpec((1, tokens, padded), lambda i, need: (row, 0, 0))
    lines = pl.BlockSpec((1, heads, 2 * tokens), lambda i, need: (row, 0, 0))

    def stack(count, width):
        return pl.BlockSpec((count, 1, tokens, width), lambda i, need: (0, row, 0, 0))

    return pl.pallas_call(
        functools.partial(attend_kernel, row, heads, blocks, padded),
        out_shape=(
            jax.ShapeDtypeStruct((rows, tokens, padded), BF16),
            jax.ShapeDtypeStruct((rows, tokens, padded), BF16),
            jax.ShapeDtypeStruct((rows, heads, 2 * tokens), F32),
        ),
        grid_spec=pltpu.PrefetchScalarGridSpec(
            num_scalar_prefetch=1,
            grid=(1,),
            in_specs=[
                pl.BlockSpec((1, 2 * tokens, 1), lambda i, need: (row, 0, 0)),
                pl.BlockSpec((1, blocks, tokens), lambda i, need: (row, 0, 0)),
                stack(2, padded),
                stack(2, 2 * padded),
                stack(blocks - 2, 2 * padded),
            ]
            + [pl.BlockSpec(memory_space=pl.ANY)] * len(before),
            out_specs=(narrow, narrow, lines),
            scratch_shapes=[
                pltpu.VMEM((heads, 2 * tokens, WIN), BF16),
                pltpu.VMEM((heads, blocks, 2 * tokens, tokens), F32),
                pltpu.VMEM((heads, 2 * tokens, 128), F32),
                pltpu.VMEM((heads, 2 * tokens, 128), F32),
                pltpu.VMEM((heads, 2 * tokens, WIN), F32),
                pltpu.VMEM((2 * tokens, 128), F32),
            ],
        ),
        input_output_aliases={6 + i: i for i in range(len(before))},
        compiler_params=params(("arbitrary",)),
        cost_estimate=NOMINAL,
        name="attend",
    )(need, seg_col, seg_row, query, near, far, *before)


def attend_back_kernel(
    row, heads, blocks, padded, need_ref, col_ref, row_ref, pick_ref, q_ref, near_ref, far_ref, *refs
):
    grads, outs, lse_ref = refs[0:2], refs[2:4], refs[4]
    dq_ref, dnear_ref, dfar_ref, sums, inner_turn, queries, incoming, dq = refs[-8:]
    tokens = grads[0].shape[1]
    sums[...] = jnp.zeros_like(sums)
    for which in range(2):
        dq_ref[which, 0] = jnp.zeros((tokens, padded), BF16)
        product = grads[which][0].astype(F32) * outs[which][0].astype(F32)
        high = product.astype(BF16)
        rest = (product - high.astype(F32)).astype(BF16)
        inner_turn[:, which * tokens : (which + 1) * tokens] = dot(pick_ref[...], high, NT) + dot(
            pick_ref[...], rest, NT
        )
    windows = [head_window(head) for head in range(heads)]
    for head, (start, width, low) in enumerate(windows):
        for which in range(2):
            there = slice(which * tokens, (which + 1) * tokens)
            here = slice(start, start + width)
            queries[head, there, :width] = only_head(q_ref[which, 0, :, here], low)
            incoming[head, there, :width] = only_head(grads[which][0, :, here], low)
    dq[...] = jnp.zeros_like(dq)
    for block in range(blocks):

        @pl.when(need_ref[row, block] != 0)
        def _():
            side = pick_block(near_ref, far_ref, block)
            seen = col_ref[0, block] == row_ref[0]
            for head, (start, width, _) in enumerate(windows):
                end = start + width
                key, value = side[:, start:end], side[:, padded + start : padded + end]
                query, grad = queries[head, :, :width], incoming[head, :, :width]
                found = dot(key, query, NT) * (SCALE * LOG2E) - lse_ref[0, head : head + 1, :]
                prob = jnp.where(seen, jnp.exp2(found), 0.0)
                inner = inner_turn[head : head + 1, :]
                slope = (prob * (dot(value, grad, NT) - inner)).astype(BF16)
                sums[block, :, start:end] += dot(slope, query)
                sums[block, :, padded + start : padded + end] += dot(prob.astype(BF16), grad)
                dq[head, :, :width] += dot(slope, key, TN)

    for head, (start, width, low) in enumerate(windows):
        mine = head_lanes(tokens, width, low)
        for which in range(2):
            kept = dq_ref[which, 0, :, start : start + width].astype(F32)
            fresh = dq[head, which * tokens : (which + 1) * tokens, :width] * SCALE
            dq_ref[which, 0, :, start : start + width] = jnp.where(mine, fresh, kept).astype(BF16)
    for block in range(blocks):
        side = pick_block(dnear_ref, dfar_ref, block)
        side[:, :padded] = (sums[block, :, :padded] * SCALE).astype(BF16)
        side[:, padded:] = sums[block, :, padded:].astype(BF16)


def attend_back(row, query, near, far, grads, outs, lse, need, seg_col, seg_row, heads, before):
    _, rows, tokens, padded = query.shape
    blocks = 2 + far.shape[0]
    column = lax.broadcasted_iota(jnp.int32, (heads, padded), 1)
    pick = (column // HEAD_DIM == lax.broadcasted_iota(jnp.int32, (heads, padded), 0)).astype(BF16)
    narrow = pl.BlockSpec((1, tokens, padded), lambda i, need: (row, 0, 0))

    def stack(count, width):
        return pl.BlockSpec((count, 1, tokens, width), lambda i, need: (0, row, 0, 0))

    return pl.pallas_call(
        functools.partial(attend_back_kernel, row, heads, blocks, padded),
        out_shape=tuple(jax.ShapeDtypeStruct(a.shape, BF16) for a in (query, near, far)),
        grid_spec=pltpu.PrefetchScalarGridSpec(
            num_scalar_prefetch=1,
            grid=(1,),
            in_specs=[
                pl.BlockSpec((1, blocks, tokens, 1), lambda i, need: (row, 0, 0, 0)),
                pl.BlockSpec((1, 1, 2 * tokens), lambda i, need: (row, 0, 0)),
                pl.BlockSpec((heads, padded), lambda i, need: (0, 0)),
                stack(2, padded),
                stack(2, 2 * padded),
                stack(blocks - 2, 2 * padded),
            ]
            + [narrow] * 4
            + [pl.BlockSpec((1, heads, 2 * tokens), lambda i, need: (row, 0, 0))]
            + [pl.BlockSpec(memory_space=pl.ANY)] * len(before),
            out_specs=(stack(2, padded), stack(2, 2 * padded), stack(blocks - 2, 2 * padded)),
            scratch_shapes=[
                pltpu.VMEM((blocks, tokens, 2 * padded), F32),
                pltpu.VMEM((heads, 2 * tokens), F32),
                pltpu.VMEM((heads, 2 * tokens, WIN), BF16),
                pltpu.VMEM((heads, 2 * tokens, WIN), BF16),
                pltpu.VMEM((heads, 2 * tokens, WIN), F32),
            ],
        ),
        input_output_aliases={12 + i: i for i in range(len(before))},
        compiler_params=params(("arbitrary",)),
        cost_estimate=NOMINAL,
        name="attend_back",
    )(need, seg_col, seg_row, pick, query, near, far, *grads, *outs, lse, *before)


def local(
    patches,
    lengths,
    first_gain,
    first_shift,
    query_weight,
    query_bias,
    key_weight,
    value_weight,
    value_bias,
    output_weight,
    output_bias,
    second_gain,
    second_shift,
    hidden_weight,
    hidden_bias,
    down_weight,
    down_bias,
    cotangent,
):
    seq_count, shards = lax.axis_size("seq"), lax.axis_size("fsdp")
    place, me = lax.axis_index("seq"), lax.axis_index("fsdp")
    core = place & 1
    is_first = core == 0
    core_flag = core[None].astype(jnp.int32)
    rows, tokens, width = patches.shape
    flat = rows * tokens
    heads = width // HEAD_DIM // 2
    half = heads * HEAD_DIM
    padded = round_up(half, 128)
    ff = hidden_bias.shape[0]
    ff_half = round_up(ff, 256) // 2
    out_cols = padded
    out_cut = width - padded
    shard_rows = width // shards
    chain = Chain()

    def my_half(array, size, padded_size):
        first, second = array[..., :size], array[..., size:]
        grow = [(0, 0)] * (array.ndim - 1)
        first = jnp.pad(first, grow + [(0, padded_size - size)])
        second = jnp.pad(second, grow + [(0, padded_size - second.shape[-1])])
        return jnp.where(is_first, first, second)

    flights = Flights(chain)
    staged = shards == 8 and seq_count == 4
    y, z, zz = 1, 2, 4
    top = bits_of(seq_count)[0]

    inputs = patches.reshape(flat, width)
    incoming = cotangent.reshape(flat, width)
    shard_qkv, shard_out = chain.done(
        *attention_shards(
            core_flag, [query_weight, key_weight, value_weight, output_weight], half, padded
        )
    )
    vectors = (
        first_gain,
        first_shift,
        query_bias,
        value_bias,
        output_bias,
        second_gain,
        second_shift,
        down_bias,
    )
    place_flag = place[None].astype(jnp.int32)

    def over(box_from, bits):
        return flights.send(box_from[0], "fsdp", bits)

    def both(stacked_lines, arrived):
        return jnp.concatenate([stacked_lines, arrived], axis=0)

    if staged:
        q = {0: [shard_qkv]}
        q[y] = over(q[0], y)
        far_raw = [flights.send(patches[0], "seq", 2)]
        q[z], q[zz] = over(q[0], z), over(q[0], zz)
        shard_ho, shard_down = chain.done(
            *mlp_shards(core_flag, shard_out, hidden_weight, down_weight, ff_half)
        )
        h, d = {0: [shard_ho]}, {0: [shard_down]}
        lengths, *vectors = flights.land(lengths, *vectors, through=far_raw[0])
        vectors = jnp.stack(vectors)[None]
        vec = flights.send(vectors, "fsdp", y)
        h[y] = over(h[0], y)
        far_raw.append(flights.send(patches[1:].reshape(flat - tokens, width), "seq", 2))
        need, seg_rows, seg_cols, seg_near_row, seg_near_col = chain.done(
            *masks(lengths, place_flag, seq_count, tokens)
        )
        vectors = flights.land(vectors, through=vec)
        vectors = both(vectors, vec[0])
        vec = flights.send(vectors, "fsdp", z)
        q[zz | z] = over(q[zz], z)
        q[z | y] = over(q[z], y)
        vectors = flights.land(vectors, through=h[y])
        q[zz | y] = over(q[zz], y)
        vectors = flights.land(vectors, through=q[zz | z])
        vectors = both(vectors, vec[0])
        vec = flights.send(vectors, "fsdp", zz)
        raw_pair = flights.send(inputs, "seq", 1)
        q[zz | z | y] = over(q[zz | z], y)
        vectors = flights.land(vectors, through=raw_pair)
        far_pair = [flights.send(box[0], "seq", 1) for box in far_raw]
        h[z], h[zz] = over(h[0], z), over(h[0], zz)
        vectors = both(vectors, vec[0])
        meta = chain(jnp.stack([core, me]).astype(jnp.int32))
        stacked, bias_q, bias_kv = chain.done(*lay_vectors(meta, vectors, half, padded))
        gain_one, shift_one = stacked[0:1], stacked[1:2]
        gain_one = chain(gain_one)
        normed_near = chain.done(norm([inputs, raw_pair[0]], gain_one, shift_one))
        bias_hidden = my_half(after(hidden_bias, gain_one).astype(F32)[None], ff_half, ff_half)
        gain_one = flights.land(gain_one, through=far_pair[-1])
        d[y] = over(d[0], y)
        incoming_pair = flights.send(incoming, "seq", 1)
        w_q, w_kv = chain.done(*assemble({k: box[0] for k, box in q.items()}, me, padded))
    else:
        parts = gather_all(shard_qkv)
        vectors = jnp.stack(vectors)[None]
        for k in range(shards.bit_length() - 1):
            vectors = both(vectors, swap(vectors, "fsdp", 1 << k))
        shard_ho, shard_down = mlp_shards(core_flag, shard_out, hidden_weight, down_weight, ff_half)
        raw = {0: inputs}
        for bit in bits_of(seq_count):
            raw.update({j | bit: swap(part, "seq", bit) for j, part in list(raw.items())})
        need, seg_rows, seg_cols, seg_near_row, seg_near_col = masks(lengths, place_flag, seq_count, tokens)
        stacked, bias_q, bias_kv = lay_vectors(
            jnp.stack([core, me]).astype(jnp.int32), vectors, half, padded
        )
        gain_one, shift_one = stacked[0:1], stacked[1:2]
        normed_near = norm([raw[0], raw[1]], gain_one, shift_one)
        far_raw, far_pair = [[raw[j]] for j in range(2, seq_count)], []
        incoming_pair = [swap(incoming, "seq", 1)]
        bias_hidden = my_half(hidden_bias.astype(F32)[None], ff_half, ff_half)
        w_q, w_kv = chain.done(*assemble(parts, me, padded))
    _, _, bias_query, bias_value, bias_output, gain_two, shift_two, bias_down = [
        stacked[i : i + 1] for i in range(8)
    ]

    near_in, w_q, w_kv = chain(normed_near, w_q, w_kv)
    (query,) = rows_matmul("query", [near_in], [w_q], with_bias, [bias_q], [like(2 * flat, padded)])
    near_in = after(near_in, query)
    (near,) = rows_matmul("near", [near_in], [w_kv], with_bias, [bias_kv], [like(2 * flat, 2 * padded)])
    chain.done(query, near)
    gain_one, w_kv = chain(gain_one, w_kv)
    normed_far = chain.done(norm([box[0] for box in far_raw + far_pair], gain_one, shift_one))
    if staged:
        w_kv, incoming = flights.land(w_kv, incoming)
        h[z | y], h[zz | y], h[zz | z] = over(h[z], y), over(h[zz], y), over(h[zz], z)
    incoming_near = jnp.concatenate([incoming, incoming_pair[0]], axis=0)
    far_in, w_kv = chain(normed_far, w_kv)
    (far,) = rows_matmul(
        "far", [far_in], [w_kv], with_bias, [bias_kv], [like(normed_far.shape[0], 2 * padded)]
    )
    chain.done(far)
    query = query.reshape(2, rows, tokens, padded)
    near = near.reshape(2, rows, tokens, 2 * padded)
    far = far.reshape(seq_count - 2, rows, tokens, 2 * padded)
    found = ()
    for row in range(rows):
        query, near, far = chain(query, near, far)
        if staged and row == 1:
            query = flights.land(query)
            h[zz | z | y] = over(h[zz | z], y)
            d[z], d[zz] = over(d[0], z), over(d[0], zz)
        found = chain.done(*attend(row, query, near, far, need, seg_near_col, seg_rows, heads, found))
    out_own, out_pair, lse = found
    if staged:
        out_own, out_pair = flights.land(out_own, out_pair)
        h_parts = {k: box[0] for k, box in h.items()}
    else:
        out_own, out_pair = flights.land(out_own, out_pair)
        h_parts = gather_all(chain(shard_ho))
    w_out_mine, w_hidden = chain.done(*assemble(h_parts, me, out_cols))
    out_pair, w_out_mine = chain(out_pair, w_out_mine)
    other_half = flights.send(out_pair, "seq", 1)
    w_out_other = flights.send(w_out_mine, "seq", 1)
    w_out_mine, w_hidden = flights.land(w_out_mine, w_hidden)
    if staged:
        d[zz | z], d[z | y] = over(d[zz], z), over(d[z], y)
    w_out = chain.done(both_cores(core_flag, w_out_mine, w_out_other[0], out_cut, width))
    own_half, w_out = chain(out_own.reshape(flat, padded), w_out)
    attended, middle, second = chain.done(
        *join(
            core_flag,
            own_half,
            other_half[0].reshape(flat, padded),
            inputs,
            w_out,
            bias_output,
            gain_two,
            shift_two,
            half,
        )
    )
    second_pair = flights.send(second, "seq", 1)
    second, w_hidden = flights.land(second, w_hidden)
    if staged:
        d[zz | y] = over(d[zz], y)
    act, slope, second_near = chain.done(*hidden([second, second_pair[0]], w_hidden, bias_hidden))

    if staged:
        incoming_near = flights.land(incoming_near)
        d[zz | z | y] = over(d[zz | z], y)
    incoming_near, act = chain(incoming_near, act)
    grad_down = chain.done(dot(incoming_near, act, TN).astype(BF16))
    part_down = lax.psum_scatter(grad_down, "fsdp", scatter_dimension=0, tiled=True)
    if staged:
        slope = flights.land(slope)
        d_parts = {k: box[0] for k, box in d.items()}
    else:
        d_parts = gather_all(chain(shard_down))
    w_down = chain.done(assemble(d_parts, me))
    incoming_near, slope, w_down = chain(incoming_near, slope, w_down)
    grad_pre, hidden_line = chain.done(
        *rows_matmul(
            "grad_pre",
            [incoming_near],
            [w_down],
            with_slope,
            [slope],
            [like(2 * flat, ff_half), like(1, ff_half, F32)],
        )
    )
    grad_pre = chain(grad_pre)
    back, back_pair = chain.done(
        *rows_matmul("back", [grad_pre], [w_hidden], plain, [], [like(2 * flat, width)], NT, True)
    )
    back_other = flights.send(back_pair, "seq", 1)
    second_near, grad_pre = chain(second_near, grad_pre)
    grad_hidden = chain.done(dot(second_near, grad_pre, TN).astype(BF16))
    part_hidden = lax.psum_scatter(grad_hidden, "fsdp", scatter_dimension=0, tiled=True)
    back = flights.land(back)
    grad_middle, branch, grad_mine, grad_send, lines = second_back(
        core_flag, middle, [back, back_other[0]], gain_two, incoming, w_out, hidden_line, half, padded
    )
    chain.done(branch, grad_send)
    grad_pair = flights.send(grad_send, "seq", 1)
    attended, branch = chain(attended, branch)
    out_keep, out_send, _ = chain.done(*weight_grad([attended], [branch], me, shards))
    out_keep, out_send = chain(out_keep, out_send)
    keep_mine, send_mine, keep_other, send_other = chain.done(
        *core_columns(core_flag, [out_keep, out_send], out_cols)
    )
    query = flights.land(query)

    small = lax.psum(lines, ("seq", "fsdp"))
    keep_back, send_back = flights.send(keep_other, "seq", 1), flights.send(send_other, "seq", 1)
    shape = (rows, tokens, padded)
    grads = [grad_mine.reshape(shape), grad_pair[0].reshape(shape)]
    found = ()
    far_bits = [2 << k for k in range(shards.bit_length() - 2)]
    out_bits = list(far_bits)

    def next_step(keep, box, bits):
        keep, send = scatter_step(keep, box[0], shard_rows)
        chain.done(keep)
        return keep, flights.send(send, "fsdp", bits.pop(0)) if bits else None

    def seq_rest(mine, arrived):
        for bit in bits_of(seq_count)[1:-1]:
            (mine,) = add_rows(mine, arrived)
            arrived = swap(mine, "seq", bit)
        return chain.done(*add_rows(mine, arrived, F32))

    for row in range(rows):
        query, near, far, *grads = chain(query, near, far, *grads)
        found = attend_back(
            row, query, near, far, grads, [out_own, out_pair], lse, need, seg_cols, seg_near_row, heads, found
        )
        chain.done(*found)
        query = flights.land(query)
        if row == 0:
            (out_keep,), (out_send,) = add_rows(keep_mine, keep_back[0]), add_rows(send_mine, send_back[0])
            chain.done(out_keep, out_send)
            out_box = flights.send(out_send, "fsdp", y)
        else:
            out_keep, out_box = next_step(out_keep, out_box, out_bits)
        if row == 1:
            part_down = chain(part_down)
            down_seq = flights.send(part_down, "seq", top)
    dq, dnear, dfar = [g.reshape(-1, g.shape[-1]) for g in found]
    dfar, w_kv = chain(dfar, w_kv)
    two = seq_count == 4
    back_far = rows_matmul("back_far", [dfar], [w_kv], plain, [], [like(dfar.shape[0], width)], NT, two)
    chain.done(*back_far)
    dnear = chain(dnear)
    if two:
        far_parts = {2 + i: part for i, part in enumerate(back_far)}
    else:
        far_parts = {j: back_far[0][(j - 2) * flat : (j - 1) * flat] for j in range(2, seq_count)}
    far_sent = {j: flights.send(part, "seq", 1) for j, part in far_parts.items() if j & 1}
    normed_near, dnear, dfar = chain(normed_near, dnear, dfar)
    kv_keep, kv_send, kv_sums = chain.done(
        *weight_grad([normed_near, normed_far], [dnear, dfar], me, shards)
    )
    dq = flights.land(dq)
    kv_box = flights.send(kv_send, "fsdp", y)
    far_sums = {j: add_rows(far_parts[j], far_sent[j | 1][0])[0] for j in far_parts if not j & 1}
    chain.done(*far_sums.values())
    arrived = []
    for bit in bits_of(seq_count)[:-1]:
        moved = {j: flights.send(part, "seq", bit) for j, part in far_sums.items() if j & bit}
        far_sums = {j: part for j, part in far_sums.items() if not j & bit}
        for j, box in moved.items():
            if j == bit:
                arrived.append(box)
            else:
                (far_sums[j ^ bit],) = add_rows(far_sums[j ^ bit], box[0])
    dq, dnear = chain(dq, dnear)
    back_own, back_pair = chain.done(
        *rows_matmul("back_near", [dq, dnear], [w_q, w_kv], plain, [], [like(2 * flat, width)], NT, True)
    )
    pair_back = flights.send(back_pair, "seq", 1)
    normed_near, dq = chain(normed_near, dq)
    q_keep, q_send, q_sums = chain.done(*weight_grad([normed_near], [dq], me, shards))
    q_box = flights.send(q_send, "fsdp", y)
    act, middle = chain(act, middle)
    (down_pair,) = rows_matmul(
        "down_pair", [act], [w_down], plain, [], [like(flat, width)], NT, first_row=flat
    )
    chain.done(down_pair)
    down_back = flights.send(down_pair, "seq", 1)
    kv_bits, q_bits = list(far_bits), list(far_bits)
    act = flights.land(act, through=kv_box)
    kv_keep, kv_box = next_step(kv_keep, kv_box, kv_bits)
    late_in = flights.land(inputs, through=pair_back)
    grad_patches, late = chain.done(
        *first_back(
            core_flag,
            late_in,
            [back_own, pair_back[0]] + [box[0] for box in arrived],
            gain_one,
            grad_middle,
            q_sums,
            kv_sums,
            half,
        )
    )
    late = lax.psum(late, ("seq", "fsdp"))
    part_hidden = chain(part_hidden)
    hidden_seq = flights.send(part_hidden, "seq", top)
    act = flights.land(act, through=down_back)
    q_keep, q_box = next_step(q_keep, q_box, q_bits)
    act, middle = chain(act, middle)
    (layer_output,) = rows_matmul(
        "down_own", [act], [w_down], layer_end, [middle, down_back[0], bias_down], [like(flat, width)], NT
    )
    layer_output = chain.done(layer_output).reshape(rows, tokens, width)
    down_total = seq_rest(part_down, down_seq[0])
    while kv_box is not None:
        act = flights.land(act, through=kv_box)
        kv_keep, kv_box = next_step(kv_keep, kv_box, kv_bits)
        if q_box is not None and kv_box is not None:
            act = flights.land(act, through=q_box)
            q_keep, q_box = next_step(q_keep, q_box, q_bits)
    kv_seq = flights.send(kv_keep, "seq", top)
    while out_box is not None:
        out_keep, out_box = next_step(out_keep, out_box, out_bits)
        if out_box is not None:
            act = flights.land(act)
    out_seq = flights.send(out_keep, "seq", top)
    down_other = flights.send(down_total, "seq", 1)
    hidden_total = seq_rest(part_hidden, hidden_seq[0])
    while q_box is not None:
        act = flights.land(act, through=q_box)
        q_keep, q_box = next_step(q_keep, q_box, q_bits)
    q_seq = flights.send(q_keep, "seq", top)
    act = flights.land(act, through=kv_seq)
    kv_total = seq_rest(kv_keep, kv_seq[0])
    kv_other = flights.send(kv_total, "seq", 1)
    hidden_other = flights.send(hidden_total, "seq", 1)
    act = flights.land(act, through=q_seq)
    out_total = seq_rest(out_keep, out_seq[0])
    q_total = seq_rest(q_keep, q_seq[0])
    q_other, out_other = flights.send(q_total, "seq", 1), flights.send(out_total, "seq", 1)
    flights.land()
    own_lines = lax.dynamic_slice_in_dim(small, me * shard_rows, shard_rows, 1)
    late_lines = lax.dynamic_slice_in_dim(late, me * shard_rows, shard_rows, 1)
    cuts = [width, ff_half - width, width, ff - ff_half - width]
    full_bias = jnp.concatenate([small[4 + i, :size] for i, size in enumerate(cuts)])
    full_down = both_columns(is_first, down_total, down_other[0], ff_half, ff).T
    full_hidden = both_columns(is_first, hidden_total, hidden_other[0], ff_half, ff)
    full_out = both_columns(is_first, out_total, out_other[0], out_cut, width)
    full_query = both_columns(is_first, q_total, q_other[0], half, width)
    full_key = both_columns(is_first, kv_total, kv_other[0], half, width)
    full_value = both_columns(is_first, kv_total, kv_other[0], half, width, padded)
    return (
        layer_output,
        grad_patches.reshape(rows, tokens, width),
        late_lines[0],
        late_lines[1],
        full_query,
        late_lines[2],
        full_key,
        full_value,
        late_lines[3],
        full_out,
        own_lines[2],
        own_lines[0],
        own_lines[1],
        full_hidden,
        full_bias,
        full_down,
        own_lines[3],
    )


def solution(mesh):
    shard, line, tokens = P("fsdp", None), P("fsdp"), P("fsdp", "seq", None)
    in_specs = (
        tokens,
        shard,
        line,
        line,
        shard,
        line,
        shard,
        shard,
        line,
        shard,
        line,
        line,
        line,
        shard,
        P(),
        P(None, "fsdp"),
        line,
        tokens,
    )
    out_specs = (
        tokens,
        tokens,
        line,
        line,
        shard,
        line,
        shard,
        shard,
        line,
        shard,
        line,
        line,
        line,
        shard,
        P(),
        P(None, "fsdp"),
        line,
    )
    return jax.shard_map(local, mesh=mesh, in_specs=in_specs, out_specs=out_specs, check_vma=False)
```

```python
import functools
import math

import jax
import jax.numpy as jnp
from jax import lax
from jax.experimental import pallas as pl
from jax.experimental.pallas import tpu as pltpu
from jax.sharding import PartitionSpec as P

HEAD_DIM = 72
EPS = 1e-06
GELU_COEF = math.sqrt(2.0 / math.pi)
MASKED = -1e30
F32 = jnp.float32
BF16 = jnp.bfloat16
SCALE = 1.0 / math.sqrt(HEAD_DIM)
WIN = 256
LOG2E = math.log2(math.e)
VMEM = 60 << 20
NOMINAL = pl.CostEstimate(flops=1, transcendentals=0, bytes_accessed=1)


def round_up(value, step):
    return (value + step - 1) // step * step


def dot(left, right, dims=((1,), (0,))):
    return lax.dot_general(left, right, (dims, ((), ())), preferred_element_type=F32)


NT = ((1,), (1,))
TN = ((0,), (0,))


def params(semantics):
    return pltpu.CompilerParams(dimension_semantics=semantics, vmem_limit_bytes=VMEM)


def swap(array, axis, bits):
    size = lax.axis_size(axis)
    return lax.ppermute(array, axis, [(i, i ^ bits) for i in range(size)])


def bits_of(size):
    return [1 << k for k in reversed(range(size.bit_length() - 1))]


def after(value, *earlier):
    return lax.optimization_barrier((value,) + tuple(earlier))[0]


class Chain:
    def __init__(self):
        self.last = ()

    def __call__(self, *values, wait=()):
        held = lax.optimization_barrier(tuple(values) + tuple(self.last) + tuple(wait))
        return held[: len(values)] if len(values) > 1 else held[0]

    def done(self, *results):
        self.last = results
        return results if len(results) > 1 else results[0]


class Flights:
    def __init__(self, chain):
        self.chain, self.open = chain, []

    def send(self, array, axis, bits):
        self.open.append([swap(array, axis, bits)])
        return self.open[-1]

    def land(self, *values, through=None, only=None):
        if only is None:
            count = len(self.open)
            if through is not None:
                count = sum(i + 1 for i, box in enumerate(self.open) if box is through)
            only = self.open[:count]
        ready = [box for box in self.open if any(box is other for other in only)]
        self.open = [box for box in self.open if not any(box is other for other in ready)]
        held = self.chain(*[box[0] for box in ready], *values)
        held = held if isinstance(held, (tuple, list)) else [held]
        for box, array in zip(ready, held):
            box[0] = array
        rest = list(held[len(ready) :])
        return rest if len(rest) > 1 else rest[0] if rest else None


def in_order(parts, me):
    count = len(parts)
    return jnp.take(jnp.stack([parts[d] for d in range(count)]), me ^ jnp.arange(count), axis=0)


def gather_all(shard):
    parts = {0: shard}
    for bit in bits_of(lax.axis_size("fsdp")):
        parts.update({d | bit: swap(part, "fsdp", bit) for d, part in list(parts.items())})
    return parts


def rel_position(distance, count):
    width = count.bit_length() - 1
    return sum(((distance >> k) & 1) << (width - 1 - k) for k in range(width))


def assemble_kernel(count, rows, single, off_ref, *refs):
    outs = refs[count:]

    def fill(out_ref):
        for distance in range(count):
            start = pl.multiple_of(off_ref[distance], 16)
            out_ref[pl.ds(start, rows), :] = refs[distance][...]

    if single:
        fill(outs[0])
    else:
        pl.when(pl.program_id(0) == 0)(lambda: fill(outs[0]))
        pl.when(pl.program_id(0) > 0)(lambda: fill(outs[1]))


def assemble(parts, me, cut=None):
    count = len(parts)
    rows, cols = parts[0].shape
    if rows % 16:
        full = in_order(parts, me).reshape(count * rows, cols)
        return (full[:, :cut], full[:, cut:]) if cut else full
    offsets = ((me ^ jnp.arange(count, dtype=jnp.int32)) * rows).astype(jnp.int32)
    tile = cut or min(cols, 1152)
    widths = [cut, cols - cut] if cut else [cols]
    maps = [lambda n, off: (0, 0), lambda n, off: (0, jnp.maximum(n - 1, 0))]
    if not cut:
        maps = [lambda n, off: (0, n)]
    outs = pl.pallas_call(
        functools.partial(assemble_kernel, count, rows, not cut),
        out_shape=[jax.ShapeDtypeStruct((count * rows, w), parts[0].dtype) for w in widths],
        grid_spec=pltpu.PrefetchScalarGridSpec(
            num_scalar_prefetch=1,
            grid=(pl.cdiv(cols, tile),),
            in_specs=[pl.BlockSpec((rows, tile), lambda n, off: (0, n))] * count,
            out_specs=[pl.BlockSpec((count * rows, tile), m) for m in maps],
        ),
        compiler_params=params(("arbitrary",)),
        cost_estimate=NOMINAL,
        name="assemble",
    )(offsets, *[parts[d] for d in range(count)])
    return outs if cut else outs[0]


def weight_grad_kernel(pairs, count, rows, pos_ref, *refs):
    lefts, rights = refs[:pairs], refs[pairs : 2 * pairs]
    keep_ref, send_ref, sum_ref = refs[2 * pairs :]
    total = dot(lefts[0][...], rights[0][...], TN)
    for i in range(1, pairs):
        total += dot(lefts[i][...], rights[i][...], TN)
    sum_ref[...] = sum(dot(jnp.ones((8, r.shape[0]), BF16), r[...]) for r in rights)
    for shard in range(count):
        start = pl.multiple_of(pos_ref[shard], 16)
        block = total[shard * rows : (shard + 1) * rows].astype(BF16)

        @pl.when(pos_ref[count] == shard % 2)
        def _():
            keep_ref[pl.ds(start, rows), :] = block

        @pl.when(pos_ref[count] != shard % 2)
        def _():
            send_ref[pl.ds(start, rows), :] = block


def weight_grad(lefts, rights, me, count):
    width = lefts[0].shape[1]
    cols = rights[0].shape[1]
    rows = width // count
    order = me ^ jnp.arange(count, dtype=jnp.int32)
    table = jnp.array([rel_position(d, count) for d in range(count)], jnp.int32)
    half = count // 2
    if rows % 16:
        total = sum(dot(a, b, TN) for a, b in zip(lefts, rights))
        by_distance = jnp.take(total.astype(BF16).reshape(count, rows, cols), order, axis=0)
        back = [0] * count
        for d in range(count):
            back[rel_position(d, count)] = d
        placed = jnp.take(by_distance, jnp.array(back), axis=0).reshape(width, cols)
        ones = [jnp.ones((8, b.shape[0]), BF16) for b in rights]
        sums = sum(dot(one, b) for one, b in zip(ones, rights))
        return placed[: width // 2], placed[width // 2 :], sums
    positions = jnp.concatenate([table[order] % half * rows, (me & 1)[None]]).astype(jnp.int32)
    tile = 256
    pairs = len(lefts)
    return pl.pallas_call(
        functools.partial(weight_grad_kernel, pairs, count, rows),
        out_shape=[jax.ShapeDtypeStruct((width // 2, cols), BF16)] * 2
        + [jax.ShapeDtypeStruct((8, cols), F32)],
        grid_spec=pltpu.PrefetchScalarGridSpec(
            num_scalar_prefetch=1,
            grid=(pl.cdiv(cols, tile),),
            in_specs=[
                pl.BlockSpec(a.shape, lambda n, off: (0, 0), pipeline_mode=pl.Buffered(1))
                for a in lefts
            ]
            + [pl.BlockSpec((b.shape[0], tile), lambda n, off: (0, n)) for b in rights],
            out_specs=[pl.BlockSpec((width // 2, tile), lambda n, off: (0, n))] * 2
            + [pl.BlockSpec((8, tile), lambda n, off: (0, n))],
        ),
        compiler_params=params(("arbitrary",)),
        cost_estimate=NOMINAL,
        name="weight_grad",
    )(positions, *lefts, *rights)


def token_dot(left, right):
    tokens, width = left.shape
    cols = right.shape[1]
    tile = 256

    def kernel(left_ref, right_ref, out_ref):
        out_ref[...] = dot(left_ref[...], right_ref[...], TN).astype(BF16)

    return pl.pallas_call(
        kernel,
        out_shape=jax.ShapeDtypeStruct((width, cols), BF16),
        grid=(pl.cdiv(cols, tile),),
        in_specs=[
            pl.BlockSpec((tokens, width), lambda n: (0, 0), pipeline_mode=pl.Buffered(1)),
            pl.BlockSpec((tokens, tile), lambda n: (0, n)),
        ],
        out_specs=pl.BlockSpec((width, tile), lambda n: (0, n)),
        compiler_params=params(("arbitrary",)),
        cost_estimate=NOMINAL,
        name="token_dot",
    )(left, right)


def normalized(values):
    center = values - jnp.mean(values, axis=-1, keepdims=True)
    spread = jnp.mean(center * center, axis=-1, keepdims=True)
    inverse = lax.rsqrt(spread + EPS)
    return center * inverse, inverse


def row_block(rows):
    return 256 if rows % 256 == 0 else 128 if rows % 128 == 0 else rows


def norm(arrays, gain, shift):
    width = arrays[0].shape[1]
    block = min(row_block(a.shape[0]) for a in arrays)
    steps = [a.shape[0] // block for a in arrays]
    firsts = [sum(steps[:k]) for k in range(len(steps))]
    count, total = len(arrays), sum(steps)

    def kernel(*refs):
        gain_ref, shift_ref, out_ref = refs[count:]
        at = pl.program_id(0)
        for k in range(count):

            @pl.when((at >= firsts[k]) & (at < firsts[k] + steps[k]))
            def _():
                hat, _ = normalized(refs[k][...].astype(F32))
                out_ref[...] = (hat * gain_ref[...] + shift_ref[...]).astype(BF16)

    line = pl.BlockSpec((1, width), lambda i: (0, 0))
    return pl.pallas_call(
        kernel,
        out_shape=jax.ShapeDtypeStruct((total * block, width), BF16),
        grid=(total,),
        in_specs=[
            pl.BlockSpec((block, width), lambda i, k=k: (jnp.clip(i - firsts[k], 0, steps[k] - 1), 0))
            for k in range(count)
        ]
        + [line, line],
        out_specs=pl.BlockSpec((block, width), lambda i: (i, 0)),
        compiler_params=params(("arbitrary",)),
        cost_estimate=NOMINAL,
        name="norm",
    )(*arrays, gain, shift)


def join_kernel(half, core_ref, own_ref, other_ref, x_ref, w_ref, b_ref, g_ref, s_ref, *outs):
    att_ref, mid_ref, out_ref = outs
    own, other = own_ref[:, :half], other_ref[:, :half]

    @pl.when(core_ref[0] == 0)
    def _():
        att_ref[...] = jnp.concatenate([own, other], axis=1)

    @pl.when(core_ref[0] != 0)
    def _():
        att_ref[...] = jnp.concatenate([other, own], axis=1)

    middle = x_ref[...].astype(F32) + dot(att_ref[...], w_ref[...]) + b_ref[...]
    mid_ref[...] = middle
    hat, _ = normalized(middle)
    out_ref[...] = (hat * g_ref[...] + s_ref[...]).astype(BF16)


def join(core, own, other, inputs, weight, bias, gain, shift, half):
    rows, width = inputs.shape
    padded = own.shape[1]
    block = row_block(rows)
    line = pl.BlockSpec((1, width), lambda i, c: (0, 0))
    wide = pl.BlockSpec((block, width), lambda i, c: (i, 0))
    part = pl.BlockSpec((block, padded), lambda i, c: (i, 0))
    return pl.pallas_call(
        functools.partial(join_kernel, half),
        out_shape=(
            jax.ShapeDtypeStruct((rows, width), BF16),
            jax.ShapeDtypeStruct((rows, width), F32),
            jax.ShapeDtypeStruct((rows, width), BF16),
        ),
        grid_spec=pltpu.PrefetchScalarGridSpec(
            num_scalar_prefetch=1,
            grid=(rows // block,),
            in_specs=[
                part,
                part,
                wide,
                pl.BlockSpec((width, width), lambda i, c: (0, 0), pipeline_mode=pl.Buffered(1)),
                line,
                line,
                line,
            ],
            out_specs=(wide, wide, wide),
        ),
        compiler_params=params(("arbitrary",)),
        cost_estimate=NOMINAL,
        name="join",
    )(core, own, other, inputs, weight, bias, gain, shift)


def norm_back_values(x_ref, grads, gain_ref, add_ref, lines_ref):
    hat, inverse = normalized(x_ref[...].astype(F32))
    grad = grads[0][...].astype(F32)
    for other in grads[1:]:
        grad += other[...].astype(F32)
    scaled = grad * gain_ref[...]
    first = jnp.mean(scaled, axis=-1, keepdims=True)
    second = jnp.mean(scaled * hat, axis=-1, keepdims=True)

    @pl.when(pl.program_id(0) == 0)
    def _():
        lines_ref[...] = jnp.zeros_like(lines_ref)

    lines_ref[0:1] += jnp.sum(grad * hat, axis=0, keepdims=True)
    lines_ref[1:2] += jnp.sum(grad, axis=0, keepdims=True)
    return add_ref[...].astype(F32) + inverse * (scaled - first - hat * second)


def first_back(core, values, grads, gain, add, q_sums, kv_sums, half):
    rows, width = values.shape
    padded = q_sums.shape[1]
    pieces = [grad for grad in grads if isinstance(grad, tuple)]
    whole_grads = [grad for grad in grads if not isinstance(grad, tuple)]
    block = min([row_block(rows)] + [row_block(part.shape[0]) for pair in pieces for part in pair])
    count = len(whole_grads) + 2 * len(pieces)
    flat_grads = whole_grads + [part for pair in pieces for part in pair]

    def kernel(core_ref, x_ref, *refs):
        gain_ref, add_ref, q_ref, kv_ref, dx_ref, lines_ref = refs[count:]
        sums = list(refs[: len(whole_grads)])
        for k, pair in enumerate(pieces):
            low, high = refs[len(whole_grads) + 2 * k : len(whole_grads) + 2 * k + 2]
            first = pl.program_id(0) < pair[0].shape[0] // block
            sums.append(jnp.where(first, low[...].astype(F32), high[...].astype(F32)))
        dx_ref[...] = norm_back_values(x_ref, sums, gain_ref, add_ref, lines_ref)
        for line, part in ((2, q_ref[0:1, :half]), (3, kv_ref[0:1, padded : padded + half])):
            none = jnp.zeros_like(part)

            @pl.when(core_ref[0] == 0)
            def _():
                lines_ref[line : line + 1] = jnp.concatenate([part, none], axis=1)

            @pl.when(core_ref[0] != 0)
            def _():
                lines_ref[line : line + 1] = jnp.concatenate([none, part], axis=1)

    def piece_specs(pair):
        steps = pair[0].shape[0] // block
        return [
            pl.BlockSpec((block, width), lambda i, c: (jnp.minimum(i, steps - 1), 0)),
            pl.BlockSpec((block, width), lambda i, c: (jnp.maximum(i - steps, 0), 0)),
        ]

    wide = pl.BlockSpec((block, width), lambda i, c: (i, 0))
    return pl.pallas_call(
        kernel,
        out_shape=(
            jax.ShapeDtypeStruct((rows, width), F32),
            jax.ShapeDtypeStruct((8, width), F32),
        ),
        grid_spec=pltpu.PrefetchScalarGridSpec(
            num_scalar_prefetch=1,
            grid=(rows // block,),
            in_specs=[wide] * (1 + len(whole_grads))
            + [spec for pair in pieces for spec in piece_specs(pair)]
            + [
                pl.BlockSpec((1, width), lambda i, c: (0, 0)),
                wide,
                pl.BlockSpec(q_sums.shape, lambda i, c: (0, 0)),
                pl.BlockSpec(kv_sums.shape, lambda i, c: (0, 0)),
            ],
            out_specs=(wide, pl.BlockSpec((8, width), lambda i, c: (0, 0))),
        ),
        compiler_params=params(("arbitrary",)),
        cost_estimate=NOMINAL,
        name="first_back",
    )(core, values, *flat_grads, gain, add, q_sums, kv_sums)


def second_back(core, values, grads, gain, add, weight, hidden_line, half, padded):
    rows, width = values.shape
    block = row_block(rows)
    count = len(grads)

    def kernel(core_ref, x_ref, *refs):
        gain_ref, add_ref, w_ref, hid_ref, dx_ref, low_ref, mine_ref, send_ref, lines_ref = refs[count:]
        total = norm_back_values(x_ref, refs[:count], gain_ref, add_ref, lines_ref)
        low = total.astype(BF16)
        dx_ref[...] = total
        low_ref[...] = low
        lines_ref[2:3] += jnp.sum(low.astype(F32), axis=0, keepdims=True)
        lines_ref[3:4] += jnp.sum(add_ref[...].astype(F32), axis=0, keepdims=True)
        spare = hid_ref.shape[1] - width
        for core in range(2):

            @pl.when(core_ref[0] == core)
            def _():
                lines_ref[4 + 2 * core : 5 + 2 * core] = hid_ref[:, :width]
                lines_ref[5 + 2 * core : 6 + 2 * core, :spare] = hid_ref[:, width:]

        back = dot(low, w_ref[...], NT).astype(BF16)
        empty = jnp.zeros((block, padded - half), BF16)
        halves = [jnp.concatenate([back[:, i * half : (i + 1) * half], empty], axis=1) for i in range(2)]

        @pl.when(core_ref[0] == 0)
        def _():
            mine_ref[...], send_ref[...] = halves[0], halves[1]

        @pl.when(core_ref[0] != 0)
        def _():
            mine_ref[...], send_ref[...] = halves[1], halves[0]

    wide = pl.BlockSpec((block, width), lambda i, c: (i, 0))
    part = pl.BlockSpec((block, padded), lambda i, c: (i, 0))
    line = pl.BlockSpec((1, width), lambda i, c: (0, 0))
    square = pl.BlockSpec((width, width), lambda i, c: (0, 0), pipeline_mode=pl.Buffered(1))
    return pl.pallas_call(
        kernel,
        out_shape=(
            jax.ShapeDtypeStruct((rows, width), F32),
            jax.ShapeDtypeStruct((rows, width), BF16),
            jax.ShapeDtypeStruct((rows, padded), BF16),
            jax.ShapeDtypeStruct((rows, padded), BF16),
            jax.ShapeDtypeStruct((8, width), F32),
        ),
        grid_spec=pltpu.PrefetchScalarGridSpec(
            num_scalar_prefetch=1,
            grid=(rows // block,),
            in_specs=[wide] * (1 + count)
            + [line, wide, square, pl.BlockSpec(hidden_line.shape, lambda i, c: (0, 0))],
            out_specs=(wide, wide, part, part, pl.BlockSpec((8, width), lambda i, c: (0, 0))),
        ),
        compiler_params=params(("arbitrary",)),
        cost_estimate=NOMINAL,
        name="second_back",
    )(core, values, *grads, gain, add, weight, hidden_line)


def rows_matmul(name, lefts, weights, finish, extras, outs, dims=((1,), (0,)), split=False, first_row=0):
    rows = outs[0].shape[0]
    block = row_block(rows)
    steps = rows // block
    half = steps // 2
    count, terms = len(lefts), len(lefts) + len(weights)

    def kernel(*refs):
        total = dot(refs[0][...], refs[count][...], dims)
        for i in range(1, count):
            total += dot(refs[i][...], refs[count + i][...], dims)
        results = finish(total, *refs[terms : terms + len(extras)])
        targets = refs[terms + len(extras) :]
        if split:

            @pl.when(pl.program_id(0) < half)
            def _():
                targets[0][...] = results[0]

            @pl.when(pl.program_id(0) >= half)
            def _():
                targets[1][...] = results[0]

            targets = targets[1:]
        else:
            targets[0][...] = results[0]
        for target, result in zip(targets[1:], results[1:]):

            @pl.when(pl.program_id(0) == 0)
            def _():
                target[...] = jnp.zeros_like(target)

            target[...] += result

    def by_rows(array):
        return pl.BlockSpec((block, array.shape[1]), lambda i: (i, 0))

    def whole(array):
        return pl.BlockSpec(array.shape, lambda i: (0, 0), pipeline_mode=pl.Buffered(1))

    first = outs[0]
    if split:
        part = jax.ShapeDtypeStruct((rows // 2, first.shape[1]), first.dtype)
        shapes = [part, part] + list(outs[1:])
        specs = [
            pl.BlockSpec((block, first.shape[1]), lambda i: (jnp.minimum(i, half - 1), 0)),
            pl.BlockSpec((block, first.shape[1]), lambda i: (jnp.maximum(i - half, 0), 0)),
        ]
    else:
        shapes, specs = list(outs), [by_rows(first)]
    specs += [pl.BlockSpec(out.shape, lambda i: (0, 0)) for out in outs[1:]]
    return pl.pallas_call(
        kernel,
        out_shape=shapes,
        grid=(steps,),
        in_specs=[
            pl.BlockSpec((block, a.shape[1]), lambda i: (i + first_row // block, 0)) for a in lefts
        ]
        + [whole(w) for w in weights]
        + [by_rows(e) if e.shape[0] == rows else whole(e) for e in extras],
        out_specs=specs,
        compiler_params=params(("arbitrary",)),
        cost_estimate=NOMINAL,
        name=name,
    )(*lefts, *weights, *extras)


def like(rows, cols, kind=BF16):
    return jax.ShapeDtypeStruct((rows, cols), kind)


def plain(total):
    return (total.astype(BF16),)


def with_bias(total, bias_ref):
    return ((total + bias_ref[...]).astype(BF16),)


def with_slope(total, slope_ref):
    low = (total * slope_ref[...].astype(F32)).astype(BF16)
    return low, jnp.sum(low.astype(F32), axis=0, keepdims=True)


def layer_end(total, middle_ref, other_ref, bias_ref):
    return ((middle_ref[...] + total + other_ref[...].astype(F32) + bias_ref[...]).astype(BF16),)


def small_call(kernel, outs, scalars, arrays, name):
    vmem = pl.BlockSpec(memory_space=pltpu.VMEM)
    return pl.pallas_call(
        kernel,
        out_shape=outs,
        in_specs=[pl.BlockSpec(memory_space=pltpu.SMEM)] * len(scalars) + [vmem] * len(arrays),
        out_specs=[vmem] * len(outs),
        compiler_params=pltpu.CompilerParams(vmem_limit_bytes=VMEM),
        cost_estimate=NOMINAL,
        name=name,
    )(*scalars, *arrays)


def add_rows(left, right, kind=BF16, pieces=1):
    size = left.shape[0] // pieces
    parts = [slice(i * size, (i + 1) * size) for i in range(pieces)]
    return [(left[part].astype(F32) + right[part].astype(F32)).astype(kind) for part in parts]


def scatter_step(keep, arrived, rows):
    if keep.shape[0] == rows:
        return add_rows(keep, arrived)[0], None
    return add_rows(keep, arrived, BF16, 2)


def both_cores(core, mine, other, size, total, start=0, turn=False):
    rows = mine.shape[0]

    def kernel(core_ref, mine_ref, other_ref, out_ref):
        for at, refs in ((0, (mine_ref, other_ref)), (1, (other_ref, mine_ref))):

            @pl.when(core_ref[0] == at)
            def _():
                first = refs[0][:, start : start + size]
                second = refs[1][:, start : start + total - size]
                if turn:
                    out_ref[:size], out_ref[size:] = first.T, second.T
                else:
                    out_ref[...] = jnp.concatenate([first, second], axis=1)

    shape = like(total, rows, mine.dtype) if turn else like(rows, total, mine.dtype)
    return small_call(kernel, [shape], [core], [mine, other], "both_cores")[0]


def both_columns(is_first, mine, other, size, total, start=0):
    mine, other = mine[:, start:], other[:, start:]
    return jnp.where(
        is_first,
        jnp.concatenate([mine[:, :size], other[:, : total - size]], axis=1),
        jnp.concatenate([other[:, :size], mine[:, : total - size]], axis=1),
    )


def core_columns(core, arrays, cols):
    rows, width = arrays[0].shape

    def kernel(core_ref, *refs):
        for at in range(2):

            @pl.when(core_ref[0] == at)
            def _():
                for i in range(len(arrays)):
                    for k, where in enumerate((at, 1 - at)):
                        low = where * (width - cols)
                        refs[len(arrays) * (1 + k) + i][...] = refs[i][:, low : low + cols]

    return small_call(kernel, [like(rows, cols)] * (2 * len(arrays)), [core], arrays, "core_columns")


def mask_kernel(rows, tokens, blocks, len_ref, place_ref, need_ref, row_ref, col_ref, near_row, near_col):
    place = place_ref[0]
    for row in range(rows):
        ends = [len_ref[row, 0]]
        for p in range(1, len_ref.shape[1]):
            ends.append(ends[-1] + len_ref[row, p])

        def pictures(position):
            return sum((position >= end).astype(jnp.int32) for end in ends)

        def segment(position):
            return jnp.where(position < ends[-1], pictures(position), 1000 + position)

        spans = []
        for block in range(blocks):
            start = jnp.bitwise_xor(place, block) * tokens
            across = segment(start + lax.broadcasted_iota(jnp.int32, (1, tokens), 1))
            down = segment(start + lax.broadcasted_iota(jnp.int32, (tokens, 1), 0))
            row_ref[row, block : block + 1] = across
            col_ref[row, block] = down
            if block < 2:
                near_row[row, :, block * tokens : (block + 1) * tokens] = across
                near_col[row, block * tokens : (block + 1) * tokens] = down
            last = jnp.minimum(start + tokens, ends[-1]) - 1
            low = sum(jnp.where(start >= end, 1, 0) for end in ends)
            high = sum(jnp.where(last >= end, 1, 0) for end in ends)
            spans.append((start < ends[-1], low, high))
        for block, (real, low, high) in enumerate(spans):
            if block < 2:
                need_ref[row, block] = 1
            else:
                need_ref[row, block] = sum(
                    jnp.where(real & ok & (low <= top) & (bottom <= high), 1, 0) for ok, bottom, top in spans[:2]
                )


def masks(lengths, place, blocks, tokens):
    rows = lengths.shape[0]
    shapes = [(rows, blocks, tokens), (rows, blocks, tokens, 1), (rows, 1, 2 * tokens), (rows, 2 * tokens, 1)]
    smem = pl.BlockSpec(memory_space=pltpu.SMEM)
    return pl.pallas_call(
        functools.partial(mask_kernel, rows, tokens, blocks),
        out_shape=[jax.ShapeDtypeStruct((rows, blocks), jnp.int32)]
        + [jax.ShapeDtypeStruct(shape, jnp.int32) for shape in shapes],
        in_specs=[smem, smem],
        out_specs=[smem] + [pl.BlockSpec(memory_space=pltpu.VMEM)] * 4,
        compiler_params=pltpu.CompilerParams(vmem_limit_bytes=VMEM),
        cost_estimate=NOMINAL,
        name="masks",
    )(lengths, place)


def lay_vectors(core, weight, lines, half, padded):
    width, cols = weight.shape
    low = half // 128 * 128

    def kernel(core_ref, weight_ref, lines_ref, q_ref, kv_ref):
        turned = weight_ref[...].astype(F32).T
        lines_ref[...] = turned[half - low : half - low + lines]
        q_ref[...] = jnp.zeros_like(q_ref)
        kv_ref[...] = jnp.zeros_like(kv_ref)
        for at in range(2):

            @pl.when(core_ref[0] == at)
            def _():
                q_ref[:, :half] = lines_ref[2:3, at * half : (at + 1) * half]
                kv_ref[:, padded : padded + half] = lines_ref[3:4, at * half : (at + 1) * half]

    outs = [like(lines, width, F32), like(1, padded, F32), like(1, 2 * padded, F32)]
    block = cols - low
    return pl.pallas_call(
        kernel,
        out_shape=outs,
        grid=(1,),
        in_specs=[
            pl.BlockSpec(memory_space=pltpu.SMEM),
            pl.BlockSpec((width, block), lambda i: (0, low // block)),
        ],
        out_specs=[pl.BlockSpec(out.shape, lambda i: (0, 0)) for out in outs],
        compiler_params=params(("arbitrary",)),
        cost_estimate=NOMINAL,
        name="lay_vectors",
    )(core, weight)


def mlp_shards(core, out_shard, hidden_weight, down_weight, cols):
    rows, total = hidden_weight.shape
    before = out_shard.shape[1]

    def kernel(core_ref, part_ref, hidden_ref, down_ref, first_out, down_out):
        first_out[:, :before] = part_ref[...]
        for at in range(2):

            @pl.when(core_ref[0] == at)
            def _():
                low = at * cols
                high = min(low + cols, total)
                size = high - low
                first_out[:, before : before + size] = hidden_ref[:, low:high]
                down_out[:, :size] = down_ref[low:high].T
                if size < cols:
                    empty = jnp.zeros((rows, cols - size), BF16)
                    first_out[:, before + size :] = empty
                    down_out[:, size:] = empty

    outs = [like(rows, before + cols), like(rows, cols)]
    return small_call(kernel, outs, [core], [out_shard, hidden_weight, down_weight], "mlp_shards")


def attention_shards(core, weights, vectors, half, padded):
    rows, width = weights[0].shape
    cut = width - padded
    count = len(vectors)

    def kernel(core_ref, q_ref, k_ref, v_ref, o_ref, *refs):
        qkv_ref, out_ref, held = refs[count:]
        for i in range(count):
            held[i : i + 1] = refs[i][...].astype(F32).reshape(1, rows)
        empty = jnp.zeros((rows, padded - half), BF16)
        spare = jnp.zeros((rows, padded - half - count), BF16)
        lines = jnp.concatenate([held[...].T.astype(BF16), spare], axis=1)
        for at in range(2):

            @pl.when(core_ref[0] == at)
            def _():
                for i, ref in enumerate((q_ref, k_ref, v_ref)):
                    part = ref[:, at * half : (at + 1) * half]
                    rest = empty if i else lines
                    qkv_ref[:, i * padded : (i + 1) * padded] = jnp.concatenate([part, rest], axis=1)
                out_ref[...] = o_ref[:, at * cut : at * cut + padded]

    vmem = pl.BlockSpec(memory_space=pltpu.VMEM)
    return pl.pallas_call(
        kernel,
        out_shape=[like(rows, 3 * padded), like(rows, padded)],
        in_specs=[pl.BlockSpec(memory_space=pltpu.SMEM)] + [vmem] * (4 + count),
        out_specs=[vmem] * 2,
        scratch_shapes=[pltpu.VMEM((count, rows), F32)],
        compiler_params=pltpu.CompilerParams(vmem_limit_bytes=VMEM),
        cost_estimate=NOMINAL,
        name="attention_shards",
    )(core, *weights, *vectors)


def hidden(arrays, weight, bias):
    rows, width = arrays[0].shape
    cols = weight.shape[1]
    block = row_block(rows)
    steps, count = rows // block, len(arrays)

    def kernel(*refs):
        w_ref, b_ref, act_ref, slope_ref, x_ref = refs[count:]
        for i in range(count):

            @pl.when(pl.program_id(0) // steps == i)
            def _():
                x_ref[...] = refs[i][...]

        pre = dot(x_ref[...], w_ref[...]) + b_ref[...]
        square = pre * pre
        turn = jnp.tanh(pre * (GELU_COEF + GELU_COEF * 0.044715 * square))
        act_ref[...] = (0.5 * pre * (1.0 + turn)).astype(BF16)
        inner = GELU_COEF + 3.0 * 0.044715 * GELU_COEF * square
        slope_ref[...] = (0.5 * (1.0 + turn) * (1.0 + pre * (1.0 - turn) * inner)).astype(BF16)

    out = pl.BlockSpec((block, cols), lambda i: (i, 0))
    return pl.pallas_call(
        kernel,
        out_shape=(
            jax.ShapeDtypeStruct((count * rows, cols), BF16),
            jax.ShapeDtypeStruct((count * rows, cols), BF16),
            jax.ShapeDtypeStruct((count * rows, width), BF16),
        ),
        grid=(count * steps,),
        in_specs=[
            pl.BlockSpec((block, width), lambda i, k=k: (jnp.clip(i - k * steps, 0, steps - 1), 0))
            for k in range(count)
        ]
        + [
            pl.BlockSpec((width, cols), lambda i: (0, 0), pipeline_mode=pl.Buffered(1)),
            pl.BlockSpec((1, cols), lambda i: (0, 0)),
        ],
        out_specs=(out, out, pl.BlockSpec((block, width), lambda i: (i, 0))),
        compiler_params=params(("arbitrary",)),
        cost_estimate=NOMINAL,
        name="hidden",
    )(*arrays, weight, bias)


def head_window(head):
    first = head * HEAD_DIM
    start = first // 128 * 128
    return start, round_up(first + HEAD_DIM, 128) - start, first - start


def head_lanes(rows, width, low):
    lane = lax.broadcasted_iota(jnp.int32, (rows, width), 1)
    return (lane >= low) & (lane < low + HEAD_DIM)


def only_head(block, low):
    mine = head_lanes(*block.shape, low)
    return jnp.where(mine, block.astype(F32), 0.0).astype(BF16)


def pick_block(near_ref, far_ref, block):
    return near_ref.at[block, 0] if block < 2 else far_ref.at[block - 2, 0]


def attend_kernel(row, heads, blocks, padded, need_ref, col_ref, row_ref, q_ref, near_ref, far_ref, *refs):
    own_ref, pair_ref, lse_ref, queries, score, peak, total, acc, lses = refs[-9:]
    outs = (own_ref, pair_ref)
    tokens = own_ref.shape[1]
    slot = lax.broadcasted_iota(jnp.int32, (2 * tokens, 128), 1)
    for which in range(2):
        outs[which][...] = jnp.zeros_like(outs[which])
    windows = [head_window(head) for head in range(heads)]
    for head, (start, width, low) in enumerate(windows):
        for which in range(2):
            queries[head, which * tokens : (which + 1) * tokens, :width] = only_head(
                q_ref[which, 0, :, start : start + width], low
            )
    peak[...] = jnp.full_like(peak, MASKED)
    total[...] = jnp.zeros_like(total)
    acc[...] = jnp.zeros_like(acc)
    for block in range(blocks):

        @pl.when(need_ref[row, block] != 0)
        def _():
            side = pick_block(near_ref, far_ref, block)
            seen = col_ref[0] == row_ref[0, block : block + 1]
            for head, (start, width, _) in enumerate(windows):
                key = side[:, start : start + width]
                found = jnp.where(seen, dot(queries[head, :, :width], key, NT), MASKED)
                score[head, block] = found
                top = peak[head]
                for at in range(0, tokens, 128):
                    top = jnp.maximum(top, found[:, at : at + 128])
                peak[head] = top

    for head in range(heads):
        top = jnp.max(peak[head], axis=-1, keepdims=True) * (SCALE * LOG2E)
        peak[head] = jnp.broadcast_to(top, peak.shape[1:])

    for block in range(blocks):

        @pl.when(need_ref[row, block] != 0)
        def _():
            side = pick_block(near_ref, far_ref, block)
            for head, (start, width, _) in enumerate(windows):
                top, share = peak[head], total[head]
                pieces = []
                for at in range(0, tokens, 128):
                    part = jnp.exp2(score[head, block, :, at : at + 128] * (SCALE * LOG2E) - top)
                    share += part
                    pieces.append(part.astype(BF16))
                total[head] = share
                value = side[:, padded + start : padded + start + width]
                acc[head, :, :width] += dot(jnp.concatenate(pieces, axis=1), value)

    for head, (start, width, low) in enumerate(windows):
        norm = jnp.sum(total[head], axis=-1, keepdims=True)
        result = acc[head, :, :width] / norm
        mine = head_lanes(tokens, width, low)
        for which in range(2):
            kept = outs[which][0, :, start : start + width].astype(F32)
            fresh = result[which * tokens : (which + 1) * tokens]
            outs[which][0, :, start : start + width] = jnp.where(mine, fresh, kept).astype(BF16)
        lse = peak[head] + jnp.log2(norm)
        lses[...] = lse if head == 0 else jnp.where(slot == head, lse, lses[...])
    lse_ref[0] = lses[...].T[:heads]


def attend(row, query, near, far, need, seg_col, seg_row, heads, before):
    _, rows, tokens, padded = query.shape
    blocks = 2 + far.shape[0]
    narrow = pl.BlockSpec((1, tokens, padded), lambda i, need: (row, 0, 0))
    lines = pl.BlockSpec((1, heads, 2 * tokens), lambda i, need: (row, 0, 0))

    def stack(count, width):
        return pl.BlockSpec((count, 1, tokens, width), lambda i, need: (0, row, 0, 0))

    return pl.pallas_call(
        functools.partial(attend_kernel, row, heads, blocks, padded),
        out_shape=(
            jax.ShapeDtypeStruct((rows, tokens, padded), BF16),
            jax.ShapeDtypeStruct((rows, tokens, padded), BF16),
            jax.ShapeDtypeStruct((rows, heads, 2 * tokens), F32),
        ),
        grid_spec=pltpu.PrefetchScalarGridSpec(
            num_scalar_prefetch=1,
            grid=(1,),
            in_specs=[
                pl.BlockSpec((1, 2 * tokens, 1), lambda i, need: (row, 0, 0)),
                pl.BlockSpec((1, blocks, tokens), lambda i, need: (row, 0, 0)),
                stack(2, padded),
                stack(2, 2 * padded),
                stack(blocks - 2, 2 * padded),
            ]
            + [pl.BlockSpec(memory_space=pl.ANY)] * len(before),
            out_specs=(narrow, narrow, lines),
            scratch_shapes=[
                pltpu.VMEM((heads, 2 * tokens, WIN), BF16),
                pltpu.VMEM((heads, blocks, 2 * tokens, tokens), F32),
                pltpu.VMEM((heads, 2 * tokens, 128), F32),
                pltpu.VMEM((heads, 2 * tokens, 128), F32),
                pltpu.VMEM((heads, 2 * tokens, WIN), F32),
                pltpu.VMEM((2 * tokens, 128), F32),
            ],
        ),
        input_output_aliases={6 + i: i for i in range(len(before))},
        compiler_params=params(("arbitrary",)),
        cost_estimate=NOMINAL,
        name="attend",
    )(need, seg_col, seg_row, query, near, far, *before)


def attend_back_kernel(
    row, heads, blocks, padded, need_ref, col_ref, row_ref, pick_ref, q_ref, near_ref, far_ref, *refs
):
    grads, outs, lse_ref = refs[0:2], refs[2:4], refs[4]
    dq_ref, dnear_ref, dfar_ref, sums, inner_turn, queries, incoming, dq = refs[-8:]
    tokens = grads[0].shape[1]
    sums[...] = jnp.zeros_like(sums)
    for which in range(2):
        dq_ref[which, 0] = jnp.zeros((tokens, padded), BF16)
        product = grads[which][0].astype(F32) * outs[which][0].astype(F32)
        high = product.astype(BF16)
        rest = (product - high.astype(F32)).astype(BF16)
        inner_turn[:, which * tokens : (which + 1) * tokens] = dot(pick_ref[...], high, NT) + dot(
            pick_ref[...], rest, NT
        )
    windows = [head_window(head) for head in range(heads)]
    for head, (start, width, low) in enumerate(windows):
        for which in range(2):
            there = slice(which * tokens, (which + 1) * tokens)
            here = slice(start, start + width)
            queries[head, there, :width] = only_head(q_ref[which, 0, :, here], low)
            incoming[head, there, :width] = only_head(grads[which][0, :, here], low)
    dq[...] = jnp.zeros_like(dq)
    for block in range(blocks):

        @pl.when(need_ref[row, block] != 0)
        def _():
            side = pick_block(near_ref, far_ref, block)
            seen = col_ref[0, block] == row_ref[0]
            for head, (start, width, _) in enumerate(windows):
                end = start + width
                key, value = side[:, start:end], side[:, padded + start : padded + end]
                query, grad = queries[head, :, :width], incoming[head, :, :width]
                found = dot(key, query, NT) * (SCALE * LOG2E) - lse_ref[0, head : head + 1, :]
                prob = jnp.where(seen, jnp.exp2(found), 0.0)
                inner = inner_turn[head : head + 1, :]
                slope = (prob * (dot(value, grad, NT) - inner)).astype(BF16)
                sums[block, :, start:end] += dot(slope, query)
                sums[block, :, padded + start : padded + end] += dot(prob.astype(BF16), grad)
                dq[head, :, :width] += dot(slope, key, TN)

    for head, (start, width, low) in enumerate(windows):
        mine = head_lanes(tokens, width, low)
        for which in range(2):
            kept = dq_ref[which, 0, :, start : start + width].astype(F32)
            fresh = dq[head, which * tokens : (which + 1) * tokens, :width] * SCALE
            dq_ref[which, 0, :, start : start + width] = jnp.where(mine, fresh, kept).astype(BF16)
    for block in range(blocks):
        side = pick_block(dnear_ref, dfar_ref, block)
        side[:, :padded] = (sums[block, :, :padded] * SCALE).astype(BF16)
        side[:, padded:] = sums[block, :, padded:].astype(BF16)


def attend_back(row, query, near, far, grads, outs, lse, need, seg_col, seg_row, heads, before):
    _, rows, tokens, padded = query.shape
    blocks = 2 + far.shape[0]
    column = lax.broadcasted_iota(jnp.int32, (heads, padded), 1)
    pick = (column // HEAD_DIM == lax.broadcasted_iota(jnp.int32, (heads, padded), 0)).astype(BF16)
    narrow = pl.BlockSpec((1, tokens, padded), lambda i, need: (row, 0, 0))

    def stack(count, width):
        return pl.BlockSpec((count, 1, tokens, width), lambda i, need: (0, row, 0, 0))

    return pl.pallas_call(
        functools.partial(attend_back_kernel, row, heads, blocks, padded),
        out_shape=tuple(jax.ShapeDtypeStruct(a.shape, BF16) for a in (query, near, far)),
        grid_spec=pltpu.PrefetchScalarGridSpec(
            num_scalar_prefetch=1,
            grid=(1,),
            in_specs=[
                pl.BlockSpec((1, blocks, tokens, 1), lambda i, need: (row, 0, 0, 0)),
                pl.BlockSpec((1, 1, 2 * tokens), lambda i, need: (row, 0, 0)),
                pl.BlockSpec((heads, padded), lambda i, need: (0, 0)),
                stack(2, padded),
                stack(2, 2 * padded),
                stack(blocks - 2, 2 * padded),
            ]
            + [narrow] * 4
            + [pl.BlockSpec((1, heads, 2 * tokens), lambda i, need: (row, 0, 0))]
            + [pl.BlockSpec(memory_space=pl.ANY)] * len(before),
            out_specs=(stack(2, padded), stack(2, 2 * padded), stack(blocks - 2, 2 * padded)),
            scratch_shapes=[
                pltpu.VMEM((blocks, tokens, 2 * padded), F32),
                pltpu.VMEM((heads, 2 * tokens), F32),
                pltpu.VMEM((heads, 2 * tokens, WIN), BF16),
                pltpu.VMEM((heads, 2 * tokens, WIN), BF16),
                pltpu.VMEM((heads, 2 * tokens, WIN), F32),
            ],
        ),
        input_output_aliases={12 + i: i for i in range(len(before))},
        compiler_params=params(("arbitrary",)),
        cost_estimate=NOMINAL,
        name="attend_back",
    )(need, seg_col, seg_row, pick, query, near, far, *grads, *outs, lse, *before)


def local(
    patches,
    lengths,
    first_gain,
    first_shift,
    query_weight,
    query_bias,
    key_weight,
    value_weight,
    value_bias,
    output_weight,
    output_bias,
    second_gain,
    second_shift,
    hidden_weight,
    hidden_bias,
    down_weight,
    down_bias,
    cotangent,
):
    seq_count, shards = lax.axis_size("seq"), lax.axis_size("fsdp")
    place, me = lax.axis_index("seq"), lax.axis_index("fsdp")
    core = place & 1
    is_first = core == 0
    core_flag = core[None].astype(jnp.int32)
    rows, tokens, width = patches.shape
    flat = rows * tokens
    heads = width // HEAD_DIM // 2
    half = heads * HEAD_DIM
    padded = round_up(half, 128)
    ff = hidden_bias.shape[0]
    ff_half = round_up(ff, 256) // 2
    out_cols = padded
    out_cut = width - padded
    shard_rows = width // shards
    chain = Chain()

    def my_half(array, size, padded_size):
        first, second = array[..., :size], array[..., size:]
        grow = [(0, 0)] * (array.ndim - 1)
        first = jnp.pad(first, grow + [(0, padded_size - size)])
        second = jnp.pad(second, grow + [(0, padded_size - second.shape[-1])])
        return jnp.where(is_first, first, second)

    flights = Flights(chain)
    staged = shards == 8 and seq_count == 4
    y, z, zz = 1, 2, 4
    top = bits_of(seq_count)[0]

    inputs = patches.reshape(flat, width)
    incoming = cotangent.reshape(flat, width)
    vectors = [
        first_gain,
        first_shift,
        query_bias,
        value_bias,
        output_bias,
        second_gain,
        second_shift,
        down_bias,
    ]
    shard_qkv, shard_out = chain.done(
        *attention_shards(
            core_flag, [query_weight, key_weight, value_weight, output_weight], vectors, half, padded
        )
    )
    place_flag = place[None].astype(jnp.int32)

    def over(box_from, bits):
        return flights.send(box_from[0], "fsdp", bits)

    if staged:
        q = {0: [shard_qkv]}
        q[y] = over(q[0], y)
        q[z], q[zz] = over(q[0], z), over(q[0], zz)
        shard_ho, shard_down = chain.done(
            *mlp_shards(core_flag, shard_out, hidden_weight, down_weight, ff_half)
        )
        h, d = {0: [shard_ho]}, {0: [shard_down]}
        need, seg_rows, seg_cols, seg_near_row, seg_near_col = chain.done(
            *masks(chain(lengths), place_flag, seq_count, tokens)
        )
        core_flag, raw_own = flights.land(core_flag, inputs)
        q[zz | z], q[z | y], q[zz | y] = over(q[zz], z), over(q[z], y), over(q[zz], y)
        far_raw = [flights.send(raw_own, "seq", 2)]
        raw_pair = flights.send(raw_own, "seq", 1)
        core_flag = flights.land(core_flag, only=[q[zz | z]])
        q[zz | z | y] = over(q[zz | z], y)
        core_flag, shard_ho = flights.land(core_flag, shard_ho, only=[q[z | y], q[zz | y], raw_pair])
        h[0] = [shard_ho]
        h[z], h[y] = over(h[0], z), over(h[0], y)
        core_flag, shard_ho, shard_down = flights.land(
            core_flag, shard_ho, shard_down, only=[q[zz | z | y], far_raw[0]]
        )
        h[0], d[0] = [shard_ho], [shard_down]
        far_pair = [flights.send(far_raw[0][0], "seq", 1)]
        h[zz], d[y] = over(h[0], zz), over(d[0], y)
        w_q, w_kv = chain.done(*assemble({k: box[0] for k, box in q.items()}, me, padded))
        stacked, bias_q, bias_kv = chain.done(
            *lay_vectors(chain(core_flag), w_q, len(vectors), half, padded)
        )
        gain_one, shift_one = stacked[0:1], stacked[1:2]
        gain_one = chain(gain_one)
        normed_near = chain.done(norm([inputs, raw_pair[0]], gain_one, shift_one))
        bias_hidden = my_half(after(hidden_bias, gain_one).astype(F32)[None], ff_half, ff_half)
        gain_one = flights.land(gain_one, only=[h[z], far_pair[0]])
        h[z | y] = over(h[z], y)
        incoming_pair = flights.send(incoming, "seq", 1)
    else:
        parts = gather_all(shard_qkv)
        shard_ho, shard_down = mlp_shards(core_flag, shard_out, hidden_weight, down_weight, ff_half)
        raw = {0: inputs}
        for bit in bits_of(seq_count):
            raw.update({j | bit: swap(part, "seq", bit) for j, part in list(raw.items())})
        need, seg_rows, seg_cols, seg_near_row, seg_near_col = masks(lengths, place_flag, seq_count, tokens)
        w_q, w_kv = chain.done(*assemble(parts, me, padded))
        stacked, bias_q, bias_kv = lay_vectors(core_flag, w_q, len(vectors), half, padded)
        gain_one, shift_one = stacked[0:1], stacked[1:2]
        normed_near = norm([raw[0], raw[1]], gain_one, shift_one)
        far_raw, far_pair = [[raw[j]] for j in range(2, seq_count)], []
        incoming_pair = [swap(incoming, "seq", 1)]
        bias_hidden = my_half(hidden_bias.astype(F32)[None], ff_half, ff_half)
    _, _, bias_query, bias_value, bias_output, gain_two, shift_two, bias_down = [
        stacked[i : i + 1] for i in range(8)
    ]

    near_in, w_q, w_kv = chain(normed_near, w_q, w_kv)
    (query,) = rows_matmul("query", [near_in], [w_q], with_bias, [bias_q], [like(2 * flat, padded)])
    near_in = after(near_in, query)
    (near,) = rows_matmul("near", [near_in], [w_kv], with_bias, [bias_kv], [like(2 * flat, 2 * padded)])
    chain.done(query, near)
    gain_one, w_kv = chain(gain_one, w_kv)
    normed_far = chain.done(norm([box[0] for box in far_raw + far_pair], gain_one, shift_one))
    if staged:
        w_kv, incoming = flights.land(w_kv, incoming)
        h[zz | y], h[zz | z] = over(h[zz], y), over(h[zz], z)
    incoming_near = jnp.concatenate([incoming, incoming_pair[0]], axis=0)
    far_in, w_kv = chain(normed_far, w_kv)
    (far,) = rows_matmul(
        "far", [far_in], [w_kv], with_bias, [bias_kv], [like(normed_far.shape[0], 2 * padded)]
    )
    chain.done(far)
    query = query.reshape(2, rows, tokens, padded)
    near = near.reshape(2, rows, tokens, 2 * padded)
    far = far.reshape(seq_count - 2, rows, tokens, 2 * padded)
    found = ()
    for row in range(rows):
        query, near, far = chain(query, near, far)
        if staged and row == 1:
            query = flights.land(query)
            h[zz | z | y] = over(h[zz | z], y)
            d[z], d[zz] = over(d[0], z), over(d[0], zz)
        found = chain.done(*attend(row, query, near, far, need, seg_near_col, seg_rows, heads, found))
    out_own, out_pair, lse = found
    if staged:
        out_own, out_pair = flights.land(out_own, out_pair)
        h_parts = {k: box[0] for k, box in h.items()}
    else:
        out_own, out_pair = flights.land(out_own, out_pair)
        h_parts = gather_all(chain(shard_ho))
    w_out_mine, w_hidden = chain.done(*assemble(h_parts, me, out_cols))
    out_pair, w_out_mine = chain(out_pair, w_out_mine)
    other_half = flights.send(out_pair, "seq", 1)
    w_out_other = flights.send(w_out_mine, "seq", 1)
    if staged:
        d[zz | z], d[z | y] = over(d[zz], z), over(d[z], y)
    w_out_mine, w_hidden = flights.land(w_out_mine, w_hidden, only=[other_half, w_out_other])
    w_out = chain.done(both_cores(core_flag, w_out_mine, w_out_other[0], out_cut, width))
    if staged:
        w_out = flights.land(w_out, only=[d[zz | z], d[z | y]])
        d[zz | y], d[zz | z | y] = over(d[zz], y), over(d[zz | z], y)
    own_half, w_out = chain(out_own.reshape(flat, padded), w_out)
    attended, middle, second = chain.done(
        *join(
            core_flag,
            own_half,
            other_half[0].reshape(flat, padded),
            inputs,
            w_out,
            bias_output,
            gain_two,
            shift_two,
            half,
        )
    )
    second_pair = flights.send(second, "seq", 1)
    second, w_hidden = flights.land(second, w_hidden, only=[second_pair])
    act, slope, second_near = chain.done(*hidden([second, second_pair[0]], w_hidden, bias_hidden))

    incoming_near, act = chain(incoming_near, act)
    grad_down = chain.done(token_dot(incoming_near, act))
    if staged:
        slope, grad_down = flights.land(slope, grad_down)
        d_parts = {k: box[0] for k, box in d.items()}
    else:
        d_parts = gather_all(chain(shard_down))
    part_down = lax.psum_scatter(grad_down, "fsdp", scatter_dimension=0, tiled=True)
    w_down = chain.done(assemble(d_parts, me))
    incoming_near, slope, w_down = chain(incoming_near, slope, w_down)
    grad_pre, hidden_line = chain.done(
        *rows_matmul(
            "grad_pre",
            [incoming_near],
            [w_down],
            with_slope,
            [slope],
            [like(2 * flat, ff_half), like(1, ff_half, F32)],
        )
    )
    grad_pre = chain(grad_pre)
    back, back_pair = chain.done(
        *rows_matmul("back", [grad_pre], [w_hidden], plain, [], [like(2 * flat, width)], NT, True)
    )
    back_other = flights.send(back_pair, "seq", 1)
    second_near, grad_pre = chain(second_near, grad_pre)
    grad_hidden = chain.done(dot(second_near, grad_pre, TN).astype(BF16))
    part_hidden = lax.psum_scatter(grad_hidden, "fsdp", scatter_dimension=0, tiled=True)
    back = flights.land(back)
    grad_middle, branch, grad_mine, grad_send, lines = second_back(
        core_flag, middle, [back, back_other[0]], gain_two, incoming, w_out, hidden_line, half, padded
    )
    chain.done(branch, grad_send)
    grad_pair = flights.send(grad_send, "seq", 1)
    attended, branch = chain(attended, branch)
    partial_out = chain(chain.done(token_dot(attended, branch)))
    out_mine, out_other = chain.done(*core_columns(core_flag, [partial_out], out_cols))
    query = flights.land(query)

    links = {"x": ("seq", top), "core": ("seq", 1)} | {bit: ("fsdp", bit) for bit in bits_of(shards)}
    out_back = flights.send(out_other, "seq", 1)
    shape = (rows, tokens, padded)
    grads = [grad_mine.reshape(shape), grad_pair[0].reshape(shape)]
    found = ()
    far_bits = [2 << k for k in range(shards.bit_length() - 2)]
    def next_step(keep, box, bits):
        keep, send = scatter_step(keep, box[0], shard_rows)
        chain.done(keep)
        return keep, flights.send(send, "fsdp", bits.pop(0)) if bits else None

    def seq_rest(mine, arrived):
        for bit in bits_of(seq_count)[1:-1]:
            (mine,) = add_rows(mine, arrived)
            arrived = swap(mine, "seq", bit)
        return chain.done(*add_rows(mine, arrived, F32))

    for row in range(rows):
        query, near, far, *grads = chain(query, near, far, *grads)
        found = attend_back(
            row, query, near, far, grads, [out_own, out_pair], lse, need, seg_cols, seg_near_row, heads, found
        )
        chain.done(*found)
        query = flights.land(query)
        if row == 0:
            out_sum = chain.done(*add_rows(out_mine, out_back[0]))
        if row == 1:
            part_down = chain(part_down)
            down_seq = flights.send(part_down, "seq", top)
    dq, dnear, dfar = [g.reshape(-1, g.shape[-1]) for g in found]
    dfar, w_kv, down_seq[0] = chain(dfar, w_kv, down_seq[0])
    two = seq_count == 4
    back_far = rows_matmul("back_far", [dfar], [w_kv], plain, [], [like(dfar.shape[0], width)], NT, two)
    chain.done(*back_far)
    dnear = chain(dnear)
    if two:
        far_parts = {2 + i: part for i, part in enumerate(back_far)}
    else:
        far_parts = {j: back_far[0][(j - 2) * flat : (j - 1) * flat] for j in range(2, seq_count)}
    far_sent = {j: flights.send(part, "seq", 1) for j, part in far_parts.items() if j & 1}
    normed_near, dnear, dfar = chain(normed_near, dnear, dfar)
    kv_keep, kv_send, kv_sums = chain.done(
        *weight_grad([normed_near, normed_far], [dnear, dfar], me, shards)
    )
    dq = flights.land(dq)
    kv_box = flights.send(kv_send, "fsdp", y)
    cut_rows = flat - tokens
    far_sums = {
        j: [add_rows(far_parts[j][part], far_sent[j | 1][0][part])[0] for part in (slice(0, cut_rows), slice(cut_rows, flat))]
        for j in far_parts
        if not j & 1
    }
    chain.done(*[part for parts in far_sums.values() for part in parts])
    arrived = []
    for bit in bits_of(seq_count)[:-1]:
        for j in [j for j in far_sums if j & bit]:
            parts = far_sums.pop(j)
            if j == bit:
                arrived.append([flights.send(parts[0], "seq", bit), parts[1], bit])
            else:
                pairs = zip(far_sums[j ^ bit], parts)
                far_sums[j ^ bit] = [add_rows(kept, swap(part, "seq", bit))[0] for kept, part in pairs]
    dq, dnear = chain(dq, dnear)
    back_own, back_pair = chain.done(
        *rows_matmul("back_near", [dq, dnear], [w_q, w_kv], plain, [], [like(2 * flat, width)], NT, True)
    )
    pair_back = flights.send(back_pair, "seq", 1)
    for entry in arrived:
        entry[1] = flights.send(chain(entry[1]), "seq", entry[2])
    normed_near, dq = chain(normed_near, dq)
    q_keep, q_send, q_sums = chain.done(*weight_grad([normed_near], [dq], me, shards))
    q_box = flights.send(q_send, "fsdp", y)
    kv_bits, q_bits = list(far_bits), list(far_bits)
    act = flights.land(act, only=[kv_box])
    kv_keep, kv_box = next_step(kv_keep, kv_box, kv_bits)
    act, middle = flights.land(act, middle, only=[entry[0] for entry in arrived])
    (down_pair,) = rows_matmul(
        "down_pair", [act], [w_down], plain, [], [like(flat, width)], NT, first_row=flat
    )
    chain.done(down_pair)
    down_back = flights.send(down_pair, "seq", 1)
    late_in = flights.land(inputs, only=[pair_back, q_box] + [entry[1] for entry in arrived])
    q_keep, q_box = next_step(q_keep, q_box, q_bits)
    late_in = chain(late_in)
    grad_patches, late = chain.done(
        *first_back(
            core_flag,
            late_in,
            [back_own, pair_back[0]] + [(entry[0][0], entry[1][0]) for entry in arrived],
            gain_one,
            grad_middle,
            q_sums,
            kv_sums,
            half,
        )
    )
    out_sum = chain(out_sum)
    part_out = lax.psum_scatter(out_sum, "fsdp", scatter_dimension=0, tiled=True)
    small = jnp.concatenate([lines, late], axis=0)
    small_todo = [zz, y, z] if staged else bits_of(shards)
    small_todo = [("fsdp", bit) for bit in small_todo] + [("seq", bit) for bit in reversed(bits_of(seq_count))]
    small_box = None

    def small_send():
        return flights.send(small, *small_todo.pop(0)) if small_todo else None

    def small_step(small, box):
        return chain.done(*add_rows(small, box[0], F32))

    small_box = small_send()
    part_hidden = chain(part_hidden)
    hidden_seq = flights.send(part_hidden, "seq", top)
    act = flights.land(act, only=[kv_box, down_back])
    if kv_box is not None:
        kv_keep, kv_box = next_step(kv_keep, kv_box, kv_bits)
    act, middle = chain(act, middle)
    (layer_output,) = rows_matmul(
        "down_own", [act], [w_down], layer_end, [middle, down_back[0], bias_down], [like(flat, width)], NT
    )
    layer_output = chain.done(layer_output).reshape(rows, tokens, width)
    lands = [small_box, hidden_seq, q_box]
    act = flights.land(act, only=lands)
    small = small_step(small, small_box)
    small_box = small_send()
    if q_box is not None:
        q_keep, q_box = next_step(q_keep, q_box, q_bits)
    hidden_total = seq_rest(part_hidden, hidden_seq[0])
    hidden_other = flights.send(hidden_total, "seq", 1)
    down_total = seq_rest(part_down, down_seq[0])
    while kv_box is not None:
        act = flights.land(act, only=[kv_box])
        kv_keep, kv_box = next_step(kv_keep, kv_box, kv_bits)
    kv_seq = flights.send(kv_keep, "seq", top)
    act = flights.land(act, only=[small_box, hidden_other])
    small = small_step(small, small_box)
    small_box = small_send()
    while q_box is not None:
        act = flights.land(act, only=[q_box])
        q_keep, q_box = next_step(q_keep, q_box, q_bits)
    q_seq = flights.send(q_keep, "seq", top)
    part_out = chain(part_out)
    out_seq = flights.send(part_out, "seq", top)
    act = flights.land(act, only=[kv_seq, small_box])
    kv_total = seq_rest(kv_keep, kv_seq[0])
    small = small_step(small, small_box)
    small_box = small_send()
    kv_other = flights.send(kv_total, "seq", 1)
    down_other = flights.send(down_total, "seq", 1)
    act = flights.land(act, only=[q_seq, out_seq, small_box])
    small = small_step(small, small_box)
    small_box = small_send()
    q_total = seq_rest(q_keep, q_seq[0])
    out_total = seq_rest(part_out, out_seq[0])
    q_other, out_other = flights.send(q_total, "seq", 1), flights.send(out_total, "seq", 1)
    while small_box is not None:
        act = flights.land(act)
        small = small_step(small, small_box)
        small_box = small_send()
    flights.land()

    own_lines = lax.dynamic_slice_in_dim(small[:8], me * shard_rows, shard_rows, 1)
    late_lines = lax.dynamic_slice_in_dim(small[8:], me * shard_rows, shard_rows, 1)
    cuts = [width, ff_half - width, width, ff - ff_half - width]
    full_bias = jnp.concatenate([small[4 + i, :size] for i, size in enumerate(cuts)])
    full_down = both_columns(is_first, down_total, down_other[0], ff_half, ff).T
    full_hidden = both_columns(is_first, hidden_total, hidden_other[0], ff_half, ff)
    full_out = both_columns(is_first, out_total, out_other[0], out_cut, width)
    full_query = both_columns(is_first, q_total, q_other[0], half, width)
    full_key = both_columns(is_first, kv_total, kv_other[0], half, width)
    full_value = both_columns(is_first, kv_total, kv_other[0], half, width, padded)
    return (
        layer_output,
        grad_patches.reshape(rows, tokens, width),
        late_lines[0],
        late_lines[1],
        full_query,
        late_lines[2],
        full_key,
        full_value,
        late_lines[3],
        full_out,
        own_lines[2],
        own_lines[0],
        own_lines[1],
        full_hidden,
        full_bias,
        full_down,
        own_lines[3],
    )


def solution(mesh):
    shard, line, tokens = P("fsdp", None), P("fsdp"), P("fsdp", "seq", None)
    in_specs = (
        tokens,
        shard,
        line,
        line,
        shard,
        line,
        shard,
        shard,
        line,
        shard,
        line,
        line,
        line,
        shard,
        P(),
        P(None, "fsdp"),
        line,
        tokens,
    )
    out_specs = (
        tokens,
        tokens,
        line,
        line,
        shard,
        line,
        shard,
        shard,
        line,
        shard,
        line,
        line,
        line,
        shard,
        P(),
        P(None, "fsdp"),
        line,
    )
    return jax.shard_map(local, mesh=mesh, in_specs=in_specs, out_specs=out_specs, check_vma=False)
```

```python
import functools
import math

import jax
import jax.numpy as jnp
from jax import lax
from jax.experimental import pallas as pl
from jax.experimental.pallas import tpu as pltpu
from jax.sharding import PartitionSpec as P

HEAD_DIM = 72
EPS = 1e-06
GELU_COEF = math.sqrt(2.0 / math.pi)
MASKED = -1e30
F32 = jnp.float32
BF16 = jnp.bfloat16
SCALE = 1.0 / math.sqrt(HEAD_DIM)
WIN = 256
LOG2E = math.log2(math.e)
VMEM = 60 << 20
NOMINAL = pl.CostEstimate(flops=1, transcendentals=0, bytes_accessed=1)


def round_up(value, step):
    return (value + step - 1) // step * step


def dot(left, right, dims=((1,), (0,))):
    return lax.dot_general(left, right, (dims, ((), ())), preferred_element_type=F32)


NT = ((1,), (1,))
TN = ((0,), (0,))


def params(semantics):
    return pltpu.CompilerParams(dimension_semantics=semantics, vmem_limit_bytes=VMEM)


def swap(array, axis, bits):
    size = lax.axis_size(axis)
    return lax.ppermute(array, axis, [(i, i ^ bits) for i in range(size)])


def bits_of(size):
    return [1 << k for k in reversed(range(size.bit_length() - 1))]


def after(value, *earlier):
    return lax.optimization_barrier((value,) + tuple(earlier))[0]


class Chain:
    def __init__(self):
        self.last = ()

    def __call__(self, *values, wait=()):
        held = lax.optimization_barrier(tuple(values) + tuple(self.last) + tuple(wait))
        return held[: len(values)] if len(values) > 1 else held[0]

    def done(self, *results):
        self.last = results
        return results if len(results) > 1 else results[0]


class Flights:
    def __init__(self, chain):
        self.chain, self.open = chain, []

    def send(self, array, axis, bits):
        self.open.append([swap(array, axis, bits)])
        return self.open[-1]

    def land(self, *values, through=None, only=None):
        if only is None:
            count = len(self.open)
            if through is not None:
                count = sum(i + 1 for i, box in enumerate(self.open) if box is through)
            only = self.open[:count]
        ready = [box for box in self.open if any(box is other for other in only)]
        self.open = [box for box in self.open if not any(box is other for other in ready)]
        held = self.chain(*[box[0] for box in ready], *values)
        held = held if isinstance(held, (tuple, list)) else [held]
        for box, array in zip(ready, held):
            box[0] = array
        rest = list(held[len(ready) :])
        return rest if len(rest) > 1 else rest[0] if rest else None


def in_order(parts, me):
    count = len(parts)
    return jnp.take(jnp.stack([parts[d] for d in range(count)]), me ^ jnp.arange(count), axis=0)


def gather_all(shard):
    parts = {0: shard}
    for bit in bits_of(lax.axis_size("fsdp")):
        parts.update({d | bit: swap(part, "fsdp", bit) for d, part in list(parts.items())})
    return parts


def rel_position(distance, count):
    width = count.bit_length() - 1
    return sum(((distance >> k) & 1) << (width - 1 - k) for k in range(width))


def assemble_kernel(count, rows, single, off_ref, *refs):
    outs = refs[count:]

    def fill(out_ref):
        for distance in range(count):
            start = pl.multiple_of(off_ref[distance], 16)
            out_ref[pl.ds(start, rows), :] = refs[distance][...]

    if single:
        fill(outs[0])
    else:
        pl.when(pl.program_id(0) == 0)(lambda: fill(outs[0]))
        pl.when(pl.program_id(0) > 0)(lambda: fill(outs[1]))


def assemble(parts, me, cut=None):
    count = len(parts)
    rows, cols = parts[0].shape
    if rows % 16:
        full = in_order(parts, me).reshape(count * rows, cols)
        return (full[:, :cut], full[:, cut:]) if cut else full
    offsets = ((me ^ jnp.arange(count, dtype=jnp.int32)) * rows).astype(jnp.int32)
    tile = cut or min(cols, 1152)
    widths = [cut, cols - cut] if cut else [cols]
    maps = [lambda n, off: (0, 0), lambda n, off: (0, jnp.maximum(n - 1, 0))]
    if not cut:
        maps = [lambda n, off: (0, n)]
    outs = pl.pallas_call(
        functools.partial(assemble_kernel, count, rows, not cut),
        out_shape=[jax.ShapeDtypeStruct((count * rows, w), parts[0].dtype) for w in widths],
        grid_spec=pltpu.PrefetchScalarGridSpec(
            num_scalar_prefetch=1,
            grid=(pl.cdiv(cols, tile),),
            in_specs=[pl.BlockSpec((rows, tile), lambda n, off: (0, n))] * count,
            out_specs=[pl.BlockSpec((count * rows, tile), m) for m in maps],
        ),
        compiler_params=params(("arbitrary",)),
        cost_estimate=NOMINAL,
        name="assemble",
    )(offsets, *[parts[d] for d in range(count)])
    return outs if cut else outs[0]


def weight_grad_kernel(pairs, count, rows, pos_ref, *refs):
    lefts, rights = refs[:pairs], refs[pairs : 2 * pairs]
    keep_ref, send_ref, sum_ref = refs[2 * pairs :]
    total = dot(lefts[0][...], rights[0][...], TN)
    for i in range(1, pairs):
        total += dot(lefts[i][...], rights[i][...], TN)
    sum_ref[...] = sum(dot(jnp.ones((8, r.shape[0]), BF16), r[...]) for r in rights)
    for shard in range(count):
        start = pl.multiple_of(pos_ref[shard], 16)
        block = total[shard * rows : (shard + 1) * rows].astype(BF16)

        @pl.when(pos_ref[count] == shard % 2)
        def _():
            keep_ref[pl.ds(start, rows), :] = block

        @pl.when(pos_ref[count] != shard % 2)
        def _():
            send_ref[pl.ds(start, rows), :] = block


def weight_grad(lefts, rights, me, count):
    width = lefts[0].shape[1]
    cols = rights[0].shape[1]
    rows = width // count
    order = me ^ jnp.arange(count, dtype=jnp.int32)
    table = jnp.array([rel_position(d, count) for d in range(count)], jnp.int32)
    half = count // 2
    if rows % 16:
        total = sum(dot(a, b, TN) for a, b in zip(lefts, rights))
        by_distance = jnp.take(total.astype(BF16).reshape(count, rows, cols), order, axis=0)
        back = [0] * count
        for d in range(count):
            back[rel_position(d, count)] = d
        placed = jnp.take(by_distance, jnp.array(back), axis=0).reshape(width, cols)
        ones = [jnp.ones((8, b.shape[0]), BF16) for b in rights]
        sums = sum(dot(one, b) for one, b in zip(ones, rights))
        return placed[: width // 2], placed[width // 2 :], sums
    positions = jnp.concatenate([table[order] % half * rows, (me & 1)[None]]).astype(jnp.int32)
    tile = 256
    pairs = len(lefts)
    return pl.pallas_call(
        functools.partial(weight_grad_kernel, pairs, count, rows),
        out_shape=[jax.ShapeDtypeStruct((width // 2, cols), BF16)] * 2
        + [jax.ShapeDtypeStruct((8, cols), F32)],
        grid_spec=pltpu.PrefetchScalarGridSpec(
            num_scalar_prefetch=1,
            grid=(pl.cdiv(cols, tile),),
            in_specs=[
                pl.BlockSpec(a.shape, lambda n, off: (0, 0), pipeline_mode=pl.Buffered(1))
                for a in lefts
            ]
            + [pl.BlockSpec((b.shape[0], tile), lambda n, off: (0, n)) for b in rights],
            out_specs=[pl.BlockSpec((width // 2, tile), lambda n, off: (0, n))] * 2
            + [pl.BlockSpec((8, tile), lambda n, off: (0, n))],
        ),
        compiler_params=params(("arbitrary",)),
        cost_estimate=NOMINAL,
        name="weight_grad",
    )(positions, *lefts, *rights)


def token_dot(left, right):
    tokens, width = left.shape
    cols = right.shape[1]
    tile = 256

    def kernel(left_ref, right_ref, out_ref):
        out_ref[...] = dot(left_ref[...], right_ref[...], TN).astype(BF16)

    return pl.pallas_call(
        kernel,
        out_shape=jax.ShapeDtypeStruct((width, cols), BF16),
        grid=(pl.cdiv(cols, tile),),
        in_specs=[
            pl.BlockSpec((tokens, width), lambda n: (0, 0), pipeline_mode=pl.Buffered(1)),
            pl.BlockSpec((tokens, tile), lambda n: (0, n)),
        ],
        out_specs=pl.BlockSpec((width, tile), lambda n: (0, n)),
        compiler_params=params(("arbitrary",)),
        cost_estimate=NOMINAL,
        name="token_dot",
    )(left, right)


def normalized(values):
    center = values - jnp.mean(values, axis=-1, keepdims=True)
    spread = jnp.mean(center * center, axis=-1, keepdims=True)
    inverse = lax.rsqrt(spread + EPS)
    return center * inverse, inverse


def row_block(rows):
    return 256 if rows % 256 == 0 else 128 if rows % 128 == 0 else rows


def norm(arrays, gain, shift):
    width = arrays[0].shape[1]
    block = min(row_block(a.shape[0]) for a in arrays)
    steps = [a.shape[0] // block for a in arrays]
    firsts = [sum(steps[:k]) for k in range(len(steps))]
    count, total = len(arrays), sum(steps)

    def kernel(*refs):
        gain_ref, shift_ref, out_ref = refs[count:]
        at = pl.program_id(0)
        for k in range(count):

            @pl.when((at >= firsts[k]) & (at < firsts[k] + steps[k]))
            def _():
                hat, _ = normalized(refs[k][...].astype(F32))
                out_ref[...] = (hat * gain_ref[...] + shift_ref[...]).astype(BF16)

    line = pl.BlockSpec((1, width), lambda i: (0, 0))
    return pl.pallas_call(
        kernel,
        out_shape=jax.ShapeDtypeStruct((total * block, width), BF16),
        grid=(total,),
        in_specs=[
            pl.BlockSpec((block, width), lambda i, k=k: (jnp.clip(i - firsts[k], 0, steps[k] - 1), 0))
            for k in range(count)
        ]
        + [line, line],
        out_specs=pl.BlockSpec((block, width), lambda i: (i, 0)),
        compiler_params=params(("arbitrary",)),
        cost_estimate=NOMINAL,
        name="norm",
    )(*arrays, gain, shift)


def join_kernel(half, core_ref, own_ref, other_ref, x_ref, w_ref, b_ref, g_ref, s_ref, *outs):
    att_ref, mid_ref, out_ref = outs
    own, other = own_ref[:, :half], other_ref[:, :half]

    @pl.when(core_ref[0] == 0)
    def _():
        att_ref[...] = jnp.concatenate([own, other], axis=1)

    @pl.when(core_ref[0] != 0)
    def _():
        att_ref[...] = jnp.concatenate([other, own], axis=1)

    middle = x_ref[...].astype(F32) + dot(att_ref[...], w_ref[...]) + b_ref[...]
    mid_ref[...] = middle
    hat, _ = normalized(middle)
    out_ref[...] = (hat * g_ref[...] + s_ref[...]).astype(BF16)


def join(core, own, other, inputs, weight, bias, gain, shift, half):
    rows, width = inputs.shape
    padded = own.shape[1]
    block = row_block(rows)
    line = pl.BlockSpec((1, width), lambda i, c: (0, 0))
    wide = pl.BlockSpec((block, width), lambda i, c: (i, 0))
    part = pl.BlockSpec((block, padded), lambda i, c: (i, 0))
    return pl.pallas_call(
        functools.partial(join_kernel, half),
        out_shape=(
            jax.ShapeDtypeStruct((rows, width), BF16),
            jax.ShapeDtypeStruct((rows, width), F32),
            jax.ShapeDtypeStruct((rows, width), BF16),
        ),
        grid_spec=pltpu.PrefetchScalarGridSpec(
            num_scalar_prefetch=1,
            grid=(rows // block,),
            in_specs=[
                part,
                part,
                wide,
                pl.BlockSpec((width, width), lambda i, c: (0, 0), pipeline_mode=pl.Buffered(1)),
                line,
                line,
                line,
            ],
            out_specs=(wide, wide, wide),
        ),
        compiler_params=params(("arbitrary",)),
        cost_estimate=NOMINAL,
        name="join",
    )(core, own, other, inputs, weight, bias, gain, shift)


def norm_back_values(x_ref, grads, gain_ref, add_ref, lines_ref):
    hat, inverse = normalized(x_ref[...].astype(F32))
    grad = grads[0][...].astype(F32)
    for other in grads[1:]:
        grad += other[...].astype(F32)
    scaled = grad * gain_ref[...]
    first = jnp.mean(scaled, axis=-1, keepdims=True)
    second = jnp.mean(scaled * hat, axis=-1, keepdims=True)

    @pl.when(pl.program_id(0) == 0)
    def _():
        lines_ref[...] = jnp.zeros_like(lines_ref)

    lines_ref[0:1] += jnp.sum(grad * hat, axis=0, keepdims=True)
    lines_ref[1:2] += jnp.sum(grad, axis=0, keepdims=True)
    return add_ref[...].astype(F32) + inverse * (scaled - first - hat * second)


def first_back(core, values, grads, gain, add, q_sums, kv_sums, half):
    rows, width = values.shape
    padded = q_sums.shape[1]
    pieces = [grad for grad in grads if isinstance(grad, tuple)]
    whole_grads = [grad for grad in grads if not isinstance(grad, tuple)]
    block = min([row_block(rows)] + [row_block(part.shape[0]) for pair in pieces for part in pair])
    count = len(whole_grads) + 2 * len(pieces)
    flat_grads = whole_grads + [part for pair in pieces for part in pair]

    def kernel(core_ref, x_ref, *refs):
        gain_ref, add_ref, q_ref, kv_ref, dx_ref, lines_ref = refs[count:]
        sums = list(refs[: len(whole_grads)])
        for k, pair in enumerate(pieces):
            low, high = refs[len(whole_grads) + 2 * k : len(whole_grads) + 2 * k + 2]
            first = pl.program_id(0) < pair[0].shape[0] // block
            sums.append(jnp.where(first, low[...].astype(F32), high[...].astype(F32)))
        dx_ref[...] = norm_back_values(x_ref, sums, gain_ref, add_ref, lines_ref)
        for line, part in ((2, q_ref[0:1, :half]), (3, kv_ref[0:1, padded : padded + half])):
            none = jnp.zeros_like(part)

            @pl.when(core_ref[0] == 0)
            def _():
                lines_ref[line : line + 1] = jnp.concatenate([part, none], axis=1)

            @pl.when(core_ref[0] != 0)
            def _():
                lines_ref[line : line + 1] = jnp.concatenate([none, part], axis=1)

    def piece_specs(pair):
        steps = pair[0].shape[0] // block
        return [
            pl.BlockSpec((block, width), lambda i, c: (jnp.minimum(i, steps - 1), 0)),
            pl.BlockSpec((block, width), lambda i, c: (jnp.maximum(i - steps, 0), 0)),
        ]

    wide = pl.BlockSpec((block, width), lambda i, c: (i, 0))
    return pl.pallas_call(
        kernel,
        out_shape=(
            jax.ShapeDtypeStruct((rows, width), F32),
            jax.ShapeDtypeStruct((8, width), F32),
        ),
        grid_spec=pltpu.PrefetchScalarGridSpec(
            num_scalar_prefetch=1,
            grid=(rows // block,),
            in_specs=[wide] * (1 + len(whole_grads))
            + [spec for pair in pieces for spec in piece_specs(pair)]
            + [
                pl.BlockSpec((1, width), lambda i, c: (0, 0)),
                wide,
                pl.BlockSpec(q_sums.shape, lambda i, c: (0, 0)),
                pl.BlockSpec(kv_sums.shape, lambda i, c: (0, 0)),
            ],
            out_specs=(wide, pl.BlockSpec((8, width), lambda i, c: (0, 0))),
        ),
        compiler_params=params(("arbitrary",)),
        cost_estimate=NOMINAL,
        name="first_back",
    )(core, values, *flat_grads, gain, add, q_sums, kv_sums)


def second_back(core, values, grads, gain, add, weight, hidden_line, half, padded):
    rows, width = values.shape
    block = row_block(rows)
    count = len(grads)

    def kernel(core_ref, x_ref, *refs):
        gain_ref, add_ref, w_ref, hid_ref, dx_ref, low_ref, mine_ref, send_ref, lines_ref = refs[count:]
        total = norm_back_values(x_ref, refs[:count], gain_ref, add_ref, lines_ref)
        low = total.astype(BF16)
        dx_ref[...] = total
        low_ref[...] = low
        lines_ref[2:3] += jnp.sum(low.astype(F32), axis=0, keepdims=True)
        lines_ref[3:4] += jnp.sum(add_ref[...].astype(F32), axis=0, keepdims=True)
        spare = hid_ref.shape[1] - width
        for core in range(2):

            @pl.when(core_ref[0] == core)
            def _():
                lines_ref[4 + 2 * core : 5 + 2 * core] = hid_ref[:, :width]
                lines_ref[5 + 2 * core : 6 + 2 * core, :spare] = hid_ref[:, width:]

        back = dot(low, w_ref[...], NT).astype(BF16)
        empty = jnp.zeros((block, padded - half), BF16)
        halves = [jnp.concatenate([back[:, i * half : (i + 1) * half], empty], axis=1) for i in range(2)]

        @pl.when(core_ref[0] == 0)
        def _():
            mine_ref[...], send_ref[...] = halves[0], halves[1]

        @pl.when(core_ref[0] != 0)
        def _():
            mine_ref[...], send_ref[...] = halves[1], halves[0]

    wide = pl.BlockSpec((block, width), lambda i, c: (i, 0))
    part = pl.BlockSpec((block, padded), lambda i, c: (i, 0))
    line = pl.BlockSpec((1, width), lambda i, c: (0, 0))
    square = pl.BlockSpec((width, width), lambda i, c: (0, 0), pipeline_mode=pl.Buffered(1))
    return pl.pallas_call(
        kernel,
        out_shape=(
            jax.ShapeDtypeStruct((rows, width), F32),
            jax.ShapeDtypeStruct((rows, width), BF16),
            jax.ShapeDtypeStruct((rows, padded), BF16),
            jax.ShapeDtypeStruct((rows, padded), BF16),
            jax.ShapeDtypeStruct((8, width), F32),
        ),
        grid_spec=pltpu.PrefetchScalarGridSpec(
            num_scalar_prefetch=1,
            grid=(rows // block,),
            in_specs=[wide] * (1 + count)
            + [line, wide, square, pl.BlockSpec(hidden_line.shape, lambda i, c: (0, 0))],
            out_specs=(wide, wide, part, part, pl.BlockSpec((8, width), lambda i, c: (0, 0))),
        ),
        compiler_params=params(("arbitrary",)),
        cost_estimate=NOMINAL,
        name="second_back",
    )(core, values, *grads, gain, add, weight, hidden_line)


def rows_matmul(name, lefts, weights, finish, extras, outs, dims=((1,), (0,)), split=False, first_row=0):
    rows = outs[0].shape[0]
    block = row_block(rows)
    steps = rows // block
    half = steps // 2
    count, terms = len(lefts), len(lefts) + len(weights)

    def kernel(*refs):
        total = dot(refs[0][...], refs[count][...], dims)
        for i in range(1, count):
            total += dot(refs[i][...], refs[count + i][...], dims)
        results = finish(total, *refs[terms : terms + len(extras)])
        targets = refs[terms + len(extras) :]
        if split:

            @pl.when(pl.program_id(0) < half)
            def _():
                targets[0][...] = results[0]

            @pl.when(pl.program_id(0) >= half)
            def _():
                targets[1][...] = results[0]

            targets = targets[1:]
        else:
            targets[0][...] = results[0]
        for target, result in zip(targets[1:], results[1:]):

            @pl.when(pl.program_id(0) == 0)
            def _():
                target[...] = jnp.zeros_like(target)

            target[...] += result

    def by_rows(array):
        return pl.BlockSpec((block, array.shape[1]), lambda i: (i, 0))

    def whole(array):
        return pl.BlockSpec(array.shape, lambda i: (0, 0), pipeline_mode=pl.Buffered(1))

    first = outs[0]
    if split:
        part = jax.ShapeDtypeStruct((rows // 2, first.shape[1]), first.dtype)
        shapes = [part, part] + list(outs[1:])
        specs = [
            pl.BlockSpec((block, first.shape[1]), lambda i: (jnp.minimum(i, half - 1), 0)),
            pl.BlockSpec((block, first.shape[1]), lambda i: (jnp.maximum(i - half, 0), 0)),
        ]
    else:
        shapes, specs = list(outs), [by_rows(first)]
    specs += [pl.BlockSpec(out.shape, lambda i: (0, 0)) for out in outs[1:]]
    return pl.pallas_call(
        kernel,
        out_shape=shapes,
        grid=(steps,),
        in_specs=[
            pl.BlockSpec((block, a.shape[1]), lambda i: (i + first_row // block, 0)) for a in lefts
        ]
        + [whole(w) for w in weights]
        + [by_rows(e) if e.shape[0] == rows else whole(e) for e in extras],
        out_specs=specs,
        compiler_params=params(("arbitrary",)),
        cost_estimate=NOMINAL,
        name=name,
    )(*lefts, *weights, *extras)


def like(rows, cols, kind=BF16):
    return jax.ShapeDtypeStruct((rows, cols), kind)


def plain(total):
    return (total.astype(BF16),)


def with_bias(total, bias_ref):
    return ((total + bias_ref[...]).astype(BF16),)


def with_slope(total, slope_ref):
    low = (total * slope_ref[...].astype(F32)).astype(BF16)
    return low, jnp.sum(low.astype(F32), axis=0, keepdims=True)


def layer_end(total, middle_ref, other_ref, bias_ref):
    return ((middle_ref[...] + total + other_ref[...].astype(F32) + bias_ref[...]).astype(BF16),)


def small_call(kernel, outs, scalars, arrays, name):
    vmem = pl.BlockSpec(memory_space=pltpu.VMEM)
    return pl.pallas_call(
        kernel,
        out_shape=outs,
        in_specs=[pl.BlockSpec(memory_space=pltpu.SMEM)] * len(scalars) + [vmem] * len(arrays),
        out_specs=[vmem] * len(outs),
        compiler_params=pltpu.CompilerParams(vmem_limit_bytes=VMEM),
        cost_estimate=NOMINAL,
        name=name,
    )(*scalars, *arrays)


def add_rows(left, right, kind=BF16, pieces=1):
    size = left.shape[0] // pieces
    parts = [slice(i * size, (i + 1) * size) for i in range(pieces)]
    return [(left[part].astype(F32) + right[part].astype(F32)).astype(kind) for part in parts]


def scatter_step(keep, arrived, rows):
    if keep.shape[0] == rows:
        return add_rows(keep, arrived)[0], None
    return add_rows(keep, arrived, BF16, 2)


def both_cores(core, mine, other, size, total, start=0, turn=False):
    rows = mine.shape[0]

    def kernel(core_ref, mine_ref, other_ref, out_ref):
        for at, refs in ((0, (mine_ref, other_ref)), (1, (other_ref, mine_ref))):

            @pl.when(core_ref[0] == at)
            def _():
                first = refs[0][:, start : start + size]
                second = refs[1][:, start : start + total - size]
                if turn:
                    out_ref[:size], out_ref[size:] = first.T, second.T
                else:
                    out_ref[...] = jnp.concatenate([first, second], axis=1)

    shape = like(total, rows, mine.dtype) if turn else like(rows, total, mine.dtype)
    return small_call(kernel, [shape], [core], [mine, other], "both_cores")[0]


def both_columns(is_first, mine, other, size, total, start=0):
    mine, other = mine[:, start:], other[:, start:]
    return jnp.where(
        is_first,
        jnp.concatenate([mine[:, :size], other[:, : total - size]], axis=1),
        jnp.concatenate([other[:, :size], mine[:, : total - size]], axis=1),
    )


def core_columns(core, arrays, cols):
    rows, width = arrays[0].shape

    def kernel(core_ref, *refs):
        for at in range(2):

            @pl.when(core_ref[0] == at)
            def _():
                for i in range(len(arrays)):
                    for k, where in enumerate((at, 1 - at)):
                        low = where * (width - cols)
                        refs[len(arrays) * (1 + k) + i][...] = refs[i][:, low : low + cols]

    return small_call(kernel, [like(rows, cols)] * (2 * len(arrays)), [core], arrays, "core_columns")


def mask_kernel(rows, tokens, blocks, len_ref, place_ref, need_ref, row_ref, col_ref, near_row, near_col):
    place = place_ref[0]
    for row in range(rows):
        ends = [len_ref[row, 0]]
        for p in range(1, len_ref.shape[1]):
            ends.append(ends[-1] + len_ref[row, p])

        def pictures(position):
            return sum((position >= end).astype(jnp.int32) for end in ends)

        def segment(position):
            return jnp.where(position < ends[-1], pictures(position), 1000 + position)

        spans = []
        for block in range(blocks):
            start = jnp.bitwise_xor(place, block) * tokens
            across = segment(start + lax.broadcasted_iota(jnp.int32, (1, tokens), 1))
            down = segment(start + lax.broadcasted_iota(jnp.int32, (tokens, 1), 0))
            row_ref[row, block : block + 1] = across
            col_ref[row, block] = down
            if block < 2:
                near_row[row, :, block * tokens : (block + 1) * tokens] = across
                near_col[row, block * tokens : (block + 1) * tokens] = down
            last = jnp.minimum(start + tokens, ends[-1]) - 1
            low = sum(jnp.where(start >= end, 1, 0) for end in ends)
            high = sum(jnp.where(last >= end, 1, 0) for end in ends)
            spans.append((start < ends[-1], low, high))
        for block, (real, low, high) in enumerate(spans):
            if block < 2:
                need_ref[row, block] = 1
            else:
                need_ref[row, block] = sum(
                    jnp.where(real & ok & (low <= top) & (bottom <= high), 1, 0) for ok, bottom, top in spans[:2]
                )


def masks(lengths, place, blocks, tokens):
    rows = lengths.shape[0]
    shapes = [(rows, blocks, tokens), (rows, blocks, tokens, 1), (rows, 1, 2 * tokens), (rows, 2 * tokens, 1)]
    smem = pl.BlockSpec(memory_space=pltpu.SMEM)
    return pl.pallas_call(
        functools.partial(mask_kernel, rows, tokens, blocks),
        out_shape=[jax.ShapeDtypeStruct((rows, blocks), jnp.int32)]
        + [jax.ShapeDtypeStruct(shape, jnp.int32) for shape in shapes],
        in_specs=[smem, smem],
        out_specs=[smem] + [pl.BlockSpec(memory_space=pltpu.VMEM)] * 4,
        compiler_params=pltpu.CompilerParams(vmem_limit_bytes=VMEM),
        cost_estimate=NOMINAL,
        name="masks",
    )(lengths, place)


def lay_vectors(core, weight, lines, half, padded):
    width, cols = weight.shape
    low = half // 128 * 128

    def kernel(core_ref, weight_ref, lines_ref, q_ref, kv_ref):
        turned = weight_ref[...].astype(F32).T
        lines_ref[...] = turned[half - low : half - low + lines]
        q_ref[...] = jnp.zeros_like(q_ref)
        kv_ref[...] = jnp.zeros_like(kv_ref)
        for at in range(2):

            @pl.when(core_ref[0] == at)
            def _():
                q_ref[:, :half] = lines_ref[2:3, at * half : (at + 1) * half]
                kv_ref[:, padded : padded + half] = lines_ref[3:4, at * half : (at + 1) * half]

    outs = [like(lines, width, F32), like(1, padded, F32), like(1, 2 * padded, F32)]
    block = cols - low
    return pl.pallas_call(
        kernel,
        out_shape=outs,
        grid=(1,),
        in_specs=[
            pl.BlockSpec(memory_space=pltpu.SMEM),
            pl.BlockSpec((width, block), lambda i: (0, low // block)),
        ],
        out_specs=[pl.BlockSpec(out.shape, lambda i: (0, 0)) for out in outs],
        compiler_params=params(("arbitrary",)),
        cost_estimate=NOMINAL,
        name="lay_vectors",
    )(core, weight)


def mlp_shards(core, out_shard, hidden_weight, down_weight, cols):
    rows, total = hidden_weight.shape
    before = out_shard.shape[1]

    def kernel(core_ref, part_ref, hidden_ref, down_ref, first_out, down_out):
        first_out[:, :before] = part_ref[...]
        for at in range(2):

            @pl.when(core_ref[0] == at)
            def _():
                low = at * cols
                high = min(low + cols, total)
                size = high - low
                first_out[:, before : before + size] = hidden_ref[:, low:high]
                down_out[:, :size] = down_ref[low:high].T
                if size < cols:
                    empty = jnp.zeros((rows, cols - size), BF16)
                    first_out[:, before + size :] = empty
                    down_out[:, size:] = empty

    outs = [like(rows, before + cols), like(rows, cols)]
    return small_call(kernel, outs, [core], [out_shard, hidden_weight, down_weight], "mlp_shards")


def attention_shards(core, weights, vectors, half, padded):
    rows, width = weights[0].shape
    cut = width - padded
    count = len(vectors)

    def kernel(core_ref, q_ref, k_ref, v_ref, o_ref, *refs):
        qkv_ref, out_ref, held = refs[count:]
        for i in range(count):
            held[i : i + 1] = refs[i][...].astype(F32).reshape(1, rows)
        empty = jnp.zeros((rows, padded - half), BF16)
        spare = jnp.zeros((rows, padded - half - count), BF16)
        lines = jnp.concatenate([held[...].T.astype(BF16), spare], axis=1)
        for at in range(2):

            @pl.when(core_ref[0] == at)
            def _():
                for i, ref in enumerate((q_ref, k_ref, v_ref)):
                    part = ref[:, at * half : (at + 1) * half]
                    rest = empty if i else lines
                    qkv_ref[:, i * padded : (i + 1) * padded] = jnp.concatenate([part, rest], axis=1)
                out_ref[...] = o_ref[:, at * cut : at * cut + padded]

    vmem = pl.BlockSpec(memory_space=pltpu.VMEM)
    return pl.pallas_call(
        kernel,
        out_shape=[like(rows, 3 * padded), like(rows, padded)],
        in_specs=[pl.BlockSpec(memory_space=pltpu.SMEM)] + [vmem] * (4 + count),
        out_specs=[vmem] * 2,
        scratch_shapes=[pltpu.VMEM((count, rows), F32)],
        compiler_params=pltpu.CompilerParams(vmem_limit_bytes=VMEM),
        cost_estimate=NOMINAL,
        name="attention_shards",
    )(core, *weights, *vectors)


def hidden(arrays, weight, bias):
    rows, width = arrays[0].shape
    cols = weight.shape[1]
    block = row_block(rows)
    steps, count = rows // block, len(arrays)

    def kernel(*refs):
        w_ref, b_ref, act_ref, slope_ref, x_ref = refs[count:]
        for i in range(count):

            @pl.when(pl.program_id(0) // steps == i)
            def _():
                x_ref[...] = refs[i][...]

        pre = dot(x_ref[...], w_ref[...]) + b_ref[...]
        square = pre * pre
        turn = jnp.tanh(pre * (GELU_COEF + GELU_COEF * 0.044715 * square))
        act_ref[...] = (0.5 * pre * (1.0 + turn)).astype(BF16)
        inner = GELU_COEF + 3.0 * 0.044715 * GELU_COEF * square
        slope_ref[...] = (0.5 * (1.0 + turn) * (1.0 + pre * (1.0 - turn) * inner)).astype(BF16)

    out = pl.BlockSpec((block, cols), lambda i: (i, 0))
    return pl.pallas_call(
        kernel,
        out_shape=(
            jax.ShapeDtypeStruct((count * rows, cols), BF16),
            jax.ShapeDtypeStruct((count * rows, cols), BF16),
            jax.ShapeDtypeStruct((count * rows, width), BF16),
        ),
        grid=(count * steps,),
        in_specs=[
            pl.BlockSpec((block, width), lambda i, k=k: (jnp.clip(i - k * steps, 0, steps - 1), 0))
            for k in range(count)
        ]
        + [
            pl.BlockSpec((width, cols), lambda i: (0, 0), pipeline_mode=pl.Buffered(1)),
            pl.BlockSpec((1, cols), lambda i: (0, 0)),
        ],
        out_specs=(out, out, pl.BlockSpec((block, width), lambda i: (i, 0))),
        compiler_params=params(("arbitrary",)),
        cost_estimate=NOMINAL,
        name="hidden",
    )(*arrays, weight, bias)


def head_window(head):
    first = head * HEAD_DIM
    start = first // 128 * 128
    return start, round_up(first + HEAD_DIM, 128) - start, first - start


def head_lanes(rows, width, low):
    lane = lax.broadcasted_iota(jnp.int32, (rows, width), 1)
    return (lane >= low) & (lane < low + HEAD_DIM)


def only_head(block, low):
    mine = head_lanes(*block.shape, low)
    return jnp.where(mine, block.astype(F32), 0.0).astype(BF16)


def pick_block(near_ref, far_ref, block):
    return near_ref.at[block, 0] if block < 2 else far_ref.at[block - 2, 0]


def attend_kernel(row, heads, blocks, padded, need_ref, col_ref, row_ref, q_ref, near_ref, far_ref, *refs):
    own_ref, pair_ref, lse_ref, queries, score, peak, total, acc, lses = refs[-9:]
    outs = (own_ref, pair_ref)
    tokens = own_ref.shape[1]
    slot = lax.broadcasted_iota(jnp.int32, (2 * tokens, 128), 1)
    for which in range(2):
        outs[which][...] = jnp.zeros_like(outs[which])
    windows = [head_window(head) for head in range(heads)]
    for head, (start, width, low) in enumerate(windows):
        for which in range(2):
            queries[head, which * tokens : (which + 1) * tokens, :width] = only_head(
                q_ref[which, 0, :, start : start + width], low
            )
    peak[...] = jnp.full_like(peak, MASKED)
    total[...] = jnp.zeros_like(total)
    acc[...] = jnp.zeros_like(acc)
    for block in range(blocks):

        @pl.when(need_ref[row, block] != 0)
        def _():
            side = pick_block(near_ref, far_ref, block)
            seen = col_ref[0] == row_ref[0, block : block + 1]
            for head, (start, width, _) in enumerate(windows):
                key = side[:, start : start + width]
                found = jnp.where(seen, dot(queries[head, :, :width], key, NT), MASKED)
                score[head, block] = found
                top = peak[head]
                for at in range(0, tokens, 128):
                    top = jnp.maximum(top, found[:, at : at + 128])
                peak[head] = top

    for head in range(heads):
        top = jnp.max(peak[head], axis=-1, keepdims=True) * (SCALE * LOG2E)
        peak[head] = jnp.broadcast_to(top, peak.shape[1:])

    for block in range(blocks):

        @pl.when(need_ref[row, block] != 0)
        def _():
            side = pick_block(near_ref, far_ref, block)
            for head, (start, width, _) in enumerate(windows):
                top, share = peak[head], total[head]
                pieces = []
                for at in range(0, tokens, 128):
                    part = jnp.exp2(score[head, block, :, at : at + 128] * (SCALE * LOG2E) - top)
                    share += part
                    pieces.append(part.astype(BF16))
                total[head] = share
                value = side[:, padded + start : padded + start + width]
                acc[head, :, :width] += dot(jnp.concatenate(pieces, axis=1), value)

    for head, (start, width, low) in enumerate(windows):
        norm = jnp.sum(total[head], axis=-1, keepdims=True)
        result = acc[head, :, :width] / norm
        mine = head_lanes(tokens, width, low)
        for which in range(2):
            kept = outs[which][0, :, start : start + width].astype(F32)
            fresh = result[which * tokens : (which + 1) * tokens]
            outs[which][0, :, start : start + width] = jnp.where(mine, fresh, kept).astype(BF16)
        lse = peak[head] + jnp.log2(norm)
        lses[...] = lse if head == 0 else jnp.where(slot == head, lse, lses[...])
    lse_ref[0] = lses[...].T[:heads]


def attend(row, query, near, far, need, seg_col, seg_row, heads, before):
    _, rows, tokens, padded = query.shape
    blocks = 2 + far.shape[0]
    narrow = pl.BlockSpec((1, tokens, padded), lambda i, need: (row, 0, 0))
    lines = pl.BlockSpec((1, heads, 2 * tokens), lambda i, need: (row, 0, 0))

    def stack(count, width):
        return pl.BlockSpec((count, 1, tokens, width), lambda i, need: (0, row, 0, 0))

    return pl.pallas_call(
        functools.partial(attend_kernel, row, heads, blocks, padded),
        out_shape=(
            jax.ShapeDtypeStruct((rows, tokens, padded), BF16),
            jax.ShapeDtypeStruct((rows, tokens, padded), BF16),
            jax.ShapeDtypeStruct((rows, heads, 2 * tokens), F32),
        ),
        grid_spec=pltpu.PrefetchScalarGridSpec(
            num_scalar_prefetch=1,
            grid=(1,),
            in_specs=[
                pl.BlockSpec((1, 2 * tokens, 1), lambda i, need: (row, 0, 0)),
                pl.BlockSpec((1, blocks, tokens), lambda i, need: (row, 0, 0)),
                stack(2, padded),
                stack(2, 2 * padded),
                stack(blocks - 2, 2 * padded),
            ]
            + [pl.BlockSpec(memory_space=pl.ANY)] * len(before),
            out_specs=(narrow, narrow, lines),
            scratch_shapes=[
                pltpu.VMEM((heads, 2 * tokens, WIN), BF16),
                pltpu.VMEM((heads, blocks, 2 * tokens, tokens), F32),
                pltpu.VMEM((heads, 2 * tokens, 128), F32),
                pltpu.VMEM((heads, 2 * tokens, 128), F32),
                pltpu.VMEM((heads, 2 * tokens, WIN), F32),
                pltpu.VMEM((2 * tokens, 128), F32),
            ],
        ),
        input_output_aliases={6 + i: i for i in range(len(before))},
        compiler_params=params(("arbitrary",)),
        cost_estimate=NOMINAL,
        name="attend",
    )(need, seg_col, seg_row, query, near, far, *before)


def attend_back_kernel(
    row, heads, blocks, padded, need_ref, col_ref, row_ref, pick_ref, q_ref, near_ref, far_ref, *refs
):
    grads, outs, lse_ref = refs[0:2], refs[2:4], refs[4]
    dq_ref, dnear_ref, dfar_ref, sums, inner_turn, queries, incoming, dq = refs[-8:]
    tokens = grads[0].shape[1]
    sums[...] = jnp.zeros_like(sums)
    for which in range(2):
        dq_ref[which, 0] = jnp.zeros((tokens, padded), BF16)
        product = grads[which][0].astype(F32) * outs[which][0].astype(F32)
        high = product.astype(BF16)
        rest = (product - high.astype(F32)).astype(BF16)
        inner_turn[:, which * tokens : (which + 1) * tokens] = dot(pick_ref[...], high, NT) + dot(
            pick_ref[...], rest, NT
        )
    windows = [head_window(head) for head in range(heads)]
    for head, (start, width, low) in enumerate(windows):
        for which in range(2):
            there = slice(which * tokens, (which + 1) * tokens)
            here = slice(start, start + width)
            queries[head, there, :width] = only_head(q_ref[which, 0, :, here], low)
            incoming[head, there, :width] = only_head(grads[which][0, :, here], low)
    dq[...] = jnp.zeros_like(dq)
    for block in range(blocks):

        @pl.when(need_ref[row, block] != 0)
        def _():
            side = pick_block(near_ref, far_ref, block)
            seen = col_ref[0, block] == row_ref[0]
            for head, (start, width, _) in enumerate(windows):
                end = start + width
                key, value = side[:, start:end], side[:, padded + start : padded + end]
                query, grad = queries[head, :, :width], incoming[head, :, :width]
                found = dot(key, query, NT) * (SCALE * LOG2E) - lse_ref[0, head : head + 1, :]
                prob = jnp.where(seen, jnp.exp2(found), 0.0)
                inner = inner_turn[head : head + 1, :]
                slope = (prob * (dot(value, grad, NT) - inner)).astype(BF16)
                sums[block, :, start:end] += dot(slope, query)
                sums[block, :, padded + start : padded + end] += dot(prob.astype(BF16), grad)
                dq[head, :, :width] += dot(slope, key, TN)

    for head, (start, width, low) in enumerate(windows):
        mine = head_lanes(tokens, width, low)
        for which in range(2):
            kept = dq_ref[which, 0, :, start : start + width].astype(F32)
            fresh = dq[head, which * tokens : (which + 1) * tokens, :width] * SCALE
            dq_ref[which, 0, :, start : start + width] = jnp.where(mine, fresh, kept).astype(BF16)
    for block in range(blocks):
        side = pick_block(dnear_ref, dfar_ref, block)
        side[:, :padded] = (sums[block, :, :padded] * SCALE).astype(BF16)
        side[:, padded:] = sums[block, :, padded:].astype(BF16)


def attend_back(row, query, near, far, grads, outs, lse, need, seg_col, seg_row, heads, before):
    _, rows, tokens, padded = query.shape
    blocks = 2 + far.shape[0]
    column = lax.broadcasted_iota(jnp.int32, (heads, padded), 1)
    pick = (column // HEAD_DIM == lax.broadcasted_iota(jnp.int32, (heads, padded), 0)).astype(BF16)
    narrow = pl.BlockSpec((1, tokens, padded), lambda i, need: (row, 0, 0))

    def stack(count, width):
        return pl.BlockSpec((count, 1, tokens, width), lambda i, need: (0, row, 0, 0))

    return pl.pallas_call(
        functools.partial(attend_back_kernel, row, heads, blocks, padded),
        out_shape=tuple(jax.ShapeDtypeStruct(a.shape, BF16) for a in (query, near, far)),
        grid_spec=pltpu.PrefetchScalarGridSpec(
            num_scalar_prefetch=1,
            grid=(1,),
            in_specs=[
                pl.BlockSpec((1, blocks, tokens, 1), lambda i, need: (row, 0, 0, 0)),
                pl.BlockSpec((1, 1, 2 * tokens), lambda i, need: (row, 0, 0)),
                pl.BlockSpec((heads, padded), lambda i, need: (0, 0)),
                stack(2, padded),
                stack(2, 2 * padded),
                stack(blocks - 2, 2 * padded),
            ]
            + [narrow] * 4
            + [pl.BlockSpec((1, heads, 2 * tokens), lambda i, need: (row, 0, 0))]
            + [pl.BlockSpec(memory_space=pl.ANY)] * len(before),
            out_specs=(stack(2, padded), stack(2, 2 * padded), stack(blocks - 2, 2 * padded)),
            scratch_shapes=[
                pltpu.VMEM((blocks, tokens, 2 * padded), F32),
                pltpu.VMEM((heads, 2 * tokens), F32),
                pltpu.VMEM((heads, 2 * tokens, WIN), BF16),
                pltpu.VMEM((heads, 2 * tokens, WIN), BF16),
                pltpu.VMEM((heads, 2 * tokens, WIN), F32),
            ],
        ),
        input_output_aliases={12 + i: i for i in range(len(before))},
        compiler_params=params(("arbitrary",)),
        cost_estimate=NOMINAL,
        name="attend_back",
    )(need, seg_col, seg_row, pick, query, near, far, *grads, *outs, lse, *before)


def local(
    patches,
    lengths,
    first_gain,
    first_shift,
    query_weight,
    query_bias,
    key_weight,
    value_weight,
    value_bias,
    output_weight,
    output_bias,
    second_gain,
    second_shift,
    hidden_weight,
    hidden_bias,
    down_weight,
    down_bias,
    cotangent,
):
    seq_count, shards = lax.axis_size("seq"), lax.axis_size("fsdp")
    place, me = lax.axis_index("seq"), lax.axis_index("fsdp")
    core = place & 1
    is_first = core == 0
    core_flag = core[None].astype(jnp.int32)
    rows, tokens, width = patches.shape
    flat = rows * tokens
    heads = width // HEAD_DIM // 2
    half = heads * HEAD_DIM
    padded = round_up(half, 128)
    ff = hidden_bias.shape[0]
    ff_half = round_up(ff, 256) // 2
    out_cols = padded
    out_cut = width - padded
    shard_rows = width // shards
    chain = Chain()

    def my_half(array, size, padded_size):
        first, second = array[..., :size], array[..., size:]
        grow = [(0, 0)] * (array.ndim - 1)
        first = jnp.pad(first, grow + [(0, padded_size - size)])
        second = jnp.pad(second, grow + [(0, padded_size - second.shape[-1])])
        return jnp.where(is_first, first, second)

    flights = Flights(chain)
    staged = shards == 8 and seq_count == 4
    y, z, zz = 1, 2, 4
    top = bits_of(seq_count)[0]

    inputs = patches.reshape(flat, width)
    incoming = cotangent.reshape(flat, width)
    vectors = [
        first_gain,
        first_shift,
        query_bias,
        value_bias,
        output_bias,
        second_gain,
        second_shift,
        down_bias,
    ]
    shard_qkv, shard_out = chain.done(
        *attention_shards(
            core_flag, [query_weight, key_weight, value_weight, output_weight], vectors, half, padded
        )
    )
    place_flag = place[None].astype(jnp.int32)

    def over(box_from, bits):
        return flights.send(box_from[0], "fsdp", bits)

    if staged:
        q = {0: [shard_qkv]}
        q[y] = over(q[0], y)
        q[z], q[zz] = over(q[0], z), over(q[0], zz)
        shard_ho, shard_down = chain.done(
            *mlp_shards(core_flag, shard_out, hidden_weight, down_weight, ff_half)
        )
        h, d = {0: [shard_ho]}, {0: [shard_down]}
        need, seg_rows, seg_cols, seg_near_row, seg_near_col = chain.done(
            *masks(chain(lengths), place_flag, seq_count, tokens)
        )
        core_flag, raw_own = flights.land(core_flag, inputs)
        q[zz | z], q[z | y], q[zz | y] = over(q[zz], z), over(q[z], y), over(q[zz], y)
        far_raw = [flights.send(raw_own, "seq", 2)]
        raw_pair = flights.send(raw_own, "seq", 1)
        core_flag = flights.land(core_flag, only=[q[zz | z]])
        q[zz | z | y] = over(q[zz | z], y)
        core_flag, shard_ho = flights.land(core_flag, shard_ho, only=[q[z | y], q[zz | y], raw_pair])
        h[0] = [shard_ho]
        h[z], h[y] = over(h[0], z), over(h[0], y)
        core_flag, shard_ho, shard_down = flights.land(
            core_flag, shard_ho, shard_down, only=[q[zz | z | y], far_raw[0]]
        )
        h[0], d[0] = [shard_ho], [shard_down]
        far_pair = [flights.send(far_raw[0][0], "seq", 1)]
        h[zz], d[y] = over(h[0], zz), over(d[0], y)
        w_q, w_kv = chain.done(*assemble({k: box[0] for k, box in q.items()}, me, padded))
        stacked, bias_q, bias_kv = chain.done(
            *lay_vectors(chain(core_flag), w_q, len(vectors), half, padded)
        )
        gain_one, shift_one = stacked[0:1], stacked[1:2]
        gain_one = chain(gain_one)
        normed_near = chain.done(norm([inputs, raw_pair[0]], gain_one, shift_one))
        bias_hidden = my_half(after(hidden_bias, gain_one).astype(F32)[None], ff_half, ff_half)
        gain_one = flights.land(gain_one, only=[h[z], far_pair[0]])
        h[z | y] = over(h[z], y)
        incoming_pair = flights.send(incoming, "seq", 1)
    else:
        parts = gather_all(shard_qkv)
        shard_ho, shard_down = mlp_shards(core_flag, shard_out, hidden_weight, down_weight, ff_half)
        raw = {0: inputs}
        for bit in bits_of(seq_count):
            raw.update({j | bit: swap(part, "seq", bit) for j, part in list(raw.items())})
        need, seg_rows, seg_cols, seg_near_row, seg_near_col = masks(lengths, place_flag, seq_count, tokens)
        w_q, w_kv = chain.done(*assemble(parts, me, padded))
        stacked, bias_q, bias_kv = lay_vectors(core_flag, w_q, len(vectors), half, padded)
        gain_one, shift_one = stacked[0:1], stacked[1:2]
        normed_near = norm([raw[0], raw[1]], gain_one, shift_one)
        far_raw, far_pair = [[raw[j]] for j in range(2, seq_count)], []
        incoming_pair = [swap(incoming, "seq", 1)]
        bias_hidden = my_half(hidden_bias.astype(F32)[None], ff_half, ff_half)
    _, _, bias_query, bias_value, bias_output, gain_two, shift_two, bias_down = [
        stacked[i : i + 1] for i in range(8)
    ]

    near_in, w_q, w_kv = chain(normed_near, w_q, w_kv)
    (query,) = rows_matmul("query", [near_in], [w_q], with_bias, [bias_q], [like(2 * flat, padded)])
    near_in = after(near_in, query)
    (near,) = rows_matmul("near", [near_in], [w_kv], with_bias, [bias_kv], [like(2 * flat, 2 * padded)])
    chain.done(query, near)
    gain_one, w_kv = chain(gain_one, w_kv)
    normed_far = chain.done(norm([box[0] for box in far_raw + far_pair], gain_one, shift_one))
    if staged:
        w_kv, incoming = flights.land(w_kv, incoming)
        h[zz | y], h[zz | z] = over(h[zz], y), over(h[zz], z)
    far_in, w_kv = chain(normed_far, w_kv)
    (far,) = rows_matmul(
        "far", [far_in], [w_kv], with_bias, [bias_kv], [like(normed_far.shape[0], 2 * padded)]
    )
    chain.done(far)
    query = query.reshape(2, rows, tokens, padded)
    near = near.reshape(2, rows, tokens, 2 * padded)
    far = far.reshape(seq_count - 2, rows, tokens, 2 * padded)
    found = ()
    for row in range(rows):
        query, near, far = chain(query, near, far)
        if staged and row == 1:
            query = flights.land(query)
            h[zz | z | y] = over(h[zz | z], y)
            d[z], d[zz] = over(d[0], z), over(d[0], zz)
        found = chain.done(*attend(row, query, near, far, need, seg_near_col, seg_rows, heads, found))
    out_own, out_pair, lse = found
    if staged:
        out_own, out_pair = flights.land(out_own, out_pair)
        h_parts = {k: box[0] for k, box in h.items()}
    else:
        out_own, out_pair = flights.land(out_own, out_pair)
        h_parts = gather_all(chain(shard_ho))
    w_out_mine, w_hidden = chain.done(*assemble(h_parts, me, out_cols))
    out_pair, w_out_mine = chain(out_pair, w_out_mine)
    other_half = flights.send(out_pair, "seq", 1)
    w_out_other = flights.send(w_out_mine, "seq", 1)
    if staged:
        d[zz | z], d[z | y] = over(d[zz], z), over(d[z], y)
    w_out_mine, w_hidden = flights.land(w_out_mine, w_hidden, only=[other_half, w_out_other])
    w_out = chain.done(both_cores(core_flag, w_out_mine, w_out_other[0], out_cut, width))
    w_out, incoming_pair[0] = chain(w_out, incoming_pair[0])
    incoming_near = chain.done(jnp.concatenate([incoming, incoming_pair[0]], axis=0))
    if staged:
        w_out = flights.land(w_out, only=[d[zz | z], d[z | y]])
        d[zz | y], d[zz | z | y] = over(d[zz], y), over(d[zz | z], y)
    own_half, w_out = chain(out_own.reshape(flat, padded), w_out)
    attended, middle, second = chain.done(
        *join(
            core_flag,
            own_half,
            other_half[0].reshape(flat, padded),
            inputs,
            w_out,
            bias_output,
            gain_two,
            shift_two,
            half,
        )
    )
    second_pair = flights.send(second, "seq", 1)
    second, w_hidden = flights.land(second, w_hidden, only=[second_pair])
    act, slope, second_near = chain.done(*hidden([second, second_pair[0]], w_hidden, bias_hidden))

    incoming_near, act = chain(incoming_near, act)
    grad_down = chain.done(token_dot(incoming_near, act))
    if staged:
        slope, grad_down = flights.land(slope, grad_down)
        d_parts = {k: box[0] for k, box in d.items()}
    else:
        d_parts = gather_all(chain(shard_down))
    part_down = lax.psum_scatter(grad_down, "fsdp", scatter_dimension=0, tiled=True)
    w_down = chain.done(assemble(d_parts, me))
    incoming_near, slope, w_down = chain(incoming_near, slope, w_down)
    grad_pre, hidden_line = chain.done(
        *rows_matmul(
            "grad_pre",
            [incoming_near],
            [w_down],
            with_slope,
            [slope],
            [like(2 * flat, ff_half), like(1, ff_half, F32)],
        )
    )
    grad_pre = chain(grad_pre)
    back, back_pair = chain.done(
        *rows_matmul("back", [grad_pre], [w_hidden], plain, [], [like(2 * flat, width)], NT, True)
    )
    back_other = flights.send(back_pair, "seq", 1)
    second_near, grad_pre = chain(second_near, grad_pre)
    grad_hidden = chain.done(dot(second_near, grad_pre, TN).astype(BF16))
    part_hidden = lax.psum_scatter(grad_hidden, "fsdp", scatter_dimension=0, tiled=True)
    back = flights.land(back)
    grad_middle, branch, grad_mine, grad_send, lines = second_back(
        core_flag, middle, [back, back_other[0]], gain_two, incoming, w_out, hidden_line, half, padded
    )
    chain.done(branch, grad_send)
    grad_pair = flights.send(grad_send, "seq", 1)
    attended, branch = chain(attended, branch)
    partial_out = chain(chain.done(token_dot(attended, branch)))
    out_mine, out_other = chain.done(*core_columns(core_flag, [partial_out], out_cols))
    query = flights.land(query)

    links = {"x": ("seq", top), "core": ("seq", 1)} | {bit: ("fsdp", bit) for bit in bits_of(shards)}
    out_back = flights.send(out_other, "seq", 1)
    shape = (rows, tokens, padded)
    grads = [grad_mine.reshape(shape), grad_pair[0].reshape(shape)]
    found = ()
    far_bits = [2 << k for k in range(shards.bit_length() - 2)]
    def next_step(keep, box, bits):
        keep, send = scatter_step(keep, box[0], shard_rows)
        chain.done(keep)
        return keep, flights.send(send, "fsdp", bits.pop(0)) if bits else None

    def seq_rest(mine, arrived):
        for bit in bits_of(seq_count)[1:-1]:
            (mine,) = add_rows(mine, arrived)
            arrived = swap(mine, "seq", bit)
        return chain.done(*add_rows(mine, arrived, F32))

    for row in range(rows):
        query, near, far, *grads = chain(query, near, far, *grads)
        found = attend_back(
            row, query, near, far, grads, [out_own, out_pair], lse, need, seg_cols, seg_near_row, heads, found
        )
        chain.done(*found)
        query = flights.land(query)
        if row == 0:
            out_sum = chain.done(*add_rows(out_mine, out_back[0]))
            part_out = lax.psum_scatter(out_sum, "fsdp", scatter_dimension=0, tiled=True)
        if row == 1:
            part_down = chain(part_down)
            down_seq = flights.send(part_down, "seq", top)
    dq, dnear, dfar = [g.reshape(-1, g.shape[-1]) for g in found]
    dfar, w_kv, down_seq[0] = chain(dfar, w_kv, down_seq[0])
    two = seq_count == 4
    back_far = rows_matmul("back_far", [dfar], [w_kv], plain, [], [like(dfar.shape[0], width)], NT, two)
    chain.done(*back_far)
    dnear = chain(dnear)
    if two:
        far_parts = {2 + i: part for i, part in enumerate(back_far)}
    else:
        far_parts = {j: back_far[0][(j - 2) * flat : (j - 1) * flat] for j in range(2, seq_count)}
    far_sent = {j: flights.send(part, "seq", 1) for j, part in far_parts.items() if j & 1}
    normed_near, dnear, dfar = chain(normed_near, dnear, dfar)
    kv_keep, kv_send, kv_sums = chain.done(
        *weight_grad([normed_near, normed_far], [dnear, dfar], me, shards)
    )
    dq = flights.land(dq)
    kv_box = flights.send(kv_send, "fsdp", y)
    far_sums = {j: add_rows(far_parts[j], far_sent[j | 1][0])[0] for j in far_parts if not j & 1}
    chain.done(*far_sums.values())
    arrived = []
    for bit in bits_of(seq_count)[:-1]:
        for j in [j for j in far_sums if j & bit]:
            part = far_sums.pop(j)
            if j == bit:
                arrived.append(flights.send(part, "seq", bit))
            else:
                (far_sums[j ^ bit],) = add_rows(far_sums[j ^ bit], swap(part, "seq", bit))
    dq, dnear = chain(dq, dnear)
    back_own, back_pair = chain.done(
        *rows_matmul("back_near", [dq, dnear], [w_q, w_kv], plain, [], [like(2 * flat, width)], NT, True)
    )
    pair_back = flights.send(back_pair, "seq", 1)
    act, middle = chain(act, middle)
    (down_pair,) = rows_matmul(
        "down_pair", [act], [w_down], plain, [], [like(flat, width)], NT, first_row=flat
    )
    chain.done(down_pair)
    down_back = flights.send(down_pair, "seq", 1)
    normed_near, dq = chain(normed_near, dq)
    q_keep, q_send, q_sums = chain.done(*weight_grad([normed_near], [dq], me, shards))
    q_box = flights.send(q_send, "fsdp", y)
    kv_bits, q_bits = list(far_bits), list(far_bits)
    act, late_in = flights.land(act, inputs, only=[kv_box] + arrived)
    kv_keep, kv_box = next_step(kv_keep, kv_box, kv_bits)
    late_in = flights.land(late_in, only=[pair_back])
    grad_patches, late = chain.done(
        *first_back(
            core_flag,
            late_in,
            [back_own, pair_back[0]] + [box[0] for box in arrived],
            gain_one,
            grad_middle,
            q_sums,
            kv_sums,
            half,
        )
    )
    small = jnp.concatenate([lines, late], axis=0)
    small_todo = [zz, y, z] if staged else bits_of(shards)
    small_todo = [("fsdp", bit) for bit in small_todo] + [("seq", bit) for bit in reversed(bits_of(seq_count))]

    def small_send():
        return flights.send(small, *small_todo.pop(0)) if small_todo else None

    def small_step(small, box):
        return chain.done(*add_rows(small, box[0], F32))

    act, middle = flights.land(act, middle, only=[q_box, down_back])
    q_keep, q_box = next_step(q_keep, q_box, q_bits)
    act, middle = chain(act, middle)
    (layer_output,) = rows_matmul(
        "down_own", [act], [w_down], layer_end, [middle, down_back[0], bias_down], [like(flat, width)], NT
    )
    layer_output = chain.done(layer_output).reshape(rows, tokens, width)
    boxes = [box for box in (kv_box, q_box) if box is not None]
    flights.land(only=boxes)
    if kv_box is not None:
        kv_keep, kv_box = next_step(kv_keep, kv_box, kv_bits)
    if q_box is not None:
        q_keep, q_box = next_step(q_keep, q_box, q_bits)
    small, part_hidden = chain(small, part_hidden)
    hidden_seq = flights.send(part_hidden, "seq", top)
    small_box = small_send()
    while kv_box is not None:
        flights.land(only=[kv_box])
        kv_keep, kv_box = next_step(kv_keep, kv_box, kv_bits)
    kv_seq = flights.send(kv_keep, "seq", top)
    flights.land(only=[hidden_seq, small_box])
    small = small_step(small, small_box)
    small_box = small_send()
    hidden_total = seq_rest(part_hidden, hidden_seq[0])
    hidden_other = flights.send(hidden_total, "seq", 1)
    part_out = chain(part_out)
    out_seq = flights.send(part_out, "seq", top)
    while q_box is not None:
        flights.land(only=[q_box])
        q_keep, q_box = next_step(q_keep, q_box, q_bits)
    q_seq = flights.send(q_keep, "seq", top)
    flights.land(only=[small_box, kv_seq])
    small = small_step(small, small_box)
    small_box = small_send()
    kv_total = seq_rest(kv_keep, kv_seq[0])
    kv_other = flights.send(kv_total, "seq", 1)
    down_total = seq_rest(part_down, down_seq[0])
    flights.land(only=[out_seq, hidden_other, small_box])
    small = small_step(small, small_box)
    small_box = small_send()
    out_total = seq_rest(part_out, out_seq[0])
    out_other = flights.send(out_total, "seq", 1)
    down_other = flights.send(down_total, "seq", 1)
    flights.land(only=[q_seq, small_box])
    q_total = seq_rest(q_keep, q_seq[0])
    q_other = flights.send(q_total, "seq", 1)
    while small_box is not None:
        small = small_step(small, small_box)
        small_box = small_send()
        if small_box is not None:
            flights.land(only=[small_box])
    flights.land()

    own_lines = lax.dynamic_slice_in_dim(small[:8], me * shard_rows, shard_rows, 1)
    late_lines = lax.dynamic_slice_in_dim(small[8:], me * shard_rows, shard_rows, 1)
    cuts = [width, ff_half - width, width, ff - ff_half - width]
    full_bias = jnp.concatenate([small[4 + i, :size] for i, size in enumerate(cuts)])
    full_down = both_columns(is_first, down_total, down_other[0], ff_half, ff).T
    full_hidden = both_columns(is_first, hidden_total, hidden_other[0], ff_half, ff)
    full_out = both_columns(is_first, out_total, out_other[0], out_cut, width)
    full_query = both_columns(is_first, q_total, q_other[0], half, width)
    full_key = both_columns(is_first, kv_total, kv_other[0], half, width)
    full_value = both_columns(is_first, kv_total, kv_other[0], half, width, padded)
    return (
        layer_output,
        grad_patches.reshape(rows, tokens, width),
        late_lines[0],
        late_lines[1],
        full_query,
        late_lines[2],
        full_key,
        full_value,
        late_lines[3],
        full_out,
        own_lines[2],
        own_lines[0],
        own_lines[1],
        full_hidden,
        full_bias,
        full_down,
        own_lines[3],
    )


def solution(mesh):
    shard, line, tokens = P("fsdp", None), P("fsdp"), P("fsdp", "seq", None)
    in_specs = (
        tokens,
        shard,
        line,
        line,
        shard,
        line,
        shard,
        shard,
        line,
        shard,
        line,
        line,
        line,
        shard,
        P(),
        P(None, "fsdp"),
        line,
        tokens,
    )
    out_specs = (
        tokens,
        tokens,
        line,
        line,
        shard,
        line,
        shard,
        shard,
        line,
        shard,
        line,
        line,
        line,
        shard,
        P(),
        P(None, "fsdp"),
        line,
    )
    return jax.shard_map(local, mesh=mesh, in_specs=in_specs, out_specs=out_specs, check_vma=False)
```

```python
import functools
import math

import jax
import jax.numpy as jnp
from jax import lax
from jax.experimental import pallas as pl
from jax.experimental.pallas import tpu as pltpu
from jax.sharding import PartitionSpec as P

HEAD_DIM = 72
EPS = 1e-06
GELU_COEF = math.sqrt(2.0 / math.pi)
MASKED = -1e30
F32 = jnp.float32
BF16 = jnp.bfloat16
SCALE = 1.0 / math.sqrt(HEAD_DIM)
WIN = 256
LOG2E = math.log2(math.e)
VMEM = 60 << 20
NOMINAL = pl.CostEstimate(flops=1, transcendentals=0, bytes_accessed=1)


def round_up(value, step):
    return (value + step - 1) // step * step


def dot(left, right, dims=((1,), (0,))):
    return lax.dot_general(left, right, (dims, ((), ())), preferred_element_type=F32)


NT = ((1,), (1,))
TN = ((0,), (0,))


def params(semantics):
    return pltpu.CompilerParams(dimension_semantics=semantics, vmem_limit_bytes=VMEM)


def swap(array, axis, bits):
    size = lax.axis_size(axis)
    return lax.ppermute(array, axis, [(i, i ^ bits) for i in range(size)])


def bits_of(size):
    return [1 << k for k in reversed(range(size.bit_length() - 1))]


def after(value, *earlier):
    return lax.optimization_barrier((value,) + tuple(earlier))[0]


class Chain:
    def __init__(self):
        self.last = ()

    def __call__(self, *values, wait=()):
        held = lax.optimization_barrier(tuple(values) + tuple(self.last) + tuple(wait))
        return held[: len(values)] if len(values) > 1 else held[0]

    def done(self, *results):
        self.last = results
        return results if len(results) > 1 else results[0]


class Flights:
    def __init__(self, chain):
        self.chain, self.open = chain, []

    def send(self, array, axis, bits):
        self.open.append([swap(array, axis, bits)])
        return self.open[-1]

    def land(self, *values, through=None, only=None):
        if only is None:
            count = len(self.open)
            if through is not None:
                count = sum(i + 1 for i, box in enumerate(self.open) if box is through)
            only = self.open[:count]
        ready = [box for box in self.open if any(box is other for other in only)]
        self.open = [box for box in self.open if not any(box is other for other in ready)]
        held = self.chain(*[box[0] for box in ready], *values)
        held = held if isinstance(held, (tuple, list)) else [held]
        for box, array in zip(ready, held):
            box[0] = array
        rest = list(held[len(ready) :])
        return rest if len(rest) > 1 else rest[0] if rest else None


def in_order(parts, me):
    count = len(parts)
    return jnp.take(jnp.stack([parts[d] for d in range(count)]), me ^ jnp.arange(count), axis=0)


def gather_all(shard):
    parts = {0: shard}
    for bit in bits_of(lax.axis_size("fsdp")):
        parts.update({d | bit: swap(part, "fsdp", bit) for d, part in list(parts.items())})
    return parts


def rel_position(distance, count):
    width = count.bit_length() - 1
    return sum(((distance >> k) & 1) << (width - 1 - k) for k in range(width))


def assemble_kernel(count, rows, single, off_ref, *refs):
    outs = refs[count:]

    def fill(out_ref):
        for distance in range(count):
            start = pl.multiple_of(off_ref[distance], 16)
            out_ref[pl.ds(start, rows), :] = refs[distance][...]

    if single:
        fill(outs[0])
    else:
        pl.when(pl.program_id(0) == 0)(lambda: fill(outs[0]))
        pl.when(pl.program_id(0) > 0)(lambda: fill(outs[1]))


def assemble(parts, me, cut=None):
    count = len(parts)
    rows, cols = parts[0].shape
    if rows % 16:
        full = in_order(parts, me).reshape(count * rows, cols)
        return (full[:, :cut], full[:, cut:]) if cut else full
    offsets = ((me ^ jnp.arange(count, dtype=jnp.int32)) * rows).astype(jnp.int32)
    tile = cut or min(cols, 1152)
    widths = [cut, cols - cut] if cut else [cols]
    maps = [lambda n, off: (0, 0), lambda n, off: (0, jnp.maximum(n - 1, 0))]
    if not cut:
        maps = [lambda n, off: (0, n)]
    outs = pl.pallas_call(
        functools.partial(assemble_kernel, count, rows, not cut),
        out_shape=[jax.ShapeDtypeStruct((count * rows, w), parts[0].dtype) for w in widths],
        grid_spec=pltpu.PrefetchScalarGridSpec(
            num_scalar_prefetch=1,
            grid=(pl.cdiv(cols, tile),),
            in_specs=[pl.BlockSpec((rows, tile), lambda n, off: (0, n))] * count,
            out_specs=[pl.BlockSpec((count * rows, tile), m) for m in maps],
        ),
        compiler_params=params(("arbitrary",)),
        cost_estimate=NOMINAL,
        name="assemble",
    )(offsets, *[parts[d] for d in range(count)])
    return outs if cut else outs[0]


def weight_grad_kernel(pairs, count, rows, pos_ref, *refs):
    lefts, rights = refs[:pairs], refs[pairs : 2 * pairs]
    keep_ref, send_ref, sum_ref = refs[2 * pairs :]
    total = dot(lefts[0][...], rights[0][...], TN)
    for i in range(1, pairs):
        total += dot(lefts[i][...], rights[i][...], TN)
    sum_ref[...] = sum(dot(jnp.ones((8, r.shape[0]), BF16), r[...]) for r in rights)
    for shard in range(count):
        start = pl.multiple_of(pos_ref[shard], 16)
        block = total[shard * rows : (shard + 1) * rows].astype(BF16)

        @pl.when(pos_ref[count] == shard % 2)
        def _():
            keep_ref[pl.ds(start, rows), :] = block

        @pl.when(pos_ref[count] != shard % 2)
        def _():
            send_ref[pl.ds(start, rows), :] = block


def weight_grad(lefts, rights, me, count):
    width = lefts[0].shape[1]
    cols = rights[0].shape[1]
    rows = width // count
    order = me ^ jnp.arange(count, dtype=jnp.int32)
    table = jnp.array([rel_position(d, count) for d in range(count)], jnp.int32)
    half = count // 2
    if rows % 16:
        total = sum(dot(a, b, TN) for a, b in zip(lefts, rights))
        by_distance = jnp.take(total.astype(BF16).reshape(count, rows, cols), order, axis=0)
        back = [0] * count
        for d in range(count):
            back[rel_position(d, count)] = d
        placed = jnp.take(by_distance, jnp.array(back), axis=0).reshape(width, cols)
        ones = [jnp.ones((8, b.shape[0]), BF16) for b in rights]
        sums = sum(dot(one, b) for one, b in zip(ones, rights))
        return placed[: width // 2], placed[width // 2 :], sums
    positions = jnp.concatenate([table[order] % half * rows, (me & 1)[None]]).astype(jnp.int32)
    tile = 256
    pairs = len(lefts)
    return pl.pallas_call(
        functools.partial(weight_grad_kernel, pairs, count, rows),
        out_shape=[jax.ShapeDtypeStruct((width // 2, cols), BF16)] * 2
        + [jax.ShapeDtypeStruct((8, cols), F32)],
        grid_spec=pltpu.PrefetchScalarGridSpec(
            num_scalar_prefetch=1,
            grid=(pl.cdiv(cols, tile),),
            in_specs=[
                pl.BlockSpec(a.shape, lambda n, off: (0, 0), pipeline_mode=pl.Buffered(1))
                for a in lefts
            ]
            + [pl.BlockSpec((b.shape[0], tile), lambda n, off: (0, n)) for b in rights],
            out_specs=[pl.BlockSpec((width // 2, tile), lambda n, off: (0, n))] * 2
            + [pl.BlockSpec((8, tile), lambda n, off: (0, n))],
        ),
        compiler_params=params(("arbitrary",)),
        cost_estimate=NOMINAL,
        name="weight_grad",
    )(positions, *lefts, *rights)


def token_dot(left, right):
    tokens, width = left.shape
    cols = right.shape[1]
    tile = 256

    def kernel(left_ref, right_ref, out_ref):
        out_ref[...] = dot(left_ref[...], right_ref[...], TN).astype(BF16)

    return pl.pallas_call(
        kernel,
        out_shape=jax.ShapeDtypeStruct((width, cols), BF16),
        grid=(pl.cdiv(cols, tile),),
        in_specs=[
            pl.BlockSpec((tokens, width), lambda n: (0, 0), pipeline_mode=pl.Buffered(1)),
            pl.BlockSpec((tokens, tile), lambda n: (0, n)),
        ],
        out_specs=pl.BlockSpec((width, tile), lambda n: (0, n)),
        compiler_params=params(("arbitrary",)),
        cost_estimate=NOMINAL,
        name="token_dot",
    )(left, right)


def normalized(values):
    center = values - jnp.mean(values, axis=-1, keepdims=True)
    spread = jnp.mean(center * center, axis=-1, keepdims=True)
    inverse = lax.rsqrt(spread + EPS)
    return center * inverse, inverse


def row_block(rows):
    return 256 if rows % 256 == 0 else 128 if rows % 128 == 0 else rows


def norm(arrays, gain, shift):
    width = arrays[0].shape[1]
    block = min(row_block(a.shape[0]) for a in arrays)
    steps = [a.shape[0] // block for a in arrays]
    firsts = [sum(steps[:k]) for k in range(len(steps))]
    count, total = len(arrays), sum(steps)

    def kernel(*refs):
        gain_ref, shift_ref, out_ref = refs[count:]
        at = pl.program_id(0)
        for k in range(count):

            @pl.when((at >= firsts[k]) & (at < firsts[k] + steps[k]))
            def _():
                hat, _ = normalized(refs[k][...].astype(F32))
                out_ref[...] = (hat * gain_ref[...] + shift_ref[...]).astype(BF16)

    line = pl.BlockSpec((1, width), lambda i: (0, 0))
    return pl.pallas_call(
        kernel,
        out_shape=jax.ShapeDtypeStruct((total * block, width), BF16),
        grid=(total,),
        in_specs=[
            pl.BlockSpec((block, width), lambda i, k=k: (jnp.clip(i - firsts[k], 0, steps[k] - 1), 0))
            for k in range(count)
        ]
        + [line, line],
        out_specs=pl.BlockSpec((block, width), lambda i: (i, 0)),
        compiler_params=params(("arbitrary",)),
        cost_estimate=NOMINAL,
        name="norm",
    )(*arrays, gain, shift)


def join_kernel(half, core_ref, own_ref, other_ref, x_ref, w_ref, b_ref, g_ref, s_ref, *outs):
    att_ref, mid_ref, out_ref = outs
    own, other = own_ref[:, :half], other_ref[:, :half]

    @pl.when(core_ref[0] == 0)
    def _():
        att_ref[...] = jnp.concatenate([own, other], axis=1)

    @pl.when(core_ref[0] != 0)
    def _():
        att_ref[...] = jnp.concatenate([other, own], axis=1)

    middle = x_ref[...].astype(F32) + dot(att_ref[...], w_ref[...]) + b_ref[...]
    mid_ref[...] = middle
    hat, _ = normalized(middle)
    out_ref[...] = (hat * g_ref[...] + s_ref[...]).astype(BF16)


def join(core, own, other, inputs, weight, bias, gain, shift, half):
    rows, width = inputs.shape
    padded = own.shape[1]
    block = row_block(rows)
    line = pl.BlockSpec((1, width), lambda i, c: (0, 0))
    wide = pl.BlockSpec((block, width), lambda i, c: (i, 0))
    part = pl.BlockSpec((block, padded), lambda i, c: (i, 0))
    return pl.pallas_call(
        functools.partial(join_kernel, half),
        out_shape=(
            jax.ShapeDtypeStruct((rows, width), BF16),
            jax.ShapeDtypeStruct((rows, width), F32),
            jax.ShapeDtypeStruct((rows, width), BF16),
        ),
        grid_spec=pltpu.PrefetchScalarGridSpec(
            num_scalar_prefetch=1,
            grid=(rows // block,),
            in_specs=[
                part,
                part,
                wide,
                pl.BlockSpec((width, width), lambda i, c: (0, 0), pipeline_mode=pl.Buffered(1)),
                line,
                line,
                line,
            ],
            out_specs=(wide, wide, wide),
        ),
        compiler_params=params(("arbitrary",)),
        cost_estimate=NOMINAL,
        name="join",
    )(core, own, other, inputs, weight, bias, gain, shift)


def norm_back_values(x_ref, grads, gain_ref, add_ref, lines_ref):
    hat, inverse = normalized(x_ref[...].astype(F32))
    grad = grads[0][...].astype(F32)
    for other in grads[1:]:
        grad += other[...].astype(F32)
    scaled = grad * gain_ref[...]
    first = jnp.mean(scaled, axis=-1, keepdims=True)
    second = jnp.mean(scaled * hat, axis=-1, keepdims=True)

    @pl.when(pl.program_id(0) == 0)
    def _():
        lines_ref[...] = jnp.zeros_like(lines_ref)

    lines_ref[0:1] += jnp.sum(grad * hat, axis=0, keepdims=True)
    lines_ref[1:2] += jnp.sum(grad, axis=0, keepdims=True)
    return add_ref[...].astype(F32) + inverse * (scaled - first - hat * second)


def first_back(core, values, grads, gain, add, q_sums, kv_sums, half):
    rows, width = values.shape
    padded = q_sums.shape[1]
    pieces = [grad for grad in grads if isinstance(grad, tuple)]
    whole_grads = [grad for grad in grads if not isinstance(grad, tuple)]
    block = min([row_block(rows)] + [row_block(part.shape[0]) for pair in pieces for part in pair])
    count = len(whole_grads) + 2 * len(pieces)
    flat_grads = whole_grads + [part for pair in pieces for part in pair]

    def kernel(core_ref, x_ref, *refs):
        gain_ref, add_ref, q_ref, kv_ref, dx_ref, lines_ref = refs[count:]
        sums = list(refs[: len(whole_grads)])
        for k, pair in enumerate(pieces):
            low, high = refs[len(whole_grads) + 2 * k : len(whole_grads) + 2 * k + 2]
            first = pl.program_id(0) < pair[0].shape[0] // block
            sums.append(jnp.where(first, low[...].astype(F32), high[...].astype(F32)))
        dx_ref[...] = norm_back_values(x_ref, sums, gain_ref, add_ref, lines_ref)
        for line, part in ((2, q_ref[0:1, :half]), (3, kv_ref[0:1, padded : padded + half])):
            none = jnp.zeros_like(part)

            @pl.when(core_ref[0] == 0)
            def _():
                lines_ref[line : line + 1] = jnp.concatenate([part, none], axis=1)

            @pl.when(core_ref[0] != 0)
            def _():
                lines_ref[line : line + 1] = jnp.concatenate([none, part], axis=1)

    def piece_specs(pair):
        steps = pair[0].shape[0] // block
        return [
            pl.BlockSpec((block, width), lambda i, c: (jnp.minimum(i, steps - 1), 0)),
            pl.BlockSpec((block, width), lambda i, c: (jnp.maximum(i - steps, 0), 0)),
        ]

    wide = pl.BlockSpec((block, width), lambda i, c: (i, 0))
    return pl.pallas_call(
        kernel,
        out_shape=(
            jax.ShapeDtypeStruct((rows, width), F32),
            jax.ShapeDtypeStruct((8, width), F32),
        ),
        grid_spec=pltpu.PrefetchScalarGridSpec(
            num_scalar_prefetch=1,
            grid=(rows // block,),
            in_specs=[wide] * (1 + len(whole_grads))
            + [spec for pair in pieces for spec in piece_specs(pair)]
            + [
                pl.BlockSpec((1, width), lambda i, c: (0, 0)),
                wide,
                pl.BlockSpec(q_sums.shape, lambda i, c: (0, 0)),
                pl.BlockSpec(kv_sums.shape, lambda i, c: (0, 0)),
            ],
            out_specs=(wide, pl.BlockSpec((8, width), lambda i, c: (0, 0))),
        ),
        compiler_params=params(("arbitrary",)),
        cost_estimate=NOMINAL,
        name="first_back",
    )(core, values, *flat_grads, gain, add, q_sums, kv_sums)


def second_back(core, values, grads, gain, add, weight, hidden_line, half, padded):
    rows, width = values.shape
    block = row_block(rows)
    count = len(grads)

    def kernel(core_ref, x_ref, *refs):
        gain_ref, add_ref, w_ref, hid_ref, dx_ref, low_ref, mine_ref, send_ref, lines_ref = refs[count:]
        total = norm_back_values(x_ref, refs[:count], gain_ref, add_ref, lines_ref)
        low = total.astype(BF16)
        dx_ref[...] = total
        low_ref[...] = low
        lines_ref[2:3] += jnp.sum(low.astype(F32), axis=0, keepdims=True)
        lines_ref[3:4] += jnp.sum(add_ref[...].astype(F32), axis=0, keepdims=True)
        spare = hid_ref.shape[1] - width
        for core in range(2):

            @pl.when(core_ref[0] == core)
            def _():
                lines_ref[4 + 2 * core : 5 + 2 * core] = hid_ref[:, :width]
                lines_ref[5 + 2 * core : 6 + 2 * core, :spare] = hid_ref[:, width:]

        back = dot(low, w_ref[...], NT).astype(BF16)
        empty = jnp.zeros((block, padded - half), BF16)
        halves = [jnp.concatenate([back[:, i * half : (i + 1) * half], empty], axis=1) for i in range(2)]

        @pl.when(core_ref[0] == 0)
        def _():
            mine_ref[...], send_ref[...] = halves[0], halves[1]

        @pl.when(core_ref[0] != 0)
        def _():
            mine_ref[...], send_ref[...] = halves[1], halves[0]

    wide = pl.BlockSpec((block, width), lambda i, c: (i, 0))
    part = pl.BlockSpec((block, padded), lambda i, c: (i, 0))
    line = pl.BlockSpec((1, width), lambda i, c: (0, 0))
    square = pl.BlockSpec((width, width), lambda i, c: (0, 0), pipeline_mode=pl.Buffered(1))
    return pl.pallas_call(
        kernel,
        out_shape=(
            jax.ShapeDtypeStruct((rows, width), F32),
            jax.ShapeDtypeStruct((rows, width), BF16),
            jax.ShapeDtypeStruct((rows, padded), BF16),
            jax.ShapeDtypeStruct((rows, padded), BF16),
            jax.ShapeDtypeStruct((8, width), F32),
        ),
        grid_spec=pltpu.PrefetchScalarGridSpec(
            num_scalar_prefetch=1,
            grid=(rows // block,),
            in_specs=[wide] * (1 + count)
            + [line, wide, square, pl.BlockSpec(hidden_line.shape, lambda i, c: (0, 0))],
            out_specs=(wide, wide, part, part, pl.BlockSpec((8, width), lambda i, c: (0, 0))),
        ),
        compiler_params=params(("arbitrary",)),
        cost_estimate=NOMINAL,
        name="second_back",
    )(core, values, *grads, gain, add, weight, hidden_line)


def rows_matmul(name, lefts, weights, finish, extras, outs, dims=((1,), (0,)), split=False, first_row=0):
    rows = outs[0].shape[0]
    block = 384 if split and rows % 768 == 0 else 512 if not split and rows % 512 == 0 else row_block(rows)
    steps = rows // block
    half = steps // 2
    count, terms = len(lefts), len(lefts) + len(weights)

    def kernel(*refs):
        total = dot(refs[0][...], refs[count][...], dims)
        for i in range(1, count):
            total += dot(refs[i][...], refs[count + i][...], dims)
        results = finish(total, *refs[terms : terms + len(extras)])
        targets = refs[terms + len(extras) :]
        if split:

            @pl.when(pl.program_id(0) < half)
            def _():
                targets[0][...] = results[0]

            @pl.when(pl.program_id(0) >= half)
            def _():
                targets[1][...] = results[0]

            targets = targets[1:]
        else:
            targets[0][...] = results[0]
        for target, result in zip(targets[1:], results[1:]):

            @pl.when(pl.program_id(0) == 0)
            def _():
                target[...] = jnp.zeros_like(target)

            target[...] += result

    def by_rows(array):
        return pl.BlockSpec((block, array.shape[1]), lambda i: (i, 0))

    def whole(array):
        return pl.BlockSpec(array.shape, lambda i: (0, 0), pipeline_mode=pl.Buffered(1))

    first = outs[0]
    if split:
        part = jax.ShapeDtypeStruct((rows // 2, first.shape[1]), first.dtype)
        shapes = [part, part] + list(outs[1:])
        specs = [
            pl.BlockSpec((block, first.shape[1]), lambda i: (jnp.minimum(i, half - 1), 0)),
            pl.BlockSpec((block, first.shape[1]), lambda i: (jnp.maximum(i - half, 0), 0)),
        ]
    else:
        shapes, specs = list(outs), [by_rows(first)]
    specs += [pl.BlockSpec(out.shape, lambda i: (0, 0)) for out in outs[1:]]
    return pl.pallas_call(
        kernel,
        out_shape=shapes,
        grid=(steps,),
        in_specs=[
            pl.BlockSpec((block, a.shape[1]), lambda i: (i + first_row // block, 0)) for a in lefts
        ]
        + [whole(w) for w in weights]
        + [by_rows(e) if e.shape[0] == rows else whole(e) for e in extras],
        out_specs=specs,
        compiler_params=params(("arbitrary",)),
        cost_estimate=NOMINAL,
        name=name,
    )(*lefts, *weights, *extras)


def like(rows, cols, kind=BF16):
    return jax.ShapeDtypeStruct((rows, cols), kind)


def plain(total):
    return (total.astype(BF16),)


def with_bias(total, bias_ref):
    return ((total + bias_ref[...]).astype(BF16),)


def with_slope(total, slope_ref):
    low = (total * slope_ref[...].astype(F32)).astype(BF16)
    return low, jnp.sum(low.astype(F32), axis=0, keepdims=True)


def layer_end(total, middle_ref, other_ref, bias_ref):
    return ((middle_ref[...] + total + other_ref[...].astype(F32) + bias_ref[...]).astype(BF16),)


def small_call(kernel, outs, scalars, arrays, name):
    vmem = pl.BlockSpec(memory_space=pltpu.VMEM)
    return pl.pallas_call(
        kernel,
        out_shape=outs,
        in_specs=[pl.BlockSpec(memory_space=pltpu.SMEM)] * len(scalars) + [vmem] * len(arrays),
        out_specs=[vmem] * len(outs),
        compiler_params=pltpu.CompilerParams(vmem_limit_bytes=VMEM),
        cost_estimate=NOMINAL,
        name=name,
    )(*scalars, *arrays)


def add_rows(left, right, kind=BF16, pieces=1):
    size = left.shape[0] // pieces
    parts = [slice(i * size, (i + 1) * size) for i in range(pieces)]
    return [(left[part].astype(F32) + right[part].astype(F32)).astype(kind) for part in parts]


def scatter_step(keep, arrived, rows):
    if keep.shape[0] == rows:
        return add_rows(keep, arrived)[0], None
    return add_rows(keep, arrived, BF16, 2)


def both_cores(core, mine, other, size, total, start=0, turn=False):
    rows = mine.shape[0]

    def kernel(core_ref, mine_ref, other_ref, out_ref):
        for at, refs in ((0, (mine_ref, other_ref)), (1, (other_ref, mine_ref))):

            @pl.when(core_ref[0] == at)
            def _():
                first = refs[0][:, start : start + size]
                second = refs[1][:, start : start + total - size]
                if turn:
                    out_ref[:size], out_ref[size:] = first.T, second.T
                else:
                    out_ref[...] = jnp.concatenate([first, second], axis=1)

    shape = like(total, rows, mine.dtype) if turn else like(rows, total, mine.dtype)
    return small_call(kernel, [shape], [core], [mine, other], "both_cores")[0]


def both_columns(is_first, mine, other, size, total, start=0):
    mine, other = mine[:, start:], other[:, start:]
    return jnp.where(
        is_first,
        jnp.concatenate([mine[:, :size], other[:, : total - size]], axis=1),
        jnp.concatenate([other[:, :size], mine[:, : total - size]], axis=1),
    )


def core_columns(core, arrays, cols):
    rows, width = arrays[0].shape

    def kernel(core_ref, *refs):
        for at in range(2):

            @pl.when(core_ref[0] == at)
            def _():
                for i in range(len(arrays)):
                    for k, where in enumerate((at, 1 - at)):
                        low = where * (width - cols)
                        refs[len(arrays) * (1 + k) + i][...] = refs[i][:, low : low + cols]

    return small_call(kernel, [like(rows, cols)] * (2 * len(arrays)), [core], arrays, "core_columns")


def mask_kernel(rows, tokens, blocks, len_ref, place_ref, need_ref, row_ref, col_ref, near_row, near_col):
    place = place_ref[0]
    for row in range(rows):
        ends = [len_ref[row, 0]]
        for p in range(1, len_ref.shape[1]):
            ends.append(ends[-1] + len_ref[row, p])

        def pictures(position):
            return sum((position >= end).astype(jnp.int32) for end in ends)

        def segment(position):
            return jnp.where(position < ends[-1], pictures(position), 1000 + position)

        spans = []
        for block in range(blocks):
            start = jnp.bitwise_xor(place, block) * tokens
            across = segment(start + lax.broadcasted_iota(jnp.int32, (1, tokens), 1))
            down = segment(start + lax.broadcasted_iota(jnp.int32, (tokens, 1), 0))
            row_ref[row, block : block + 1] = across
            col_ref[row, block] = down
            if block < 2:
                near_row[row, :, block * tokens : (block + 1) * tokens] = across
                near_col[row, block * tokens : (block + 1) * tokens] = down
            last = jnp.minimum(start + tokens, ends[-1]) - 1
            low = sum(jnp.where(start >= end, 1, 0) for end in ends)
            high = sum(jnp.where(last >= end, 1, 0) for end in ends)
            spans.append((start < ends[-1], low, high))
        for block, (real, low, high) in enumerate(spans):
            if block < 2:
                need_ref[row, block] = 1
            else:
                need_ref[row, block] = sum(
                    jnp.where(real & ok & (low <= top) & (bottom <= high), 1, 0) for ok, bottom, top in spans[:2]
                )


def masks(lengths, place, blocks, tokens):
    rows = lengths.shape[0]
    shapes = [(rows, blocks, tokens), (rows, blocks, tokens, 1), (rows, 1, 2 * tokens), (rows, 2 * tokens, 1)]
    smem = pl.BlockSpec(memory_space=pltpu.SMEM)
    return pl.pallas_call(
        functools.partial(mask_kernel, rows, tokens, blocks),
        out_shape=[jax.ShapeDtypeStruct((rows, blocks), jnp.int32)]
        + [jax.ShapeDtypeStruct(shape, jnp.int32) for shape in shapes],
        in_specs=[smem, smem],
        out_specs=[smem] + [pl.BlockSpec(memory_space=pltpu.VMEM)] * 4,
        compiler_params=pltpu.CompilerParams(vmem_limit_bytes=VMEM),
        cost_estimate=NOMINAL,
        name="masks",
    )(lengths, place)


def lay_vectors(core, weight, lines, half, padded):
    width, cols = weight.shape
    low = half // 128 * 128

    def kernel(core_ref, weight_ref, lines_ref, q_ref, kv_ref):
        turned = weight_ref[...].astype(F32).T
        lines_ref[...] = turned[half - low : half - low + lines]
        q_ref[...] = jnp.zeros_like(q_ref)
        kv_ref[...] = jnp.zeros_like(kv_ref)
        for at in range(2):

            @pl.when(core_ref[0] == at)
            def _():
                q_ref[:, :half] = lines_ref[2:3, at * half : (at + 1) * half]
                kv_ref[:, padded : padded + half] = lines_ref[3:4, at * half : (at + 1) * half]

    outs = [like(lines, width, F32), like(1, padded, F32), like(1, 2 * padded, F32)]
    block = cols - low
    return pl.pallas_call(
        kernel,
        out_shape=outs,
        grid=(1,),
        in_specs=[
            pl.BlockSpec(memory_space=pltpu.SMEM),
            pl.BlockSpec((width, block), lambda i: (0, low // block)),
        ],
        out_specs=[pl.BlockSpec(out.shape, lambda i: (0, 0)) for out in outs],
        compiler_params=params(("arbitrary",)),
        cost_estimate=NOMINAL,
        name="lay_vectors",
    )(core, weight)


def mlp_shards(core, out_shard, hidden_weight, down_weight, cols):
    rows, total = hidden_weight.shape
    before = out_shard.shape[1]

    def kernel(core_ref, part_ref, hidden_ref, down_ref, first_out, down_out):
        first_out[:, :before] = part_ref[...]
        for at in range(2):

            @pl.when(core_ref[0] == at)
            def _():
                low = at * cols
                high = min(low + cols, total)
                size = high - low
                first_out[:, before : before + size] = hidden_ref[:, low:high]
                down_out[:, :size] = down_ref[low:high].T
                if size < cols:
                    empty = jnp.zeros((rows, cols - size), BF16)
                    first_out[:, before + size :] = empty
                    down_out[:, size:] = empty

    outs = [like(rows, before + cols), like(rows, cols)]
    return small_call(kernel, outs, [core], [out_shard, hidden_weight, down_weight], "mlp_shards")


def attention_shards(core, weights, vectors, half, padded):
    rows, width = weights[0].shape
    cut = width - padded
    count = len(vectors)

    def kernel(core_ref, q_ref, k_ref, v_ref, o_ref, *refs):
        qkv_ref, out_ref, held = refs[count:]
        for i in range(count):
            held[i : i + 1] = refs[i][...].astype(F32).reshape(1, rows)
        empty = jnp.zeros((rows, padded - half), BF16)
        spare = jnp.zeros((rows, padded - half - count), BF16)
        lines = jnp.concatenate([held[...].T.astype(BF16), spare], axis=1)
        for at in range(2):

            @pl.when(core_ref[0] == at)
            def _():
                for i, ref in enumerate((q_ref, k_ref, v_ref)):
                    part = ref[:, at * half : (at + 1) * half]
                    rest = empty if i else lines
                    qkv_ref[:, i * padded : (i + 1) * padded] = jnp.concatenate([part, rest], axis=1)
                out_ref[...] = o_ref[:, at * cut : at * cut + padded]

    vmem = pl.BlockSpec(memory_space=pltpu.VMEM)
    return pl.pallas_call(
        kernel,
        out_shape=[like(rows, 3 * padded), like(rows, padded)],
        in_specs=[pl.BlockSpec(memory_space=pltpu.SMEM)] + [vmem] * (4 + count),
        out_specs=[vmem] * 2,
        scratch_shapes=[pltpu.VMEM((count, rows), F32)],
        compiler_params=pltpu.CompilerParams(vmem_limit_bytes=VMEM),
        cost_estimate=NOMINAL,
        name="attention_shards",
    )(core, *weights, *vectors)


def hidden(arrays, weight, bias):
    rows, width = arrays[0].shape
    cols = weight.shape[1]
    block = row_block(rows)
    steps, count = rows // block, len(arrays)

    def kernel(*refs):
        w_ref, b_ref, act_ref, slope_ref, x_ref = refs[count:]
        for i in range(count):

            @pl.when(pl.program_id(0) // steps == i)
            def _():
                x_ref[...] = refs[i][...]

        pre = dot(x_ref[...], w_ref[...]) + b_ref[...]
        square = pre * pre
        turn = jnp.tanh(pre * (GELU_COEF + GELU_COEF * 0.044715 * square))
        act_ref[...] = (0.5 * pre * (1.0 + turn)).astype(BF16)
        inner = GELU_COEF + 3.0 * 0.044715 * GELU_COEF * square
        slope_ref[...] = (0.5 * (1.0 + turn) * (1.0 + pre * (1.0 - turn) * inner)).astype(BF16)

    out = pl.BlockSpec((block, cols), lambda i: (i, 0))
    return pl.pallas_call(
        kernel,
        out_shape=(
            jax.ShapeDtypeStruct((count * rows, cols), BF16),
            jax.ShapeDtypeStruct((count * rows, cols), BF16),
            jax.ShapeDtypeStruct((count * rows, width), BF16),
        ),
        grid=(count * steps,),
        in_specs=[
            pl.BlockSpec((block, width), lambda i, k=k: (jnp.clip(i - k * steps, 0, steps - 1), 0))
            for k in range(count)
        ]
        + [
            pl.BlockSpec((width, cols), lambda i: (0, 0), pipeline_mode=pl.Buffered(1)),
            pl.BlockSpec((1, cols), lambda i: (0, 0)),
        ],
        out_specs=(out, out, pl.BlockSpec((block, width), lambda i: (i, 0))),
        compiler_params=params(("arbitrary",)),
        cost_estimate=NOMINAL,
        name="hidden",
    )(*arrays, weight, bias)


def head_window(head):
    first = head * HEAD_DIM
    start = first // 128 * 128
    return start, round_up(first + HEAD_DIM, 128) - start, first - start


def head_lanes(rows, width, low):
    lane = lax.broadcasted_iota(jnp.int32, (rows, width), 1)
    return (lane >= low) & (lane < low + HEAD_DIM)


def only_head(block, low):
    mine = head_lanes(*block.shape, low)
    return jnp.where(mine, block.astype(F32), 0.0).astype(BF16)


def pick_block(near_ref, far_ref, block):
    return near_ref.at[block, 0] if block < 2 else far_ref.at[block - 2, 0]


def attend_kernel(row, heads, blocks, padded, need_ref, col_ref, row_ref, q_ref, near_ref, far_ref, *refs):
    own_ref, pair_ref, lse_ref, queries, score, peak, total, acc, lses = refs[-9:]
    outs = (own_ref, pair_ref)
    tokens = own_ref.shape[1]
    slot = lax.broadcasted_iota(jnp.int32, (2 * tokens, 128), 1)
    for which in range(2):
        outs[which][...] = jnp.zeros_like(outs[which])
    windows = [head_window(head) for head in range(heads)]
    for head, (start, width, low) in enumerate(windows):
        for which in range(2):
            queries[head, which * tokens : (which + 1) * tokens, :width] = only_head(
                q_ref[which, 0, :, start : start + width], low
            )
    peak[...] = jnp.full_like(peak, MASKED)
    total[...] = jnp.zeros_like(total)
    acc[...] = jnp.zeros_like(acc)
    for block in range(blocks):

        @pl.when(need_ref[row, block] != 0)
        def _():
            side = pick_block(near_ref, far_ref, block)
            seen = col_ref[0] == row_ref[0, block : block + 1]
            for head, (start, width, _) in enumerate(windows):
                key = side[:, start : start + width]
                found = jnp.where(seen, dot(queries[head, :, :width], key, NT), MASKED)
                score[head, block] = found
                top = peak[head]
                for at in range(0, tokens, 128):
                    top = jnp.maximum(top, found[:, at : at + 128])
                peak[head] = top

    for head in range(heads):
        top = jnp.max(peak[head], axis=-1, keepdims=True) * (SCALE * LOG2E)
        peak[head] = jnp.broadcast_to(top, peak.shape[1:])

    for block in range(blocks):

        @pl.when(need_ref[row, block] != 0)
        def _():
            side = pick_block(near_ref, far_ref, block)
            for head, (start, width, _) in enumerate(windows):
                top, share = peak[head], total[head]
                pieces = []
                for at in range(0, tokens, 128):
                    part = jnp.exp2(score[head, block, :, at : at + 128] * (SCALE * LOG2E) - top)
                    share += part
                    pieces.append(part.astype(BF16))
                total[head] = share
                value = side[:, padded + start : padded + start + width]
                acc[head, :, :width] += dot(jnp.concatenate(pieces, axis=1), value)

    for head, (start, width, low) in enumerate(windows):
        norm = jnp.sum(total[head], axis=-1, keepdims=True)
        result = acc[head, :, :width] / norm
        mine = head_lanes(tokens, width, low)
        for which in range(2):
            kept = outs[which][0, :, start : start + width].astype(F32)
            fresh = result[which * tokens : (which + 1) * tokens]
            outs[which][0, :, start : start + width] = jnp.where(mine, fresh, kept).astype(BF16)
        lse = peak[head] + jnp.log2(norm)
        lses[...] = lse if head == 0 else jnp.where(slot == head, lse, lses[...])
    lse_ref[0] = lses[...].T[:heads]


def attend(row, query, near, far, need, seg_col, seg_row, heads, before):
    _, rows, tokens, padded = query.shape
    blocks = 2 + far.shape[0]
    narrow = pl.BlockSpec((1, tokens, padded), lambda i, need: (row, 0, 0))
    lines = pl.BlockSpec((1, heads, 2 * tokens), lambda i, need: (row, 0, 0))

    def stack(count, width):
        return pl.BlockSpec((count, 1, tokens, width), lambda i, need: (0, row, 0, 0))

    return pl.pallas_call(
        functools.partial(attend_kernel, row, heads, blocks, padded),
        out_shape=(
            jax.ShapeDtypeStruct((rows, tokens, padded), BF16),
            jax.ShapeDtypeStruct((rows, tokens, padded), BF16),
            jax.ShapeDtypeStruct((rows, heads, 2 * tokens), F32),
        ),
        grid_spec=pltpu.PrefetchScalarGridSpec(
            num_scalar_prefetch=1,
            grid=(1,),
            in_specs=[
                pl.BlockSpec((1, 2 * tokens, 1), lambda i, need: (row, 0, 0)),
                pl.BlockSpec((1, blocks, tokens), lambda i, need: (row, 0, 0)),
                stack(2, padded),
                stack(2, 2 * padded),
                stack(blocks - 2, 2 * padded),
            ]
            + [pl.BlockSpec(memory_space=pl.ANY)] * len(before),
            out_specs=(narrow, narrow, lines),
            scratch_shapes=[
                pltpu.VMEM((heads, 2 * tokens, WIN), BF16),
                pltpu.VMEM((heads, blocks, 2 * tokens, tokens), F32),
                pltpu.VMEM((heads, 2 * tokens, 128), F32),
                pltpu.VMEM((heads, 2 * tokens, 128), F32),
                pltpu.VMEM((heads, 2 * tokens, WIN), F32),
                pltpu.VMEM((2 * tokens, 128), F32),
            ],
        ),
        input_output_aliases={6 + i: i for i in range(len(before))},
        compiler_params=params(("arbitrary",)),
        cost_estimate=NOMINAL,
        name="attend",
    )(need, seg_col, seg_row, query, near, far, *before)


def attend_back_kernel(
    row, heads, blocks, padded, need_ref, col_ref, row_ref, pick_ref, q_ref, near_ref, far_ref, *refs
):
    grads, outs, lse_ref = refs[0:2], refs[2:4], refs[4]
    dq_ref, dnear_ref, dfar_ref, sums, inner_turn, queries, incoming, dq = refs[-8:]
    tokens = grads[0].shape[1]
    sums[...] = jnp.zeros_like(sums)
    for which in range(2):
        dq_ref[which, 0] = jnp.zeros((tokens, padded), BF16)
        product = grads[which][0].astype(F32) * outs[which][0].astype(F32)
        high = product.astype(BF16)
        rest = (product - high.astype(F32)).astype(BF16)
        inner_turn[:, which * tokens : (which + 1) * tokens] = dot(pick_ref[...], high, NT) + dot(
            pick_ref[...], rest, NT
        )
    windows = [head_window(head) for head in range(heads)]
    for head, (start, width, low) in enumerate(windows):
        for which in range(2):
            there = slice(which * tokens, (which + 1) * tokens)
            here = slice(start, start + width)
            queries[head, there, :width] = only_head(q_ref[which, 0, :, here], low)
            incoming[head, there, :width] = only_head(grads[which][0, :, here], low)
    dq[...] = jnp.zeros_like(dq)
    for block in range(blocks):

        @pl.when(need_ref[row, block] != 0)
        def _():
            side = pick_block(near_ref, far_ref, block)
            seen = col_ref[0, block] == row_ref[0]
            for head, (start, width, _) in enumerate(windows):
                end = start + width
                key, value = side[:, start:end], side[:, padded + start : padded + end]
                query, grad = queries[head, :, :width], incoming[head, :, :width]
                found = dot(key, query, NT) * (SCALE * LOG2E) - lse_ref[0, head : head + 1, :]
                prob = jnp.where(seen, jnp.exp2(found), 0.0)
                inner = inner_turn[head : head + 1, :]
                slope = (prob * (dot(value, grad, NT) - inner)).astype(BF16)
                sums[block, :, start:end] += dot(slope, query)
                sums[block, :, padded + start : padded + end] += dot(prob.astype(BF16), grad)
                dq[head, :, :width] += dot(slope, key, TN)

    for head, (start, width, low) in enumerate(windows):
        mine = head_lanes(tokens, width, low)
        for which in range(2):
            kept = dq_ref[which, 0, :, start : start + width].astype(F32)
            fresh = dq[head, which * tokens : (which + 1) * tokens, :width] * SCALE
            dq_ref[which, 0, :, start : start + width] = jnp.where(mine, fresh, kept).astype(BF16)
    for block in range(blocks):
        side = pick_block(dnear_ref, dfar_ref, block)
        side[:, :padded] = (sums[block, :, :padded] * SCALE).astype(BF16)
        side[:, padded:] = sums[block, :, padded:].astype(BF16)


def attend_back(row, query, near, far, grads, outs, lse, need, seg_col, seg_row, heads, before):
    _, rows, tokens, padded = query.shape
    blocks = 2 + far.shape[0]
    column = lax.broadcasted_iota(jnp.int32, (heads, padded), 1)
    pick = (column // HEAD_DIM == lax.broadcasted_iota(jnp.int32, (heads, padded), 0)).astype(BF16)
    narrow = pl.BlockSpec((1, tokens, padded), lambda i, need: (row, 0, 0))

    def stack(count, width):
        return pl.BlockSpec((count, 1, tokens, width), lambda i, need: (0, row, 0, 0))

    return pl.pallas_call(
        functools.partial(attend_back_kernel, row, heads, blocks, padded),
        out_shape=tuple(jax.ShapeDtypeStruct(a.shape, BF16) for a in (query, near, far)),
        grid_spec=pltpu.PrefetchScalarGridSpec(
            num_scalar_prefetch=1,
            grid=(1,),
            in_specs=[
                pl.BlockSpec((1, blocks, tokens, 1), lambda i, need: (row, 0, 0, 0)),
                pl.BlockSpec((1, 1, 2 * tokens), lambda i, need: (row, 0, 0)),
                pl.BlockSpec((heads, padded), lambda i, need: (0, 0)),
                stack(2, padded),
                stack(2, 2 * padded),
                stack(blocks - 2, 2 * padded),
            ]
            + [narrow] * 4
            + [pl.BlockSpec((1, heads, 2 * tokens), lambda i, need: (row, 0, 0))]
            + [pl.BlockSpec(memory_space=pl.ANY)] * len(before),
            out_specs=(stack(2, padded), stack(2, 2 * padded), stack(blocks - 2, 2 * padded)),
            scratch_shapes=[
                pltpu.VMEM((blocks, tokens, 2 * padded), F32),
                pltpu.VMEM((heads, 2 * tokens), F32),
                pltpu.VMEM((heads, 2 * tokens, WIN), BF16),
                pltpu.VMEM((heads, 2 * tokens, WIN), BF16),
                pltpu.VMEM((heads, 2 * tokens, WIN), F32),
            ],
        ),
        input_output_aliases={12 + i: i for i in range(len(before))},
        compiler_params=params(("arbitrary",)),
        cost_estimate=NOMINAL,
        name="attend_back",
    )(need, seg_col, seg_row, pick, query, near, far, *grads, *outs, lse, *before)


def local(
    patches,
    lengths,
    first_gain,
    first_shift,
    query_weight,
    query_bias,
    key_weight,
    value_weight,
    value_bias,
    output_weight,
    output_bias,
    second_gain,
    second_shift,
    hidden_weight,
    hidden_bias,
    down_weight,
    down_bias,
    cotangent,
):
    seq_count, shards = lax.axis_size("seq"), lax.axis_size("fsdp")
    place, me = lax.axis_index("seq"), lax.axis_index("fsdp")
    core = place & 1
    is_first = core == 0
    core_flag = core[None].astype(jnp.int32)
    rows, tokens, width = patches.shape
    flat = rows * tokens
    heads = width // HEAD_DIM // 2
    half = heads * HEAD_DIM
    padded = round_up(half, 128)
    ff = hidden_bias.shape[0]
    ff_half = round_up(ff, 256) // 2
    out_cols = padded
    out_cut = width - padded
    shard_rows = width // shards
    chain = Chain()

    def my_half(array, size, padded_size):
        first, second = array[..., :size], array[..., size:]
        grow = [(0, 0)] * (array.ndim - 1)
        first = jnp.pad(first, grow + [(0, padded_size - size)])
        second = jnp.pad(second, grow + [(0, padded_size - second.shape[-1])])
        return jnp.where(is_first, first, second)

    flights = Flights(chain)
    staged = shards == 8 and seq_count == 4
    y, z, zz = 1, 2, 4
    top = bits_of(seq_count)[0]

    inputs = patches.reshape(flat, width)
    incoming = cotangent.reshape(flat, width)
    vectors = [
        first_gain,
        first_shift,
        query_bias,
        value_bias,
        output_bias,
        second_gain,
        second_shift,
        down_bias,
    ]
    shard_qkv, shard_out = chain.done(
        *attention_shards(
            core_flag, [query_weight, key_weight, value_weight, output_weight], vectors, half, padded
        )
    )
    place_flag = place[None].astype(jnp.int32)

    def over(box_from, bits):
        return flights.send(box_from[0], "fsdp", bits)

    if staged:
        q = {0: [shard_qkv]}
        q[y] = over(q[0], y)
        q[z], q[zz] = over(q[0], z), over(q[0], zz)
        shard_ho, shard_down = chain.done(
            *mlp_shards(core_flag, shard_out, hidden_weight, down_weight, ff_half)
        )
        h, d = {0: [shard_ho]}, {0: [shard_down]}
        need, seg_rows, seg_cols, seg_near_row, seg_near_col = chain.done(
            *masks(chain(lengths), place_flag, seq_count, tokens)
        )
        core_flag, raw_own = flights.land(core_flag, inputs)
        q[zz | z], q[z | y], q[zz | y] = over(q[zz], z), over(q[z], y), over(q[zz], y)
        far_raw = [flights.send(raw_own, "seq", 2)]
        raw_pair = flights.send(raw_own, "seq", 1)
        core_flag = flights.land(core_flag, only=[q[zz | z]])
        q[zz | z | y] = over(q[zz | z], y)
        core_flag, shard_ho = flights.land(core_flag, shard_ho, only=[q[z | y], q[zz | y], raw_pair])
        h[0] = [shard_ho]
        h[z], h[y] = over(h[0], z), over(h[0], y)
        core_flag, shard_ho, shard_down = flights.land(
            core_flag, shard_ho, shard_down, only=[q[zz | z | y], far_raw[0]]
        )
        h[0], d[0] = [shard_ho], [shard_down]
        far_pair = [flights.send(far_raw[0][0], "seq", 1)]
        h[zz] = over(h[0], zz)
        w_q, w_kv = chain.done(*assemble({k: box[0] for k, box in q.items()}, me, padded))
        stacked, bias_q, bias_kv = chain.done(
            *lay_vectors(chain(core_flag), w_q, len(vectors), half, padded)
        )
        gain_one, shift_one = stacked[0:1], stacked[1:2]
        gain_one = chain(gain_one)
        normed_near = chain.done(norm([inputs, raw_pair[0]], gain_one, shift_one))
        bias_hidden = my_half(after(hidden_bias, gain_one).astype(F32)[None], ff_half, ff_half)
        gain_one = flights.land(gain_one, only=[h[z], far_pair[0]])
        h[z | y] = over(h[z], y)
        incoming_pair = flights.send(incoming, "seq", 1)
    else:
        parts = gather_all(shard_qkv)
        shard_ho, shard_down = mlp_shards(core_flag, shard_out, hidden_weight, down_weight, ff_half)
        raw = {0: inputs}
        for bit in bits_of(seq_count):
            raw.update({j | bit: swap(part, "seq", bit) for j, part in list(raw.items())})
        need, seg_rows, seg_cols, seg_near_row, seg_near_col = masks(lengths, place_flag, seq_count, tokens)
        w_q, w_kv = chain.done(*assemble(parts, me, padded))
        stacked, bias_q, bias_kv = lay_vectors(core_flag, w_q, len(vectors), half, padded)
        gain_one, shift_one = stacked[0:1], stacked[1:2]
        normed_near = norm([raw[0], raw[1]], gain_one, shift_one)
        far_raw, far_pair = [[raw[j]] for j in range(2, seq_count)], []
        incoming_pair = [swap(incoming, "seq", 1)]
        bias_hidden = my_half(hidden_bias.astype(F32)[None], ff_half, ff_half)
    _, _, bias_query, bias_value, bias_output, gain_two, shift_two, bias_down = [
        stacked[i : i + 1] for i in range(8)
    ]

    near_in, w_q, w_kv = chain(normed_near, w_q, w_kv)
    (query,) = rows_matmul("query", [near_in], [w_q], with_bias, [bias_q], [like(2 * flat, padded)])
    near_in = after(near_in, query)
    (near,) = rows_matmul("near", [near_in], [w_kv], with_bias, [bias_kv], [like(2 * flat, 2 * padded)])
    chain.done(query, near)
    gain_one, w_kv = chain(gain_one, w_kv)
    normed_far = chain.done(norm([box[0] for box in far_raw + far_pair], gain_one, shift_one))
    if staged:
        w_kv, incoming = flights.land(w_kv, incoming)
        h[zz | y], h[zz | z] = over(h[zz], y), over(h[zz], z)
    far_in, w_kv = chain(normed_far, w_kv)
    (far,) = rows_matmul(
        "far", [far_in], [w_kv], with_bias, [bias_kv], [like(normed_far.shape[0], 2 * padded)]
    )
    chain.done(far)
    query = query.reshape(2, rows, tokens, padded)
    near = near.reshape(2, rows, tokens, 2 * padded)
    far = far.reshape(seq_count - 2, rows, tokens, 2 * padded)
    found = ()
    for row in range(rows):
        query, near, far = chain(query, near, far)
        if staged and row == 1:
            query = flights.land(query)
            h[zz | z | y] = over(h[zz | z], y)
            d[y], d[z], d[zz] = over(d[0], y), over(d[0], z), over(d[0], zz)
        found = chain.done(*attend(row, query, near, far, need, seg_near_col, seg_rows, heads, found))
    out_own, out_pair, lse = found
    if staged:
        out_own, out_pair = flights.land(out_own, out_pair)
        h_parts = {k: box[0] for k, box in h.items()}
    else:
        out_own, out_pair = flights.land(out_own, out_pair)
        h_parts = gather_all(chain(shard_ho))
    w_out_mine, w_hidden = chain.done(*assemble(h_parts, me, out_cols))
    out_pair, w_out_mine = chain(out_pair, w_out_mine)
    other_half = flights.send(out_pair, "seq", 1)
    w_out_other = flights.send(w_out_mine, "seq", 1)
    if staged:
        d[zz | z], d[z | y] = over(d[zz], z), over(d[z], y)
    w_out_mine, w_hidden = flights.land(w_out_mine, w_hidden, only=[other_half, w_out_other])
    w_out = chain.done(both_cores(core_flag, w_out_mine, w_out_other[0], out_cut, width))
    w_out, incoming_pair[0] = chain(w_out, incoming_pair[0])
    incoming_near = chain.done(jnp.concatenate([incoming, incoming_pair[0]], axis=0))
    own_half, w_out = chain(out_own.reshape(flat, padded), w_out)
    attended, middle, second = chain.done(
        *join(
            core_flag,
            own_half,
            other_half[0].reshape(flat, padded),
            inputs,
            w_out,
            bias_output,
            gain_two,
            shift_two,
            half,
        )
    )
    if staged:
        second = flights.land(second, only=[d[zz | z], d[z | y]])
    second_pair = flights.send(second, "seq", 1)
    if staged:
        d[zz | y], d[zz | z | y] = over(d[zz], y), over(d[zz | z], y)
    second, w_hidden = flights.land(second, w_hidden, only=[second_pair])
    act, slope, second_near = chain.done(*hidden([second, second_pair[0]], w_hidden, bias_hidden))

    incoming_near, act = chain(incoming_near, act)
    grad_down = chain.done(token_dot(incoming_near, act))
    if staged:
        slope, grad_down = flights.land(slope, grad_down)
        d_parts = {k: box[0] for k, box in d.items()}
    else:
        d_parts = gather_all(chain(shard_down))
    part_down = lax.psum_scatter(grad_down, "fsdp", scatter_dimension=0, tiled=True)
    w_down = chain.done(assemble(d_parts, me))
    incoming_near, slope, w_down = chain(incoming_near, slope, w_down)
    grad_pre, hidden_line = chain.done(
        *rows_matmul(
            "grad_pre",
            [incoming_near],
            [w_down],
            with_slope,
            [slope],
            [like(2 * flat, ff_half), like(1, ff_half, F32)],
        )
    )
    grad_pre = chain(grad_pre)
    back, back_pair = chain.done(
        *rows_matmul("back", [grad_pre], [w_hidden], plain, [], [like(2 * flat, width)], NT, True)
    )
    back_other = flights.send(back_pair, "seq", 1)
    second_near, grad_pre = chain(second_near, grad_pre)
    grad_hidden = chain.done(dot(second_near, grad_pre, TN).astype(BF16))
    back = flights.land(back)
    grad_middle, branch, grad_mine, grad_send, lines = second_back(
        core_flag, middle, [back, back_other[0]], gain_two, incoming, w_out, hidden_line, half, padded
    )
    chain.done(branch, grad_send)
    grad_pair = flights.send(grad_send, "seq", 1)
    attended, branch = chain(attended, branch)
    partial_out = chain(chain.done(token_dot(attended, branch)))
    out_mine, out_other = chain.done(*core_columns(core_flag, [partial_out], out_cols))
    query = flights.land(query)

    links = {"x": ("seq", top), "core": ("seq", 1)} | {bit: ("fsdp", bit) for bit in bits_of(shards)}
    out_back = flights.send(out_other, "seq", 1)
    shape = (rows, tokens, padded)
    grads = [grad_mine.reshape(shape), grad_pair[0].reshape(shape)]
    found = ()
    far_bits = [2 << k for k in range(shards.bit_length() - 2)]
    def next_step(keep, box, bits):
        keep, send = scatter_step(keep, box[0], shard_rows)
        chain.done(keep)
        return keep, flights.send(send, "fsdp", bits.pop(0)) if bits else None

    def seq_rest(mine, arrived):
        for bit in bits_of(seq_count)[1:-1]:
            (mine,) = add_rows(mine, arrived)
            arrived = swap(mine, "seq", bit)
        return chain.done(*add_rows(mine, arrived, F32))

    for row in range(rows):
        query, near, far, *grads = chain(query, near, far, *grads)
        found = attend_back(
            row, query, near, far, grads, [out_own, out_pair], lse, need, seg_cols, seg_near_row, heads, found
        )
        chain.done(*found)
        query = flights.land(query)
        if row == 0:
            out_sum = chain.done(*add_rows(out_mine, out_back[0]))
            grad_ho = chain.done(jnp.concatenate([grad_hidden, out_sum], axis=1))
            part_hidden = lax.psum_scatter(grad_ho, "fsdp", scatter_dimension=0, tiled=True)
        if row == 1:
            part_down = chain(part_down)
            down_seq = flights.send(part_down, "seq", top)
    dq, dnear, dfar = [g.reshape(-1, g.shape[-1]) for g in found]
    dfar, w_kv, down_seq[0] = chain(dfar, w_kv, down_seq[0])
    two = seq_count == 4
    back_far = rows_matmul("back_far", [dfar], [w_kv], plain, [], [like(dfar.shape[0], width)], NT, two)
    chain.done(*back_far)
    dnear = chain(dnear)
    if two:
        far_parts = {2 + i: part for i, part in enumerate(back_far)}
    else:
        far_parts = {j: back_far[0][(j - 2) * flat : (j - 1) * flat] for j in range(2, seq_count)}
    far_sent = {j: flights.send(part, "seq", 1) for j, part in far_parts.items() if j & 1}
    normed_near, dnear, dfar = chain(normed_near, dnear, dfar)
    kv_keep, kv_send, kv_sums = chain.done(
        *weight_grad([normed_near, normed_far], [dnear, dfar], me, shards)
    )
    dq = flights.land(dq)
    kv_box = flights.send(kv_send, "fsdp", y)
    far_sums = {j: add_rows(far_parts[j], far_sent[j | 1][0])[0] for j in far_parts if not j & 1}
    chain.done(*far_sums.values())
    arrived = []
    for bit in bits_of(seq_count)[:-1]:
        for j in [j for j in far_sums if j & bit]:
            part = far_sums.pop(j)
            if j == bit:
                arrived.append(flights.send(part, "seq", bit))
            else:
                (far_sums[j ^ bit],) = add_rows(far_sums[j ^ bit], swap(part, "seq", bit))
    dq, dnear = chain(dq, dnear)
    back_own, back_pair = chain.done(
        *rows_matmul("back_near", [dq, dnear], [w_q, w_kv], plain, [], [like(2 * flat, width)], NT, True)
    )
    pair_back = flights.send(back_pair, "seq", 1)
    act, middle = chain(act, middle)
    (down_pair,) = rows_matmul(
        "down_pair", [act], [w_down], plain, [], [like(flat, width)], NT, first_row=flat
    )
    chain.done(down_pair)
    down_back = flights.send(down_pair, "seq", 1)
    normed_near, dq = chain(normed_near, dq)
    q_keep, q_send, q_sums = chain.done(*weight_grad([normed_near], [dq], me, shards))
    q_box = flights.send(q_send, "fsdp", y)
    kv_bits, q_bits = list(far_bits), list(far_bits)
    act, late_in = flights.land(act, inputs, only=[kv_box] + arrived)
    kv_keep, kv_box = next_step(kv_keep, kv_box, kv_bits)
    late_in = flights.land(late_in, only=[pair_back])
    grad_patches, late = chain.done(
        *first_back(
            core_flag,
            late_in,
            [back_own, pair_back[0]] + [box[0] for box in arrived],
            gain_one,
            grad_middle,
            q_sums,
            kv_sums,
            half,
        )
    )
    small = jnp.concatenate([lines, late], axis=0)
    small_todo = [zz, y, z] if staged else bits_of(shards)
    small_todo = [("fsdp", bit) for bit in small_todo] + [("seq", bit) for bit in reversed(bits_of(seq_count))]

    def small_send():
        return flights.send(small, *small_todo.pop(0)) if small_todo else None

    def small_step(small, box):
        return chain.done(*add_rows(small, box[0], F32))

    act, middle = flights.land(act, middle, only=[q_box, down_back])
    q_keep, q_box = next_step(q_keep, q_box, q_bits)
    act, middle = chain(act, middle)
    (layer_output,) = rows_matmul(
        "down_own", [act], [w_down], layer_end, [middle, down_back[0], bias_down], [like(flat, width)], NT
    )
    layer_output = chain.done(layer_output).reshape(rows, tokens, width)
    boxes = [box for box in (kv_box, q_box) if box is not None]
    flights.land(only=boxes)
    if kv_box is not None:
        kv_keep, kv_box = next_step(kv_keep, kv_box, kv_bits)
    if q_box is not None:
        q_keep, q_box = next_step(q_keep, q_box, q_bits)
    small, part_hidden = chain(small, part_hidden)
    hidden_seq = flights.send(part_hidden, "seq", top)
    small_box = small_send()
    while kv_box is not None:
        flights.land(only=[kv_box])
        kv_keep, kv_box = next_step(kv_keep, kv_box, kv_bits)
    kv_seq = flights.send(kv_keep, "seq", top)
    flights.land(only=[hidden_seq, small_box])
    small = small_step(small, small_box)
    small_box = small_send()
    hidden_total = seq_rest(part_hidden, hidden_seq[0])
    hidden_other = flights.send(hidden_total, "seq", 1)
    while q_box is not None:
        flights.land(only=[q_box])
        q_keep, q_box = next_step(q_keep, q_box, q_bits)
    q_seq = flights.send(q_keep, "seq", top)
    flights.land(only=[small_box, kv_seq])
    small = small_step(small, small_box)
    small_box = small_send()
    kv_total = seq_rest(kv_keep, kv_seq[0])
    kv_other = flights.send(kv_total, "seq", 1)
    down_total = seq_rest(part_down, down_seq[0])
    flights.land(only=[hidden_other, small_box])
    small = small_step(small, small_box)
    small_box = small_send()
    down_other = flights.send(down_total, "seq", 1)
    flights.land(only=[q_seq, small_box])
    q_total = seq_rest(q_keep, q_seq[0])
    q_other = flights.send(q_total, "seq", 1)
    while small_box is not None:
        small = small_step(small, small_box)
        small_box = small_send()
        if small_box is not None:
            flights.land(only=[small_box])
    flights.land()

    own_lines = lax.dynamic_slice_in_dim(small[:8], me * shard_rows, shard_rows, 1)
    late_lines = lax.dynamic_slice_in_dim(small[8:], me * shard_rows, shard_rows, 1)
    cuts = [width, ff_half - width, width, ff - ff_half - width]
    full_bias = jnp.concatenate([small[4 + i, :size] for i, size in enumerate(cuts)])
    full_down = both_columns(is_first, down_total, down_other[0], ff_half, ff).T
    full_hidden = both_columns(is_first, hidden_total, hidden_other[0], ff_half, ff)
    full_out = both_columns(is_first, hidden_total, hidden_other[0], out_cut, width, ff_half)
    full_query = both_columns(is_first, q_total, q_other[0], half, width)
    full_key = both_columns(is_first, kv_total, kv_other[0], half, width)
    full_value = both_columns(is_first, kv_total, kv_other[0], half, width, padded)
    return (
        layer_output,
        grad_patches.reshape(rows, tokens, width),
        late_lines[0],
        late_lines[1],
        full_query,
        late_lines[2],
        full_key,
        full_value,
        late_lines[3],
        full_out,
        own_lines[2],
        own_lines[0],
        own_lines[1],
        full_hidden,
        full_bias,
        full_down,
        own_lines[3],
    )


def solution(mesh):
    shard, line, tokens = P("fsdp", None), P("fsdp"), P("fsdp", "seq", None)
    in_specs = (
        tokens,
        shard,
        line,
        line,
        shard,
        line,
        shard,
        shard,
        line,
        shard,
        line,
        line,
        line,
        shard,
        P(),
        P(None, "fsdp"),
        line,
        tokens,
    )
    out_specs = (
        tokens,
        tokens,
        line,
        line,
        shard,
        line,
        shard,
        shard,
        line,
        shard,
        line,
        line,
        line,
        shard,
        P(),
        P(None, "fsdp"),
        line,
    )
    return jax.shard_map(local, mesh=mesh, in_specs=in_specs, out_specs=out_specs, check_vma=False)
```

```python
import functools
import math

import jax
import jax.numpy as jnp
from jax import lax
from jax.experimental import pallas as pl
from jax.experimental.pallas import tpu as pltpu
from jax.sharding import PartitionSpec as P

HEAD_DIM = 72
EPS = 1e-06
GELU_COEF = math.sqrt(2.0 / math.pi)
MASKED = -1e30
F32 = jnp.float32
BF16 = jnp.bfloat16
SCALE = 1.0 / math.sqrt(HEAD_DIM)
WIN = 256
LOG2E = math.log2(math.e)
VMEM = 60 << 20
NOMINAL = pl.CostEstimate(flops=1, transcendentals=0, bytes_accessed=1)


def round_up(value, step):
    return (value + step - 1) // step * step


def dot(left, right, dims=((1,), (0,))):
    return lax.dot_general(left, right, (dims, ((), ())), preferred_element_type=F32)


NT = ((1,), (1,))
TN = ((0,), (0,))


def params(semantics):
    return pltpu.CompilerParams(dimension_semantics=semantics, vmem_limit_bytes=VMEM)


def swap(array, axis, bits):
    size = lax.axis_size(axis)
    return lax.ppermute(array, axis, [(i, i ^ bits) for i in range(size)])


def bits_of(size):
    return [1 << k for k in reversed(range(size.bit_length() - 1))]


def after(value, *earlier):
    return lax.optimization_barrier((value,) + tuple(earlier))[0]


class Chain:
    def __init__(self):
        self.last = ()

    def __call__(self, *values, wait=()):
        held = lax.optimization_barrier(tuple(values) + tuple(self.last) + tuple(wait))
        return held[: len(values)] if len(values) > 1 else held[0]

    def done(self, *results):
        self.last = results
        return results if len(results) > 1 else results[0]


class Flights:
    def __init__(self, chain):
        self.chain, self.open = chain, []

    def send(self, array, axis, bits):
        self.open.append([swap(array, axis, bits)])
        return self.open[-1]

    def land(self, *values, through=None, only=None):
        if only is None:
            count = len(self.open)
            if through is not None:
                count = sum(i + 1 for i, box in enumerate(self.open) if box is through)
            only = self.open[:count]
        ready = [box for box in self.open if any(box is other for other in only)]
        self.open = [box for box in self.open if not any(box is other for other in ready)]
        held = self.chain(*[box[0] for box in ready], *values)
        held = held if isinstance(held, (tuple, list)) else [held]
        for box, array in zip(ready, held):
            box[0] = array
        rest = list(held[len(ready) :])
        return rest if len(rest) > 1 else rest[0] if rest else None


def in_order(parts, me):
    count = len(parts)
    return jnp.take(jnp.stack([parts[d] for d in range(count)]), me ^ jnp.arange(count), axis=0)


def gather_all(shard):
    parts = {0: shard}
    for bit in bits_of(lax.axis_size("fsdp")):
        parts.update({d | bit: swap(part, "fsdp", bit) for d, part in list(parts.items())})
    return parts


def rel_position(distance, count):
    width = count.bit_length() - 1
    return sum(((distance >> k) & 1) << (width - 1 - k) for k in range(width))


def assemble_kernel(count, rows, single, off_ref, *refs):
    outs = refs[count:]

    def fill(out_ref):
        for distance in range(count):
            start = pl.multiple_of(off_ref[distance], 16)
            out_ref[pl.ds(start, rows), :] = refs[distance][...]

    if single:
        fill(outs[0])
    else:
        pl.when(pl.program_id(0) == 0)(lambda: fill(outs[0]))
        pl.when(pl.program_id(0) > 0)(lambda: fill(outs[1]))


def assemble(parts, me, cut=None):
    count = len(parts)
    rows, cols = parts[0].shape
    if rows % 16:
        full = in_order(parts, me).reshape(count * rows, cols)
        return (full[:, :cut], full[:, cut:]) if cut else full
    offsets = ((me ^ jnp.arange(count, dtype=jnp.int32)) * rows).astype(jnp.int32)
    tile = cut or min(cols, 1152)
    widths = [cut, cols - cut] if cut else [cols]
    maps = [lambda n, off: (0, 0), lambda n, off: (0, jnp.maximum(n - 1, 0))]
    if not cut:
        maps = [lambda n, off: (0, n)]
    outs = pl.pallas_call(
        functools.partial(assemble_kernel, count, rows, not cut),
        out_shape=[jax.ShapeDtypeStruct((count * rows, w), parts[0].dtype) for w in widths],
        grid_spec=pltpu.PrefetchScalarGridSpec(
            num_scalar_prefetch=1,
            grid=(pl.cdiv(cols, tile),),
            in_specs=[pl.BlockSpec((rows, tile), lambda n, off: (0, n))] * count,
            out_specs=[pl.BlockSpec((count * rows, tile), m) for m in maps],
        ),
        compiler_params=params(("arbitrary",)),
        cost_estimate=NOMINAL,
        name="assemble",
    )(offsets, *[parts[d] for d in range(count)])
    return outs if cut else outs[0]


def weight_grad_kernel(pairs, count, rows, pos_ref, *refs):
    lefts, rights = refs[:pairs], refs[pairs : 2 * pairs]
    keep_ref, send_ref, sum_ref = refs[2 * pairs :]
    total = dot(lefts[0][...], rights[0][...], TN)
    for i in range(1, pairs):
        total += dot(lefts[i][...], rights[i][...], TN)
    sum_ref[...] = sum(dot(jnp.ones((8, r.shape[0]), BF16), r[...]) for r in rights)
    for shard in range(count):
        start = pl.multiple_of(pos_ref[shard], 16)
        block = total[shard * rows : (shard + 1) * rows].astype(BF16)

        @pl.when(pos_ref[count] == shard % 2)
        def _():
            keep_ref[pl.ds(start, rows), :] = block

        @pl.when(pos_ref[count] != shard % 2)
        def _():
            send_ref[pl.ds(start, rows), :] = block


def weight_grad(lefts, rights, me, count):
    width = lefts[0].shape[1]
    cols = rights[0].shape[1]
    rows = width // count
    order = me ^ jnp.arange(count, dtype=jnp.int32)
    table = jnp.array([rel_position(d, count) for d in range(count)], jnp.int32)
    half = count // 2
    if rows % 16:
        total = sum(dot(a, b, TN) for a, b in zip(lefts, rights))
        by_distance = jnp.take(total.astype(BF16).reshape(count, rows, cols), order, axis=0)
        back = [0] * count
        for d in range(count):
            back[rel_position(d, count)] = d
        placed = jnp.take(by_distance, jnp.array(back), axis=0).reshape(width, cols)
        ones = [jnp.ones((8, b.shape[0]), BF16) for b in rights]
        sums = sum(dot(one, b) for one, b in zip(ones, rights))
        return placed[: width // 2], placed[width // 2 :], sums
    positions = jnp.concatenate([table[order] % half * rows, (me & 1)[None]]).astype(jnp.int32)
    tile = 256
    pairs = len(lefts)
    return pl.pallas_call(
        functools.partial(weight_grad_kernel, pairs, count, rows),
        out_shape=[jax.ShapeDtypeStruct((width // 2, cols), BF16)] * 2
        + [jax.ShapeDtypeStruct((8, cols), F32)],
        grid_spec=pltpu.PrefetchScalarGridSpec(
            num_scalar_prefetch=1,
            grid=(pl.cdiv(cols, tile),),
            in_specs=[
                pl.BlockSpec(a.shape, lambda n, off: (0, 0), pipeline_mode=pl.Buffered(1))
                for a in lefts
            ]
            + [pl.BlockSpec((b.shape[0], tile), lambda n, off: (0, n)) for b in rights],
            out_specs=[pl.BlockSpec((width // 2, tile), lambda n, off: (0, n))] * 2
            + [pl.BlockSpec((8, tile), lambda n, off: (0, n))],
        ),
        compiler_params=params(("arbitrary",)),
        cost_estimate=NOMINAL,
        name="weight_grad",
    )(positions, *lefts, *rights)


def token_dot(left, right):
    tokens, width = left.shape
    cols = right.shape[1]
    tile = 256

    def kernel(left_ref, right_ref, out_ref):
        out_ref[...] = dot(left_ref[...], right_ref[...], TN).astype(BF16)

    return pl.pallas_call(
        kernel,
        out_shape=jax.ShapeDtypeStruct((width, cols), BF16),
        grid=(pl.cdiv(cols, tile),),
        in_specs=[
            pl.BlockSpec((tokens, width), lambda n: (0, 0), pipeline_mode=pl.Buffered(1)),
            pl.BlockSpec((tokens, tile), lambda n: (0, n)),
        ],
        out_specs=pl.BlockSpec((width, tile), lambda n: (0, n)),
        compiler_params=params(("arbitrary",)),
        cost_estimate=NOMINAL,
        name="token_dot",
    )(left, right)


def normalized(values):
    center = values - jnp.mean(values, axis=-1, keepdims=True)
    spread = jnp.mean(center * center, axis=-1, keepdims=True)
    inverse = lax.rsqrt(spread + EPS)
    return center * inverse, inverse


def row_block(rows):
    return 256 if rows % 256 == 0 else 128 if rows % 128 == 0 else rows


def norm(arrays, gain, shift):
    width = arrays[0].shape[1]
    block = min(row_block(a.shape[0]) for a in arrays)
    steps = [a.shape[0] // block for a in arrays]
    firsts = [sum(steps[:k]) for k in range(len(steps))]
    count, total = len(arrays), sum(steps)

    def kernel(*refs):
        gain_ref, shift_ref, out_ref = refs[count:]
        at = pl.program_id(0)
        for k in range(count):

            @pl.when((at >= firsts[k]) & (at < firsts[k] + steps[k]))
            def _():
                hat, _ = normalized(refs[k][...].astype(F32))
                out_ref[...] = (hat * gain_ref[...] + shift_ref[...]).astype(BF16)

    line = pl.BlockSpec((1, width), lambda i: (0, 0))
    return pl.pallas_call(
        kernel,
        out_shape=jax.ShapeDtypeStruct((total * block, width), BF16),
        grid=(total,),
        in_specs=[
            pl.BlockSpec((block, width), lambda i, k=k: (jnp.clip(i - firsts[k], 0, steps[k] - 1), 0))
            for k in range(count)
        ]
        + [line, line],
        out_specs=pl.BlockSpec((block, width), lambda i: (i, 0)),
        compiler_params=params(("arbitrary",)),
        cost_estimate=NOMINAL,
        name="norm",
    )(*arrays, gain, shift)


def join_kernel(half, core_ref, own_ref, other_ref, x_ref, w_ref, b_ref, g_ref, s_ref, *outs):
    att_ref, mid_ref, out_ref = outs
    own, other = own_ref[:, :half], other_ref[:, :half]

    @pl.when(core_ref[0] == 0)
    def _():
        att_ref[...] = jnp.concatenate([own, other], axis=1)

    @pl.when(core_ref[0] != 0)
    def _():
        att_ref[...] = jnp.concatenate([other, own], axis=1)

    middle = x_ref[...].astype(F32) + dot(att_ref[...], w_ref[...]) + b_ref[...]
    mid_ref[...] = middle
    hat, _ = normalized(middle)
    out_ref[...] = (hat * g_ref[...] + s_ref[...]).astype(BF16)


def join(core, own, other, inputs, weight, bias, gain, shift, half):
    rows, width = inputs.shape
    padded = own.shape[1]
    block = row_block(rows)
    line = pl.BlockSpec((1, width), lambda i, c: (0, 0))
    wide = pl.BlockSpec((block, width), lambda i, c: (i, 0))
    part = pl.BlockSpec((block, padded), lambda i, c: (i, 0))
    return pl.pallas_call(
        functools.partial(join_kernel, half),
        out_shape=(
            jax.ShapeDtypeStruct((rows, width), BF16),
            jax.ShapeDtypeStruct((rows, width), F32),
            jax.ShapeDtypeStruct((rows, width), BF16),
        ),
        grid_spec=pltpu.PrefetchScalarGridSpec(
            num_scalar_prefetch=1,
            grid=(rows // block,),
            in_specs=[
                part,
                part,
                wide,
                pl.BlockSpec((width, width), lambda i, c: (0, 0), pipeline_mode=pl.Buffered(1)),
                line,
                line,
                line,
            ],
            out_specs=(wide, wide, wide),
        ),
        compiler_params=params(("arbitrary",)),
        cost_estimate=NOMINAL,
        name="join",
    )(core, own, other, inputs, weight, bias, gain, shift)


def norm_back_values(x_ref, grads, gain_ref, add_ref, lines_ref):
    hat, inverse = normalized(x_ref[...].astype(F32))
    grad = grads[0][...].astype(F32)
    for other in grads[1:]:
        grad += other[...].astype(F32)
    scaled = grad * gain_ref[...]
    first = jnp.mean(scaled, axis=-1, keepdims=True)
    second = jnp.mean(scaled * hat, axis=-1, keepdims=True)

    @pl.when(pl.program_id(0) == 0)
    def _():
        lines_ref[...] = jnp.zeros_like(lines_ref)

    lines_ref[0:1] += jnp.sum(grad * hat, axis=0, keepdims=True)
    lines_ref[1:2] += jnp.sum(grad, axis=0, keepdims=True)
    return add_ref[...].astype(F32) + inverse * (scaled - first - hat * second)


def first_back(core, values, grads, gain, add, q_sums, kv_sums, half):
    rows, width = values.shape
    padded = q_sums.shape[1]
    pieces = [grad for grad in grads if isinstance(grad, tuple)]
    whole_grads = [grad for grad in grads if not isinstance(grad, tuple)]
    block = min([row_block(rows)] + [row_block(part.shape[0]) for pair in pieces for part in pair])
    count = len(whole_grads) + 2 * len(pieces)
    flat_grads = whole_grads + [part for pair in pieces for part in pair]

    def kernel(core_ref, x_ref, *refs):
        gain_ref, add_ref, q_ref, kv_ref, dx_ref, lines_ref = refs[count:]
        sums = list(refs[: len(whole_grads)])
        for k, pair in enumerate(pieces):
            low, high = refs[len(whole_grads) + 2 * k : len(whole_grads) + 2 * k + 2]
            first = pl.program_id(0) < pair[0].shape[0] // block
            sums.append(jnp.where(first, low[...].astype(F32), high[...].astype(F32)))
        dx_ref[...] = norm_back_values(x_ref, sums, gain_ref, add_ref, lines_ref)
        for line, part in ((2, q_ref[0:1, :half]), (3, kv_ref[0:1, padded : padded + half])):
            none = jnp.zeros_like(part)

            @pl.when(core_ref[0] == 0)
            def _():
                lines_ref[line : line + 1] = jnp.concatenate([part, none], axis=1)

            @pl.when(core_ref[0] != 0)
            def _():
                lines_ref[line : line + 1] = jnp.concatenate([none, part], axis=1)

    def piece_specs(pair):
        steps = pair[0].shape[0] // block
        return [
            pl.BlockSpec((block, width), lambda i, c: (jnp.minimum(i, steps - 1), 0)),
            pl.BlockSpec((block, width), lambda i, c: (jnp.maximum(i - steps, 0), 0)),
        ]

    wide = pl.BlockSpec((block, width), lambda i, c: (i, 0))
    return pl.pallas_call(
        kernel,
        out_shape=(
            jax.ShapeDtypeStruct((rows, width), F32),
            jax.ShapeDtypeStruct((8, width), F32),
        ),
        grid_spec=pltpu.PrefetchScalarGridSpec(
            num_scalar_prefetch=1,
            grid=(rows // block,),
            in_specs=[wide] * (1 + len(whole_grads))
            + [spec for pair in pieces for spec in piece_specs(pair)]
            + [
                pl.BlockSpec((1, width), lambda i, c: (0, 0)),
                wide,
                pl.BlockSpec(q_sums.shape, lambda i, c: (0, 0)),
                pl.BlockSpec(kv_sums.shape, lambda i, c: (0, 0)),
            ],
            out_specs=(wide, pl.BlockSpec((8, width), lambda i, c: (0, 0))),
        ),
        compiler_params=params(("arbitrary",)),
        cost_estimate=NOMINAL,
        name="first_back",
    )(core, values, *flat_grads, gain, add, q_sums, kv_sums)


def second_back(core, values, grads, gain, add, weight, hidden_line, half, padded):
    rows, width = values.shape
    block = row_block(rows)
    count = len(grads)

    def kernel(core_ref, x_ref, *refs):
        gain_ref, add_ref, w_ref, hid_ref, dx_ref, low_ref, mine_ref, send_ref, lines_ref = refs[count:]
        total = norm_back_values(x_ref, refs[:count], gain_ref, add_ref, lines_ref)
        low = total.astype(BF16)
        dx_ref[...] = total
        low_ref[...] = low
        lines_ref[2:3] += jnp.sum(low.astype(F32), axis=0, keepdims=True)
        lines_ref[3:4] += jnp.sum(add_ref[...].astype(F32), axis=0, keepdims=True)
        spare = hid_ref.shape[1] - width
        for core in range(2):

            @pl.when(core_ref[0] == core)
            def _():
                lines_ref[4 + 2 * core : 5 + 2 * core] = hid_ref[:, :width]
                lines_ref[5 + 2 * core : 6 + 2 * core, :spare] = hid_ref[:, width:]

        back = dot(low, w_ref[...], NT).astype(BF16)
        empty = jnp.zeros((block, padded - half), BF16)
        halves = [jnp.concatenate([back[:, i * half : (i + 1) * half], empty], axis=1) for i in range(2)]

        @pl.when(core_ref[0] == 0)
        def _():
            mine_ref[...], send_ref[...] = halves[0], halves[1]

        @pl.when(core_ref[0] != 0)
        def _():
            mine_ref[...], send_ref[...] = halves[1], halves[0]

    wide = pl.BlockSpec((block, width), lambda i, c: (i, 0))
    part = pl.BlockSpec((block, padded), lambda i, c: (i, 0))
    line = pl.BlockSpec((1, width), lambda i, c: (0, 0))
    square = pl.BlockSpec((width, width), lambda i, c: (0, 0), pipeline_mode=pl.Buffered(1))
    return pl.pallas_call(
        kernel,
        out_shape=(
            jax.ShapeDtypeStruct((rows, width), F32),
            jax.ShapeDtypeStruct((rows, width), BF16),
            jax.ShapeDtypeStruct((rows, padded), BF16),
            jax.ShapeDtypeStruct((rows, padded), BF16),
            jax.ShapeDtypeStruct((8, width), F32),
        ),
        grid_spec=pltpu.PrefetchScalarGridSpec(
            num_scalar_prefetch=1,
            grid=(rows // block,),
            in_specs=[wide] * (1 + count)
            + [line, wide, square, pl.BlockSpec(hidden_line.shape, lambda i, c: (0, 0))],
            out_specs=(wide, wide, part, part, pl.BlockSpec((8, width), lambda i, c: (0, 0))),
        ),
        compiler_params=params(("arbitrary",)),
        cost_estimate=NOMINAL,
        name="second_back",
    )(core, values, *grads, gain, add, weight, hidden_line)


def rows_matmul(name, lefts, weights, finish, extras, outs, dims=((1,), (0,)), split=False, first_row=0):
    rows = outs[0].shape[0]
    block = 384 if split and rows % 768 == 0 else 512 if not split and rows % 512 == 0 else row_block(rows)
    steps = rows // block
    half = steps // 2
    count, terms = len(lefts), len(lefts) + len(weights)

    def kernel(*refs):
        total = dot(refs[0][...], refs[count][...], dims)
        for i in range(1, count):
            total += dot(refs[i][...], refs[count + i][...], dims)
        results = finish(total, *refs[terms : terms + len(extras)])
        targets = refs[terms + len(extras) :]
        if split:

            @pl.when(pl.program_id(0) < half)
            def _():
                targets[0][...] = results[0]

            @pl.when(pl.program_id(0) >= half)
            def _():
                targets[1][...] = results[0]

            targets = targets[1:]
        else:
            targets[0][...] = results[0]
        for target, result in zip(targets[1:], results[1:]):

            @pl.when(pl.program_id(0) == 0)
            def _():
                target[...] = jnp.zeros_like(target)

            target[...] += result

    def by_rows(array):
        return pl.BlockSpec((block, array.shape[1]), lambda i: (i, 0))

    def whole(array):
        return pl.BlockSpec(array.shape, lambda i: (0, 0), pipeline_mode=pl.Buffered(1))

    first = outs[0]
    if split:
        part = jax.ShapeDtypeStruct((rows // 2, first.shape[1]), first.dtype)
        shapes = [part, part] + list(outs[1:])
        specs = [
            pl.BlockSpec((block, first.shape[1]), lambda i: (jnp.minimum(i, half - 1), 0)),
            pl.BlockSpec((block, first.shape[1]), lambda i: (jnp.maximum(i - half, 0), 0)),
        ]
    else:
        shapes, specs = list(outs), [by_rows(first)]
    specs += [pl.BlockSpec(out.shape, lambda i: (0, 0)) for out in outs[1:]]
    return pl.pallas_call(
        kernel,
        out_shape=shapes,
        grid=(steps,),
        in_specs=[
            pl.BlockSpec((block, a.shape[1]), lambda i: (i + first_row // block, 0)) for a in lefts
        ]
        + [whole(w) for w in weights]
        + [by_rows(e) if e.shape[0] == rows else whole(e) for e in extras],
        out_specs=specs,
        compiler_params=params(("arbitrary",)),
        cost_estimate=NOMINAL,
        name=name,
    )(*lefts, *weights, *extras)


def like(rows, cols, kind=BF16):
    return jax.ShapeDtypeStruct((rows, cols), kind)


def plain(total):
    return (total.astype(BF16),)


def with_bias(total, bias_ref):
    return ((total + bias_ref[...]).astype(BF16),)


def with_slope(total, slope_ref):
    low = (total * slope_ref[...].astype(F32)).astype(BF16)
    return low, jnp.sum(low.astype(F32), axis=0, keepdims=True)


def layer_end(total, middle_ref, other_ref, bias_ref):
    return ((middle_ref[...] + total + other_ref[...].astype(F32) + bias_ref[...]).astype(BF16),)


def small_call(kernel, outs, scalars, arrays, name):
    vmem = pl.BlockSpec(memory_space=pltpu.VMEM)
    return pl.pallas_call(
        kernel,
        out_shape=outs,
        in_specs=[pl.BlockSpec(memory_space=pltpu.SMEM)] * len(scalars) + [vmem] * len(arrays),
        out_specs=[vmem] * len(outs),
        compiler_params=pltpu.CompilerParams(vmem_limit_bytes=VMEM),
        cost_estimate=NOMINAL,
        name=name,
    )(*scalars, *arrays)


def add_rows(left, right, kind=BF16, pieces=1):
    size = left.shape[0] // pieces
    parts = [slice(i * size, (i + 1) * size) for i in range(pieces)]
    return [(left[part].astype(F32) + right[part].astype(F32)).astype(kind) for part in parts]


def scatter_step(keep, arrived, rows):
    if keep.shape[0] == rows:
        return add_rows(keep, arrived)[0], None
    return add_rows(keep, arrived, BF16, 2)


def both_cores(core, mine, other, size, total, start=0, turn=False):
    rows = mine.shape[0]

    def kernel(core_ref, mine_ref, other_ref, out_ref):
        for at, refs in ((0, (mine_ref, other_ref)), (1, (other_ref, mine_ref))):

            @pl.when(core_ref[0] == at)
            def _():
                first = refs[0][:, start : start + size]
                second = refs[1][:, start : start + total - size]
                if turn:
                    out_ref[:size], out_ref[size:] = first.T, second.T
                else:
                    out_ref[...] = jnp.concatenate([first, second], axis=1)

    shape = like(total, rows, mine.dtype) if turn else like(rows, total, mine.dtype)
    return small_call(kernel, [shape], [core], [mine, other], "both_cores")[0]


def both_columns(is_first, mine, other, size, total, start=0):
    mine, other = mine[:, start:], other[:, start:]
    return jnp.where(
        is_first,
        jnp.concatenate([mine[:, :size], other[:, : total - size]], axis=1),
        jnp.concatenate([other[:, :size], mine[:, : total - size]], axis=1),
    )


def core_columns(core, arrays, cols):
    rows, width = arrays[0].shape

    def kernel(core_ref, *refs):
        for at in range(2):

            @pl.when(core_ref[0] == at)
            def _():
                for i in range(len(arrays)):
                    for k, where in enumerate((at, 1 - at)):
                        low = where * (width - cols)
                        refs[len(arrays) * (1 + k) + i][...] = refs[i][:, low : low + cols]

    return small_call(kernel, [like(rows, cols)] * (2 * len(arrays)), [core], arrays, "core_columns")


def mask_kernel(rows, tokens, blocks, len_ref, place_ref, need_ref, row_ref, col_ref, near_row, near_col):
    place = place_ref[0]
    for row in range(rows):
        ends = [len_ref[row, 0]]
        for p in range(1, len_ref.shape[1]):
            ends.append(ends[-1] + len_ref[row, p])

        def pictures(position):
            return sum((position >= end).astype(jnp.int32) for end in ends)

        def segment(position):
            return jnp.where(position < ends[-1], pictures(position), 1000 + position)

        spans = []
        for block in range(blocks):
            start = jnp.bitwise_xor(place, block) * tokens
            across = segment(start + lax.broadcasted_iota(jnp.int32, (1, tokens), 1))
            down = segment(start + lax.broadcasted_iota(jnp.int32, (tokens, 1), 0))
            row_ref[row, block : block + 1] = across
            col_ref[row, block] = down
            if block < 2:
                near_row[row, :, block * tokens : (block + 1) * tokens] = across
                near_col[row, block * tokens : (block + 1) * tokens] = down
            last = jnp.minimum(start + tokens, ends[-1]) - 1
            low = sum(jnp.where(start >= end, 1, 0) for end in ends)
            high = sum(jnp.where(last >= end, 1, 0) for end in ends)
            spans.append((start < ends[-1], low, high))
        for block, (real, low, high) in enumerate(spans):
            if block < 2:
                need_ref[row, block] = 1
            else:
                need_ref[row, block] = sum(
                    jnp.where(real & ok & (low <= top) & (bottom <= high), 1, 0) for ok, bottom, top in spans[:2]
                )


def masks(lengths, place, blocks, tokens):
    rows = lengths.shape[0]
    shapes = [(rows, blocks, tokens), (rows, blocks, tokens, 1), (rows, 1, 2 * tokens), (rows, 2 * tokens, 1)]
    smem = pl.BlockSpec(memory_space=pltpu.SMEM)
    return pl.pallas_call(
        functools.partial(mask_kernel, rows, tokens, blocks),
        out_shape=[jax.ShapeDtypeStruct((rows, blocks), jnp.int32)]
        + [jax.ShapeDtypeStruct(shape, jnp.int32) for shape in shapes],
        in_specs=[smem, smem],
        out_specs=[smem] + [pl.BlockSpec(memory_space=pltpu.VMEM)] * 4,
        compiler_params=pltpu.CompilerParams(vmem_limit_bytes=VMEM),
        cost_estimate=NOMINAL,
        name="masks",
    )(lengths, place)


def lay_vectors(core, weight, lines, half, padded):
    width, cols = weight.shape
    low = half // 128 * 128

    def kernel(core_ref, weight_ref, lines_ref, q_ref, kv_ref):
        turned = weight_ref[...].astype(F32).T
        lines_ref[...] = turned[half - low : half - low + lines]
        q_ref[...] = jnp.zeros_like(q_ref)
        kv_ref[...] = jnp.zeros_like(kv_ref)
        for at in range(2):

            @pl.when(core_ref[0] == at)
            def _():
                q_ref[:, :half] = lines_ref[2:3, at * half : (at + 1) * half]
                kv_ref[:, padded : padded + half] = lines_ref[3:4, at * half : (at + 1) * half]

    outs = [like(lines, width, F32), like(1, padded, F32), like(1, 2 * padded, F32)]
    block = cols - low
    return pl.pallas_call(
        kernel,
        out_shape=outs,
        grid=(1,),
        in_specs=[
            pl.BlockSpec(memory_space=pltpu.SMEM),
            pl.BlockSpec((width, block), lambda i: (0, low // block)),
        ],
        out_specs=[pl.BlockSpec(out.shape, lambda i: (0, 0)) for out in outs],
        compiler_params=params(("arbitrary",)),
        cost_estimate=NOMINAL,
        name="lay_vectors",
    )(core, weight)


def mlp_shards(core, out_shard, hidden_weight, down_weight, cols):
    rows, total = hidden_weight.shape
    before = out_shard.shape[1]

    def kernel(core_ref, part_ref, hidden_ref, down_ref, first_out, down_out):
        first_out[:, :before] = part_ref[...]
        for at in range(2):

            @pl.when(core_ref[0] == at)
            def _():
                low = at * cols
                high = min(low + cols, total)
                size = high - low
                first_out[:, before : before + size] = hidden_ref[:, low:high]
                down_out[:, :size] = down_ref[low:high].T
                if size < cols:
                    empty = jnp.zeros((rows, cols - size), BF16)
                    first_out[:, before + size :] = empty
                    down_out[:, size:] = empty

    outs = [like(rows, before + cols), like(rows, cols)]
    return small_call(kernel, outs, [core], [out_shard, hidden_weight, down_weight], "mlp_shards")


def attention_shards(core, weights, vectors, half, padded):
    rows, width = weights[0].shape
    cut = width - padded
    count = len(vectors)

    def kernel(core_ref, q_ref, k_ref, v_ref, o_ref, *refs):
        qkv_ref, out_ref, held = refs[count:]
        for i in range(count):
            held[i : i + 1] = refs[i][...].astype(F32).reshape(1, rows)
        empty = jnp.zeros((rows, padded - half), BF16)
        spare = jnp.zeros((rows, padded - half - count), BF16)
        lines = jnp.concatenate([held[...].T.astype(BF16), spare], axis=1)
        for at in range(2):

            @pl.when(core_ref[0] == at)
            def _():
                for i, ref in enumerate((q_ref, k_ref, v_ref)):
                    part = ref[:, at * half : (at + 1) * half]
                    rest = empty if i else lines
                    qkv_ref[:, i * padded : (i + 1) * padded] = jnp.concatenate([part, rest], axis=1)
                out_ref[...] = o_ref[:, at * cut : at * cut + padded]

    vmem = pl.BlockSpec(memory_space=pltpu.VMEM)
    return pl.pallas_call(
        kernel,
        out_shape=[like(rows, 3 * padded), like(rows, padded)],
        in_specs=[pl.BlockSpec(memory_space=pltpu.SMEM)] + [vmem] * (4 + count),
        out_specs=[vmem] * 2,
        scratch_shapes=[pltpu.VMEM((count, rows), F32)],
        compiler_params=pltpu.CompilerParams(vmem_limit_bytes=VMEM),
        cost_estimate=NOMINAL,
        name="attention_shards",
    )(core, *weights, *vectors)


def hidden(arrays, weight, bias):
    rows, width = arrays[0].shape
    cols = weight.shape[1]
    block = row_block(rows)
    steps, count = rows // block, len(arrays)

    def kernel(*refs):
        w_ref, b_ref, act_ref, slope_ref, x_ref = refs[count:]
        for i in range(count):

            @pl.when(pl.program_id(0) // steps == i)
            def _():
                x_ref[...] = refs[i][...]

        pre = dot(x_ref[...], w_ref[...]) + b_ref[...]
        square = pre * pre
        turn = jnp.tanh(pre * (GELU_COEF + GELU_COEF * 0.044715 * square))
        act_ref[...] = (0.5 * pre * (1.0 + turn)).astype(BF16)
        inner = GELU_COEF + 3.0 * 0.044715 * GELU_COEF * square
        slope_ref[...] = (0.5 * (1.0 + turn) * (1.0 + pre * (1.0 - turn) * inner)).astype(BF16)

    out = pl.BlockSpec((block, cols), lambda i: (i, 0))
    return pl.pallas_call(
        kernel,
        out_shape=(
            jax.ShapeDtypeStruct((count * rows, cols), BF16),
            jax.ShapeDtypeStruct((count * rows, cols), BF16),
            jax.ShapeDtypeStruct((count * rows, width), BF16),
        ),
        grid=(count * steps,),
        in_specs=[
            pl.BlockSpec((block, width), lambda i, k=k: (jnp.clip(i - k * steps, 0, steps - 1), 0))
            for k in range(count)
        ]
        + [
            pl.BlockSpec((width, cols), lambda i: (0, 0), pipeline_mode=pl.Buffered(1)),
            pl.BlockSpec((1, cols), lambda i: (0, 0)),
        ],
        out_specs=(out, out, pl.BlockSpec((block, width), lambda i: (i, 0))),
        compiler_params=params(("arbitrary",)),
        cost_estimate=NOMINAL,
        name="hidden",
    )(*arrays, weight, bias)


def head_window(head):
    first = head * HEAD_DIM
    start = first // 128 * 128
    return start, round_up(first + HEAD_DIM, 128) - start, first - start


def head_lanes(rows, width, low):
    lane = lax.broadcasted_iota(jnp.int32, (rows, width), 1)
    return (lane >= low) & (lane < low + HEAD_DIM)


def only_head(block, low):
    mine = head_lanes(*block.shape, low)
    return jnp.where(mine, block.astype(F32), 0.0).astype(BF16)


def pick_block(near_ref, far_ref, block):
    return near_ref.at[block, 0] if block < 2 else far_ref.at[block - 2, 0]


def attend_kernel(row, heads, blocks, padded, need_ref, col_ref, row_ref, q_ref, near_ref, far_ref, *refs):
    own_ref, pair_ref, lse_ref, queries, score, peak, total, acc, lses = refs[-9:]
    outs = (own_ref, pair_ref)
    tokens = own_ref.shape[1]
    slot = lax.broadcasted_iota(jnp.int32, (2 * tokens, 128), 1)
    for which in range(2):
        outs[which][...] = jnp.zeros_like(outs[which])
    windows = [head_window(head) for head in range(heads)]
    for head, (start, width, low) in enumerate(windows):
        for which in range(2):
            queries[head, which * tokens : (which + 1) * tokens, :width] = only_head(
                q_ref[which, 0, :, start : start + width], low
            )
    peak[...] = jnp.full_like(peak, MASKED)
    total[...] = jnp.zeros_like(total)
    acc[...] = jnp.zeros_like(acc)
    for block in range(blocks):

        @pl.when(need_ref[row, block] != 0)
        def _():
            side = pick_block(near_ref, far_ref, block)
            seen = col_ref[0] == row_ref[0, block : block + 1]
            for head, (start, width, _) in enumerate(windows):
                key = side[:, start : start + width]
                found = jnp.where(seen, dot(queries[head, :, :width], key, NT), MASKED)
                score[head, block] = found
                top = peak[head]
                for at in range(0, tokens, 128):
                    top = jnp.maximum(top, found[:, at : at + 128])
                peak[head] = top

    for head in range(heads):
        top = jnp.max(peak[head], axis=-1, keepdims=True) * (SCALE * LOG2E)
        peak[head] = jnp.broadcast_to(top, peak.shape[1:])

    for block in range(blocks):

        @pl.when(need_ref[row, block] != 0)
        def _():
            side = pick_block(near_ref, far_ref, block)
            for head, (start, width, _) in enumerate(windows):
                top, share = peak[head], total[head]
                pieces = []
                for at in range(0, tokens, 128):
                    part = jnp.exp2(score[head, block, :, at : at + 128] * (SCALE * LOG2E) - top)
                    share += part
                    pieces.append(part.astype(BF16))
                total[head] = share
                value = side[:, padded + start : padded + start + width]
                acc[head, :, :width] += dot(jnp.concatenate(pieces, axis=1), value)

    for head, (start, width, low) in enumerate(windows):
        norm = jnp.sum(total[head], axis=-1, keepdims=True)
        result = acc[head, :, :width] / norm
        mine = head_lanes(tokens, width, low)
        for which in range(2):
            kept = outs[which][0, :, start : start + width].astype(F32)
            fresh = result[which * tokens : (which + 1) * tokens]
            outs[which][0, :, start : start + width] = jnp.where(mine, fresh, kept).astype(BF16)
        lse = peak[head] + jnp.log2(norm)
        lses[...] = lse if head == 0 else jnp.where(slot == head, lse, lses[...])
    lse_ref[0] = lses[...].T[:heads]


def attend(row, query, near, far, need, seg_col, seg_row, heads, before):
    _, rows, tokens, padded = query.shape
    blocks = 2 + far.shape[0]
    narrow = pl.BlockSpec((1, tokens, padded), lambda i, need: (row, 0, 0))
    lines = pl.BlockSpec((1, heads, 2 * tokens), lambda i, need: (row, 0, 0))

    def stack(count, width):
        return pl.BlockSpec((count, 1, tokens, width), lambda i, need: (0, row, 0, 0))

    return pl.pallas_call(
        functools.partial(attend_kernel, row, heads, blocks, padded),
        out_shape=(
            jax.ShapeDtypeStruct((rows, tokens, padded), BF16),
            jax.ShapeDtypeStruct((rows, tokens, padded), BF16),
            jax.ShapeDtypeStruct((rows, heads, 2 * tokens), F32),
        ),
        grid_spec=pltpu.PrefetchScalarGridSpec(
            num_scalar_prefetch=1,
            grid=(1,),
            in_specs=[
                pl.BlockSpec((1, 2 * tokens, 1), lambda i, need: (row, 0, 0)),
                pl.BlockSpec((1, blocks, tokens), lambda i, need: (row, 0, 0)),
                stack(2, padded),
                stack(2, 2 * padded),
                stack(blocks - 2, 2 * padded),
            ]
            + [pl.BlockSpec(memory_space=pl.ANY)] * len(before),
            out_specs=(narrow, narrow, lines),
            scratch_shapes=[
                pltpu.VMEM((heads, 2 * tokens, WIN), BF16),
                pltpu.VMEM((heads, blocks, 2 * tokens, tokens), F32),
                pltpu.VMEM((heads, 2 * tokens, 128), F32),
                pltpu.VMEM((heads, 2 * tokens, 128), F32),
                pltpu.VMEM((heads, 2 * tokens, WIN), F32),
                pltpu.VMEM((2 * tokens, 128), F32),
            ],
        ),
        input_output_aliases={6 + i: i for i in range(len(before))},
        compiler_params=params(("arbitrary",)),
        cost_estimate=NOMINAL,
        name="attend",
    )(need, seg_col, seg_row, query, near, far, *before)


def attend_back_kernel(
    row, heads, blocks, padded, need_ref, col_ref, row_ref, pick_ref, q_ref, near_ref, far_ref, *refs
):
    grads, outs, lse_ref = refs[0:2], refs[2:4], refs[4]
    dq_ref, dnear_ref, dfar_ref, sums, inner_turn, queries, incoming, dq = refs[-8:]
    tokens = grads[0].shape[1]
    sums[...] = jnp.zeros_like(sums)
    for which in range(2):
        dq_ref[which, 0] = jnp.zeros((tokens, padded), BF16)
        product = grads[which][0].astype(F32) * outs[which][0].astype(F32)
        high = product.astype(BF16)
        rest = (product - high.astype(F32)).astype(BF16)
        inner_turn[:, which * tokens : (which + 1) * tokens] = dot(pick_ref[...], high, NT) + dot(
            pick_ref[...], rest, NT
        )
    windows = [head_window(head) for head in range(heads)]
    for head, (start, width, low) in enumerate(windows):
        for which in range(2):
            there = slice(which * tokens, (which + 1) * tokens)
            here = slice(start, start + width)
            queries[head, there, :width] = only_head(q_ref[which, 0, :, here], low)
            incoming[head, there, :width] = only_head(grads[which][0, :, here], low)
    dq[...] = jnp.zeros_like(dq)
    for block in range(blocks):

        @pl.when(need_ref[row, block] != 0)
        def _():
            side = pick_block(near_ref, far_ref, block)
            seen = col_ref[0, block] == row_ref[0]
            for head, (start, width, _) in enumerate(windows):
                end = start + width
                key, value = side[:, start:end], side[:, padded + start : padded + end]
                query, grad = queries[head, :, :width], incoming[head, :, :width]
                found = dot(key, query, NT) * (SCALE * LOG2E) - lse_ref[0, head : head + 1, :]
                prob = jnp.where(seen, jnp.exp2(found), 0.0)
                inner = inner_turn[head : head + 1, :]
                slope = (prob * (dot(value, grad, NT) - inner)).astype(BF16)
                sums[block, :, start:end] += dot(slope, query)
                sums[block, :, padded + start : padded + end] += dot(prob.astype(BF16), grad)
                dq[head, :, :width] += dot(slope, key, TN)

    for head, (start, width, low) in enumerate(windows):
        mine = head_lanes(tokens, width, low)
        for which in range(2):
            kept = dq_ref[which, 0, :, start : start + width].astype(F32)
            fresh = dq[head, which * tokens : (which + 1) * tokens, :width] * SCALE
            dq_ref[which, 0, :, start : start + width] = jnp.where(mine, fresh, kept).astype(BF16)
    for block in range(blocks):
        side = pick_block(dnear_ref, dfar_ref, block)
        side[:, :padded] = (sums[block, :, :padded] * SCALE).astype(BF16)
        side[:, padded:] = sums[block, :, padded:].astype(BF16)


def attend_back(row, query, near, far, grads, outs, lse, need, seg_col, seg_row, heads, before):
    _, rows, tokens, padded = query.shape
    blocks = 2 + far.shape[0]
    column = lax.broadcasted_iota(jnp.int32, (heads, padded), 1)
    pick = (column // HEAD_DIM == lax.broadcasted_iota(jnp.int32, (heads, padded), 0)).astype(BF16)
    narrow = pl.BlockSpec((1, tokens, padded), lambda i, need: (row, 0, 0))

    def stack(count, width):
        return pl.BlockSpec((count, 1, tokens, width), lambda i, need: (0, row, 0, 0))

    return pl.pallas_call(
        functools.partial(attend_back_kernel, row, heads, blocks, padded),
        out_shape=tuple(jax.ShapeDtypeStruct(a.shape, BF16) for a in (query, near, far)),
        grid_spec=pltpu.PrefetchScalarGridSpec(
            num_scalar_prefetch=1,
            grid=(1,),
            in_specs=[
                pl.BlockSpec((1, blocks, tokens, 1), lambda i, need: (row, 0, 0, 0)),
                pl.BlockSpec((1, 1, 2 * tokens), lambda i, need: (row, 0, 0)),
                pl.BlockSpec((heads, padded), lambda i, need: (0, 0)),
                stack(2, padded),
                stack(2, 2 * padded),
                stack(blocks - 2, 2 * padded),
            ]
            + [narrow] * 4
            + [pl.BlockSpec((1, heads, 2 * tokens), lambda i, need: (row, 0, 0))]
            + [pl.BlockSpec(memory_space=pl.ANY)] * len(before),
            out_specs=(stack(2, padded), stack(2, 2 * padded), stack(blocks - 2, 2 * padded)),
            scratch_shapes=[
                pltpu.VMEM((blocks, tokens, 2 * padded), F32),
                pltpu.VMEM((heads, 2 * tokens), F32),
                pltpu.VMEM((heads, 2 * tokens, WIN), BF16),
                pltpu.VMEM((heads, 2 * tokens, WIN), BF16),
                pltpu.VMEM((heads, 2 * tokens, WIN), F32),
            ],
        ),
        input_output_aliases={12 + i: i for i in range(len(before))},
        compiler_params=params(("arbitrary",)),
        cost_estimate=NOMINAL,
        name="attend_back",
    )(need, seg_col, seg_row, pick, query, near, far, *grads, *outs, lse, *before)


def local(
    patches,
    lengths,
    first_gain,
    first_shift,
    query_weight,
    query_bias,
    key_weight,
    value_weight,
    value_bias,
    output_weight,
    output_bias,
    second_gain,
    second_shift,
    hidden_weight,
    hidden_bias,
    down_weight,
    down_bias,
    cotangent,
):
    seq_count, shards = lax.axis_size("seq"), lax.axis_size("fsdp")
    place, me = lax.axis_index("seq"), lax.axis_index("fsdp")
    core = place & 1
    is_first = core == 0
    core_flag = core[None].astype(jnp.int32)
    rows, tokens, width = patches.shape
    flat = rows * tokens
    heads = width // HEAD_DIM // 2
    half = heads * HEAD_DIM
    padded = round_up(half, 128)
    ff = hidden_bias.shape[0]
    ff_half = round_up(ff, 256) // 2
    out_cols = padded
    out_cut = width - padded
    shard_rows = width // shards
    chain = Chain()

    def my_half(array, size, padded_size):
        first, second = array[..., :size], array[..., size:]
        grow = [(0, 0)] * (array.ndim - 1)
        first = jnp.pad(first, grow + [(0, padded_size - size)])
        second = jnp.pad(second, grow + [(0, padded_size - second.shape[-1])])
        return jnp.where(is_first, first, second)

    flights = Flights(chain)
    staged = shards == 8 and seq_count == 4
    y, z, zz = 1, 2, 4
    top = bits_of(seq_count)[0]

    inputs = patches.reshape(flat, width)
    incoming = cotangent.reshape(flat, width)
    vectors = [
        first_gain,
        first_shift,
        query_bias,
        value_bias,
        output_bias,
        second_gain,
        second_shift,
        down_bias,
    ]
    shard_qkv, shard_out = chain.done(
        *attention_shards(
            core_flag, [query_weight, key_weight, value_weight, output_weight], vectors, half, padded
        )
    )
    place_flag = place[None].astype(jnp.int32)

    def over(box_from, bits):
        return flights.send(box_from[0], "fsdp", bits)

    if staged:
        q = {0: [shard_qkv]}
        q[y] = over(q[0], y)
        q[z], q[zz] = over(q[0], z), over(q[0], zz)
        shard_ho, shard_down = chain.done(
            *mlp_shards(core_flag, shard_out, hidden_weight, down_weight, ff_half)
        )
        h, d = {0: [shard_ho]}, {0: [shard_down]}
        need, seg_rows, seg_cols, seg_near_row, seg_near_col = chain.done(
            *masks(chain(lengths), place_flag, seq_count, tokens)
        )
        core_flag, raw_own = flights.land(core_flag, inputs)
        q[zz | z], q[z | y], q[zz | y] = over(q[zz], z), over(q[z], y), over(q[zz], y)
        far_raw = [flights.send(raw_own, "seq", 2)]
        raw_pair = flights.send(raw_own, "seq", 1)
        core_flag = flights.land(core_flag, only=[q[zz | z]])
        q[zz | z | y] = over(q[zz | z], y)
        core_flag, shard_ho = flights.land(core_flag, shard_ho, only=[q[z | y], q[zz | y], raw_pair])
        h[0] = [shard_ho]
        h[z], h[y] = over(h[0], z), over(h[0], y)
        core_flag, shard_ho, shard_down = flights.land(
            core_flag, shard_ho, shard_down, only=[q[zz | z | y], far_raw[0]]
        )
        h[0], d[0] = [shard_ho], [shard_down]
        far_pair = [flights.send(far_raw[0][0], "seq", 1)]
        h[zz] = over(h[0], zz)
        w_q, w_kv = chain.done(*assemble({k: box[0] for k, box in q.items()}, me, padded))
        stacked, bias_q, bias_kv = chain.done(
            *lay_vectors(chain(core_flag), w_q, len(vectors), half, padded)
        )
        gain_one, shift_one = stacked[0:1], stacked[1:2]
        gain_one = chain(gain_one)
        normed_near = chain.done(norm([inputs, raw_pair[0]], gain_one, shift_one))
        bias_hidden = my_half(after(hidden_bias, gain_one).astype(F32)[None], ff_half, ff_half)
    else:
        parts = gather_all(shard_qkv)
        shard_ho, shard_down = mlp_shards(core_flag, shard_out, hidden_weight, down_weight, ff_half)
        raw = {0: inputs}
        for bit in bits_of(seq_count):
            raw.update({j | bit: swap(part, "seq", bit) for j, part in list(raw.items())})
        need, seg_rows, seg_cols, seg_near_row, seg_near_col = masks(lengths, place_flag, seq_count, tokens)
        w_q, w_kv = chain.done(*assemble(parts, me, padded))
        stacked, bias_q, bias_kv = lay_vectors(core_flag, w_q, len(vectors), half, padded)
        gain_one, shift_one = stacked[0:1], stacked[1:2]
        normed_near = norm([raw[0], raw[1]], gain_one, shift_one)
        far_raw, far_pair = [[raw[j]] for j in range(2, seq_count)], []
        incoming_pair = [swap(incoming, "seq", 1)]
        bias_hidden = my_half(hidden_bias.astype(F32)[None], ff_half, ff_half)
    _, _, bias_query, bias_value, bias_output, gain_two, shift_two, bias_down = [
        stacked[i : i + 1] for i in range(8)
    ]

    near_in, w_q, w_kv = chain(normed_near, w_q, w_kv)
    (query,) = rows_matmul("query", [near_in], [w_q], with_bias, [bias_q], [like(2 * flat, padded)])
    near_in = after(near_in, query)
    (near,) = rows_matmul("near", [near_in], [w_kv], with_bias, [bias_kv], [like(2 * flat, 2 * padded)])
    chain.done(query, near)
    if staged:
        gain_one = flights.land(gain_one, only=[h[z], far_pair[0]])
        h[z | y] = over(h[z], y)
        incoming_pair = flights.send(incoming, "seq", 1)
    gain_one, w_kv = chain(gain_one, w_kv)
    normed_far = chain.done(norm([box[0] for box in far_raw + far_pair], gain_one, shift_one))
    if staged:
        w_kv = flights.land(w_kv, only=[h[y], h[zz]])
        h[zz | y], h[zz | z] = over(h[zz], y), over(h[zz], z)
    far_in, w_kv = chain(normed_far, w_kv)
    (far,) = rows_matmul(
        "far", [far_in], [w_kv], with_bias, [bias_kv], [like(normed_far.shape[0], 2 * padded)]
    )
    chain.done(far)
    query = query.reshape(2, rows, tokens, padded)
    near = near.reshape(2, rows, tokens, 2 * padded)
    far = far.reshape(seq_count - 2, rows, tokens, 2 * padded)
    found = ()
    for row in range(rows):
        query, near, far = chain(query, near, far)
        if staged and row == 1:
            query = flights.land(query, only=[h[zz | z]])
            h[zz | z | y] = over(h[zz | z], y)
            d[y], d[z], d[zz] = over(d[0], y), over(d[0], z), over(d[0], zz)
        found = chain.done(*attend(row, query, near, far, need, seg_near_col, seg_rows, heads, found))
    out_own, out_pair, lse = found
    if staged:
        out_own, out_pair = flights.land(out_own, out_pair, only=[incoming_pair, *h.values()])
        h_parts = {k: box[0] for k, box in h.items()}
    else:
        out_own, out_pair = flights.land(out_own, out_pair)
        h_parts = gather_all(chain(shard_ho))
    w_out_mine, w_hidden = chain.done(*assemble(h_parts, me, out_cols))
    if staged:
        out_pair, w_out_mine = flights.land(out_pair, w_out_mine, only=[d[y], d[z], d[zz]])
    else:
        out_pair, w_out_mine = chain(out_pair, w_out_mine)
    other_half = flights.send(out_pair, "seq", 1)
    w_out_other = flights.send(w_out_mine, "seq", 1)
    if staged:
        d[zz | z], d[z | y] = over(d[zz], z), over(d[z], y)
    w_out_mine, w_hidden = flights.land(w_out_mine, w_hidden, only=[other_half, w_out_other])
    w_out = chain.done(both_cores(core_flag, w_out_mine, w_out_other[0], out_cut, width))
    w_out, incoming_pair[0] = chain(w_out, incoming_pair[0])
    incoming_near = chain.done(jnp.concatenate([incoming, incoming_pair[0]], axis=0))
    own_half, w_out = chain(out_own.reshape(flat, padded), w_out)
    attended, middle, second = chain.done(
        *join(
            core_flag,
            own_half,
            other_half[0].reshape(flat, padded),
            inputs,
            w_out,
            bias_output,
            gain_two,
            shift_two,
            half,
        )
    )
    if staged:
        second = flights.land(second, only=[d[zz | z], d[z | y]])
    second_pair = flights.send(second, "seq", 1)
    if staged:
        d[zz | y], d[zz | z | y] = over(d[zz], y), over(d[zz | z], y)
    second, w_hidden = flights.land(second, w_hidden, only=[second_pair])
    act, slope, second_near = chain.done(*hidden([second, second_pair[0]], w_hidden, bias_hidden))

    incoming_near, act = chain(incoming_near, act)
    grad_down = chain.done(token_dot(incoming_near, act))
    if staged:
        slope, grad_down = flights.land(slope, grad_down)
        d_parts = {k: box[0] for k, box in d.items()}
    else:
        d_parts = gather_all(chain(shard_down))
    part_down = lax.psum_scatter(grad_down, "fsdp", scatter_dimension=0, tiled=True)
    w_down = chain.done(assemble(d_parts, me))
    incoming_near, slope, w_down = chain(incoming_near, slope, w_down)
    grad_pre, hidden_line = chain.done(
        *rows_matmul(
            "grad_pre",
            [incoming_near],
            [w_down],
            with_slope,
            [slope],
            [like(2 * flat, ff_half), like(1, ff_half, F32)],
        )
    )
    grad_pre = chain(grad_pre)
    back, back_pair = chain.done(
        *rows_matmul("back", [grad_pre], [w_hidden], plain, [], [like(2 * flat, width)], NT, True)
    )
    back_other = flights.send(back_pair, "seq", 1)
    second_near, grad_pre = chain(second_near, grad_pre)
    grad_hidden = chain.done(dot(second_near, grad_pre, TN).astype(BF16))
    back = flights.land(back)
    grad_middle, branch, grad_mine, grad_send, lines = second_back(
        core_flag, middle, [back, back_other[0]], gain_two, incoming, w_out, hidden_line, half, padded
    )
    chain.done(branch, grad_send)
    grad_pair = flights.send(grad_send, "seq", 1)
    attended, branch = chain(attended, branch)
    partial_out = chain(chain.done(token_dot(attended, branch)))
    out_mine, out_other = chain.done(*core_columns(core_flag, [partial_out], out_cols))
    query = flights.land(query)

    links = {"x": ("seq", top), "core": ("seq", 1)} | {bit: ("fsdp", bit) for bit in bits_of(shards)}
    out_back = flights.send(out_other, "seq", 1)
    shape = (rows, tokens, padded)
    grads = [grad_mine.reshape(shape), grad_pair[0].reshape(shape)]
    found = ()
    far_bits = [2 << k for k in range(shards.bit_length() - 2)]
    def next_step(keep, box, bits):
        keep, send = scatter_step(keep, box[0], shard_rows)
        chain.done(keep)
        return keep, flights.send(send, "fsdp", bits.pop(0)) if bits else None

    def seq_rest(mine, arrived):
        for bit in bits_of(seq_count)[1:-1]:
            (mine,) = add_rows(mine, arrived)
            arrived = swap(mine, "seq", bit)
        return chain.done(*add_rows(mine, arrived, F32))

    for row in range(rows):
        query, near, far, *grads = chain(query, near, far, *grads)
        found = attend_back(
            row, query, near, far, grads, [out_own, out_pair], lse, need, seg_cols, seg_near_row, heads, found
        )
        chain.done(*found)
        query = flights.land(query)
        if row == 0:
            out_sum = chain.done(*add_rows(out_mine, out_back[0]))
            grad_ho = chain.done(jnp.concatenate([grad_hidden, out_sum], axis=1))
            part_hidden = lax.psum_scatter(grad_ho, "fsdp", scatter_dimension=0, tiled=True)
        if row == 1:
            part_down = chain(part_down)
            down_seq = flights.send(part_down, "seq", top)
    dq, dnear, dfar = [g.reshape(-1, g.shape[-1]) for g in found]
    dfar, w_kv, down_seq[0] = chain(dfar, w_kv, down_seq[0])
    two = seq_count == 4
    back_far = rows_matmul("back_far", [dfar], [w_kv], plain, [], [like(dfar.shape[0], width)], NT, two)
    chain.done(*back_far)
    dnear = chain(dnear)
    if two:
        far_parts = {2 + i: part for i, part in enumerate(back_far)}
    else:
        far_parts = {j: back_far[0][(j - 2) * flat : (j - 1) * flat] for j in range(2, seq_count)}
    far_sent = {j: flights.send(part, "seq", 1) for j, part in far_parts.items() if j & 1}
    normed_near, dnear, dfar = chain(normed_near, dnear, dfar)
    kv_keep, kv_send, kv_sums = chain.done(
        *weight_grad([normed_near, normed_far], [dnear, dfar], me, shards)
    )
    dq = flights.land(dq)
    kv_box = flights.send(kv_send, "fsdp", y)
    far_sums = {j: add_rows(far_parts[j], far_sent[j | 1][0])[0] for j in far_parts if not j & 1}
    chain.done(*far_sums.values())
    arrived = []
    for bit in bits_of(seq_count)[:-1]:
        for j in [j for j in far_sums if j & bit]:
            part = far_sums.pop(j)
            if j == bit:
                arrived.append(flights.send(part, "seq", bit))
            else:
                (far_sums[j ^ bit],) = add_rows(far_sums[j ^ bit], swap(part, "seq", bit))
    dq, dnear = chain(dq, dnear)
    back_own, back_pair = chain.done(
        *rows_matmul("back_near", [dq, dnear], [w_q, w_kv], plain, [], [like(2 * flat, width)], NT, True)
    )
    pair_back = flights.send(back_pair, "seq", 1)
    act, middle = chain(act, middle)
    (down_pair,) = rows_matmul(
        "down_pair", [act], [w_down], plain, [], [like(flat, width)], NT, first_row=flat
    )
    chain.done(down_pair)
    down_back = flights.send(down_pair, "seq", 1)
    normed_near, dq = chain(normed_near, dq)
    q_keep, q_send, q_sums = chain.done(*weight_grad([normed_near], [dq], me, shards))
    q_box = flights.send(q_send, "fsdp", y)
    kv_bits, q_bits = list(far_bits), list(far_bits)
    act, late_in = flights.land(act, inputs, only=[kv_box] + arrived)
    kv_keep, kv_box = next_step(kv_keep, kv_box, kv_bits)
    late_in = flights.land(late_in, only=[pair_back])
    grad_patches, late = chain.done(
        *first_back(
            core_flag,
            late_in,
            [back_own, pair_back[0]] + [box[0] for box in arrived],
            gain_one,
            grad_middle,
            q_sums,
            kv_sums,
            half,
        )
    )
    small = jnp.concatenate([lines, late], axis=0)
    small_todo = [zz, y, z] if staged else bits_of(shards)
    small_todo = [("fsdp", bit) for bit in small_todo] + [("seq", bit) for bit in reversed(bits_of(seq_count))]

    def small_send():
        return flights.send(small, *small_todo.pop(0)) if small_todo else None

    def small_step(small, box):
        return chain.done(*add_rows(small, box[0], F32))

    act, middle = flights.land(act, middle, only=[q_box, down_back])
    q_keep, q_box = next_step(q_keep, q_box, q_bits)
    act, middle = chain(act, middle)
    (layer_output,) = rows_matmul(
        "down_own", [act], [w_down], layer_end, [middle, down_back[0], bias_down], [like(flat, width)], NT
    )
    layer_output = chain.done(layer_output).reshape(rows, tokens, width)
    boxes = [box for box in (kv_box, q_box) if box is not None]
    flights.land(only=boxes)
    if kv_box is not None:
        kv_keep, kv_box = next_step(kv_keep, kv_box, kv_bits)
    if q_box is not None:
        q_keep, q_box = next_step(q_keep, q_box, q_bits)
    small, part_hidden = chain(small, part_hidden)
    hidden_seq = flights.send(part_hidden, "seq", top)
    small_box = small_send()
    while kv_box is not None or q_box is not None:
        flights.land(only=[box for box in (kv_box, q_box) if box is not None])
        if kv_box is not None:
            kv_keep, kv_box = next_step(kv_keep, kv_box, kv_bits)
        if q_box is not None:
            q_keep, q_box = next_step(q_keep, q_box, q_bits)
    kv_seq = flights.send(kv_keep, "seq", top)
    q_seq = flights.send(q_keep, "seq", top)
    flights.land(only=[hidden_seq, small_box])
    small = small_step(small, small_box)
    small_box = small_send()
    hidden_total = seq_rest(part_hidden, hidden_seq[0])
    hidden_other = flights.send(hidden_total, "seq", 1)
    flights.land(only=[small_box, kv_seq])
    small = small_step(small, small_box)
    small_box = small_send()
    kv_total = seq_rest(kv_keep, kv_seq[0])
    kv_other = flights.send(kv_total, "seq", 1)
    down_total = seq_rest(part_down, down_seq[0])
    flights.land(only=[q_seq, hidden_other, small_box])
    small = small_step(small, small_box)
    small_box = small_send()
    down_other = flights.send(down_total, "seq", 1)
    q_total = seq_rest(q_keep, q_seq[0])
    q_other = flights.send(q_total, "seq", 1)
    if small_box is not None:
        flights.land(only=[small_box])
    while small_box is not None:
        small = small_step(small, small_box)
        small_box = small_send()
        if small_box is not None:
            flights.land(only=[small_box])
    flights.land()

    own_lines = lax.dynamic_slice_in_dim(small[:8], me * shard_rows, shard_rows, 1)
    late_lines = lax.dynamic_slice_in_dim(small[8:], me * shard_rows, shard_rows, 1)
    cuts = [width, ff_half - width, width, ff - ff_half - width]
    full_bias = jnp.concatenate([small[4 + i, :size] for i, size in enumerate(cuts)])
    full_down = both_columns(is_first, down_total, down_other[0], ff_half, ff).T
    full_hidden = both_columns(is_first, hidden_total, hidden_other[0], ff_half, ff)
    full_out = both_columns(is_first, hidden_total, hidden_other[0], out_cut, width, ff_half)
    full_query = both_columns(is_first, q_total, q_other[0], half, width)
    full_key = both_columns(is_first, kv_total, kv_other[0], half, width)
    full_value = both_columns(is_first, kv_total, kv_other[0], half, width, padded)
    return (
        layer_output,
        grad_patches.reshape(rows, tokens, width),
        late_lines[0],
        late_lines[1],
        full_query,
        late_lines[2],
        full_key,
        full_value,
        late_lines[3],
        full_out,
        own_lines[2],
        own_lines[0],
        own_lines[1],
        full_hidden,
        full_bias,
        full_down,
        own_lines[3],
    )


def solution(mesh):
    shard, line, tokens = P("fsdp", None), P("fsdp"), P("fsdp", "seq", None)
    in_specs = (
        tokens,
        shard,
        line,
        line,
        shard,
        line,
        shard,
        shard,
        line,
        shard,
        line,
        line,
        line,
        shard,
        P(),
        P(None, "fsdp"),
        line,
        tokens,
    )
    out_specs = (
        tokens,
        tokens,
        line,
        line,
        shard,
        line,
        shard,
        shard,
        line,
        shard,
        line,
        line,
        line,
        shard,
        P(),
        P(None, "fsdp"),
        line,
    )
    return jax.shard_map(local, mesh=mesh, in_specs=in_specs, out_specs=out_specs, check_vma=False)
```

```python
import functools
import math

import jax
import jax.numpy as jnp
from jax import lax
from jax.experimental import pallas as pl
from jax.experimental.pallas import tpu as pltpu
from jax.sharding import PartitionSpec as P

HEAD_DIM = 72
EPS = 1e-06
GELU_COEF = math.sqrt(2.0 / math.pi)
MASKED = -1e30
F32 = jnp.float32
BF16 = jnp.bfloat16
SCALE = 1.0 / math.sqrt(HEAD_DIM)
WIN = 256
LOG2E = math.log2(math.e)
VMEM = 60 << 20
NOMINAL = pl.CostEstimate(flops=1, transcendentals=0, bytes_accessed=1)


def round_up(value, step):
    return (value + step - 1) // step * step


def dot(left, right, dims=((1,), (0,))):
    return lax.dot_general(left, right, (dims, ((), ())), preferred_element_type=F32)


NT = ((1,), (1,))
TN = ((0,), (0,))


def params(semantics):
    return pltpu.CompilerParams(dimension_semantics=semantics, vmem_limit_bytes=VMEM)


def swap(array, axis, bits):
    size = lax.axis_size(axis)
    return lax.ppermute(array, axis, [(i, i ^ bits) for i in range(size)])


def bits_of(size):
    return [1 << k for k in reversed(range(size.bit_length() - 1))]


def after(value, *earlier):
    return lax.optimization_barrier((value,) + tuple(earlier))[0]


class Chain:
    def __init__(self):
        self.last = ()

    def __call__(self, *values, wait=()):
        held = lax.optimization_barrier(tuple(values) + tuple(self.last) + tuple(wait))
        return held[: len(values)] if len(values) > 1 else held[0]

    def done(self, *results):
        self.last = results
        return results if len(results) > 1 else results[0]


class Flights:
    def __init__(self, chain):
        self.chain, self.open = chain, []

    def send(self, array, axis, bits):
        self.open.append([swap(array, axis, bits)])
        return self.open[-1]

    def land(self, *values, through=None, only=None):
        if only is None:
            count = len(self.open)
            if through is not None:
                count = sum(i + 1 for i, box in enumerate(self.open) if box is through)
            only = self.open[:count]
        ready = [box for box in self.open if any(box is other for other in only)]
        self.open = [box for box in self.open if not any(box is other for other in ready)]
        held = self.chain(*[box[0] for box in ready], *values)
        held = held if isinstance(held, (tuple, list)) else [held]
        for box, array in zip(ready, held):
            box[0] = array
        rest = list(held[len(ready) :])
        return rest if len(rest) > 1 else rest[0] if rest else None


def in_order(parts, me):
    count = len(parts)
    return jnp.take(jnp.stack([parts[d] for d in range(count)]), me ^ jnp.arange(count), axis=0)


def gather_all(shard):
    parts = {0: shard}
    for bit in bits_of(lax.axis_size("fsdp")):
        parts.update({d | bit: swap(part, "fsdp", bit) for d, part in list(parts.items())})
    return parts


def rel_position(distance, count):
    width = count.bit_length() - 1
    return sum(((distance >> k) & 1) << (width - 1 - k) for k in range(width))


def assemble_kernel(count, rows, single, off_ref, *refs):
    outs = refs[count:]

    def fill(out_ref):
        for distance in range(count):
            start = pl.multiple_of(off_ref[distance], 16)
            out_ref[pl.ds(start, rows), :] = refs[distance][...]

    if single:
        fill(outs[0])
    else:
        pl.when(pl.program_id(0) == 0)(lambda: fill(outs[0]))
        pl.when(pl.program_id(0) > 0)(lambda: fill(outs[1]))


def assemble(parts, me, cut=None):
    count = len(parts)
    rows, cols = parts[0].shape
    if rows % 16:
        full = in_order(parts, me).reshape(count * rows, cols)
        return (full[:, :cut], full[:, cut:]) if cut else full
    offsets = ((me ^ jnp.arange(count, dtype=jnp.int32)) * rows).astype(jnp.int32)
    tile = cut or min(cols, 1152)
    widths = [cut, cols - cut] if cut else [cols]
    maps = [lambda n, off: (0, 0), lambda n, off: (0, jnp.maximum(n - 1, 0))]
    if not cut:
        maps = [lambda n, off: (0, n)]
    outs = pl.pallas_call(
        functools.partial(assemble_kernel, count, rows, not cut),
        out_shape=[jax.ShapeDtypeStruct((count * rows, w), parts[0].dtype) for w in widths],
        grid_spec=pltpu.PrefetchScalarGridSpec(
            num_scalar_prefetch=1,
            grid=(pl.cdiv(cols, tile),),
            in_specs=[pl.BlockSpec((rows, tile), lambda n, off: (0, n))] * count,
            out_specs=[pl.BlockSpec((count * rows, tile), m) for m in maps],
        ),
        compiler_params=params(("arbitrary",)),
        cost_estimate=NOMINAL,
        name="assemble",
    )(offsets, *[parts[d] for d in range(count)])
    return outs if cut else outs[0]


def weight_grad_kernel(pairs, count, rows, pos_ref, *refs):
    lefts, rights = refs[:pairs], refs[pairs : 2 * pairs]
    keep_ref, send_ref, sum_ref = refs[2 * pairs :]
    total = dot(lefts[0][...], rights[0][...], TN)
    for i in range(1, pairs):
        total += dot(lefts[i][...], rights[i][...], TN)
    sum_ref[...] = sum(dot(jnp.ones((8, r.shape[0]), BF16), r[...]) for r in rights)
    for shard in range(count):
        start = pl.multiple_of(pos_ref[shard], 16)
        block = total[shard * rows : (shard + 1) * rows].astype(BF16)

        @pl.when(pos_ref[count] == shard % 2)
        def _():
            keep_ref[pl.ds(start, rows), :] = block

        @pl.when(pos_ref[count] != shard % 2)
        def _():
            send_ref[pl.ds(start, rows), :] = block


def weight_grad(lefts, rights, me, count):
    width = lefts[0].shape[1]
    cols = rights[0].shape[1]
    rows = width // count
    order = me ^ jnp.arange(count, dtype=jnp.int32)
    table = jnp.array([rel_position(d, count) for d in range(count)], jnp.int32)
    half = count // 2
    if rows % 16:
        total = sum(dot(a, b, TN) for a, b in zip(lefts, rights))
        by_distance = jnp.take(total.astype(BF16).reshape(count, rows, cols), order, axis=0)
        back = [0] * count
        for d in range(count):
            back[rel_position(d, count)] = d
        placed = jnp.take(by_distance, jnp.array(back), axis=0).reshape(width, cols)
        ones = [jnp.ones((8, b.shape[0]), BF16) for b in rights]
        sums = sum(dot(one, b) for one, b in zip(ones, rights))
        return placed[: width // 2], placed[width // 2 :], sums
    positions = jnp.concatenate([table[order] % half * rows, (me & 1)[None]]).astype(jnp.int32)
    tile = 256
    pairs = len(lefts)
    return pl.pallas_call(
        functools.partial(weight_grad_kernel, pairs, count, rows),
        out_shape=[jax.ShapeDtypeStruct((width // 2, cols), BF16)] * 2
        + [jax.ShapeDtypeStruct((8, cols), F32)],
        grid_spec=pltpu.PrefetchScalarGridSpec(
            num_scalar_prefetch=1,
            grid=(pl.cdiv(cols, tile),),
            in_specs=[
                pl.BlockSpec(a.shape, lambda n, off: (0, 0), pipeline_mode=pl.Buffered(1))
                for a in lefts
            ]
            + [pl.BlockSpec((b.shape[0], tile), lambda n, off: (0, n)) for b in rights],
            out_specs=[pl.BlockSpec((width // 2, tile), lambda n, off: (0, n))] * 2
            + [pl.BlockSpec((8, tile), lambda n, off: (0, n))],
        ),
        compiler_params=params(("arbitrary",)),
        cost_estimate=NOMINAL,
        name="weight_grad",
    )(positions, *lefts, *rights)


def token_dot(left, right):
    tokens, width = left.shape
    cols = right.shape[1]
    tile = 256

    def kernel(left_ref, right_ref, out_ref):
        out_ref[...] = dot(left_ref[...], right_ref[...], TN).astype(BF16)

    return pl.pallas_call(
        kernel,
        out_shape=jax.ShapeDtypeStruct((width, cols), BF16),
        grid=(pl.cdiv(cols, tile),),
        in_specs=[
            pl.BlockSpec((tokens, width), lambda n: (0, 0), pipeline_mode=pl.Buffered(1)),
            pl.BlockSpec((tokens, tile), lambda n: (0, n)),
        ],
        out_specs=pl.BlockSpec((width, tile), lambda n: (0, n)),
        compiler_params=params(("arbitrary",)),
        cost_estimate=NOMINAL,
        name="token_dot",
    )(left, right)


def normalized(values):
    center = values - jnp.mean(values, axis=-1, keepdims=True)
    spread = jnp.mean(center * center, axis=-1, keepdims=True)
    inverse = lax.rsqrt(spread + EPS)
    return center * inverse, inverse


def row_block(rows):
    return 256 if rows % 256 == 0 else 128 if rows % 128 == 0 else rows


def norm(arrays, gain, shift):
    width = arrays[0].shape[1]
    block = min(row_block(a.shape[0]) for a in arrays)
    steps = [a.shape[0] // block for a in arrays]
    firsts = [sum(steps[:k]) for k in range(len(steps))]
    count, total = len(arrays), sum(steps)

    def kernel(*refs):
        gain_ref, shift_ref, out_ref = refs[count:]
        at = pl.program_id(0)
        for k in range(count):

            @pl.when((at >= firsts[k]) & (at < firsts[k] + steps[k]))
            def _():
                hat, _ = normalized(refs[k][...].astype(F32))
                out_ref[...] = (hat * gain_ref[...] + shift_ref[...]).astype(BF16)

    line = pl.BlockSpec((1, width), lambda i: (0, 0))
    return pl.pallas_call(
        kernel,
        out_shape=jax.ShapeDtypeStruct((total * block, width), BF16),
        grid=(total,),
        in_specs=[
            pl.BlockSpec((block, width), lambda i, k=k: (jnp.clip(i - firsts[k], 0, steps[k] - 1), 0))
            for k in range(count)
        ]
        + [line, line],
        out_specs=pl.BlockSpec((block, width), lambda i: (i, 0)),
        compiler_params=params(("arbitrary",)),
        cost_estimate=NOMINAL,
        name="norm",
    )(*arrays, gain, shift)


def join_kernel(half, core_ref, own_ref, other_ref, x_ref, w_ref, b_ref, g_ref, s_ref, *outs):
    att_ref, mid_ref, out_ref = outs
    own, other = own_ref[:, :half], other_ref[:, :half]

    @pl.when(core_ref[0] == 0)
    def _():
        att_ref[...] = jnp.concatenate([own, other], axis=1)

    @pl.when(core_ref[0] != 0)
    def _():
        att_ref[...] = jnp.concatenate([other, own], axis=1)

    middle = x_ref[...].astype(F32) + dot(att_ref[...], w_ref[...]) + b_ref[...]
    mid_ref[...] = middle
    hat, _ = normalized(middle)
    out_ref[...] = (hat * g_ref[...] + s_ref[...]).astype(BF16)


def join(core, own, other, inputs, weight, bias, gain, shift, half):
    rows, width = inputs.shape
    padded = own.shape[1]
    block = row_block(rows)
    line = pl.BlockSpec((1, width), lambda i, c: (0, 0))
    wide = pl.BlockSpec((block, width), lambda i, c: (i, 0))
    part = pl.BlockSpec((block, padded), lambda i, c: (i, 0))
    return pl.pallas_call(
        functools.partial(join_kernel, half),
        out_shape=(
            jax.ShapeDtypeStruct((rows, width), BF16),
            jax.ShapeDtypeStruct((rows, width), F32),
            jax.ShapeDtypeStruct((rows, width), BF16),
        ),
        grid_spec=pltpu.PrefetchScalarGridSpec(
            num_scalar_prefetch=1,
            grid=(rows // block,),
            in_specs=[
                part,
                part,
                wide,
                pl.BlockSpec((width, width), lambda i, c: (0, 0), pipeline_mode=pl.Buffered(1)),
                line,
                line,
                line,
            ],
            out_specs=(wide, wide, wide),
        ),
        compiler_params=params(("arbitrary",)),
        cost_estimate=NOMINAL,
        name="join",
    )(core, own, other, inputs, weight, bias, gain, shift)


def norm_back_values(x_ref, grads, gain_ref, add_ref, lines_ref):
    hat, inverse = normalized(x_ref[...].astype(F32))
    grad = grads[0][...].astype(F32)
    for other in grads[1:]:
        grad += other[...].astype(F32)
    scaled = grad * gain_ref[...]
    first = jnp.mean(scaled, axis=-1, keepdims=True)
    second = jnp.mean(scaled * hat, axis=-1, keepdims=True)

    @pl.when(pl.program_id(0) == 0)
    def _():
        lines_ref[...] = jnp.zeros_like(lines_ref)

    lines_ref[0:1] += jnp.sum(grad * hat, axis=0, keepdims=True)
    lines_ref[1:2] += jnp.sum(grad, axis=0, keepdims=True)
    return add_ref[...].astype(F32) + inverse * (scaled - first - hat * second)


def first_back(core, values, grads, gain, add, q_sums, kv_sums, half):
    rows, width = values.shape
    padded = q_sums.shape[1]
    pieces = [grad for grad in grads if isinstance(grad, tuple)]
    whole_grads = [grad for grad in grads if not isinstance(grad, tuple)]
    block = min([row_block(rows)] + [row_block(part.shape[0]) for pair in pieces for part in pair])
    count = len(whole_grads) + 2 * len(pieces)
    flat_grads = whole_grads + [part for pair in pieces for part in pair]

    def kernel(core_ref, x_ref, *refs):
        gain_ref, add_ref, q_ref, kv_ref, dx_ref, lines_ref = refs[count:]
        sums = list(refs[: len(whole_grads)])
        for k, pair in enumerate(pieces):
            low, high = refs[len(whole_grads) + 2 * k : len(whole_grads) + 2 * k + 2]
            first = pl.program_id(0) < pair[0].shape[0] // block
            sums.append(jnp.where(first, low[...].astype(F32), high[...].astype(F32)))
        dx_ref[...] = norm_back_values(x_ref, sums, gain_ref, add_ref, lines_ref)
        for line, part in ((2, q_ref[0:1, :half]), (3, kv_ref[0:1, padded : padded + half])):
            none = jnp.zeros_like(part)

            @pl.when(core_ref[0] == 0)
            def _():
                lines_ref[line : line + 1] = jnp.concatenate([part, none], axis=1)

            @pl.when(core_ref[0] != 0)
            def _():
                lines_ref[line : line + 1] = jnp.concatenate([none, part], axis=1)

    def piece_specs(pair):
        steps = pair[0].shape[0] // block
        return [
            pl.BlockSpec((block, width), lambda i, c: (jnp.minimum(i, steps - 1), 0)),
            pl.BlockSpec((block, width), lambda i, c: (jnp.maximum(i - steps, 0), 0)),
        ]

    wide = pl.BlockSpec((block, width), lambda i, c: (i, 0))
    return pl.pallas_call(
        kernel,
        out_shape=(
            jax.ShapeDtypeStruct((rows, width), F32),
            jax.ShapeDtypeStruct((8, width), F32),
        ),
        grid_spec=pltpu.PrefetchScalarGridSpec(
            num_scalar_prefetch=1,
            grid=(rows // block,),
            in_specs=[wide] * (1 + len(whole_grads))
            + [spec for pair in pieces for spec in piece_specs(pair)]
            + [
                pl.BlockSpec((1, width), lambda i, c: (0, 0)),
                wide,
                pl.BlockSpec(q_sums.shape, lambda i, c: (0, 0)),
                pl.BlockSpec(kv_sums.shape, lambda i, c: (0, 0)),
            ],
            out_specs=(wide, pl.BlockSpec((8, width), lambda i, c: (0, 0))),
        ),
        compiler_params=params(("arbitrary",)),
        cost_estimate=NOMINAL,
        name="first_back",
    )(core, values, *flat_grads, gain, add, q_sums, kv_sums)


def second_back(core, values, grads, gain, add, weight, hidden_line, half, padded):
    rows, width = values.shape
    block = row_block(rows)
    count = len(grads)

    def kernel(core_ref, x_ref, *refs):
        gain_ref, add_ref, w_ref, hid_ref, dx_ref, low_ref, mine_ref, send_ref, lines_ref = refs[count:]
        total = norm_back_values(x_ref, refs[:count], gain_ref, add_ref, lines_ref)
        low = total.astype(BF16)
        dx_ref[...] = total
        low_ref[...] = low
        lines_ref[2:3] += jnp.sum(low.astype(F32), axis=0, keepdims=True)
        lines_ref[3:4] += jnp.sum(add_ref[...].astype(F32), axis=0, keepdims=True)
        spare = hid_ref.shape[1] - width
        for core in range(2):

            @pl.when(core_ref[0] == core)
            def _():
                lines_ref[4 + 2 * core : 5 + 2 * core] = hid_ref[:, :width]
                lines_ref[5 + 2 * core : 6 + 2 * core, :spare] = hid_ref[:, width:]

        back = dot(low, w_ref[...], NT).astype(BF16)
        empty = jnp.zeros((block, padded - half), BF16)
        halves = [jnp.concatenate([back[:, i * half : (i + 1) * half], empty], axis=1) for i in range(2)]

        @pl.when(core_ref[0] == 0)
        def _():
            mine_ref[...], send_ref[...] = halves[0], halves[1]

        @pl.when(core_ref[0] != 0)
        def _():
            mine_ref[...], send_ref[...] = halves[1], halves[0]

    wide = pl.BlockSpec((block, width), lambda i, c: (i, 0))
    part = pl.BlockSpec((block, padded), lambda i, c: (i, 0))
    line = pl.BlockSpec((1, width), lambda i, c: (0, 0))
    square = pl.BlockSpec((width, width), lambda i, c: (0, 0), pipeline_mode=pl.Buffered(1))
    return pl.pallas_call(
        kernel,
        out_shape=(
            jax.ShapeDtypeStruct((rows, width), F32),
            jax.ShapeDtypeStruct((rows, width), BF16),
            jax.ShapeDtypeStruct((rows, padded), BF16),
            jax.ShapeDtypeStruct((rows, padded), BF16),
            jax.ShapeDtypeStruct((8, width), F32),
        ),
        grid_spec=pltpu.PrefetchScalarGridSpec(
            num_scalar_prefetch=1,
            grid=(rows // block,),
            in_specs=[wide] * (1 + count)
            + [line, wide, square, pl.BlockSpec(hidden_line.shape, lambda i, c: (0, 0))],
            out_specs=(wide, wide, part, part, pl.BlockSpec((8, width), lambda i, c: (0, 0))),
        ),
        compiler_params=params(("arbitrary",)),
        cost_estimate=NOMINAL,
        name="second_back",
    )(core, values, *grads, gain, add, weight, hidden_line)


def rows_matmul(name, lefts, weights, finish, extras, outs, dims=((1,), (0,)), split=False, first_row=0):
    rows = outs[0].shape[0]
    block = 384 if split and rows % 768 == 0 else 512 if not split and rows % 512 == 0 else row_block(rows)
    steps = rows // block
    half = steps // 2
    count, terms = len(lefts), len(lefts) + len(weights)

    def kernel(*refs):
        total = dot(refs[0][...], refs[count][...], dims)
        for i in range(1, count):
            total += dot(refs[i][...], refs[count + i][...], dims)
        results = finish(total, *refs[terms : terms + len(extras)])
        targets = refs[terms + len(extras) :]
        if split:

            @pl.when(pl.program_id(0) < half)
            def _():
                targets[0][...] = results[0]

            @pl.when(pl.program_id(0) >= half)
            def _():
                targets[1][...] = results[0]

            targets = targets[1:]
        else:
            targets[0][...] = results[0]
        for target, result in zip(targets[1:], results[1:]):

            @pl.when(pl.program_id(0) == 0)
            def _():
                target[...] = jnp.zeros_like(target)

            target[...] += result

    def by_rows(array):
        return pl.BlockSpec((block, array.shape[1]), lambda i: (i, 0))

    def whole(array):
        return pl.BlockSpec(array.shape, lambda i: (0, 0), pipeline_mode=pl.Buffered(1))

    first = outs[0]
    if split:
        part = jax.ShapeDtypeStruct((rows // 2, first.shape[1]), first.dtype)
        shapes = [part, part] + list(outs[1:])
        specs = [
            pl.BlockSpec((block, first.shape[1]), lambda i: (jnp.minimum(i, half - 1), 0)),
            pl.BlockSpec((block, first.shape[1]), lambda i: (jnp.maximum(i - half, 0), 0)),
        ]
    else:
        shapes, specs = list(outs), [by_rows(first)]
    specs += [pl.BlockSpec(out.shape, lambda i: (0, 0)) for out in outs[1:]]
    return pl.pallas_call(
        kernel,
        out_shape=shapes,
        grid=(steps,),
        in_specs=[
            pl.BlockSpec((block, a.shape[1]), lambda i: (i + first_row // block, 0)) for a in lefts
        ]
        + [whole(w) for w in weights]
        + [by_rows(e) if e.shape[0] == rows else whole(e) for e in extras],
        out_specs=specs,
        compiler_params=params(("arbitrary",)),
        cost_estimate=NOMINAL,
        name=name,
    )(*lefts, *weights, *extras)


def like(rows, cols, kind=BF16):
    return jax.ShapeDtypeStruct((rows, cols), kind)


def plain(total):
    return (total.astype(BF16),)


def with_bias(total, bias_ref):
    return ((total + bias_ref[...]).astype(BF16),)


def with_slope(total, slope_ref):
    low = (total * slope_ref[...].astype(F32)).astype(BF16)
    return low, jnp.sum(low.astype(F32), axis=0, keepdims=True)


def layer_end(total, middle_ref, other_ref, bias_ref):
    return ((middle_ref[...] + total + other_ref[...].astype(F32) + bias_ref[...]).astype(BF16),)


def small_call(kernel, outs, scalars, arrays, name):
    vmem = pl.BlockSpec(memory_space=pltpu.VMEM)
    return pl.pallas_call(
        kernel,
        out_shape=outs,
        in_specs=[pl.BlockSpec(memory_space=pltpu.SMEM)] * len(scalars) + [vmem] * len(arrays),
        out_specs=[vmem] * len(outs),
        compiler_params=pltpu.CompilerParams(vmem_limit_bytes=VMEM),
        cost_estimate=NOMINAL,
        name=name,
    )(*scalars, *arrays)


def add_rows(left, right, kind=BF16, pieces=1):
    size = left.shape[0] // pieces
    parts = [slice(i * size, (i + 1) * size) for i in range(pieces)]
    return [(left[part].astype(F32) + right[part].astype(F32)).astype(kind) for part in parts]


def scatter_step(keep, arrived, rows):
    if keep.shape[0] == rows:
        return add_rows(keep, arrived)[0], None
    return add_rows(keep, arrived, BF16, 2)


def both_cores(core, mine, other, size, total, start=0, turn=False):
    rows = mine.shape[0]

    def kernel(core_ref, mine_ref, other_ref, out_ref):
        for at, refs in ((0, (mine_ref, other_ref)), (1, (other_ref, mine_ref))):

            @pl.when(core_ref[0] == at)
            def _():
                first = refs[0][:, start : start + size]
                second = refs[1][:, start : start + total - size]
                if turn:
                    out_ref[:size], out_ref[size:] = first.T, second.T
                else:
                    out_ref[...] = jnp.concatenate([first, second], axis=1)

    shape = like(total, rows, mine.dtype) if turn else like(rows, total, mine.dtype)
    return small_call(kernel, [shape], [core], [mine, other], "both_cores")[0]


def both_columns(is_first, mine, other, size, total, start=0):
    mine, other = mine[:, start:], other[:, start:]
    return jnp.where(
        is_first,
        jnp.concatenate([mine[:, :size], other[:, : total - size]], axis=1),
        jnp.concatenate([other[:, :size], mine[:, : total - size]], axis=1),
    )


def core_columns(core, arrays, cols):
    rows, width = arrays[0].shape

    def kernel(core_ref, *refs):
        for at in range(2):

            @pl.when(core_ref[0] == at)
            def _():
                for i in range(len(arrays)):
                    for k, where in enumerate((at, 1 - at)):
                        low = where * (width - cols)
                        refs[len(arrays) * (1 + k) + i][...] = refs[i][:, low : low + cols]

    return small_call(kernel, [like(rows, cols)] * (2 * len(arrays)), [core], arrays, "core_columns")


def mask_kernel(rows, tokens, blocks, len_ref, place_ref, need_ref, row_ref, col_ref, near_row, near_col):
    place = place_ref[0]
    for row in range(rows):
        ends = [len_ref[row, 0]]
        for p in range(1, len_ref.shape[1]):
            ends.append(ends[-1] + len_ref[row, p])

        def pictures(position):
            return sum((position >= end).astype(jnp.int32) for end in ends)

        def segment(position):
            return jnp.where(position < ends[-1], pictures(position), 1000 + position)

        spans = []
        for block in range(blocks):
            start = jnp.bitwise_xor(place, block) * tokens
            across = segment(start + lax.broadcasted_iota(jnp.int32, (1, tokens), 1))
            down = segment(start + lax.broadcasted_iota(jnp.int32, (tokens, 1), 0))
            row_ref[row, block : block + 1] = across
            col_ref[row, block] = down
            if block < 2:
                near_row[row, :, block * tokens : (block + 1) * tokens] = across
                near_col[row, block * tokens : (block + 1) * tokens] = down
            last = jnp.minimum(start + tokens, ends[-1]) - 1
            low = sum(jnp.where(start >= end, 1, 0) for end in ends)
            high = sum(jnp.where(last >= end, 1, 0) for end in ends)
            spans.append((start < ends[-1], low, high))
        for block, (real, low, high) in enumerate(spans):
            if block < 2:
                need_ref[row, block] = 1
            else:
                need_ref[row, block] = sum(
                    jnp.where(real & ok & (low <= top) & (bottom <= high), 1, 0) for ok, bottom, top in spans[:2]
                )


def masks(lengths, place, blocks, tokens):
    rows = lengths.shape[0]
    shapes = [(rows, blocks, tokens), (rows, blocks, tokens, 1), (rows, 1, 2 * tokens), (rows, 2 * tokens, 1)]
    smem = pl.BlockSpec(memory_space=pltpu.SMEM)
    return pl.pallas_call(
        functools.partial(mask_kernel, rows, tokens, blocks),
        out_shape=[jax.ShapeDtypeStruct((rows, blocks), jnp.int32)]
        + [jax.ShapeDtypeStruct(shape, jnp.int32) for shape in shapes],
        in_specs=[smem, smem],
        out_specs=[smem] + [pl.BlockSpec(memory_space=pltpu.VMEM)] * 4,
        compiler_params=pltpu.CompilerParams(vmem_limit_bytes=VMEM),
        cost_estimate=NOMINAL,
        name="masks",
    )(lengths, place)


def lay_vectors(core, weight, lines, half, padded):
    width, cols = weight.shape
    low = half // 128 * 128

    def kernel(core_ref, weight_ref, lines_ref, q_ref, kv_ref):
        turned = weight_ref[...].astype(F32).T
        lines_ref[...] = turned[half - low : half - low + lines]
        q_ref[...] = jnp.zeros_like(q_ref)
        kv_ref[...] = jnp.zeros_like(kv_ref)
        for at in range(2):

            @pl.when(core_ref[0] == at)
            def _():
                q_ref[:, :half] = lines_ref[2:3, at * half : (at + 1) * half]
                kv_ref[:, padded : padded + half] = lines_ref[3:4, at * half : (at + 1) * half]

    outs = [like(lines, width, F32), like(1, padded, F32), like(1, 2 * padded, F32)]
    block = cols - low
    return pl.pallas_call(
        kernel,
        out_shape=outs,
        grid=(1,),
        in_specs=[
            pl.BlockSpec(memory_space=pltpu.SMEM),
            pl.BlockSpec((width, block), lambda i: (0, low // block)),
        ],
        out_specs=[pl.BlockSpec(out.shape, lambda i: (0, 0)) for out in outs],
        compiler_params=params(("arbitrary",)),
        cost_estimate=NOMINAL,
        name="lay_vectors",
    )(core, weight)


def mlp_shards(core, out_shard, hidden_weight, down_weight, cols):
    rows, total = hidden_weight.shape
    before = out_shard.shape[1]

    def kernel(core_ref, part_ref, hidden_ref, down_ref, first_out, down_out):
        first_out[:, :before] = part_ref[...]
        for at in range(2):

            @pl.when(core_ref[0] == at)
            def _():
                low = at * cols
                high = min(low + cols, total)
                size = high - low
                first_out[:, before : before + size] = hidden_ref[:, low:high]
                down_out[:, :size] = down_ref[low:high].T
                if size < cols:
                    empty = jnp.zeros((rows, cols - size), BF16)
                    first_out[:, before + size :] = empty
                    down_out[:, size:] = empty

    outs = [like(rows, before + cols), like(rows, cols)]
    return small_call(kernel, outs, [core], [out_shard, hidden_weight, down_weight], "mlp_shards")


def attention_shards(core, weights, vectors, half, padded):
    rows, width = weights[0].shape
    cut = width - padded
    count = len(vectors)

    def kernel(core_ref, q_ref, k_ref, v_ref, o_ref, *refs):
        qkv_ref, out_ref, held = refs[count:]
        for i in range(count):
            held[i : i + 1] = refs[i][...].astype(F32).reshape(1, rows)
        empty = jnp.zeros((rows, padded - half), BF16)
        spare = jnp.zeros((rows, padded - half - count), BF16)
        lines = jnp.concatenate([held[...].T.astype(BF16), spare], axis=1)
        for at in range(2):

            @pl.when(core_ref[0] == at)
            def _():
                for i, ref in enumerate((q_ref, k_ref, v_ref)):
                    part = ref[:, at * half : (at + 1) * half]
                    rest = empty if i else lines
                    qkv_ref[:, i * padded : (i + 1) * padded] = jnp.concatenate([part, rest], axis=1)
                out_ref[...] = o_ref[:, at * cut : at * cut + padded]

    vmem = pl.BlockSpec(memory_space=pltpu.VMEM)
    return pl.pallas_call(
        kernel,
        out_shape=[like(rows, 3 * padded), like(rows, padded)],
        in_specs=[pl.BlockSpec(memory_space=pltpu.SMEM)] + [vmem] * (4 + count),
        out_specs=[vmem] * 2,
        scratch_shapes=[pltpu.VMEM((count, rows), F32)],
        compiler_params=pltpu.CompilerParams(vmem_limit_bytes=VMEM),
        cost_estimate=NOMINAL,
        name="attention_shards",
    )(core, *weights, *vectors)


def hidden(arrays, weight, bias):
    rows, width = arrays[0].shape
    cols = weight.shape[1]
    block = row_block(rows)
    steps, count = rows // block, len(arrays)

    def kernel(*refs):
        w_ref, b_ref, act_ref, slope_ref, x_ref = refs[count:]
        for i in range(count):

            @pl.when(pl.program_id(0) // steps == i)
            def _():
                x_ref[...] = refs[i][...]

        pre = dot(x_ref[...], w_ref[...]) + b_ref[...]
        square = pre * pre
        turn = jnp.tanh(pre * (GELU_COEF + GELU_COEF * 0.044715 * square))
        act_ref[...] = (0.5 * pre * (1.0 + turn)).astype(BF16)
        inner = GELU_COEF + 3.0 * 0.044715 * GELU_COEF * square
        slope_ref[...] = (0.5 * (1.0 + turn) * (1.0 + pre * (1.0 - turn) * inner)).astype(BF16)

    out = pl.BlockSpec((block, cols), lambda i: (i, 0))
    return pl.pallas_call(
        kernel,
        out_shape=(
            jax.ShapeDtypeStruct((count * rows, cols), BF16),
            jax.ShapeDtypeStruct((count * rows, cols), BF16),
            jax.ShapeDtypeStruct((count * rows, width), BF16),
        ),
        grid=(count * steps,),
        in_specs=[
            pl.BlockSpec((block, width), lambda i, k=k: (jnp.clip(i - k * steps, 0, steps - 1), 0))
            for k in range(count)
        ]
        + [
            pl.BlockSpec((width, cols), lambda i: (0, 0), pipeline_mode=pl.Buffered(1)),
            pl.BlockSpec((1, cols), lambda i: (0, 0)),
        ],
        out_specs=(out, out, pl.BlockSpec((block, width), lambda i: (i, 0))),
        compiler_params=params(("arbitrary",)),
        cost_estimate=NOMINAL,
        name="hidden",
    )(*arrays, weight, bias)


def head_window(head):
    first = head * HEAD_DIM
    start = first // 128 * 128
    return start, round_up(first + HEAD_DIM, 128) - start, first - start


def head_lanes(rows, width, low):
    lane = lax.broadcasted_iota(jnp.int32, (rows, width), 1)
    return (lane >= low) & (lane < low + HEAD_DIM)


def only_head(block, low):
    mine = head_lanes(*block.shape, low)
    return jnp.where(mine, block.astype(F32), 0.0).astype(BF16)


def pick_block(near_ref, far_ref, block):
    return near_ref.at[block, 0] if block < 2 else far_ref.at[block - 2, 0]


def attend_kernel(row, heads, blocks, padded, need_ref, col_ref, row_ref, q_ref, near_ref, far_ref, *refs):
    own_ref, pair_ref, lse_ref, queries, score, peak, total, acc, lses = refs[-9:]
    outs = (own_ref, pair_ref)
    tokens = own_ref.shape[1]
    slot = lax.broadcasted_iota(jnp.int32, (2 * tokens, 128), 1)
    for which in range(2):
        outs[which][...] = jnp.zeros_like(outs[which])
    windows = [head_window(head) for head in range(heads)]
    for head, (start, width, low) in enumerate(windows):
        for which in range(2):
            queries[head, which * tokens : (which + 1) * tokens, :width] = only_head(
                q_ref[which, 0, :, start : start + width], low
            )
    peak[...] = jnp.full_like(peak, MASKED)
    total[...] = jnp.zeros_like(total)
    acc[...] = jnp.zeros_like(acc)
    for block in range(blocks):

        @pl.when(need_ref[row, block] != 0)
        def _():
            side = pick_block(near_ref, far_ref, block)
            seen = col_ref[0] == row_ref[0, block : block + 1]
            for head, (start, width, _) in enumerate(windows):
                key = side[:, start : start + width]
                found = jnp.where(seen, dot(queries[head, :, :width], key, NT), MASKED)
                score[head, block] = found
                top = peak[head]
                for at in range(0, tokens, 128):
                    top = jnp.maximum(top, found[:, at : at + 128])
                peak[head] = top

    for head in range(heads):
        top = jnp.max(peak[head], axis=-1, keepdims=True) * (SCALE * LOG2E)
        peak[head] = jnp.broadcast_to(top, peak.shape[1:])

    for block in range(blocks):

        @pl.when(need_ref[row, block] != 0)
        def _():
            side = pick_block(near_ref, far_ref, block)
            for head, (start, width, _) in enumerate(windows):
                top, share = peak[head], total[head]
                pieces = []
                for at in range(0, tokens, 128):
                    part = jnp.exp2(score[head, block, :, at : at + 128] * (SCALE * LOG2E) - top)
                    share += part
                    pieces.append(part.astype(BF16))
                total[head] = share
                value = side[:, padded + start : padded + start + width]
                acc[head, :, :width] += dot(jnp.concatenate(pieces, axis=1), value)

    for head, (start, width, low) in enumerate(windows):
        norm = jnp.sum(total[head], axis=-1, keepdims=True)
        result = acc[head, :, :width] / norm
        mine = head_lanes(tokens, width, low)
        for which in range(2):
            kept = outs[which][0, :, start : start + width].astype(F32)
            fresh = result[which * tokens : (which + 1) * tokens]
            outs[which][0, :, start : start + width] = jnp.where(mine, fresh, kept).astype(BF16)
        lse = peak[head] + jnp.log2(norm)
        lses[...] = lse if head == 0 else jnp.where(slot == head, lse, lses[...])
    lse_ref[0] = lses[...].T[:heads]


def attend(row, query, near, far, need, seg_col, seg_row, heads, before):
    _, rows, tokens, padded = query.shape
    blocks = 2 + far.shape[0]
    narrow = pl.BlockSpec((1, tokens, padded), lambda i, need: (row, 0, 0))
    lines = pl.BlockSpec((1, heads, 2 * tokens), lambda i, need: (row, 0, 0))

    def stack(count, width):
        return pl.BlockSpec((count, 1, tokens, width), lambda i, need: (0, row, 0, 0))

    return pl.pallas_call(
        functools.partial(attend_kernel, row, heads, blocks, padded),
        out_shape=(
            jax.ShapeDtypeStruct((rows, tokens, padded), BF16),
            jax.ShapeDtypeStruct((rows, tokens, padded), BF16),
            jax.ShapeDtypeStruct((rows, heads, 2 * tokens), F32),
        ),
        grid_spec=pltpu.PrefetchScalarGridSpec(
            num_scalar_prefetch=1,
            grid=(1,),
            in_specs=[
                pl.BlockSpec((1, 2 * tokens, 1), lambda i, need: (row, 0, 0)),
                pl.BlockSpec((1, blocks, tokens), lambda i, need: (row, 0, 0)),
                stack(2, padded),
                stack(2, 2 * padded),
                stack(blocks - 2, 2 * padded),
            ]
            + [pl.BlockSpec(memory_space=pl.ANY)] * len(before),
            out_specs=(narrow, narrow, lines),
            scratch_shapes=[
                pltpu.VMEM((heads, 2 * tokens, WIN), BF16),
                pltpu.VMEM((heads, blocks, 2 * tokens, tokens), F32),
                pltpu.VMEM((heads, 2 * tokens, 128), F32),
                pltpu.VMEM((heads, 2 * tokens, 128), F32),
                pltpu.VMEM((heads, 2 * tokens, WIN), F32),
                pltpu.VMEM((2 * tokens, 128), F32),
            ],
        ),
        input_output_aliases={6 + i: i for i in range(len(before))},
        compiler_params=params(("arbitrary",)),
        cost_estimate=NOMINAL,
        name="attend",
    )(need, seg_col, seg_row, query, near, far, *before)


def attend_back_kernel(
    row, heads, blocks, padded, need_ref, col_ref, row_ref, pick_ref, q_ref, near_ref, far_ref, *refs
):
    grads, outs, lse_ref = refs[0:2], refs[2:4], refs[4]
    dq_ref, dnear_ref, dfar_ref, sums, inner_turn, queries, incoming, dq = refs[-8:]
    tokens = grads[0].shape[1]
    sums[...] = jnp.zeros_like(sums)
    for which in range(2):
        dq_ref[which, 0] = jnp.zeros((tokens, padded), BF16)
        product = grads[which][0].astype(F32) * outs[which][0].astype(F32)
        high = product.astype(BF16)
        rest = (product - high.astype(F32)).astype(BF16)
        inner_turn[:, which * tokens : (which + 1) * tokens] = dot(pick_ref[...], high, NT) + dot(
            pick_ref[...], rest, NT
        )
    windows = [head_window(head) for head in range(heads)]
    for head, (start, width, low) in enumerate(windows):
        for which in range(2):
            there = slice(which * tokens, (which + 1) * tokens)
            here = slice(start, start + width)
            queries[head, there, :width] = only_head(q_ref[which, 0, :, here], low)
            incoming[head, there, :width] = only_head(grads[which][0, :, here], low)
    dq[...] = jnp.zeros_like(dq)
    for block in range(blocks):

        @pl.when(need_ref[row, block] != 0)
        def _():
            side = pick_block(near_ref, far_ref, block)
            seen = col_ref[0, block] == row_ref[0]
            for head, (start, width, _) in enumerate(windows):
                end = start + width
                key, value = side[:, start:end], side[:, padded + start : padded + end]
                query, grad = queries[head, :, :width], incoming[head, :, :width]
                found = dot(key, query, NT) * (SCALE * LOG2E) - lse_ref[0, head : head + 1, :]
                prob = jnp.where(seen, jnp.exp2(found), 0.0)
                inner = inner_turn[head : head + 1, :]
                slope = (prob * (dot(value, grad, NT) - inner)).astype(BF16)
                sums[block, :, start:end] += dot(slope, query)
                sums[block, :, padded + start : padded + end] += dot(prob.astype(BF16), grad)
                dq[head, :, :width] += dot(slope, key, TN)

    for head, (start, width, low) in enumerate(windows):
        mine = head_lanes(tokens, width, low)
        for which in range(2):
            kept = dq_ref[which, 0, :, start : start + width].astype(F32)
            fresh = dq[head, which * tokens : (which + 1) * tokens, :width] * SCALE
            dq_ref[which, 0, :, start : start + width] = jnp.where(mine, fresh, kept).astype(BF16)
    for block in range(blocks):
        side = pick_block(dnear_ref, dfar_ref, block)
        side[:, :padded] = (sums[block, :, :padded] * SCALE).astype(BF16)
        side[:, padded:] = sums[block, :, padded:].astype(BF16)


def attend_back(row, query, near, far, grads, outs, lse, need, seg_col, seg_row, heads, before):
    _, rows, tokens, padded = query.shape
    blocks = 2 + far.shape[0]
    column = lax.broadcasted_iota(jnp.int32, (heads, padded), 1)
    pick = (column // HEAD_DIM == lax.broadcasted_iota(jnp.int32, (heads, padded), 0)).astype(BF16)
    narrow = pl.BlockSpec((1, tokens, padded), lambda i, need: (row, 0, 0))

    def stack(count, width):
        return pl.BlockSpec((count, 1, tokens, width), lambda i, need: (0, row, 0, 0))

    return pl.pallas_call(
        functools.partial(attend_back_kernel, row, heads, blocks, padded),
        out_shape=tuple(jax.ShapeDtypeStruct(a.shape, BF16) for a in (query, near, far)),
        grid_spec=pltpu.PrefetchScalarGridSpec(
            num_scalar_prefetch=1,
            grid=(1,),
            in_specs=[
                pl.BlockSpec((1, blocks, tokens, 1), lambda i, need: (row, 0, 0, 0)),
                pl.BlockSpec((1, 1, 2 * tokens), lambda i, need: (row, 0, 0)),
                pl.BlockSpec((heads, padded), lambda i, need: (0, 0)),
                stack(2, padded),
                stack(2, 2 * padded),
                stack(blocks - 2, 2 * padded),
            ]
            + [narrow] * 4
            + [pl.BlockSpec((1, heads, 2 * tokens), lambda i, need: (row, 0, 0))]
            + [pl.BlockSpec(memory_space=pl.ANY)] * len(before),
            out_specs=(stack(2, padded), stack(2, 2 * padded), stack(blocks - 2, 2 * padded)),
            scratch_shapes=[
                pltpu.VMEM((blocks, tokens, 2 * padded), F32),
                pltpu.VMEM((heads, 2 * tokens), F32),
                pltpu.VMEM((heads, 2 * tokens, WIN), BF16),
                pltpu.VMEM((heads, 2 * tokens, WIN), BF16),
                pltpu.VMEM((heads, 2 * tokens, WIN), F32),
            ],
        ),
        input_output_aliases={12 + i: i for i in range(len(before))},
        compiler_params=params(("arbitrary",)),
        cost_estimate=NOMINAL,
        name="attend_back",
    )(need, seg_col, seg_row, pick, query, near, far, *grads, *outs, lse, *before)


def local(
    patches,
    lengths,
    first_gain,
    first_shift,
    query_weight,
    query_bias,
    key_weight,
    value_weight,
    value_bias,
    output_weight,
    output_bias,
    second_gain,
    second_shift,
    hidden_weight,
    hidden_bias,
    down_weight,
    down_bias,
    cotangent,
):
    seq_count, shards = lax.axis_size("seq"), lax.axis_size("fsdp")
    place, me = lax.axis_index("seq"), lax.axis_index("fsdp")
    core = place & 1
    is_first = core == 0
    core_flag = core[None].astype(jnp.int32)
    rows, tokens, width = patches.shape
    flat = rows * tokens
    heads = width // HEAD_DIM // 2
    half = heads * HEAD_DIM
    padded = round_up(half, 128)
    ff = hidden_bias.shape[0]
    ff_half = round_up(ff, 256) // 2
    out_cols = padded
    out_cut = width - padded
    shard_rows = width // shards
    chain = Chain()

    def my_half(array, size, padded_size):
        first, second = array[..., :size], array[..., size:]
        grow = [(0, 0)] * (array.ndim - 1)
        first = jnp.pad(first, grow + [(0, padded_size - size)])
        second = jnp.pad(second, grow + [(0, padded_size - second.shape[-1])])
        return jnp.where(is_first, first, second)

    flights = Flights(chain)
    staged = shards == 8 and seq_count == 4
    y, z, zz = 1, 2, 4
    top = bits_of(seq_count)[0]

    inputs = patches.reshape(flat, width)
    incoming = cotangent.reshape(flat, width)
    vectors = [
        first_gain,
        first_shift,
        query_bias,
        value_bias,
        output_bias,
        second_gain,
        second_shift,
        down_bias,
    ]
    shard_qkv, shard_out = chain.done(
        *attention_shards(
            core_flag, [query_weight, key_weight, value_weight, output_weight], vectors, half, padded
        )
    )
    place_flag = place[None].astype(jnp.int32)

    def over(box_from, bits):
        return flights.send(box_from[0], "fsdp", bits)

    if staged:
        q = {0: [shard_qkv]}
        q[y] = over(q[0], y)
        q[z], q[zz] = over(q[0], z), over(q[0], zz)
        incoming_pair = flights.send(incoming, "seq", 1)
        shard_ho, shard_down = chain.done(
            *mlp_shards(core_flag, shard_out, hidden_weight, down_weight, ff_half)
        )
        h, d = {0: [shard_ho]}, {0: [shard_down]}
        need, seg_rows, seg_cols, seg_near_row, seg_near_col = chain.done(
            *masks(chain(lengths), place_flag, seq_count, tokens)
        )
        core_flag, raw_own = flights.land(core_flag, inputs)
        q[zz | z], q[z | y], q[zz | y] = over(q[zz], z), over(q[z], y), over(q[zz], y)
        far_raw = [flights.send(raw_own, "seq", 2)]
        raw_pair = flights.send(raw_own, "seq", 1)
        core_flag, incoming_pair[0] = flights.land(core_flag, incoming_pair[0], only=[q[zz | z]])
        q[zz | z | y] = over(q[zz | z], y)
        incoming_near = chain.done(jnp.concatenate([incoming, incoming_pair[0]], axis=0))
        core_flag, shard_ho = flights.land(core_flag, shard_ho, only=[q[z | y], q[zz | y], raw_pair])
        h[0] = [shard_ho]
        h[z], h[y] = over(h[0], z), over(h[0], y)
        core_flag, shard_ho, shard_down = flights.land(
            core_flag, shard_ho, shard_down, only=[q[zz | z | y], far_raw[0]]
        )
        h[0], d[0] = [shard_ho], [shard_down]
        far_pair = [flights.send(far_raw[0][0], "seq", 1)]
        h[zz] = over(h[0], zz)
        w_q, w_kv = chain.done(*assemble({k: box[0] for k, box in q.items()}, me, padded))
        stacked, bias_q, bias_kv = chain.done(
            *lay_vectors(chain(core_flag), w_q, len(vectors), half, padded)
        )
        gain_one, shift_one = stacked[0:1], stacked[1:2]
        gain_one = chain(gain_one)
        normed_near = chain.done(norm([inputs, raw_pair[0]], gain_one, shift_one))
        bias_hidden = my_half(after(hidden_bias, gain_one).astype(F32)[None], ff_half, ff_half)
    else:
        parts = gather_all(shard_qkv)
        shard_ho, shard_down = mlp_shards(core_flag, shard_out, hidden_weight, down_weight, ff_half)
        raw = {0: inputs}
        for bit in bits_of(seq_count):
            raw.update({j | bit: swap(part, "seq", bit) for j, part in list(raw.items())})
        need, seg_rows, seg_cols, seg_near_row, seg_near_col = masks(lengths, place_flag, seq_count, tokens)
        w_q, w_kv = chain.done(*assemble(parts, me, padded))
        stacked, bias_q, bias_kv = lay_vectors(core_flag, w_q, len(vectors), half, padded)
        gain_one, shift_one = stacked[0:1], stacked[1:2]
        normed_near = norm([raw[0], raw[1]], gain_one, shift_one)
        far_raw, far_pair = [[raw[j]] for j in range(2, seq_count)], []
        incoming_near = jnp.concatenate([incoming, swap(incoming, "seq", 1)], axis=0)
        bias_hidden = my_half(hidden_bias.astype(F32)[None], ff_half, ff_half)
    _, _, bias_query, bias_value, bias_output, gain_two, shift_two, bias_down = [
        stacked[i : i + 1] for i in range(8)
    ]

    near_in, w_q, w_kv = chain(normed_near, w_q, w_kv)
    (query,) = rows_matmul("query", [near_in], [w_q], with_bias, [bias_q], [like(2 * flat, padded)])
    near_in = after(near_in, query)
    (near,) = rows_matmul("near", [near_in], [w_kv], with_bias, [bias_kv], [like(2 * flat, 2 * padded)])
    chain.done(query, near)
    if staged:
        gain_one = flights.land(gain_one, only=[h[z], far_pair[0]])
        h[z | y] = over(h[z], y)
    gain_one, w_kv = chain(gain_one, w_kv)
    normed_far = chain.done(norm([box[0] for box in far_raw + far_pair], gain_one, shift_one))
    if staged:
        w_kv = flights.land(w_kv, only=[h[y], h[zz]])
        h[zz | y], h[zz | z] = over(h[zz], y), over(h[zz], z)
    far_in, w_kv = chain(normed_far, w_kv)
    (far,) = rows_matmul(
        "far", [far_in], [w_kv], with_bias, [bias_kv], [like(normed_far.shape[0], 2 * padded)]
    )
    chain.done(far)
    query = query.reshape(2, rows, tokens, padded)
    near = near.reshape(2, rows, tokens, 2 * padded)
    far = far.reshape(seq_count - 2, rows, tokens, 2 * padded)
    found = ()
    for row in range(rows):
        query, near, far = chain(query, near, far)
        if staged and row == 1:
            query = flights.land(query, only=[h[zz | z]])
            h[zz | z | y] = over(h[zz | z], y)
            d[y], d[z], d[zz] = over(d[0], y), over(d[0], z), over(d[0], zz)
        found = chain.done(*attend(row, query, near, far, need, seg_near_col, seg_rows, heads, found))
    out_own, out_pair, lse = found
    if staged:
        out_own, out_pair = flights.land(out_own, out_pair, only=list(h.values()))
        h_parts = {k: box[0] for k, box in h.items()}
    else:
        out_own, out_pair = flights.land(out_own, out_pair)
        h_parts = gather_all(chain(shard_ho))
    w_out_mine, w_hidden = chain.done(*assemble(h_parts, me, out_cols))
    if staged:
        out_pair, w_out_mine = flights.land(out_pair, w_out_mine, only=[d[y], d[z], d[zz]])
    else:
        out_pair, w_out_mine = chain(out_pair, w_out_mine)
    other_half = flights.send(out_pair, "seq", 1)
    w_out_other = flights.send(w_out_mine, "seq", 1)
    if staged:
        d[zz | z], d[z | y] = over(d[zz], z), over(d[z], y)
    w_out_mine, w_hidden = flights.land(w_out_mine, w_hidden, only=[other_half, w_out_other])
    w_out = chain.done(both_cores(core_flag, w_out_mine, w_out_other[0], out_cut, width))
    own_half, w_out = chain(out_own.reshape(flat, padded), w_out)
    attended, middle, second = chain.done(
        *join(
            core_flag,
            own_half,
            other_half[0].reshape(flat, padded),
            inputs,
            w_out,
            bias_output,
            gain_two,
            shift_two,
            half,
        )
    )
    if staged:
        second = flights.land(second, only=[d[zz | z], d[z | y]])
    second_pair = flights.send(second, "seq", 1)
    if staged:
        d[zz | y], d[zz | z | y] = over(d[zz], y), over(d[zz | z], y)
    second, w_hidden = flights.land(second, w_hidden, only=[second_pair])
    act, slope, second_near = chain.done(*hidden([second, second_pair[0]], w_hidden, bias_hidden))

    incoming_near, act = chain(incoming_near, act)
    grad_down = chain.done(token_dot(incoming_near, act))
    if staged:
        slope, grad_down = flights.land(slope, grad_down)
        d_parts = {k: box[0] for k, box in d.items()}
    else:
        d_parts = gather_all(chain(shard_down))
    part_down = lax.psum_scatter(grad_down, "fsdp", scatter_dimension=0, tiled=True)
    w_down = chain.done(assemble(d_parts, me))
    incoming_near, slope, w_down = chain(incoming_near, slope, w_down)
    grad_pre, hidden_line = chain.done(
        *rows_matmul(
            "grad_pre",
            [incoming_near],
            [w_down],
            with_slope,
            [slope],
            [like(2 * flat, ff_half), like(1, ff_half, F32)],
        )
    )
    grad_pre = chain(grad_pre)
    back, back_pair = chain.done(
        *rows_matmul("back", [grad_pre], [w_hidden], plain, [], [like(2 * flat, width)], NT, True)
    )
    back_other = flights.send(back_pair, "seq", 1)
    second_near, grad_pre = chain(second_near, grad_pre)
    grad_hidden = chain.done(dot(second_near, grad_pre, TN).astype(BF16))
    back = flights.land(back)
    grad_middle, branch, grad_mine, grad_send, lines = second_back(
        core_flag, middle, [back, back_other[0]], gain_two, incoming, w_out, hidden_line, half, padded
    )
    chain.done(branch, grad_send)
    grad_pair = flights.send(grad_send, "seq", 1)
    attended, branch = chain(attended, branch)
    partial_out = flights.land(chain.done(token_dot(attended, branch)))
    out_mine, out_other = chain.done(*core_columns(core_flag, [partial_out], out_cols))
    query = flights.land(query)

    links = {"x": ("seq", top), "core": ("seq", 1)} | {bit: ("fsdp", bit) for bit in bits_of(shards)}
    out_back = flights.send(out_other, "seq", 1)
    shape = (rows, tokens, padded)
    grads = [grad_mine.reshape(shape), grad_pair[0].reshape(shape)]
    found = ()
    far_bits = [2 << k for k in range(shards.bit_length() - 2)]
    def next_step(keep, box, bits):
        keep, send = scatter_step(keep, box[0], shard_rows)
        chain.done(keep)
        return keep, flights.send(send, "fsdp", bits.pop(0)) if bits else None

    def seq_rest(mine, arrived):
        for bit in bits_of(seq_count)[1:-1]:
            (mine,) = add_rows(mine, arrived)
            arrived = swap(mine, "seq", bit)
        return chain.done(*add_rows(mine, arrived, F32))

    for row in range(rows):
        query, near, far, *grads = chain(query, near, far, *grads)
        found = attend_back(
            row, query, near, far, grads, [out_own, out_pair], lse, need, seg_cols, seg_near_row, heads, found
        )
        chain.done(*found)
        query = flights.land(query)
        if row == 0:
            out_sum = chain.done(*add_rows(out_mine, out_back[0]))
            grad_ho = chain.done(jnp.concatenate([grad_hidden, out_sum], axis=1))
            part_hidden = lax.psum_scatter(grad_ho, "fsdp", scatter_dimension=0, tiled=True)
        if row == 1:
            part_down = chain(part_down)
            down_seq = flights.send(part_down, "seq", top)
    dq, dnear, dfar = [g.reshape(-1, g.shape[-1]) for g in found]
    dfar, w_kv, down_seq[0] = chain(dfar, w_kv, down_seq[0])
    two = seq_count == 4
    back_far = rows_matmul("back_far", [dfar], [w_kv], plain, [], [like(dfar.shape[0], width)], NT, two)
    chain.done(*back_far)
    dnear = chain(dnear)
    if two:
        far_parts = {2 + i: part for i, part in enumerate(back_far)}
    else:
        far_parts = {j: back_far[0][(j - 2) * flat : (j - 1) * flat] for j in range(2, seq_count)}
    far_sent = {j: flights.send(part, "seq", 1) for j, part in far_parts.items() if j & 1}
    normed_near, dnear, dfar = chain(normed_near, dnear, dfar)
    kv_keep, kv_send, kv_sums = chain.done(
        *weight_grad([normed_near, normed_far], [dnear, dfar], me, shards)
    )
    dq = flights.land(dq)
    kv_box = flights.send(kv_send, "fsdp", y)
    far_sums = {j: add_rows(far_parts[j], far_sent[j | 1][0])[0] for j in far_parts if not j & 1}
    chain.done(*far_sums.values())
    arrived = []
    for bit in bits_of(seq_count)[:-1]:
        for j in [j for j in far_sums if j & bit]:
            part = far_sums.pop(j)
            if j == bit:
                arrived.append(flights.send(part, "seq", bit))
            else:
                (far_sums[j ^ bit],) = add_rows(far_sums[j ^ bit], swap(part, "seq", bit))
    dq, dnear = chain(dq, dnear)
    back_own, back_pair = chain.done(
        *rows_matmul("back_near", [dq, dnear], [w_q, w_kv], plain, [], [like(2 * flat, width)], NT, True)
    )
    pair_back = flights.send(back_pair, "seq", 1)
    act, middle = chain(act, middle)
    (down_pair,) = rows_matmul(
        "down_pair", [act], [w_down], plain, [], [like(flat, width)], NT, first_row=flat
    )
    chain.done(down_pair)
    down_back = flights.send(down_pair, "seq", 1)
    normed_near, dq = chain(normed_near, dq)
    q_keep, q_send, q_sums = chain.done(*weight_grad([normed_near], [dq], me, shards))
    q_box = flights.send(q_send, "fsdp", y)
    kv_bits, q_bits = list(far_bits), list(far_bits)
    act, late_in = flights.land(act, inputs, only=[kv_box] + arrived)
    kv_keep, kv_box = next_step(kv_keep, kv_box, kv_bits)
    late_in = flights.land(late_in, only=[pair_back])
    grad_patches, late = chain.done(
        *first_back(
            core_flag,
            late_in,
            [back_own, pair_back[0]] + [box[0] for box in arrived],
            gain_one,
            grad_middle,
            q_sums,
            kv_sums,
            half,
        )
    )
    small = jnp.concatenate([lines, late], axis=0)
    if staged:
        small_todo = [("fsdp", zz), ("fsdp", y), ("seq", top), ("fsdp", z), ("seq", 1)]
    else:
        small_todo = [("fsdp", bit) for bit in bits_of(shards)] + [("seq", bit) for bit in bits_of(seq_count)]

    def small_send():
        return flights.send(small, *small_todo.pop(0)) if small_todo else None

    def small_step(small, box):
        return chain.done(*add_rows(small, box[0], F32))

    act, middle, small = flights.land(act, middle, small, only=[q_box, down_back])
    q_keep, q_box = next_step(q_keep, q_box, q_bits)
    small_box = small_send()
    act, middle = chain(act, middle)
    (layer_output,) = rows_matmul(
        "down_own", [act], [w_down], layer_end, [middle, down_back[0], bias_down], [like(flat, width)], NT
    )
    layer_output = chain.done(layer_output).reshape(rows, tokens, width)

    def move_on(*also):
        nonlocal small, small_box, kv_keep, kv_box, q_keep, q_box
        flights.land(only=[box for box in (kv_box, q_box, small_box, *also) if box is not None])
        if kv_box is not None:
            kv_keep, kv_box = next_step(kv_keep, kv_box, kv_bits)
        if q_box is not None:
            q_keep, q_box = next_step(q_keep, q_box, q_bits)
        if small_box is not None:
            small = small_step(small, small_box)
            small_box = small_send()

    move_on()
    part_hidden = chain(part_hidden)
    hidden_seq = flights.send(part_hidden, "seq", top)
    while kv_box is not None or q_box is not None:
        move_on()
    kv_seq = flights.send(kv_keep, "seq", top)
    q_seq = flights.send(q_keep, "seq", top)
    flights.land(only=[hidden_seq])
    hidden_total = seq_rest(part_hidden, hidden_seq[0])
    hidden_other = flights.send(hidden_total, "seq", 1)
    move_on(kv_seq, q_seq)
    kv_total = seq_rest(kv_keep, kv_seq[0])
    kv_other = flights.send(kv_total, "seq", 1)
    q_total = seq_rest(q_keep, q_seq[0])
    q_other = flights.send(q_total, "seq", 1)
    flights.land(only=[hidden_other])
    down_total = seq_rest(part_down, down_seq[0])
    down_other = flights.send(down_total, "seq", 1)
    while small_box is not None:
        move_on()
    flights.land()

    own_lines = lax.dynamic_slice_in_dim(small[:8], me * shard_rows, shard_rows, 1)
    late_lines = lax.dynamic_slice_in_dim(small[8:], me * shard_rows, shard_rows, 1)
    cuts = [width, ff_half - width, width, ff - ff_half - width]
    full_bias = jnp.concatenate([small[4 + i, :size] for i, size in enumerate(cuts)])
    full_down = both_columns(is_first, down_total, down_other[0], ff_half, ff).T
    full_hidden = both_columns(is_first, hidden_total, hidden_other[0], ff_half, ff)
    full_out = both_columns(is_first, hidden_total, hidden_other[0], out_cut, width, ff_half)
    full_query = both_columns(is_first, q_total, q_other[0], half, width)
    full_key = both_columns(is_first, kv_total, kv_other[0], half, width)
    full_value = both_columns(is_first, kv_total, kv_other[0], half, width, padded)
    return (
        layer_output,
        grad_patches.reshape(rows, tokens, width),
        late_lines[0],
        late_lines[1],
        full_query,
        late_lines[2],
        full_key,
        full_value,
        late_lines[3],
        full_out,
        own_lines[2],
        own_lines[0],
        own_lines[1],
        full_hidden,
        full_bias,
        full_down,
        own_lines[3],
    )


def solution(mesh):
    shard, line, tokens = P("fsdp", None), P("fsdp"), P("fsdp", "seq", None)
    in_specs = (
        tokens,
        shard,
        line,
        line,
        shard,
        line,
        shard,
        shard,
        line,
        shard,
        line,
        line,
        line,
        shard,
        P(),
        P(None, "fsdp"),
        line,
        tokens,
    )
    out_specs = (
        tokens,
        tokens,
        line,
        line,
        shard,
        line,
        shard,
        shard,
        line,
        shard,
        line,
        line,
        line,
        shard,
        P(),
        P(None, "fsdp"),
        line,
    )
    return jax.shard_map(local, mesh=mesh, in_specs=in_specs, out_specs=out_specs, check_vma=False)
```

```python
import functools
import math

import jax
import jax.numpy as jnp
from jax import lax
from jax.experimental import pallas as pl
from jax.experimental.pallas import tpu as pltpu
from jax.sharding import PartitionSpec as P

HEAD_DIM = 72
EPS = 1e-06
GELU_COEF = math.sqrt(2.0 / math.pi)
MASKED = -1e30
F32 = jnp.float32
BF16 = jnp.bfloat16
SCALE = 1.0 / math.sqrt(HEAD_DIM)
WIN = 256
LOG2E = math.log2(math.e)
VMEM = 60 << 20
NOMINAL = pl.CostEstimate(flops=1, transcendentals=0, bytes_accessed=1)


def round_up(value, step):
    return (value + step - 1) // step * step


def dot(left, right, dims=((1,), (0,))):
    return lax.dot_general(left, right, (dims, ((), ())), preferred_element_type=F32)


NT = ((1,), (1,))
TN = ((0,), (0,))


def params(semantics):
    return pltpu.CompilerParams(dimension_semantics=semantics, vmem_limit_bytes=VMEM)


def swap(array, axis, bits):
    size = lax.axis_size(axis)
    return lax.ppermute(array, axis, [(i, i ^ bits) for i in range(size)])


def bits_of(size):
    return [1 << k for k in reversed(range(size.bit_length() - 1))]


def after(value, *earlier):
    return lax.optimization_barrier((value,) + tuple(earlier))[0]


class Chain:
    def __init__(self):
        self.last = ()

    def __call__(self, *values, wait=()):
        held = lax.optimization_barrier(tuple(values) + tuple(self.last) + tuple(wait))
        return held[: len(values)] if len(values) > 1 else held[0]

    def done(self, *results):
        self.last = results
        return results if len(results) > 1 else results[0]


class Flights:
    def __init__(self, chain):
        self.chain, self.open = chain, []

    def send(self, array, axis, bits):
        self.open.append([swap(array, axis, bits)])
        return self.open[-1]

    def land(self, *values, through=None, only=None):
        if only is None:
            count = len(self.open)
            if through is not None:
                count = sum(i + 1 for i, box in enumerate(self.open) if box is through)
            only = self.open[:count]
        ready = [box for box in self.open if any(box is other for other in only)]
        self.open = [box for box in self.open if not any(box is other for other in ready)]
        held = self.chain(*[box[0] for box in ready], *values)
        held = held if isinstance(held, (tuple, list)) else [held]
        for box, array in zip(ready, held):
            box[0] = array
        rest = list(held[len(ready) :])
        return rest if len(rest) > 1 else rest[0] if rest else None


def in_order(parts, me):
    count = len(parts)
    return jnp.take(jnp.stack([parts[d] for d in range(count)]), me ^ jnp.arange(count), axis=0)


def gather_all(shard):
    parts = {0: shard}
    for bit in bits_of(lax.axis_size("fsdp")):
        parts.update({d | bit: swap(part, "fsdp", bit) for d, part in list(parts.items())})
    return parts


def rel_position(distance, count):
    width = count.bit_length() - 1
    return sum(((distance >> k) & 1) << (width - 1 - k) for k in range(width))


def assemble_kernel(count, rows, single, off_ref, *refs):
    outs = refs[count:]

    def fill(out_ref):
        for distance in range(count):
            start = pl.multiple_of(off_ref[distance], 16)
            out_ref[pl.ds(start, rows), :] = refs[distance][...]

    if single:
        fill(outs[0])
    else:
        pl.when(pl.program_id(0) == 0)(lambda: fill(outs[0]))
        pl.when(pl.program_id(0) > 0)(lambda: fill(outs[1]))


def assemble(parts, me, cut=None):
    count = len(parts)
    rows, cols = parts[0].shape
    if rows % 16:
        full = in_order(parts, me).reshape(count * rows, cols)
        return (full[:, :cut], full[:, cut:]) if cut else full
    offsets = ((me ^ jnp.arange(count, dtype=jnp.int32)) * rows).astype(jnp.int32)
    tile = cut or min(cols, 1152)
    widths = [cut, cols - cut] if cut else [cols]
    maps = [lambda n, off: (0, 0), lambda n, off: (0, jnp.maximum(n - 1, 0))]
    if not cut:
        maps = [lambda n, off: (0, n)]
    outs = pl.pallas_call(
        functools.partial(assemble_kernel, count, rows, not cut),
        out_shape=[jax.ShapeDtypeStruct((count * rows, w), parts[0].dtype) for w in widths],
        grid_spec=pltpu.PrefetchScalarGridSpec(
            num_scalar_prefetch=1,
            grid=(pl.cdiv(cols, tile),),
            in_specs=[pl.BlockSpec((rows, tile), lambda n, off: (0, n))] * count,
            out_specs=[pl.BlockSpec((count * rows, tile), m) for m in maps],
        ),
        compiler_params=params(("arbitrary",)),
        cost_estimate=NOMINAL,
        name="assemble",
    )(offsets, *[parts[d] for d in range(count)])
    return outs if cut else outs[0]


def weight_grad_kernel(pairs, count, rows, pos_ref, *refs):
    lefts, rights = refs[:pairs], refs[pairs : 2 * pairs]
    keep_ref, send_ref, sum_ref = refs[2 * pairs :]
    total = dot(lefts[0][...], rights[0][...], TN)
    for i in range(1, pairs):
        total += dot(lefts[i][...], rights[i][...], TN)
    sum_ref[...] = sum(dot(jnp.ones((8, r.shape[0]), BF16), r[...]) for r in rights)
    for shard in range(count):
        start = pl.multiple_of(pos_ref[shard], 16)
        block = total[shard * rows : (shard + 1) * rows].astype(BF16)

        @pl.when(pos_ref[count] == shard % 2)
        def _():
            keep_ref[pl.ds(start, rows), :] = block

        @pl.when(pos_ref[count] != shard % 2)
        def _():
            send_ref[pl.ds(start, rows), :] = block


def weight_grad(lefts, rights, me, count):
    width = lefts[0].shape[1]
    cols = rights[0].shape[1]
    rows = width // count
    order = me ^ jnp.arange(count, dtype=jnp.int32)
    table = jnp.array([rel_position(d, count) for d in range(count)], jnp.int32)
    half = count // 2
    if rows % 16:
        total = sum(dot(a, b, TN) for a, b in zip(lefts, rights))
        by_distance = jnp.take(total.astype(BF16).reshape(count, rows, cols), order, axis=0)
        back = [0] * count
        for d in range(count):
            back[rel_position(d, count)] = d
        placed = jnp.take(by_distance, jnp.array(back), axis=0).reshape(width, cols)
        ones = [jnp.ones((8, b.shape[0]), BF16) for b in rights]
        sums = sum(dot(one, b) for one, b in zip(ones, rights))
        return placed[: width // 2], placed[width // 2 :], sums
    positions = jnp.concatenate([table[order] % half * rows, (me & 1)[None]]).astype(jnp.int32)
    tile = 256
    pairs = len(lefts)
    return pl.pallas_call(
        functools.partial(weight_grad_kernel, pairs, count, rows),
        out_shape=[jax.ShapeDtypeStruct((width // 2, cols), BF16)] * 2
        + [jax.ShapeDtypeStruct((8, cols), F32)],
        grid_spec=pltpu.PrefetchScalarGridSpec(
            num_scalar_prefetch=1,
            grid=(pl.cdiv(cols, tile),),
            in_specs=[
                pl.BlockSpec(a.shape, lambda n, off: (0, 0), pipeline_mode=pl.Buffered(1))
                for a in lefts
            ]
            + [pl.BlockSpec((b.shape[0], tile), lambda n, off: (0, n)) for b in rights],
            out_specs=[pl.BlockSpec((width // 2, tile), lambda n, off: (0, n))] * 2
            + [pl.BlockSpec((8, tile), lambda n, off: (0, n))],
        ),
        compiler_params=params(("arbitrary",)),
        cost_estimate=NOMINAL,
        name="weight_grad",
    )(positions, *lefts, *rights)


def add_into(array, left, right, first_col):
    rows, cols = left.shape
    tile = 128
    base = first_col // tile
    part = pl.BlockSpec((rows, tile), lambda n: (0, n))

    def kernel(left_ref, right_ref, _, out_ref):
        out_ref[...] = (left_ref[...].astype(F32) + right_ref[...].astype(F32)).astype(BF16)

    return pl.pallas_call(
        kernel,
        out_shape=jax.ShapeDtypeStruct(array.shape, BF16),
        grid=(cols // tile,),
        in_specs=[part, part, pl.BlockSpec(memory_space=pl.ANY)],
        out_specs=pl.BlockSpec((rows, tile), lambda n: (0, n + base)),
        input_output_aliases={2: 0},
        compiler_params=params(("arbitrary",)),
        cost_estimate=NOMINAL,
        name="add_into",
    )(left, right, array)


def token_dot(left, right, room=0):
    tokens, width = left.shape
    cols = right.shape[1]
    tile = 256

    def kernel(left_ref, right_ref, out_ref):
        out_ref[...] = dot(left_ref[...], right_ref[...], TN).astype(BF16)

    return pl.pallas_call(
        kernel,
        out_shape=jax.ShapeDtypeStruct((width, cols + room), BF16),
        grid=(pl.cdiv(cols, tile),),
        in_specs=[
            pl.BlockSpec((tokens, width), lambda n: (0, 0), pipeline_mode=pl.Buffered(1)),
            pl.BlockSpec((tokens, tile), lambda n: (0, n)),
        ],
        out_specs=pl.BlockSpec((width, tile), lambda n: (0, n)),
        compiler_params=params(("arbitrary",)),
        cost_estimate=NOMINAL,
        name="token_dot",
    )(left, right)


def normalized(values):
    center = values - jnp.mean(values, axis=-1, keepdims=True)
    spread = jnp.mean(center * center, axis=-1, keepdims=True)
    inverse = lax.rsqrt(spread + EPS)
    return center * inverse, inverse


def row_block(rows):
    return 256 if rows % 256 == 0 else 128 if rows % 128 == 0 else rows


def norm(arrays, gain, shift):
    width = arrays[0].shape[1]
    block = min(row_block(a.shape[0]) for a in arrays)
    steps = [a.shape[0] // block for a in arrays]
    firsts = [sum(steps[:k]) for k in range(len(steps))]
    count, total = len(arrays), sum(steps)

    def kernel(*refs):
        gain_ref, shift_ref, out_ref = refs[count:]
        at = pl.program_id(0)
        for k in range(count):

            @pl.when((at >= firsts[k]) & (at < firsts[k] + steps[k]))
            def _():
                hat, _ = normalized(refs[k][...].astype(F32))
                out_ref[...] = (hat * gain_ref[...] + shift_ref[...]).astype(BF16)

    line = pl.BlockSpec((1, width), lambda i: (0, 0))
    return pl.pallas_call(
        kernel,
        out_shape=jax.ShapeDtypeStruct((total * block, width), BF16),
        grid=(total,),
        in_specs=[
            pl.BlockSpec((block, width), lambda i, k=k: (jnp.clip(i - firsts[k], 0, steps[k] - 1), 0))
            for k in range(count)
        ]
        + [line, line],
        out_specs=pl.BlockSpec((block, width), lambda i: (i, 0)),
        compiler_params=params(("arbitrary",)),
        cost_estimate=NOMINAL,
        name="norm",
    )(*arrays, gain, shift)


def join_kernel(half, core_ref, own_ref, other_ref, x_ref, w_ref, b_ref, g_ref, s_ref, *outs):
    att_ref, mid_ref, out_ref = outs
    own, other = own_ref[:, :half], other_ref[:, :half]

    @pl.when(core_ref[0] == 0)
    def _():
        att_ref[...] = jnp.concatenate([own, other], axis=1)

    @pl.when(core_ref[0] != 0)
    def _():
        att_ref[...] = jnp.concatenate([other, own], axis=1)

    middle = x_ref[...].astype(F32) + dot(att_ref[...], w_ref[...]) + b_ref[...]
    mid_ref[...] = middle
    hat, _ = normalized(middle)
    out_ref[...] = (hat * g_ref[...] + s_ref[...]).astype(BF16)


def join(core, own, other, inputs, weight, bias, gain, shift, half):
    rows, width = inputs.shape
    padded = own.shape[1]
    block = row_block(rows)
    line = pl.BlockSpec((1, width), lambda i, c: (0, 0))
    wide = pl.BlockSpec((block, width), lambda i, c: (i, 0))
    part = pl.BlockSpec((block, padded), lambda i, c: (i, 0))
    return pl.pallas_call(
        functools.partial(join_kernel, half),
        out_shape=(
            jax.ShapeDtypeStruct((rows, width), BF16),
            jax.ShapeDtypeStruct((rows, width), F32),
            jax.ShapeDtypeStruct((rows, width), BF16),
        ),
        grid_spec=pltpu.PrefetchScalarGridSpec(
            num_scalar_prefetch=1,
            grid=(rows // block,),
            in_specs=[
                part,
                part,
                wide,
                pl.BlockSpec((width, width), lambda i, c: (0, 0), pipeline_mode=pl.Buffered(1)),
                line,
                line,
                line,
            ],
            out_specs=(wide, wide, wide),
        ),
        compiler_params=params(("arbitrary",)),
        cost_estimate=NOMINAL,
        name="join",
    )(core, own, other, inputs, weight, bias, gain, shift)


def norm_back_values(x_ref, grads, gain_ref, add_ref, lines_ref):
    hat, inverse = normalized(x_ref[...].astype(F32))
    grad = grads[0][...].astype(F32)
    for other in grads[1:]:
        grad += other[...].astype(F32)
    scaled = grad * gain_ref[...]
    first = jnp.mean(scaled, axis=-1, keepdims=True)
    second = jnp.mean(scaled * hat, axis=-1, keepdims=True)

    @pl.when(pl.program_id(0) == 0)
    def _():
        lines_ref[...] = jnp.zeros_like(lines_ref)

    lines_ref[0:1] += jnp.sum(grad * hat, axis=0, keepdims=True)
    lines_ref[1:2] += jnp.sum(grad, axis=0, keepdims=True)
    return add_ref[...].astype(F32) + inverse * (scaled - first - hat * second)


def first_back(core, values, grads, gain, add, q_sums, kv_sums, half):
    rows, width = values.shape
    padded = q_sums.shape[1]
    pieces = [grad for grad in grads if isinstance(grad, tuple)]
    whole_grads = [grad for grad in grads if not isinstance(grad, tuple)]
    block = min([row_block(rows)] + [row_block(part.shape[0]) for pair in pieces for part in pair])
    count = len(whole_grads) + 2 * len(pieces)
    flat_grads = whole_grads + [part for pair in pieces for part in pair]

    def kernel(core_ref, x_ref, *refs):
        gain_ref, add_ref, q_ref, kv_ref, dx_ref, lines_ref = refs[count:]
        sums = list(refs[: len(whole_grads)])
        for k, pair in enumerate(pieces):
            low, high = refs[len(whole_grads) + 2 * k : len(whole_grads) + 2 * k + 2]
            first = pl.program_id(0) < pair[0].shape[0] // block
            sums.append(jnp.where(first, low[...].astype(F32), high[...].astype(F32)))
        dx_ref[...] = norm_back_values(x_ref, sums, gain_ref, add_ref, lines_ref)
        for line, part in ((2, q_ref[0:1, :half]), (3, kv_ref[0:1, padded : padded + half])):
            none = jnp.zeros_like(part)

            @pl.when(core_ref[0] == 0)
            def _():
                lines_ref[line : line + 1] = jnp.concatenate([part, none], axis=1)

            @pl.when(core_ref[0] != 0)
            def _():
                lines_ref[line : line + 1] = jnp.concatenate([none, part], axis=1)

    def piece_specs(pair):
        steps = pair[0].shape[0] // block
        return [
            pl.BlockSpec((block, width), lambda i, c: (jnp.minimum(i, steps - 1), 0)),
            pl.BlockSpec((block, width), lambda i, c: (jnp.maximum(i - steps, 0), 0)),
        ]

    wide = pl.BlockSpec((block, width), lambda i, c: (i, 0))
    return pl.pallas_call(
        kernel,
        out_shape=(
            jax.ShapeDtypeStruct((rows, width), F32),
            jax.ShapeDtypeStruct((8, width), F32),
        ),
        grid_spec=pltpu.PrefetchScalarGridSpec(
            num_scalar_prefetch=1,
            grid=(rows // block,),
            in_specs=[wide] * (1 + len(whole_grads))
            + [spec for pair in pieces for spec in piece_specs(pair)]
            + [
                pl.BlockSpec((1, width), lambda i, c: (0, 0)),
                wide,
                pl.BlockSpec(q_sums.shape, lambda i, c: (0, 0)),
                pl.BlockSpec(kv_sums.shape, lambda i, c: (0, 0)),
            ],
            out_specs=(wide, pl.BlockSpec((8, width), lambda i, c: (0, 0))),
        ),
        compiler_params=params(("arbitrary",)),
        cost_estimate=NOMINAL,
        name="first_back",
    )(core, values, *flat_grads, gain, add, q_sums, kv_sums)


def second_back(core, values, grads, gain, add, weight, hidden_line, half, padded):
    rows, width = values.shape
    block = row_block(rows)
    count = len(grads)

    def kernel(core_ref, x_ref, *refs):
        gain_ref, add_ref, w_ref, hid_ref, dx_ref, low_ref, mine_ref, send_ref, lines_ref = refs[count:]
        total = norm_back_values(x_ref, refs[:count], gain_ref, add_ref, lines_ref)
        low = total.astype(BF16)
        dx_ref[...] = total
        low_ref[...] = low
        lines_ref[2:3] += jnp.sum(low.astype(F32), axis=0, keepdims=True)
        lines_ref[3:4] += jnp.sum(add_ref[...].astype(F32), axis=0, keepdims=True)
        spare = hid_ref.shape[1] - width
        for core in range(2):

            @pl.when(core_ref[0] == core)
            def _():
                lines_ref[4 + 2 * core : 5 + 2 * core] = hid_ref[:, :width]
                lines_ref[5 + 2 * core : 6 + 2 * core, :spare] = hid_ref[:, width:]

        back = dot(low, w_ref[...], NT).astype(BF16)
        empty = jnp.zeros((block, padded - half), BF16)
        halves = [jnp.concatenate([back[:, i * half : (i + 1) * half], empty], axis=1) for i in range(2)]

        @pl.when(core_ref[0] == 0)
        def _():
            mine_ref[...], send_ref[...] = halves[0], halves[1]

        @pl.when(core_ref[0] != 0)
        def _():
            mine_ref[...], send_ref[...] = halves[1], halves[0]

    wide = pl.BlockSpec((block, width), lambda i, c: (i, 0))
    part = pl.BlockSpec((block, padded), lambda i, c: (i, 0))
    line = pl.BlockSpec((1, width), lambda i, c: (0, 0))
    square = pl.BlockSpec((width, width), lambda i, c: (0, 0), pipeline_mode=pl.Buffered(1))
    return pl.pallas_call(
        kernel,
        out_shape=(
            jax.ShapeDtypeStruct((rows, width), F32),
            jax.ShapeDtypeStruct((rows, width), BF16),
            jax.ShapeDtypeStruct((rows, padded), BF16),
            jax.ShapeDtypeStruct((rows, padded), BF16),
            jax.ShapeDtypeStruct((8, width), F32),
        ),
        grid_spec=pltpu.PrefetchScalarGridSpec(
            num_scalar_prefetch=1,
            grid=(rows // block,),
            in_specs=[wide] * (1 + count)
            + [line, wide, square, pl.BlockSpec(hidden_line.shape, lambda i, c: (0, 0))],
            out_specs=(wide, wide, part, part, pl.BlockSpec((8, width), lambda i, c: (0, 0))),
        ),
        compiler_params=params(("arbitrary",)),
        cost_estimate=NOMINAL,
        name="second_back",
    )(core, values, *grads, gain, add, weight, hidden_line)


def rows_matmul(name, lefts, weights, finish, extras, outs, dims=((1,), (0,)), split=False, first_row=0):
    rows = outs[0].shape[0]
    block = 384 if split and rows % 768 == 0 else 512 if not split and rows % 512 == 0 else row_block(rows)
    steps = rows // block
    half = steps // 2
    count, terms = len(lefts), len(lefts) + len(weights)

    def kernel(*refs):
        total = dot(refs[0][...], refs[count][...], dims)
        for i in range(1, count):
            total += dot(refs[i][...], refs[count + i][...], dims)
        results = finish(total, *refs[terms : terms + len(extras)])
        targets = refs[terms + len(extras) :]
        if split:

            @pl.when(pl.program_id(0) < half)
            def _():
                targets[0][...] = results[0]

            @pl.when(pl.program_id(0) >= half)
            def _():
                targets[1][...] = results[0]

            targets = targets[1:]
        else:
            targets[0][...] = results[0]
        for target, result in zip(targets[1:], results[1:]):

            @pl.when(pl.program_id(0) == 0)
            def _():
                target[...] = jnp.zeros_like(target)

            target[...] += result

    def by_rows(array):
        return pl.BlockSpec((block, array.shape[1]), lambda i: (i, 0))

    def whole(array):
        return pl.BlockSpec(array.shape, lambda i: (0, 0), pipeline_mode=pl.Buffered(1))

    first = outs[0]
    if split:
        part = jax.ShapeDtypeStruct((rows // 2, first.shape[1]), first.dtype)
        shapes = [part, part] + list(outs[1:])
        specs = [
            pl.BlockSpec((block, first.shape[1]), lambda i: (jnp.minimum(i, half - 1), 0)),
            pl.BlockSpec((block, first.shape[1]), lambda i: (jnp.maximum(i - half, 0), 0)),
        ]
    else:
        shapes, specs = list(outs), [by_rows(first)]
    specs += [pl.BlockSpec(out.shape, lambda i: (0, 0)) for out in outs[1:]]
    return pl.pallas_call(
        kernel,
        out_shape=shapes,
        grid=(steps,),
        in_specs=[
            pl.BlockSpec((block, a.shape[1]), lambda i: (i + first_row // block, 0)) for a in lefts
        ]
        + [whole(w) for w in weights]
        + [by_rows(e) if e.shape[0] == rows else whole(e) for e in extras],
        out_specs=specs,
        compiler_params=params(("arbitrary",)),
        cost_estimate=NOMINAL,
        name=name,
    )(*lefts, *weights, *extras)


def like(rows, cols, kind=BF16):
    return jax.ShapeDtypeStruct((rows, cols), kind)


def plain(total):
    return (total.astype(BF16),)


def with_bias(total, bias_ref):
    return ((total + bias_ref[...]).astype(BF16),)


def with_slope(total, slope_ref):
    low = (total * slope_ref[...].astype(F32)).astype(BF16)
    return low, jnp.sum(low.astype(F32), axis=0, keepdims=True)


def layer_end(total, middle_ref, other_ref, bias_ref):
    return ((middle_ref[...] + total + other_ref[...].astype(F32) + bias_ref[...]).astype(BF16),)


def small_call(kernel, outs, scalars, arrays, name):
    vmem = pl.BlockSpec(memory_space=pltpu.VMEM)
    return pl.pallas_call(
        kernel,
        out_shape=outs,
        in_specs=[pl.BlockSpec(memory_space=pltpu.SMEM)] * len(scalars) + [vmem] * len(arrays),
        out_specs=[vmem] * len(outs),
        compiler_params=pltpu.CompilerParams(vmem_limit_bytes=VMEM),
        cost_estimate=NOMINAL,
        name=name,
    )(*scalars, *arrays)


def add_rows(left, right, kind=BF16, pieces=1):
    size = left.shape[0] // pieces
    parts = [slice(i * size, (i + 1) * size) for i in range(pieces)]
    return [(left[part].astype(F32) + right[part].astype(F32)).astype(kind) for part in parts]


def scatter_step(keep, arrived, rows):
    if keep.shape[0] == rows:
        return add_rows(keep, arrived)[0], None
    return add_rows(keep, arrived, BF16, 2)


def both_cores(core, mine, other, size, total, start=0, turn=False):
    rows = mine.shape[0]

    def kernel(core_ref, mine_ref, other_ref, out_ref):
        for at, refs in ((0, (mine_ref, other_ref)), (1, (other_ref, mine_ref))):

            @pl.when(core_ref[0] == at)
            def _():
                first = refs[0][:, start : start + size]
                second = refs[1][:, start : start + total - size]
                if turn:
                    out_ref[:size], out_ref[size:] = first.T, second.T
                else:
                    out_ref[...] = jnp.concatenate([first, second], axis=1)

    shape = like(total, rows, mine.dtype) if turn else like(rows, total, mine.dtype)
    return small_call(kernel, [shape], [core], [mine, other], "both_cores")[0]


def both_columns(is_first, mine, other, size, total, start=0):
    mine, other = mine[:, start:], other[:, start:]
    return jnp.where(
        is_first,
        jnp.concatenate([mine[:, :size], other[:, : total - size]], axis=1),
        jnp.concatenate([other[:, :size], mine[:, : total - size]], axis=1),
    )


def core_columns(core, arrays, cols):
    rows, width = arrays[0].shape

    def kernel(core_ref, *refs):
        for at in range(2):

            @pl.when(core_ref[0] == at)
            def _():
                for i in range(len(arrays)):
                    for k, where in enumerate((at, 1 - at)):
                        low = where * (width - cols)
                        refs[len(arrays) * (1 + k) + i][...] = refs[i][:, low : low + cols]

    return small_call(kernel, [like(rows, cols)] * (2 * len(arrays)), [core], arrays, "core_columns")


def mask_kernel(rows, tokens, blocks, len_ref, place_ref, need_ref, row_ref, col_ref, near_row, near_col):
    place = place_ref[0]
    for row in range(rows):
        ends = [len_ref[row, 0]]
        for p in range(1, len_ref.shape[1]):
            ends.append(ends[-1] + len_ref[row, p])

        def pictures(position):
            return sum((position >= end).astype(jnp.int32) for end in ends)

        def segment(position):
            return jnp.where(position < ends[-1], pictures(position), 1000 + position)

        spans = []
        for block in range(blocks):
            start = jnp.bitwise_xor(place, block) * tokens
            across = segment(start + lax.broadcasted_iota(jnp.int32, (1, tokens), 1))
            down = segment(start + lax.broadcasted_iota(jnp.int32, (tokens, 1), 0))
            row_ref[row, block : block + 1] = across
            col_ref[row, block] = down
            if block < 2:
                near_row[row, :, block * tokens : (block + 1) * tokens] = across
                near_col[row, block * tokens : (block + 1) * tokens] = down
            last = jnp.minimum(start + tokens, ends[-1]) - 1
            low = sum(jnp.where(start >= end, 1, 0) for end in ends)
            high = sum(jnp.where(last >= end, 1, 0) for end in ends)
            spans.append((start < ends[-1], low, high))
        for block, (real, low, high) in enumerate(spans):
            if block < 2:
                need_ref[row, block] = 1
            else:
                need_ref[row, block] = sum(
                    jnp.where(real & ok & (low <= top) & (bottom <= high), 1, 0) for ok, bottom, top in spans[:2]
                )


def masks(lengths, place, blocks, tokens):
    rows = lengths.shape[0]
    shapes = [(rows, blocks, tokens), (rows, blocks, tokens, 1), (rows, 1, 2 * tokens), (rows, 2 * tokens, 1)]
    smem = pl.BlockSpec(memory_space=pltpu.SMEM)
    return pl.pallas_call(
        functools.partial(mask_kernel, rows, tokens, blocks),
        out_shape=[jax.ShapeDtypeStruct((rows, blocks), jnp.int32)]
        + [jax.ShapeDtypeStruct(shape, jnp.int32) for shape in shapes],
        in_specs=[smem, smem],
        out_specs=[smem] + [pl.BlockSpec(memory_space=pltpu.VMEM)] * 4,
        compiler_params=pltpu.CompilerParams(vmem_limit_bytes=VMEM),
        cost_estimate=NOMINAL,
        name="masks",
    )(lengths, place)


def lay_vectors(core, weight, lines, half, padded):
    width, cols = weight.shape
    low = half // 128 * 128

    def kernel(core_ref, weight_ref, lines_ref, q_ref, kv_ref):
        turned = weight_ref[...].astype(F32).T
        lines_ref[...] = turned[half - low : half - low + lines]
        q_ref[...] = jnp.zeros_like(q_ref)
        kv_ref[...] = jnp.zeros_like(kv_ref)
        for at in range(2):

            @pl.when(core_ref[0] == at)
            def _():
                q_ref[:, :half] = lines_ref[2:3, at * half : (at + 1) * half]
                kv_ref[:, padded : padded + half] = lines_ref[3:4, at * half : (at + 1) * half]

    outs = [like(lines, width, F32), like(1, padded, F32), like(1, 2 * padded, F32)]
    block = cols - low
    return pl.pallas_call(
        kernel,
        out_shape=outs,
        grid=(1,),
        in_specs=[
            pl.BlockSpec(memory_space=pltpu.SMEM),
            pl.BlockSpec((width, block), lambda i: (0, low // block)),
        ],
        out_specs=[pl.BlockSpec(out.shape, lambda i: (0, 0)) for out in outs],
        compiler_params=params(("arbitrary",)),
        cost_estimate=NOMINAL,
        name="lay_vectors",
    )(core, weight)


def mlp_shards(core, out_shard, hidden_weight, down_weight, cols):
    rows, total = hidden_weight.shape
    before = out_shard.shape[1]

    def kernel(core_ref, part_ref, hidden_ref, down_ref, first_out, down_out):
        first_out[:, :before] = part_ref[...]
        for at in range(2):

            @pl.when(core_ref[0] == at)
            def _():
                low = at * cols
                high = min(low + cols, total)
                size = high - low
                first_out[:, before : before + size] = hidden_ref[:, low:high]
                down_out[:, :size] = down_ref[low:high].T
                if size < cols:
                    empty = jnp.zeros((rows, cols - size), BF16)
                    first_out[:, before + size :] = empty
                    down_out[:, size:] = empty

    outs = [like(rows, before + cols), like(rows, cols)]
    return small_call(kernel, outs, [core], [out_shard, hidden_weight, down_weight], "mlp_shards")


def attention_shards(core, weights, vectors, half, padded):
    rows, width = weights[0].shape
    cut = width - padded
    count = len(vectors)

    def kernel(core_ref, q_ref, k_ref, v_ref, o_ref, *refs):
        qkv_ref, out_ref, held = refs[count:]
        for i in range(count):
            held[i : i + 1] = refs[i][...].astype(F32).reshape(1, rows)
        empty = jnp.zeros((rows, padded - half), BF16)
        spare = jnp.zeros((rows, padded - half - count), BF16)
        lines = jnp.concatenate([held[...].T.astype(BF16), spare], axis=1)
        for at in range(2):

            @pl.when(core_ref[0] == at)
            def _():
                for i, ref in enumerate((q_ref, k_ref, v_ref)):
                    part = ref[:, at * half : (at + 1) * half]
                    rest = empty if i else lines
                    qkv_ref[:, i * padded : (i + 1) * padded] = jnp.concatenate([part, rest], axis=1)
                out_ref[...] = o_ref[:, at * cut : at * cut + padded]

    vmem = pl.BlockSpec(memory_space=pltpu.VMEM)
    return pl.pallas_call(
        kernel,
        out_shape=[like(rows, 3 * padded), like(rows, padded)],
        in_specs=[pl.BlockSpec(memory_space=pltpu.SMEM)] + [vmem] * (4 + count),
        out_specs=[vmem] * 2,
        scratch_shapes=[pltpu.VMEM((count, rows), F32)],
        compiler_params=pltpu.CompilerParams(vmem_limit_bytes=VMEM),
        cost_estimate=NOMINAL,
        name="attention_shards",
    )(core, *weights, *vectors)


def hidden(arrays, weight, bias):
    rows, width = arrays[0].shape
    cols = weight.shape[1]
    block = row_block(rows)
    steps, count = rows // block, len(arrays)

    def kernel(*refs):
        w_ref, b_ref, act_ref, slope_ref, x_ref = refs[count:]
        for i in range(count):

            @pl.when(pl.program_id(0) // steps == i)
            def _():
                x_ref[...] = refs[i][...]

        pre = dot(x_ref[...], w_ref[...]) + b_ref[...]
        square = pre * pre
        turn = jnp.tanh(pre * (GELU_COEF + GELU_COEF * 0.044715 * square))
        act_ref[...] = (0.5 * pre * (1.0 + turn)).astype(BF16)
        inner = GELU_COEF + 3.0 * 0.044715 * GELU_COEF * square
        slope_ref[...] = (0.5 * (1.0 + turn) * (1.0 + pre * (1.0 - turn) * inner)).astype(BF16)

    out = pl.BlockSpec((block, cols), lambda i: (i, 0))
    return pl.pallas_call(
        kernel,
        out_shape=(
            jax.ShapeDtypeStruct((count * rows, cols), BF16),
            jax.ShapeDtypeStruct((count * rows, cols), BF16),
            jax.ShapeDtypeStruct((count * rows, width), BF16),
        ),
        grid=(count * steps,),
        in_specs=[
            pl.BlockSpec((block, width), lambda i, k=k: (jnp.clip(i - k * steps, 0, steps - 1), 0))
            for k in range(count)
        ]
        + [
            pl.BlockSpec((width, cols), lambda i: (0, 0), pipeline_mode=pl.Buffered(1)),
            pl.BlockSpec((1, cols), lambda i: (0, 0)),
        ],
        out_specs=(out, out, pl.BlockSpec((block, width), lambda i: (i, 0))),
        compiler_params=params(("arbitrary",)),
        cost_estimate=NOMINAL,
        name="hidden",
    )(*arrays, weight, bias)


def head_window(head):
    first = head * HEAD_DIM
    start = first // 128 * 128
    return start, round_up(first + HEAD_DIM, 128) - start, first - start


def head_lanes(rows, width, low):
    lane = lax.broadcasted_iota(jnp.int32, (rows, width), 1)
    return (lane >= low) & (lane < low + HEAD_DIM)


def only_head(block, low):
    mine = head_lanes(*block.shape, low)
    return jnp.where(mine, block.astype(F32), 0.0).astype(BF16)


def pick_block(near_ref, far_ref, block):
    return near_ref.at[block, 0] if block < 2 else far_ref.at[block - 2, 0]


def attend_kernel(row, heads, blocks, padded, need_ref, col_ref, row_ref, q_ref, near_ref, far_ref, *refs):
    own_ref, pair_ref, lse_ref, queries, score, peak, total, acc, lses = refs[-9:]
    outs = (own_ref, pair_ref)
    tokens = own_ref.shape[1]
    slot = lax.broadcasted_iota(jnp.int32, (2 * tokens, 128), 1)
    for which in range(2):
        outs[which][...] = jnp.zeros_like(outs[which])
    windows = [head_window(head) for head in range(heads)]
    for head, (start, width, low) in enumerate(windows):
        for which in range(2):
            queries[head, which * tokens : (which + 1) * tokens, :width] = only_head(
                q_ref[which, 0, :, start : start + width], low
            )
    peak[...] = jnp.full_like(peak, MASKED)
    total[...] = jnp.zeros_like(total)
    acc[...] = jnp.zeros_like(acc)
    for block in range(blocks):

        @pl.when(need_ref[row, block] != 0)
        def _():
            side = pick_block(near_ref, far_ref, block)
            seen = col_ref[0] == row_ref[0, block : block + 1]
            for head, (start, width, _) in enumerate(windows):
                key = side[:, start : start + width]
                found = jnp.where(seen, dot(queries[head, :, :width], key, NT), MASKED)
                score[head, block] = found
                top = peak[head]
                for at in range(0, tokens, 128):
                    top = jnp.maximum(top, found[:, at : at + 128])
                peak[head] = top

    for head in range(heads):
        top = jnp.max(peak[head], axis=-1, keepdims=True) * (SCALE * LOG2E)
        peak[head] = jnp.broadcast_to(top, peak.shape[1:])

    for block in range(blocks):

        @pl.when(need_ref[row, block] != 0)
        def _():
            side = pick_block(near_ref, far_ref, block)
            for head, (start, width, _) in enumerate(windows):
                top, share = peak[head], total[head]
                pieces = []
                for at in range(0, tokens, 128):
                    part = jnp.exp2(score[head, block, :, at : at + 128] * (SCALE * LOG2E) - top)
                    share += part
                    pieces.append(part.astype(BF16))
                total[head] = share
                value = side[:, padded + start : padded + start + width]
                acc[head, :, :width] += dot(jnp.concatenate(pieces, axis=1), value)

    for head, (start, width, low) in enumerate(windows):
        norm = jnp.sum(total[head], axis=-1, keepdims=True)
        result = acc[head, :, :width] / norm
        mine = head_lanes(tokens, width, low)
        for which in range(2):
            kept = outs[which][0, :, start : start + width].astype(F32)
            fresh = result[which * tokens : (which + 1) * tokens]
            outs[which][0, :, start : start + width] = jnp.where(mine, fresh, kept).astype(BF16)
        lse = peak[head] + jnp.log2(norm)
        lses[...] = lse if head == 0 else jnp.where(slot == head, lse, lses[...])
    lse_ref[0] = lses[...].T[:heads]


def attend(row, query, near, far, need, seg_col, seg_row, heads, before):
    _, rows, tokens, padded = query.shape
    blocks = 2 + far.shape[0]
    narrow = pl.BlockSpec((1, tokens, padded), lambda i, need: (row, 0, 0))
    lines = pl.BlockSpec((1, heads, 2 * tokens), lambda i, need: (row, 0, 0))

    def stack(count, width):
        return pl.BlockSpec((count, 1, tokens, width), lambda i, need: (0, row, 0, 0))

    return pl.pallas_call(
        functools.partial(attend_kernel, row, heads, blocks, padded),
        out_shape=(
            jax.ShapeDtypeStruct((rows, tokens, padded), BF16),
            jax.ShapeDtypeStruct((rows, tokens, padded), BF16),
            jax.ShapeDtypeStruct((rows, heads, 2 * tokens), F32),
        ),
        grid_spec=pltpu.PrefetchScalarGridSpec(
            num_scalar_prefetch=1,
            grid=(1,),
            in_specs=[
                pl.BlockSpec((1, 2 * tokens, 1), lambda i, need: (row, 0, 0)),
                pl.BlockSpec((1, blocks, tokens), lambda i, need: (row, 0, 0)),
                stack(2, padded),
                stack(2, 2 * padded),
                stack(blocks - 2, 2 * padded),
            ]
            + [pl.BlockSpec(memory_space=pl.ANY)] * len(before),
            out_specs=(narrow, narrow, lines),
            scratch_shapes=[
                pltpu.VMEM((heads, 2 * tokens, WIN), BF16),
                pltpu.VMEM((heads, blocks, 2 * tokens, tokens), F32),
                pltpu.VMEM((heads, 2 * tokens, 128), F32),
                pltpu.VMEM((heads, 2 * tokens, 128), F32),
                pltpu.VMEM((heads, 2 * tokens, WIN), F32),
                pltpu.VMEM((2 * tokens, 128), F32),
            ],
        ),
        input_output_aliases={6 + i: i for i in range(len(before))},
        compiler_params=params(("arbitrary",)),
        cost_estimate=NOMINAL,
        name="attend",
    )(need, seg_col, seg_row, query, near, far, *before)


def attend_back_kernel(
    row, heads, blocks, padded, need_ref, col_ref, row_ref, pick_ref, q_ref, near_ref, far_ref, *refs
):
    grads, outs, lse_ref = refs[0:2], refs[2:4], refs[4]
    dq_ref, dnear_ref, dfar_ref, sums, inner_turn, queries, incoming, dq = refs[-8:]
    tokens = grads[0].shape[1]
    sums[...] = jnp.zeros_like(sums)
    for which in range(2):
        dq_ref[which, 0] = jnp.zeros((tokens, padded), BF16)
        product = grads[which][0].astype(F32) * outs[which][0].astype(F32)
        high = product.astype(BF16)
        rest = (product - high.astype(F32)).astype(BF16)
        inner_turn[:, which * tokens : (which + 1) * tokens] = dot(pick_ref[...], high, NT) + dot(
            pick_ref[...], rest, NT
        )
    windows = [head_window(head) for head in range(heads)]
    for head, (start, width, low) in enumerate(windows):
        for which in range(2):
            there = slice(which * tokens, (which + 1) * tokens)
            here = slice(start, start + width)
            queries[head, there, :width] = only_head(q_ref[which, 0, :, here], low)
            incoming[head, there, :width] = only_head(grads[which][0, :, here], low)
    dq[...] = jnp.zeros_like(dq)
    for block in range(blocks):

        @pl.when(need_ref[row, block] != 0)
        def _():
            side = pick_block(near_ref, far_ref, block)
            seen = col_ref[0, block] == row_ref[0]
            for head, (start, width, _) in enumerate(windows):
                end = start + width
                key, value = side[:, start:end], side[:, padded + start : padded + end]
                query, grad = queries[head, :, :width], incoming[head, :, :width]
                found = dot(key, query, NT) * (SCALE * LOG2E) - lse_ref[0, head : head + 1, :]
                prob = jnp.where(seen, jnp.exp2(found), 0.0)
                inner = inner_turn[head : head + 1, :]
                slope = (prob * (dot(value, grad, NT) - inner)).astype(BF16)
                sums[block, :, start:end] += dot(slope, query)
                sums[block, :, padded + start : padded + end] += dot(prob.astype(BF16), grad)
                dq[head, :, :width] += dot(slope, key, TN)

    for head, (start, width, low) in enumerate(windows):
        mine = head_lanes(tokens, width, low)
        for which in range(2):
            kept = dq_ref[which, 0, :, start : start + width].astype(F32)
            fresh = dq[head, which * tokens : (which + 1) * tokens, :width] * SCALE
            dq_ref[which, 0, :, start : start + width] = jnp.where(mine, fresh, kept).astype(BF16)
    for block in range(blocks):
        side = pick_block(dnear_ref, dfar_ref, block)
        side[:, :padded] = (sums[block, :, :padded] * SCALE).astype(BF16)
        side[:, padded:] = sums[block, :, padded:].astype(BF16)


def attend_back(row, query, near, far, grads, outs, lse, need, seg_col, seg_row, heads, before):
    _, rows, tokens, padded = query.shape
    blocks = 2 + far.shape[0]
    column = lax.broadcasted_iota(jnp.int32, (heads, padded), 1)
    pick = (column // HEAD_DIM == lax.broadcasted_iota(jnp.int32, (heads, padded), 0)).astype(BF16)
    narrow = pl.BlockSpec((1, tokens, padded), lambda i, need: (row, 0, 0))

    def stack(count, width):
        return pl.BlockSpec((count, 1, tokens, width), lambda i, need: (0, row, 0, 0))

    return pl.pallas_call(
        functools.partial(attend_back_kernel, row, heads, blocks, padded),
        out_shape=tuple(jax.ShapeDtypeStruct(a.shape, BF16) for a in (query, near, far)),
        grid_spec=pltpu.PrefetchScalarGridSpec(
            num_scalar_prefetch=1,
            grid=(1,),
            in_specs=[
                pl.BlockSpec((1, blocks, tokens, 1), lambda i, need: (row, 0, 0, 0)),
                pl.BlockSpec((1, 1, 2 * tokens), lambda i, need: (row, 0, 0)),
                pl.BlockSpec((heads, padded), lambda i, need: (0, 0)),
                stack(2, padded),
                stack(2, 2 * padded),
                stack(blocks - 2, 2 * padded),
            ]
            + [narrow] * 4
            + [pl.BlockSpec((1, heads, 2 * tokens), lambda i, need: (row, 0, 0))]
            + [pl.BlockSpec(memory_space=pl.ANY)] * len(before),
            out_specs=(stack(2, padded), stack(2, 2 * padded), stack(blocks - 2, 2 * padded)),
            scratch_shapes=[
                pltpu.VMEM((blocks, tokens, 2 * padded), F32),
                pltpu.VMEM((heads, 2 * tokens), F32),
                pltpu.VMEM((heads, 2 * tokens, WIN), BF16),
                pltpu.VMEM((heads, 2 * tokens, WIN), BF16),
                pltpu.VMEM((heads, 2 * tokens, WIN), F32),
            ],
        ),
        input_output_aliases={12 + i: i for i in range(len(before))},
        compiler_params=params(("arbitrary",)),
        cost_estimate=NOMINAL,
        name="attend_back",
    )(need, seg_col, seg_row, pick, query, near, far, *grads, *outs, lse, *before)


def local(
    patches,
    lengths,
    first_gain,
    first_shift,
    query_weight,
    query_bias,
    key_weight,
    value_weight,
    value_bias,
    output_weight,
    output_bias,
    second_gain,
    second_shift,
    hidden_weight,
    hidden_bias,
    down_weight,
    down_bias,
    cotangent,
):
    seq_count, shards = lax.axis_size("seq"), lax.axis_size("fsdp")
    place, me = lax.axis_index("seq"), lax.axis_index("fsdp")
    core = place & 1
    is_first = core == 0
    core_flag = core[None].astype(jnp.int32)
    rows, tokens, width = patches.shape
    flat = rows * tokens
    heads = width // HEAD_DIM // 2
    half = heads * HEAD_DIM
    padded = round_up(half, 128)
    ff = hidden_bias.shape[0]
    ff_half = round_up(ff, 256) // 2
    out_cols = padded
    out_cut = width - padded
    shard_rows = width // shards
    chain = Chain()

    def my_half(array, size, padded_size):
        first, second = array[..., :size], array[..., size:]
        grow = [(0, 0)] * (array.ndim - 1)
        first = jnp.pad(first, grow + [(0, padded_size - size)])
        second = jnp.pad(second, grow + [(0, padded_size - second.shape[-1])])
        return jnp.where(is_first, first, second)

    flights = Flights(chain)
    staged = shards == 8 and seq_count == 4
    y, z, zz = 1, 2, 4
    top = bits_of(seq_count)[0]

    inputs = patches.reshape(flat, width)
    incoming = cotangent.reshape(flat, width)
    vectors = [
        first_gain,
        first_shift,
        query_bias,
        value_bias,
        output_bias,
        second_gain,
        second_shift,
        down_bias,
    ]
    shard_qkv, shard_out = chain.done(
        *attention_shards(
            core_flag, [query_weight, key_weight, value_weight, output_weight], vectors, half, padded
        )
    )
    place_flag = place[None].astype(jnp.int32)

    def over(box_from, bits):
        return flights.send(box_from[0], "fsdp", bits)

    if staged:
        q = {0: [shard_qkv]}
        q[y] = over(q[0], y)
        q[z], q[zz] = over(q[0], z), over(q[0], zz)
        incoming_pair = flights.send(incoming, "seq", 1)
        shard_ho, shard_down = chain.done(
            *mlp_shards(core_flag, shard_out, hidden_weight, down_weight, ff_half)
        )
        h, d = {0: [shard_ho]}, {0: [shard_down]}
        need, seg_rows, seg_cols, seg_near_row, seg_near_col = chain.done(
            *masks(chain(lengths), place_flag, seq_count, tokens)
        )
        core_flag, raw_own = flights.land(core_flag, inputs)
        q[zz | z], q[z | y], q[zz | y] = over(q[zz], z), over(q[z], y), over(q[zz], y)
        far_raw = [flights.send(raw_own, "seq", 2)]
        raw_pair = flights.send(raw_own, "seq", 1)
        core_flag, incoming_pair[0] = flights.land(core_flag, incoming_pair[0], only=[q[zz | z]])
        q[zz | z | y] = over(q[zz | z], y)
        incoming_near = chain.done(jnp.concatenate([incoming, incoming_pair[0]], axis=0))
        core_flag, shard_ho = flights.land(core_flag, shard_ho, only=[q[z | y], q[zz | y], raw_pair])
        h[0] = [shard_ho]
        h[z], h[y] = over(h[0], z), over(h[0], y)
        core_flag, shard_ho, shard_down = flights.land(
            core_flag, shard_ho, shard_down, only=[q[zz | z | y], far_raw[0]]
        )
        h[0], d[0] = [shard_ho], [shard_down]
        far_pair = [flights.send(far_raw[0][0], "seq", 1)]
        h[zz] = over(h[0], zz)
        w_q, w_kv = chain.done(*assemble({k: box[0] for k, box in q.items()}, me, padded))
        stacked, bias_q, bias_kv = chain.done(
            *lay_vectors(chain(core_flag), w_q, len(vectors), half, padded)
        )
        gain_one, shift_one = stacked[0:1], stacked[1:2]
        gain_one = chain(gain_one)
        normed_near = chain.done(norm([inputs, raw_pair[0]], gain_one, shift_one))
        bias_hidden = my_half(after(hidden_bias, gain_one).astype(F32)[None], ff_half, ff_half)
    else:
        parts = gather_all(shard_qkv)
        shard_ho, shard_down = mlp_shards(core_flag, shard_out, hidden_weight, down_weight, ff_half)
        raw = {0: inputs}
        for bit in bits_of(seq_count):
            raw.update({j | bit: swap(part, "seq", bit) for j, part in list(raw.items())})
        need, seg_rows, seg_cols, seg_near_row, seg_near_col = masks(lengths, place_flag, seq_count, tokens)
        w_q, w_kv = chain.done(*assemble(parts, me, padded))
        stacked, bias_q, bias_kv = lay_vectors(core_flag, w_q, len(vectors), half, padded)
        gain_one, shift_one = stacked[0:1], stacked[1:2]
        normed_near = norm([raw[0], raw[1]], gain_one, shift_one)
        far_raw, far_pair = [[raw[j]] for j in range(2, seq_count)], []
        incoming_near = jnp.concatenate([incoming, swap(incoming, "seq", 1)], axis=0)
        bias_hidden = my_half(hidden_bias.astype(F32)[None], ff_half, ff_half)
    _, _, bias_query, bias_value, bias_output, gain_two, shift_two, bias_down = [
        stacked[i : i + 1] for i in range(8)
    ]

    near_in, w_q, w_kv = chain(normed_near, w_q, w_kv)
    (query,) = rows_matmul("query", [near_in], [w_q], with_bias, [bias_q], [like(2 * flat, padded)])
    near_in = after(near_in, query)
    (near,) = rows_matmul("near", [near_in], [w_kv], with_bias, [bias_kv], [like(2 * flat, 2 * padded)])
    chain.done(query, near)
    if staged:
        gain_one = flights.land(gain_one, only=[h[z], far_pair[0]])
        h[z | y] = over(h[z], y)
    gain_one, w_kv = chain(gain_one, w_kv)
    normed_far = chain.done(norm([box[0] for box in far_raw + far_pair], gain_one, shift_one))
    if staged:
        w_kv = flights.land(w_kv, only=[h[y], h[zz]])
        h[zz | y], h[zz | z] = over(h[zz], y), over(h[zz], z)
    far_in, w_kv = chain(normed_far, w_kv)
    (far,) = rows_matmul(
        "far", [far_in], [w_kv], with_bias, [bias_kv], [like(normed_far.shape[0], 2 * padded)]
    )
    chain.done(far)
    query = query.reshape(2, rows, tokens, padded)
    near = near.reshape(2, rows, tokens, 2 * padded)
    far = far.reshape(seq_count - 2, rows, tokens, 2 * padded)
    found = ()
    for row in range(rows):
        query, near, far = chain(query, near, far)
        if staged and row == 1:
            query = flights.land(query, only=[h[z | y], h[zz | z]])
            h[zz | z | y] = over(h[zz | z], y)
            d[y], d[z], d[zz] = over(d[0], y), over(d[0], z), over(d[0], zz)
        found = chain.done(*attend(row, query, near, far, need, seg_near_col, seg_rows, heads, found))
    out_own, out_pair, lse = found
    if staged:
        out_own, out_pair = flights.land(out_own, out_pair, only=list(h.values()))
        h_parts = {k: box[0] for k, box in h.items()}
    else:
        out_own, out_pair = flights.land(out_own, out_pair)
        h_parts = gather_all(chain(shard_ho))
    w_out_mine, w_hidden = chain.done(*assemble(h_parts, me, out_cols))
    if staged:
        out_pair, w_out_mine = flights.land(out_pair, w_out_mine, only=[d[y], d[z], d[zz]])
    else:
        out_pair, w_out_mine = chain(out_pair, w_out_mine)
    other_half = flights.send(out_pair, "seq", 1)
    w_out_other = flights.send(w_out_mine, "seq", 1)
    if staged:
        d[zz | z], d[z | y] = over(d[zz], z), over(d[z], y)
    w_out_mine, w_hidden = flights.land(w_out_mine, w_hidden, only=[other_half, w_out_other])
    w_out = chain.done(both_cores(core_flag, w_out_mine, w_out_other[0], out_cut, width))
    own_half, w_out = chain(out_own.reshape(flat, padded), w_out)
    attended, middle, second = chain.done(
        *join(
            core_flag,
            own_half,
            other_half[0].reshape(flat, padded),
            inputs,
            w_out,
            bias_output,
            gain_two,
            shift_two,
            half,
        )
    )
    if staged:
        second = flights.land(second, only=[d[zz | z], d[z | y]])
    second_pair = flights.send(second, "seq", 1)
    if staged:
        d[zz | y], d[zz | z | y] = over(d[zz], y), over(d[zz | z], y)
    second, w_hidden = flights.land(second, w_hidden, only=[second_pair])
    act, slope, second_near = chain.done(*hidden([second, second_pair[0]], w_hidden, bias_hidden))

    incoming_near, act = chain(incoming_near, act)
    grad_down = chain.done(token_dot(incoming_near, act))
    if staged:
        slope, grad_down = flights.land(slope, grad_down)
        d_parts = {k: box[0] for k, box in d.items()}
    else:
        d_parts = gather_all(chain(shard_down))
    part_down = lax.psum_scatter(grad_down, "fsdp", scatter_dimension=0, tiled=True)
    w_down = chain.done(assemble(d_parts, me))
    incoming_near, slope, w_down = chain(incoming_near, slope, w_down)
    grad_pre, hidden_line = chain.done(
        *rows_matmul(
            "grad_pre",
            [incoming_near],
            [w_down],
            with_slope,
            [slope],
            [like(2 * flat, ff_half), like(1, ff_half, F32)],
        )
    )
    grad_pre = chain(grad_pre)
    back, back_pair = chain.done(
        *rows_matmul("back", [grad_pre], [w_hidden], plain, [], [like(2 * flat, width)], NT, True)
    )
    back_other = flights.send(back_pair, "seq", 1)
    second_near, grad_pre = chain(second_near, grad_pre)
    grad_hidden = chain.done(token_dot(second_near, grad_pre, out_cols))
    back = flights.land(back)
    grad_middle, branch, grad_mine, grad_send, lines = second_back(
        core_flag, middle, [back, back_other[0]], gain_two, incoming, w_out, hidden_line, half, padded
    )
    chain.done(branch, grad_send)
    grad_pair = flights.send(grad_send, "seq", 1)
    attended, branch = chain(attended, branch)
    partial_out = flights.land(chain.done(token_dot(attended, branch)))
    out_mine, out_other = chain.done(*core_columns(core_flag, [partial_out], out_cols))
    query = flights.land(query)

    links = {"x": ("seq", top), "core": ("seq", 1)} | {bit: ("fsdp", bit) for bit in bits_of(shards)}
    out_back = flights.send(out_other, "seq", 1)
    shape = (rows, tokens, padded)
    grads = [grad_mine.reshape(shape), grad_pair[0].reshape(shape)]
    found = ()
    far_bits = [2 << k for k in range(shards.bit_length() - 2)]
    def next_step(keep, box, bits):
        keep, send = scatter_step(keep, box[0], shard_rows)
        chain.done(keep)
        return keep, flights.send(send, "fsdp", bits.pop(0)) if bits else None

    def seq_rest(mine, arrived):
        for bit in bits_of(seq_count)[1:-1]:
            (mine,) = add_rows(mine, arrived)
            arrived = swap(mine, "seq", bit)
        return chain.done(*add_rows(mine, arrived, F32))

    for row in range(rows):
        query, near, far, *grads = chain(query, near, far, *grads)
        found = attend_back(
            row, query, near, far, grads, [out_own, out_pair], lse, need, seg_cols, seg_near_row, heads, found
        )
        chain.done(*found)
        query = flights.land(query)
        if row == 0:
            grad_ho = chain.done(add_into(grad_hidden, out_mine, out_back[0], ff_half))
            part_hidden = lax.psum_scatter(grad_ho, "fsdp", scatter_dimension=0, tiled=True)
        if row == 1:
            part_down = chain(part_down)
            down_seq = flights.send(part_down, "seq", top)
    dq, dnear, dfar = [g.reshape(-1, g.shape[-1]) for g in found]
    dfar, w_kv, down_seq[0] = chain(dfar, w_kv, down_seq[0])
    two = seq_count == 4
    back_far = rows_matmul("back_far", [dfar], [w_kv], plain, [], [like(dfar.shape[0], width)], NT, two)
    chain.done(*back_far)
    dnear = chain(dnear)
    if two:
        far_parts = {2 + i: part for i, part in enumerate(back_far)}
    else:
        far_parts = {j: back_far[0][(j - 2) * flat : (j - 1) * flat] for j in range(2, seq_count)}
    far_sent = {j: flights.send(part, "seq", 1) for j, part in far_parts.items() if j & 1}
    normed_near, dnear, dfar = chain(normed_near, dnear, dfar)
    kv_keep, kv_send, kv_sums = chain.done(
        *weight_grad([normed_near, normed_far], [dnear, dfar], me, shards)
    )
    dq = flights.land(dq)
    kv_box = flights.send(kv_send, "fsdp", y)
    far_sums = {j: add_rows(far_parts[j], far_sent[j | 1][0])[0] for j in far_parts if not j & 1}
    chain.done(*far_sums.values())
    arrived = []
    for bit in bits_of(seq_count)[:-1]:
        for j in [j for j in far_sums if j & bit]:
            part = far_sums.pop(j)
            if j == bit:
                arrived.append(flights.send(part, "seq", bit))
            else:
                (far_sums[j ^ bit],) = add_rows(far_sums[j ^ bit], swap(part, "seq", bit))
    dq, dnear = chain(dq, dnear)
    back_own, back_pair = chain.done(
        *rows_matmul("back_near", [dq, dnear], [w_q, w_kv], plain, [], [like(2 * flat, width)], NT, True)
    )
    pair_back = flights.send(back_pair, "seq", 1)
    act, middle = chain(act, middle)
    (down_pair,) = rows_matmul(
        "down_pair", [act], [w_down], plain, [], [like(flat, width)], NT, first_row=flat
    )
    chain.done(down_pair)
    down_back = flights.send(down_pair, "seq", 1)
    normed_near, dq = chain(normed_near, dq)
    q_keep, q_send, q_sums = chain.done(*weight_grad([normed_near], [dq], me, shards))
    q_box = flights.send(q_send, "fsdp", y)
    kv_bits, q_bits = list(far_bits), list(far_bits)
    act, late_in = flights.land(act, inputs, only=[kv_box] + arrived)
    kv_keep, kv_box = next_step(kv_keep, kv_box, kv_bits)
    late_in = flights.land(late_in, only=[pair_back])
    grad_patches, late = chain.done(
        *first_back(
            core_flag,
            late_in,
            [back_own, pair_back[0]] + [box[0] for box in arrived],
            gain_one,
            grad_middle,
            q_sums,
            kv_sums,
            half,
        )
    )
    small = jnp.concatenate([lines, late], axis=0)
    if staged:
        small_todo = [("fsdp", zz), ("fsdp", y), ("seq", top), ("fsdp", z), ("seq", 1)]
    else:
        small_todo = [("fsdp", bit) for bit in bits_of(shards)] + [("seq", bit) for bit in bits_of(seq_count)]

    def small_send():
        return flights.send(small, *small_todo.pop(0)) if small_todo else None

    def small_step(small, box):
        return chain.done(*add_rows(small, box[0], F32))

    act, middle, small = flights.land(act, middle, small, only=[q_box, down_back])
    q_keep, q_box = next_step(q_keep, q_box, q_bits)
    small_box = small_send()
    act, middle = chain(act, middle)
    (layer_output,) = rows_matmul(
        "down_own", [act], [w_down], layer_end, [middle, down_back[0], bias_down], [like(flat, width)], NT
    )
    layer_output = chain.done(layer_output).reshape(rows, tokens, width)

    def move_on(*also):
        nonlocal small, small_box, kv_keep, kv_box, q_keep, q_box
        flights.land(only=[box for box in (kv_box, q_box, small_box, *also) if box is not None])
        if kv_box is not None:
            kv_keep, kv_box = next_step(kv_keep, kv_box, kv_bits)
        if q_box is not None:
            q_keep, q_box = next_step(q_keep, q_box, q_bits)
        if small_box is not None:
            small = small_step(small, small_box)
            small_box = small_send()

    move_on()
    part_hidden = chain(part_hidden)
    hidden_seq = flights.send(part_hidden, "seq", top)
    while kv_box is not None or q_box is not None:
        move_on()
    kv_seq = flights.send(kv_keep, "seq", top)
    q_seq = flights.send(q_keep, "seq", top)
    flights.land(only=[hidden_seq])
    hidden_total = seq_rest(part_hidden, hidden_seq[0])
    hidden_other = flights.send(hidden_total, "seq", 1)
    move_on(kv_seq, q_seq)
    kv_total = seq_rest(kv_keep, kv_seq[0])
    kv_other = flights.send(kv_total, "seq", 1)
    q_total = seq_rest(q_keep, q_seq[0])
    q_other = flights.send(q_total, "seq", 1)
    flights.land(only=[hidden_other])
    down_total = seq_rest(part_down, down_seq[0])
    down_other = flights.send(down_total, "seq", 1)
    while small_box is not None:
        move_on()
    flights.land()

    own_lines = lax.dynamic_slice_in_dim(small[:8], me * shard_rows, shard_rows, 1)
    late_lines = lax.dynamic_slice_in_dim(small[8:], me * shard_rows, shard_rows, 1)
    cuts = [width, ff_half - width, width, ff - ff_half - width]
    full_bias = jnp.concatenate([small[4 + i, :size] for i, size in enumerate(cuts)])
    full_down = both_columns(is_first, down_total, down_other[0], ff_half, ff).T
    full_hidden = both_columns(is_first, hidden_total, hidden_other[0], ff_half, ff)
    full_out = both_columns(is_first, hidden_total, hidden_other[0], out_cut, width, ff_half)
    full_query = both_columns(is_first, q_total, q_other[0], half, width)
    full_key = both_columns(is_first, kv_total, kv_other[0], half, width)
    full_value = both_columns(is_first, kv_total, kv_other[0], half, width, padded)
    return (
        layer_output,
        grad_patches.reshape(rows, tokens, width),
        late_lines[0],
        late_lines[1],
        full_query,
        late_lines[2],
        full_key,
        full_value,
        late_lines[3],
        full_out,
        own_lines[2],
        own_lines[0],
        own_lines[1],
        full_hidden,
        full_bias,
        full_down,
        own_lines[3],
    )


def solution(mesh):
    shard, line, tokens = P("fsdp", None), P("fsdp"), P("fsdp", "seq", None)
    in_specs = (
        tokens,
        shard,
        line,
        line,
        shard,
        line,
        shard,
        shard,
        line,
        shard,
        line,
        line,
        line,
        shard,
        P(),
        P(None, "fsdp"),
        line,
        tokens,
    )
    out_specs = (
        tokens,
        tokens,
        line,
        line,
        shard,
        line,
        shard,
        shard,
        line,
        shard,
        line,
        line,
        line,
        shard,
        P(),
        P(None, "fsdp"),
        line,
    )
    return jax.shard_map(local, mesh=mesh, in_specs=in_specs, out_specs=out_specs, check_vma=False)
```

```python
import functools
import math

import jax
import jax.numpy as jnp
from jax import lax
from jax.experimental import pallas as pl
from jax.experimental.pallas import tpu as pltpu
from jax.sharding import PartitionSpec as P

HEAD_DIM = 72
EPS = 1e-06
GELU_COEF = math.sqrt(2.0 / math.pi)
MASKED = -1e30
F32 = jnp.float32
BF16 = jnp.bfloat16
SCALE = 1.0 / math.sqrt(HEAD_DIM)
WIN = 256
LOG2E = math.log2(math.e)
VMEM = 60 << 20
NOMINAL = pl.CostEstimate(flops=1, transcendentals=0, bytes_accessed=1)


def round_up(value, step):
    return (value + step - 1) // step * step


def dot(left, right, dims=((1,), (0,))):
    return lax.dot_general(left, right, (dims, ((), ())), preferred_element_type=F32)


NT = ((1,), (1,))
TN = ((0,), (0,))


def params(semantics):
    return pltpu.CompilerParams(dimension_semantics=semantics, vmem_limit_bytes=VMEM)


def swap(array, axis, bits):
    size = lax.axis_size(axis)
    return lax.ppermute(array, axis, [(i, i ^ bits) for i in range(size)])


def bits_of(size):
    return [1 << k for k in reversed(range(size.bit_length() - 1))]


def after(value, *earlier):
    return lax.optimization_barrier((value,) + tuple(earlier))[0]


class Chain:
    def __init__(self):
        self.last = ()

    def __call__(self, *values, wait=()):
        held = lax.optimization_barrier(tuple(values) + tuple(self.last) + tuple(wait))
        return held[: len(values)] if len(values) > 1 else held[0]

    def done(self, *results):
        self.last = results
        return results if len(results) > 1 else results[0]


class Flights:
    def __init__(self, chain):
        self.chain, self.open = chain, []

    def send(self, array, axis, bits):
        self.open.append([swap(array, axis, bits)])
        return self.open[-1]

    def land(self, *values, through=None, only=None):
        if only is None:
            count = len(self.open)
            if through is not None:
                count = sum(i + 1 for i, box in enumerate(self.open) if box is through)
            only = self.open[:count]
        ready = [box for box in self.open if any(box is other for other in only)]
        self.open = [box for box in self.open if not any(box is other for other in ready)]
        held = self.chain(*[box[0] for box in ready], *values)
        held = held if isinstance(held, (tuple, list)) else [held]
        for box, array in zip(ready, held):
            box[0] = array
        rest = list(held[len(ready) :])
        return rest if len(rest) > 1 else rest[0] if rest else None


def in_order(parts, me):
    count = len(parts)
    return jnp.take(jnp.stack([parts[d] for d in range(count)]), me ^ jnp.arange(count), axis=0)


def gather_all(shard):
    parts = {0: shard}
    for bit in bits_of(lax.axis_size("fsdp")):
        parts.update({d | bit: swap(part, "fsdp", bit) for d, part in list(parts.items())})
    return parts


def rel_position(distance, count):
    width = count.bit_length() - 1
    return sum(((distance >> k) & 1) << (width - 1 - k) for k in range(width))


def assemble_kernel(count, rows, single, off_ref, *refs):
    outs = refs[count:]

    def fill(out_ref):
        for distance in range(count):
            start = pl.multiple_of(off_ref[distance], 16)
            out_ref[pl.ds(start, rows), :] = refs[distance][...]

    if single:
        fill(outs[0])
    else:
        pl.when(pl.program_id(0) == 0)(lambda: fill(outs[0]))
        pl.when(pl.program_id(0) > 0)(lambda: fill(outs[1]))


def assemble(parts, me, cut=None):
    count = len(parts)
    rows, cols = parts[0].shape
    if rows % 16:
        full = in_order(parts, me).reshape(count * rows, cols)
        return (full[:, :cut], full[:, cut:]) if cut else full
    offsets = ((me ^ jnp.arange(count, dtype=jnp.int32)) * rows).astype(jnp.int32)
    tile = cut or min(cols, 1152)
    widths = [cut, cols - cut] if cut else [cols]
    maps = [lambda n, off: (0, 0), lambda n, off: (0, jnp.maximum(n - 1, 0))]
    if not cut:
        maps = [lambda n, off: (0, n)]
    outs = pl.pallas_call(
        functools.partial(assemble_kernel, count, rows, not cut),
        out_shape=[jax.ShapeDtypeStruct((count * rows, w), parts[0].dtype) for w in widths],
        grid_spec=pltpu.PrefetchScalarGridSpec(
            num_scalar_prefetch=1,
            grid=(pl.cdiv(cols, tile),),
            in_specs=[pl.BlockSpec((rows, tile), lambda n, off: (0, n))] * count,
            out_specs=[pl.BlockSpec((count * rows, tile), m) for m in maps],
        ),
        compiler_params=params(("arbitrary",)),
        cost_estimate=NOMINAL,
        name="assemble",
    )(offsets, *[parts[d] for d in range(count)])
    return outs if cut else outs[0]


def weight_grad_kernel(pairs, count, rows, pos_ref, *refs):
    lefts, rights = refs[:pairs], refs[pairs : 2 * pairs]
    keep_ref, send_ref, sum_ref = refs[2 * pairs :]
    total = dot(lefts[0][...], rights[0][...], TN)
    for i in range(1, pairs):
        total += dot(lefts[i][...], rights[i][...], TN)
    sum_ref[...] = sum(dot(jnp.ones((8, r.shape[0]), BF16), r[...]) for r in rights)
    for shard in range(count):
        start = pl.multiple_of(pos_ref[shard], 16)
        block = total[shard * rows : (shard + 1) * rows].astype(BF16)

        @pl.when(pos_ref[count] == shard % 2)
        def _():
            keep_ref[pl.ds(start, rows), :] = block

        @pl.when(pos_ref[count] != shard % 2)
        def _():
            send_ref[pl.ds(start, rows), :] = block


def weight_grad(lefts, rights, me, count):
    width = lefts[0].shape[1]
    cols = rights[0].shape[1]
    rows = width // count
    order = me ^ jnp.arange(count, dtype=jnp.int32)
    table = jnp.array([rel_position(d, count) for d in range(count)], jnp.int32)
    half = count // 2
    if rows % 16:
        total = sum(dot(a, b, TN) for a, b in zip(lefts, rights))
        by_distance = jnp.take(total.astype(BF16).reshape(count, rows, cols), order, axis=0)
        back = [0] * count
        for d in range(count):
            back[rel_position(d, count)] = d
        placed = jnp.take(by_distance, jnp.array(back), axis=0).reshape(width, cols)
        ones = [jnp.ones((8, b.shape[0]), BF16) for b in rights]
        sums = sum(dot(one, b) for one, b in zip(ones, rights))
        return placed[: width // 2], placed[width // 2 :], sums
    positions = jnp.concatenate([table[order] % half * rows, (me & 1)[None]]).astype(jnp.int32)
    tile = 256
    pairs = len(lefts)
    return pl.pallas_call(
        functools.partial(weight_grad_kernel, pairs, count, rows),
        out_shape=[jax.ShapeDtypeStruct((width // 2, cols), BF16)] * 2
        + [jax.ShapeDtypeStruct((8, cols), F32)],
        grid_spec=pltpu.PrefetchScalarGridSpec(
            num_scalar_prefetch=1,
            grid=(pl.cdiv(cols, tile),),
            in_specs=[
                pl.BlockSpec(a.shape, lambda n, off: (0, 0), pipeline_mode=pl.Buffered(1))
                for a in lefts
            ]
            + [pl.BlockSpec((b.shape[0], tile), lambda n, off: (0, n)) for b in rights],
            out_specs=[pl.BlockSpec((width // 2, tile), lambda n, off: (0, n))] * 2
            + [pl.BlockSpec((8, tile), lambda n, off: (0, n))],
        ),
        compiler_params=params(("arbitrary",)),
        cost_estimate=NOMINAL,
        name="weight_grad",
    )(positions, *lefts, *rights)


def add_into(array, left, right, first_col):
    rows, cols = left.shape
    tile = 128
    base = first_col // tile
    part = pl.BlockSpec((rows, tile), lambda n: (0, n))

    def kernel(left_ref, right_ref, _, out_ref):
        out_ref[...] = (left_ref[...].astype(F32) + right_ref[...].astype(F32)).astype(BF16)

    return pl.pallas_call(
        kernel,
        out_shape=jax.ShapeDtypeStruct(array.shape, BF16),
        grid=(cols // tile,),
        in_specs=[part, part, pl.BlockSpec(memory_space=pl.ANY)],
        out_specs=pl.BlockSpec((rows, tile), lambda n: (0, n + base)),
        input_output_aliases={2: 0},
        compiler_params=params(("arbitrary",)),
        cost_estimate=NOMINAL,
        name="add_into",
    )(left, right, array)


def token_dot(left, right, room=0):
    tokens, width = left.shape
    cols = right.shape[1]
    tile = 256

    def kernel(left_ref, right_ref, out_ref):
        out_ref[...] = dot(left_ref[...], right_ref[...], TN).astype(BF16)

    return pl.pallas_call(
        kernel,
        out_shape=jax.ShapeDtypeStruct((width, cols + room), BF16),
        grid=(pl.cdiv(cols, tile),),
        in_specs=[
            pl.BlockSpec((tokens, width), lambda n: (0, 0), pipeline_mode=pl.Buffered(1)),
            pl.BlockSpec((tokens, tile), lambda n: (0, n)),
        ],
        out_specs=pl.BlockSpec((width, tile), lambda n: (0, n)),
        compiler_params=params(("arbitrary",)),
        cost_estimate=NOMINAL,
        name="token_dot",
    )(left, right)


def normalized(values):
    center = values - jnp.mean(values, axis=-1, keepdims=True)
    spread = jnp.mean(center * center, axis=-1, keepdims=True)
    inverse = lax.rsqrt(spread + EPS)
    return center * inverse, inverse


def row_block(rows):
    return 256 if rows % 256 == 0 else 128 if rows % 128 == 0 else rows


def norm(arrays, gain, shift):
    width = arrays[0].shape[1]
    block = min(row_block(a.shape[0]) for a in arrays)
    steps = [a.shape[0] // block for a in arrays]
    firsts = [sum(steps[:k]) for k in range(len(steps))]
    count, total = len(arrays), sum(steps)

    def kernel(*refs):
        gain_ref, shift_ref, out_ref = refs[count:]
        at = pl.program_id(0)
        for k in range(count):

            @pl.when((at >= firsts[k]) & (at < firsts[k] + steps[k]))
            def _():
                hat, _ = normalized(refs[k][...].astype(F32))
                out_ref[...] = (hat * gain_ref[...] + shift_ref[...]).astype(BF16)

    line = pl.BlockSpec((1, width), lambda i: (0, 0))
    return pl.pallas_call(
        kernel,
        out_shape=jax.ShapeDtypeStruct((total * block, width), BF16),
        grid=(total,),
        in_specs=[
            pl.BlockSpec((block, width), lambda i, k=k: (jnp.clip(i - firsts[k], 0, steps[k] - 1), 0))
            for k in range(count)
        ]
        + [line, line],
        out_specs=pl.BlockSpec((block, width), lambda i: (i, 0)),
        compiler_params=params(("arbitrary",)),
        cost_estimate=NOMINAL,
        name="norm",
    )(*arrays, gain, shift)


def join_kernel(half, core_ref, own_ref, other_ref, x_ref, w_ref, b_ref, g_ref, s_ref, *outs):
    att_ref, mid_ref, out_ref = outs
    own, other = own_ref[:, :half], other_ref[:, :half]

    @pl.when(core_ref[0] == 0)
    def _():
        att_ref[...] = jnp.concatenate([own, other], axis=1)

    @pl.when(core_ref[0] != 0)
    def _():
        att_ref[...] = jnp.concatenate([other, own], axis=1)

    middle = x_ref[...].astype(F32) + dot(att_ref[...], w_ref[...]) + b_ref[...]
    mid_ref[...] = middle
    hat, _ = normalized(middle)
    out_ref[...] = (hat * g_ref[...] + s_ref[...]).astype(BF16)


def join(core, own, other, inputs, weight, bias, gain, shift, half):
    rows, width = inputs.shape
    padded = own.shape[1]
    block = row_block(rows)
    line = pl.BlockSpec((1, width), lambda i, c: (0, 0))
    wide = pl.BlockSpec((block, width), lambda i, c: (i, 0))
    part = pl.BlockSpec((block, padded), lambda i, c: (i, 0))
    return pl.pallas_call(
        functools.partial(join_kernel, half),
        out_shape=(
            jax.ShapeDtypeStruct((rows, width), BF16),
            jax.ShapeDtypeStruct((rows, width), F32),
            jax.ShapeDtypeStruct((rows, width), BF16),
        ),
        grid_spec=pltpu.PrefetchScalarGridSpec(
            num_scalar_prefetch=1,
            grid=(rows // block,),
            in_specs=[
                part,
                part,
                wide,
                pl.BlockSpec((width, width), lambda i, c: (0, 0), pipeline_mode=pl.Buffered(1)),
                line,
                line,
                line,
            ],
            out_specs=(wide, wide, wide),
        ),
        compiler_params=params(("arbitrary",)),
        cost_estimate=NOMINAL,
        name="join",
    )(core, own, other, inputs, weight, bias, gain, shift)


def norm_back_values(x_ref, grads, gain_ref, add_ref, lines_ref):
    hat, inverse = normalized(x_ref[...].astype(F32))
    grad = grads[0][...].astype(F32)
    for other in grads[1:]:
        grad += other[...].astype(F32)
    scaled = grad * gain_ref[...]
    first = jnp.mean(scaled, axis=-1, keepdims=True)
    second = jnp.mean(scaled * hat, axis=-1, keepdims=True)

    @pl.when(pl.program_id(0) == 0)
    def _():
        lines_ref[...] = jnp.zeros_like(lines_ref)

    lines_ref[0:1] += jnp.sum(grad * hat, axis=0, keepdims=True)
    lines_ref[1:2] += jnp.sum(grad, axis=0, keepdims=True)
    return add_ref[...].astype(F32) + inverse * (scaled - first - hat * second)


def first_back(core, values, grads, gain, add, q_sums, kv_sums, half):
    rows, width = values.shape
    padded = q_sums.shape[1]
    pieces = [grad for grad in grads if isinstance(grad, tuple)]
    whole_grads = [grad for grad in grads if not isinstance(grad, tuple)]
    block = min([row_block(rows)] + [row_block(part.shape[0]) for pair in pieces for part in pair])
    count = len(whole_grads) + 2 * len(pieces)
    flat_grads = whole_grads + [part for pair in pieces for part in pair]

    def kernel(core_ref, x_ref, *refs):
        gain_ref, add_ref, q_ref, kv_ref, dx_ref, lines_ref = refs[count:]
        sums = list(refs[: len(whole_grads)])
        for k, pair in enumerate(pieces):
            low, high = refs[len(whole_grads) + 2 * k : len(whole_grads) + 2 * k + 2]
            first = pl.program_id(0) < pair[0].shape[0] // block
            sums.append(jnp.where(first, low[...].astype(F32), high[...].astype(F32)))
        dx_ref[...] = norm_back_values(x_ref, sums, gain_ref, add_ref, lines_ref)
        for line, part in ((2, q_ref[0:1, :half]), (3, kv_ref[0:1, padded : padded + half])):
            none = jnp.zeros_like(part)

            @pl.when(core_ref[0] == 0)
            def _():
                lines_ref[line : line + 1] = jnp.concatenate([part, none], axis=1)

            @pl.when(core_ref[0] != 0)
            def _():
                lines_ref[line : line + 1] = jnp.concatenate([none, part], axis=1)

    def piece_specs(pair):
        steps = pair[0].shape[0] // block
        return [
            pl.BlockSpec((block, width), lambda i, c: (jnp.minimum(i, steps - 1), 0)),
            pl.BlockSpec((block, width), lambda i, c: (jnp.maximum(i - steps, 0), 0)),
        ]

    wide = pl.BlockSpec((block, width), lambda i, c: (i, 0))
    return pl.pallas_call(
        kernel,
        out_shape=(
            jax.ShapeDtypeStruct((rows, width), F32),
            jax.ShapeDtypeStruct((8, width), F32),
        ),
        grid_spec=pltpu.PrefetchScalarGridSpec(
            num_scalar_prefetch=1,
            grid=(rows // block,),
            in_specs=[wide] * (1 + len(whole_grads))
            + [spec for pair in pieces for spec in piece_specs(pair)]
            + [
                pl.BlockSpec((1, width), lambda i, c: (0, 0)),
                wide,
                pl.BlockSpec(q_sums.shape, lambda i, c: (0, 0)),
                pl.BlockSpec(kv_sums.shape, lambda i, c: (0, 0)),
            ],
            out_specs=(wide, pl.BlockSpec((8, width), lambda i, c: (0, 0))),
        ),
        compiler_params=params(("arbitrary",)),
        cost_estimate=NOMINAL,
        name="first_back",
    )(core, values, *flat_grads, gain, add, q_sums, kv_sums)


def second_back(core, values, grads, gain, add, weight, hidden_line, half, padded):
    rows, width = values.shape
    block = row_block(rows)
    count = len(grads)

    def kernel(core_ref, x_ref, *refs):
        gain_ref, add_ref, w_ref, hid_ref, dx_ref, low_ref, mine_ref, send_ref, lines_ref = refs[count:]
        total = norm_back_values(x_ref, refs[:count], gain_ref, add_ref, lines_ref)
        low = total.astype(BF16)
        dx_ref[...] = total
        low_ref[...] = low
        lines_ref[2:3] += jnp.sum(low.astype(F32), axis=0, keepdims=True)
        lines_ref[3:4] += jnp.sum(add_ref[...].astype(F32), axis=0, keepdims=True)
        spare = hid_ref.shape[1] - width
        for core in range(2):

            @pl.when(core_ref[0] == core)
            def _():
                lines_ref[4 + 2 * core : 5 + 2 * core] = hid_ref[:, :width]
                lines_ref[5 + 2 * core : 6 + 2 * core, :spare] = hid_ref[:, width:]

        back = dot(low, w_ref[...], NT).astype(BF16)
        empty = jnp.zeros((block, padded - half), BF16)
        halves = [jnp.concatenate([back[:, i * half : (i + 1) * half], empty], axis=1) for i in range(2)]

        @pl.when(core_ref[0] == 0)
        def _():
            mine_ref[...], send_ref[...] = halves[0], halves[1]

        @pl.when(core_ref[0] != 0)
        def _():
            mine_ref[...], send_ref[...] = halves[1], halves[0]

    wide = pl.BlockSpec((block, width), lambda i, c: (i, 0))
    part = pl.BlockSpec((block, padded), lambda i, c: (i, 0))
    line = pl.BlockSpec((1, width), lambda i, c: (0, 0))
    square = pl.BlockSpec((width, width), lambda i, c: (0, 0), pipeline_mode=pl.Buffered(1))
    return pl.pallas_call(
        kernel,
        out_shape=(
            jax.ShapeDtypeStruct((rows, width), F32),
            jax.ShapeDtypeStruct((rows, width), BF16),
            jax.ShapeDtypeStruct((rows, padded), BF16),
            jax.ShapeDtypeStruct((rows, padded), BF16),
            jax.ShapeDtypeStruct((8, width), F32),
        ),
        grid_spec=pltpu.PrefetchScalarGridSpec(
            num_scalar_prefetch=1,
            grid=(rows // block,),
            in_specs=[wide] * (1 + count)
            + [line, wide, square, pl.BlockSpec(hidden_line.shape, lambda i, c: (0, 0))],
            out_specs=(wide, wide, part, part, pl.BlockSpec((8, width), lambda i, c: (0, 0))),
        ),
        compiler_params=params(("arbitrary",)),
        cost_estimate=NOMINAL,
        name="second_back",
    )(core, values, *grads, gain, add, weight, hidden_line)


def rows_matmul(name, lefts, weights, finish, extras, outs, dims=((1,), (0,)), split=False, first_row=0):
    rows = outs[0].shape[0]
    block = 512 if not split and rows % 512 == 0 else 384 if rows % 768 == 0 else row_block(rows)
    steps = rows // block
    half = steps // 2
    count, terms = len(lefts), len(lefts) + len(weights)

    def kernel(*refs):
        total = dot(refs[0][...], refs[count][...], dims)
        for i in range(1, count):
            total += dot(refs[i][...], refs[count + i][...], dims)
        results = finish(total, *refs[terms : terms + len(extras)])
        targets = refs[terms + len(extras) :]
        if split:

            @pl.when(pl.program_id(0) < half)
            def _():
                targets[0][...] = results[0]

            @pl.when(pl.program_id(0) >= half)
            def _():
                targets[1][...] = results[0]

            targets = targets[1:]
        else:
            targets[0][...] = results[0]
        for target, result in zip(targets[1:], results[1:]):

            @pl.when(pl.program_id(0) == 0)
            def _():
                target[...] = jnp.zeros_like(target)

            target[...] += result

    def by_rows(array):
        return pl.BlockSpec((block, array.shape[1]), lambda i: (i, 0))

    def whole(array):
        return pl.BlockSpec(array.shape, lambda i: (0, 0), pipeline_mode=pl.Buffered(1))

    first = outs[0]
    if split:
        part = jax.ShapeDtypeStruct((rows // 2, first.shape[1]), first.dtype)
        shapes = [part, part] + list(outs[1:])
        specs = [
            pl.BlockSpec((block, first.shape[1]), lambda i: (jnp.minimum(i, half - 1), 0)),
            pl.BlockSpec((block, first.shape[1]), lambda i: (jnp.maximum(i - half, 0), 0)),
        ]
    else:
        shapes, specs = list(outs), [by_rows(first)]
    specs += [pl.BlockSpec(out.shape, lambda i: (0, 0)) for out in outs[1:]]
    return pl.pallas_call(
        kernel,
        out_shape=shapes,
        grid=(steps,),
        in_specs=[
            pl.BlockSpec((block, a.shape[1]), lambda i: (i + first_row // block, 0)) for a in lefts
        ]
        + [whole(w) for w in weights]
        + [by_rows(e) if e.shape[0] == rows else whole(e) for e in extras],
        out_specs=specs,
        compiler_params=params(("arbitrary",)),
        cost_estimate=NOMINAL,
        name=name,
    )(*lefts, *weights, *extras)


def like(rows, cols, kind=BF16):
    return jax.ShapeDtypeStruct((rows, cols), kind)


def plain(total):
    return (total.astype(BF16),)


def with_bias(total, bias_ref):
    return ((total + bias_ref[...]).astype(BF16),)


def with_slope(total, slope_ref):
    low = (total * slope_ref[...].astype(F32)).astype(BF16)
    return low, jnp.sum(low.astype(F32), axis=0, keepdims=True)


def layer_end(total, middle_ref, other_ref, bias_ref):
    return ((middle_ref[...] + total + other_ref[...].astype(F32) + bias_ref[...]).astype(BF16),)


def small_call(kernel, outs, scalars, arrays, name):
    vmem = pl.BlockSpec(memory_space=pltpu.VMEM)
    return pl.pallas_call(
        kernel,
        out_shape=outs,
        in_specs=[pl.BlockSpec(memory_space=pltpu.SMEM)] * len(scalars) + [vmem] * len(arrays),
        out_specs=[vmem] * len(outs),
        compiler_params=pltpu.CompilerParams(vmem_limit_bytes=VMEM),
        cost_estimate=NOMINAL,
        name=name,
    )(*scalars, *arrays)


def add_rows(left, right, kind=BF16, pieces=1):
    size = left.shape[0] // pieces
    parts = [slice(i * size, (i + 1) * size) for i in range(pieces)]
    return [(left[part].astype(F32) + right[part].astype(F32)).astype(kind) for part in parts]


def scatter_step(keep, arrived, rows):
    if keep.shape[0] == rows:
        return add_rows(keep, arrived)[0], None
    return add_rows(keep, arrived, BF16, 2)


def both_cores(core, mine, other, size, total, start=0, turn=False):
    rows = mine.shape[0]

    def kernel(core_ref, mine_ref, other_ref, out_ref):
        for at, refs in ((0, (mine_ref, other_ref)), (1, (other_ref, mine_ref))):

            @pl.when(core_ref[0] == at)
            def _():
                first = refs[0][:, start : start + size]
                second = refs[1][:, start : start + total - size]
                if turn:
                    out_ref[:size], out_ref[size:] = first.T, second.T
                else:
                    out_ref[...] = jnp.concatenate([first, second], axis=1)

    shape = like(total, rows, mine.dtype) if turn else like(rows, total, mine.dtype)
    return small_call(kernel, [shape], [core], [mine, other], "both_cores")[0]


def both_columns(is_first, mine, other, size, total, start=0):
    mine, other = mine[:, start:], other[:, start:]
    return jnp.where(
        is_first,
        jnp.concatenate([mine[:, :size], other[:, : total - size]], axis=1),
        jnp.concatenate([other[:, :size], mine[:, : total - size]], axis=1),
    )


def core_columns(core, arrays, cols):
    rows, width = arrays[0].shape

    def kernel(core_ref, *refs):
        for at in range(2):

            @pl.when(core_ref[0] == at)
            def _():
                for i in range(len(arrays)):
                    for k, where in enumerate((at, 1 - at)):
                        low = where * (width - cols)
                        refs[len(arrays) * (1 + k) + i][...] = refs[i][:, low : low + cols]

    return small_call(kernel, [like(rows, cols)] * (2 * len(arrays)), [core], arrays, "core_columns")


def mask_kernel(rows, tokens, blocks, len_ref, place_ref, need_ref, row_ref, col_ref, near_row, near_col):
    place = place_ref[0]
    for row in range(rows):
        ends = [len_ref[row, 0]]
        for p in range(1, len_ref.shape[1]):
            ends.append(ends[-1] + len_ref[row, p])

        def pictures(position):
            return sum((position >= end).astype(jnp.int32) for end in ends)

        def segment(position):
            return jnp.where(position < ends[-1], pictures(position), 1000 + position)

        spans = []
        for block in range(blocks):
            start = jnp.bitwise_xor(place, block) * tokens
            across = segment(start + lax.broadcasted_iota(jnp.int32, (1, tokens), 1))
            down = segment(start + lax.broadcasted_iota(jnp.int32, (tokens, 1), 0))
            row_ref[row, block : block + 1] = across
            col_ref[row, block] = down
            if block < 2:
                near_row[row, :, block * tokens : (block + 1) * tokens] = across
                near_col[row, block * tokens : (block + 1) * tokens] = down
            last = jnp.minimum(start + tokens, ends[-1]) - 1
            low = sum(jnp.where(start >= end, 1, 0) for end in ends)
            high = sum(jnp.where(last >= end, 1, 0) for end in ends)
            spans.append((start < ends[-1], low, high))
        for block, (real, low, high) in enumerate(spans):
            if block < 2:
                need_ref[row, block] = 1
            else:
                need_ref[row, block] = sum(
                    jnp.where(real & ok & (low <= top) & (bottom <= high), 1, 0) for ok, bottom, top in spans[:2]
                )


def masks(lengths, place, blocks, tokens):
    rows = lengths.shape[0]
    shapes = [(rows, blocks, tokens), (rows, blocks, tokens, 1), (rows, 1, 2 * tokens), (rows, 2 * tokens, 1)]
    smem = pl.BlockSpec(memory_space=pltpu.SMEM)
    return pl.pallas_call(
        functools.partial(mask_kernel, rows, tokens, blocks),
        out_shape=[jax.ShapeDtypeStruct((rows, blocks), jnp.int32)]
        + [jax.ShapeDtypeStruct(shape, jnp.int32) for shape in shapes],
        in_specs=[smem, smem],
        out_specs=[smem] + [pl.BlockSpec(memory_space=pltpu.VMEM)] * 4,
        compiler_params=pltpu.CompilerParams(vmem_limit_bytes=VMEM),
        cost_estimate=NOMINAL,
        name="masks",
    )(lengths, place)


def lay_vectors(core, weight, lines, half, padded):
    width, cols = weight.shape
    low = half // 128 * 128

    def kernel(core_ref, weight_ref, lines_ref, q_ref, kv_ref):
        turned = weight_ref[...].astype(F32).T
        lines_ref[...] = turned[half - low : half - low + lines]
        q_ref[...] = jnp.zeros_like(q_ref)
        kv_ref[...] = jnp.zeros_like(kv_ref)
        for at in range(2):

            @pl.when(core_ref[0] == at)
            def _():
                q_ref[:, :half] = lines_ref[2:3, at * half : (at + 1) * half]
                kv_ref[:, padded : padded + half] = lines_ref[3:4, at * half : (at + 1) * half]

    outs = [like(lines, width, F32), like(1, padded, F32), like(1, 2 * padded, F32)]
    block = cols - low
    return pl.pallas_call(
        kernel,
        out_shape=outs,
        grid=(1,),
        in_specs=[
            pl.BlockSpec(memory_space=pltpu.SMEM),
            pl.BlockSpec((width, block), lambda i: (0, low // block)),
        ],
        out_specs=[pl.BlockSpec(out.shape, lambda i: (0, 0)) for out in outs],
        compiler_params=params(("arbitrary",)),
        cost_estimate=NOMINAL,
        name="lay_vectors",
    )(core, weight)


def mlp_shards(core, out_shard, hidden_weight, down_weight, cols):
    rows, total = hidden_weight.shape
    before = out_shard.shape[1]

    def kernel(core_ref, part_ref, hidden_ref, down_ref, first_out, down_out):
        first_out[:, :before] = part_ref[...]
        for at in range(2):

            @pl.when(core_ref[0] == at)
            def _():
                low = at * cols
                high = min(low + cols, total)
                size = high - low
                first_out[:, before : before + size] = hidden_ref[:, low:high]
                down_out[:, :size] = down_ref[low:high].T
                if size < cols:
                    empty = jnp.zeros((rows, cols - size), BF16)
                    first_out[:, before + size :] = empty
                    down_out[:, size:] = empty

    outs = [like(rows, before + cols), like(rows, cols)]
    return small_call(kernel, outs, [core], [out_shard, hidden_weight, down_weight], "mlp_shards")


def attention_shards(core, weights, vectors, half, padded):
    rows, width = weights[0].shape
    cut = width - padded
    count = len(vectors)

    def kernel(core_ref, q_ref, k_ref, v_ref, o_ref, *refs):
        qkv_ref, out_ref, held = refs[count:]
        for i in range(count):
            held[i : i + 1] = refs[i][...].astype(F32).reshape(1, rows)
        empty = jnp.zeros((rows, padded - half), BF16)
        spare = jnp.zeros((rows, padded - half - count), BF16)
        lines = jnp.concatenate([held[...].T.astype(BF16), spare], axis=1)
        for at in range(2):

            @pl.when(core_ref[0] == at)
            def _():
                for i, ref in enumerate((q_ref, k_ref, v_ref)):
                    part = ref[:, at * half : (at + 1) * half]
                    rest = empty if i else lines
                    qkv_ref[:, i * padded : (i + 1) * padded] = jnp.concatenate([part, rest], axis=1)
                out_ref[...] = o_ref[:, at * cut : at * cut + padded]

    vmem = pl.BlockSpec(memory_space=pltpu.VMEM)
    return pl.pallas_call(
        kernel,
        out_shape=[like(rows, 3 * padded), like(rows, padded)],
        in_specs=[pl.BlockSpec(memory_space=pltpu.SMEM)] + [vmem] * (4 + count),
        out_specs=[vmem] * 2,
        scratch_shapes=[pltpu.VMEM((count, rows), F32)],
        compiler_params=pltpu.CompilerParams(vmem_limit_bytes=VMEM),
        cost_estimate=NOMINAL,
        name="attention_shards",
    )(core, *weights, *vectors)


def hidden(arrays, weight, bias):
    rows, width = arrays[0].shape
    cols = weight.shape[1]
    block = 384 if rows % 384 == 0 else row_block(rows)
    steps, count = rows // block, len(arrays)

    def kernel(*refs):
        w_ref, b_ref, act_ref, slope_ref, x_ref = refs[count:]
        for i in range(count):

            @pl.when(pl.program_id(0) // steps == i)
            def _():
                x_ref[...] = refs[i][...]

        pre = dot(x_ref[...], w_ref[...]) + b_ref[...]
        square = pre * pre
        turn = jnp.tanh(pre * (GELU_COEF + GELU_COEF * 0.044715 * square))
        act_ref[...] = (0.5 * pre * (1.0 + turn)).astype(BF16)
        inner = GELU_COEF + 3.0 * 0.044715 * GELU_COEF * square
        slope_ref[...] = (0.5 * (1.0 + turn) * (1.0 + pre * (1.0 - turn) * inner)).astype(BF16)

    out = pl.BlockSpec((block, cols), lambda i: (i, 0))
    return pl.pallas_call(
        kernel,
        out_shape=(
            jax.ShapeDtypeStruct((count * rows, cols), BF16),
            jax.ShapeDtypeStruct((count * rows, cols), BF16),
            jax.ShapeDtypeStruct((count * rows, width), BF16),
        ),
        grid=(count * steps,),
        in_specs=[
            pl.BlockSpec((block, width), lambda i, k=k: (jnp.clip(i - k * steps, 0, steps - 1), 0))
            for k in range(count)
        ]
        + [
            pl.BlockSpec((width, cols), lambda i: (0, 0), pipeline_mode=pl.Buffered(1)),
            pl.BlockSpec((1, cols), lambda i: (0, 0)),
        ],
        out_specs=(out, out, pl.BlockSpec((block, width), lambda i: (i, 0))),
        compiler_params=params(("arbitrary",)),
        cost_estimate=NOMINAL,
        name="hidden",
    )(*arrays, weight, bias)


def head_window(head):
    first = head * HEAD_DIM
    start = first // 128 * 128
    return start, round_up(first + HEAD_DIM, 128) - start, first - start


def head_lanes(rows, width, low):
    lane = lax.broadcasted_iota(jnp.int32, (rows, width), 1)
    return (lane >= low) & (lane < low + HEAD_DIM)


def only_head(block, low):
    mine = head_lanes(*block.shape, low)
    return jnp.where(mine, block.astype(F32), 0.0).astype(BF16)


def pick_block(near_ref, far_ref, block):
    return near_ref.at[block, 0] if block < 2 else far_ref.at[block - 2, 0]


def attend_kernel(row, heads, blocks, padded, need_ref, col_ref, row_ref, q_ref, near_ref, far_ref, *refs):
    own_ref, pair_ref, lse_ref, queries, score, peak, total, acc, lses = refs[-9:]
    outs = (own_ref, pair_ref)
    tokens = own_ref.shape[1]
    slot = lax.broadcasted_iota(jnp.int32, (2 * tokens, 128), 1)
    for which in range(2):
        outs[which][...] = jnp.zeros_like(outs[which])
    windows = [head_window(head) for head in range(heads)]
    for head, (start, width, low) in enumerate(windows):
        for which in range(2):
            queries[head, which * tokens : (which + 1) * tokens, :width] = only_head(
                q_ref[which, 0, :, start : start + width], low
            )
    peak[...] = jnp.full_like(peak, MASKED)
    total[...] = jnp.zeros_like(total)
    acc[...] = jnp.zeros_like(acc)
    for block in range(blocks):

        @pl.when(need_ref[row, block] != 0)
        def _():
            side = pick_block(near_ref, far_ref, block)
            seen = col_ref[0] == row_ref[0, block : block + 1]
            for head, (start, width, _) in enumerate(windows):
                key = side[:, start : start + width]
                found = jnp.where(seen, dot(queries[head, :, :width], key, NT), MASKED)
                score[head, block] = found
                top = peak[head]
                for at in range(0, tokens, 128):
                    top = jnp.maximum(top, found[:, at : at + 128])
                peak[head] = top

    for head in range(heads):
        top = jnp.max(peak[head], axis=-1, keepdims=True) * (SCALE * LOG2E)
        peak[head] = jnp.broadcast_to(top, peak.shape[1:])

    for block in range(blocks):

        @pl.when(need_ref[row, block] != 0)
        def _():
            side = pick_block(near_ref, far_ref, block)
            for head, (start, width, _) in enumerate(windows):
                top, share = peak[head], total[head]
                pieces = []
                for at in range(0, tokens, 128):
                    part = jnp.exp2(score[head, block, :, at : at + 128] * (SCALE * LOG2E) - top)
                    share += part
                    pieces.append(part.astype(BF16))
                total[head] = share
                value = side[:, padded + start : padded + start + width]
                acc[head, :, :width] += dot(jnp.concatenate(pieces, axis=1), value)

    for head, (start, width, low) in enumerate(windows):
        norm = jnp.sum(total[head], axis=-1, keepdims=True)
        result = acc[head, :, :width] / norm
        mine = head_lanes(tokens, width, low)
        for which in range(2):
            kept = outs[which][0, :, start : start + width].astype(F32)
            fresh = result[which * tokens : (which + 1) * tokens]
            outs[which][0, :, start : start + width] = jnp.where(mine, fresh, kept).astype(BF16)
        lse = peak[head] + jnp.log2(norm)
        lses[...] = lse if head == 0 else jnp.where(slot == head, lse, lses[...])
    lse_ref[0] = lses[...].T[:heads]


def attend(row, query, near, far, need, seg_col, seg_row, heads, before):
    _, rows, tokens, padded = query.shape
    blocks = 2 + far.shape[0]
    narrow = pl.BlockSpec((1, tokens, padded), lambda i, need: (row, 0, 0))
    lines = pl.BlockSpec((1, heads, 2 * tokens), lambda i, need: (row, 0, 0))

    def stack(count, width):
        return pl.BlockSpec((count, 1, tokens, width), lambda i, need: (0, row, 0, 0))

    return pl.pallas_call(
        functools.partial(attend_kernel, row, heads, blocks, padded),
        out_shape=(
            jax.ShapeDtypeStruct((rows, tokens, padded), BF16),
            jax.ShapeDtypeStruct((rows, tokens, padded), BF16),
            jax.ShapeDtypeStruct((rows, heads, 2 * tokens), F32),
        ),
        grid_spec=pltpu.PrefetchScalarGridSpec(
            num_scalar_prefetch=1,
            grid=(1,),
            in_specs=[
                pl.BlockSpec((1, 2 * tokens, 1), lambda i, need: (row, 0, 0)),
                pl.BlockSpec((1, blocks, tokens), lambda i, need: (row, 0, 0)),
                stack(2, padded),
                stack(2, 2 * padded),
                stack(blocks - 2, 2 * padded),
            ]
            + [pl.BlockSpec(memory_space=pl.ANY)] * len(before),
            out_specs=(narrow, narrow, lines),
            scratch_shapes=[
                pltpu.VMEM((heads, 2 * tokens, WIN), BF16),
                pltpu.VMEM((heads, blocks, 2 * tokens, tokens), F32),
                pltpu.VMEM((heads, 2 * tokens, 128), F32),
                pltpu.VMEM((heads, 2 * tokens, 128), F32),
                pltpu.VMEM((heads, 2 * tokens, WIN), F32),
                pltpu.VMEM((2 * tokens, 128), F32),
            ],
        ),
        input_output_aliases={6 + i: i for i in range(len(before))},
        compiler_params=params(("arbitrary",)),
        cost_estimate=NOMINAL,
        name="attend",
    )(need, seg_col, seg_row, query, near, far, *before)


def attend_back_kernel(
    row, heads, blocks, padded, need_ref, col_ref, row_ref, pick_ref, q_ref, near_ref, far_ref, *refs
):
    grads, outs, lse_ref = refs[0:2], refs[2:4], refs[4]
    dq_ref, dnear_ref, dfar_ref, sums, inner_turn, queries, incoming, dq = refs[-8:]
    tokens = grads[0].shape[1]
    sums[...] = jnp.zeros_like(sums)
    for which in range(2):
        dq_ref[which, 0] = jnp.zeros((tokens, padded), BF16)
        product = grads[which][0].astype(F32) * outs[which][0].astype(F32)
        high = product.astype(BF16)
        rest = (product - high.astype(F32)).astype(BF16)
        inner_turn[:, which * tokens : (which + 1) * tokens] = dot(pick_ref[...], high, NT) + dot(
            pick_ref[...], rest, NT
        )
    windows = [head_window(head) for head in range(heads)]
    for head, (start, width, low) in enumerate(windows):
        for which in range(2):
            there = slice(which * tokens, (which + 1) * tokens)
            here = slice(start, start + width)
            queries[head, there, :width] = only_head(q_ref[which, 0, :, here], low)
            incoming[head, there, :width] = only_head(grads[which][0, :, here], low)
    dq[...] = jnp.zeros_like(dq)
    for block in range(blocks):

        @pl.when(need_ref[row, block] != 0)
        def _():
            side = pick_block(near_ref, far_ref, block)
            seen = col_ref[0, block] == row_ref[0]
            for head, (start, width, _) in enumerate(windows):
                end = start + width
                key, value = side[:, start:end], side[:, padded + start : padded + end]
                query, grad = queries[head, :, :width], incoming[head, :, :width]
                found = dot(key, query, NT) * (SCALE * LOG2E) - lse_ref[0, head : head + 1, :]
                prob = jnp.where(seen, jnp.exp2(found), 0.0)
                inner = inner_turn[head : head + 1, :]
                slope = (prob * (dot(value, grad, NT) - inner)).astype(BF16)
                sums[block, :, start:end] += dot(slope, query)
                sums[block, :, padded + start : padded + end] += dot(prob.astype(BF16), grad)
                dq[head, :, :width] += dot(slope, key, TN)

    for head, (start, width, low) in enumerate(windows):
        mine = head_lanes(tokens, width, low)
        for which in range(2):
            kept = dq_ref[which, 0, :, start : start + width].astype(F32)
            fresh = dq[head, which * tokens : (which + 1) * tokens, :width] * SCALE
            dq_ref[which, 0, :, start : start + width] = jnp.where(mine, fresh, kept).astype(BF16)
    for block in range(blocks):
        side = pick_block(dnear_ref, dfar_ref, block)
        side[:, :padded] = (sums[block, :, :padded] * SCALE).astype(BF16)
        side[:, padded:] = sums[block, :, padded:].astype(BF16)


def attend_back(row, query, near, far, grads, outs, lse, need, seg_col, seg_row, heads, before):
    _, rows, tokens, padded = query.shape
    blocks = 2 + far.shape[0]
    column = lax.broadcasted_iota(jnp.int32, (heads, padded), 1)
    pick = (column // HEAD_DIM == lax.broadcasted_iota(jnp.int32, (heads, padded), 0)).astype(BF16)
    narrow = pl.BlockSpec((1, tokens, padded), lambda i, need: (row, 0, 0))

    def stack(count, width):
        return pl.BlockSpec((count, 1, tokens, width), lambda i, need: (0, row, 0, 0))

    return pl.pallas_call(
        functools.partial(attend_back_kernel, row, heads, blocks, padded),
        out_shape=tuple(jax.ShapeDtypeStruct(a.shape, BF16) for a in (query, near, far)),
        grid_spec=pltpu.PrefetchScalarGridSpec(
            num_scalar_prefetch=1,
            grid=(1,),
            in_specs=[
                pl.BlockSpec((1, blocks, tokens, 1), lambda i, need: (row, 0, 0, 0)),
                pl.BlockSpec((1, 1, 2 * tokens), lambda i, need: (row, 0, 0)),
                pl.BlockSpec((heads, padded), lambda i, need: (0, 0)),
                stack(2, padded),
                stack(2, 2 * padded),
                stack(blocks - 2, 2 * padded),
            ]
            + [narrow] * 4
            + [pl.BlockSpec((1, heads, 2 * tokens), lambda i, need: (row, 0, 0))]
            + [pl.BlockSpec(memory_space=pl.ANY)] * len(before),
            out_specs=(stack(2, padded), stack(2, 2 * padded), stack(blocks - 2, 2 * padded)),
            scratch_shapes=[
                pltpu.VMEM((blocks, tokens, 2 * padded), F32),
                pltpu.VMEM((heads, 2 * tokens), F32),
                pltpu.VMEM((heads, 2 * tokens, WIN), BF16),
                pltpu.VMEM((heads, 2 * tokens, WIN), BF16),
                pltpu.VMEM((heads, 2 * tokens, WIN), F32),
            ],
        ),
        input_output_aliases={12 + i: i for i in range(len(before))},
        compiler_params=params(("arbitrary",)),
        cost_estimate=NOMINAL,
        name="attend_back",
    )(need, seg_col, seg_row, pick, query, near, far, *grads, *outs, lse, *before)


def local(
    patches,
    lengths,
    first_gain,
    first_shift,
    query_weight,
    query_bias,
    key_weight,
    value_weight,
    value_bias,
    output_weight,
    output_bias,
    second_gain,
    second_shift,
    hidden_weight,
    hidden_bias,
    down_weight,
    down_bias,
    cotangent,
):
    seq_count, shards = lax.axis_size("seq"), lax.axis_size("fsdp")
    place, me = lax.axis_index("seq"), lax.axis_index("fsdp")
    core = place & 1
    is_first = core == 0
    core_flag = core[None].astype(jnp.int32)
    rows, tokens, width = patches.shape
    flat = rows * tokens
    heads = width // HEAD_DIM // 2
    half = heads * HEAD_DIM
    padded = round_up(half, 128)
    ff = hidden_bias.shape[0]
    ff_half = round_up(ff, 256) // 2
    out_cols = padded
    out_cut = width - padded
    shard_rows = width // shards
    chain = Chain()

    def my_half(array, size, padded_size):
        first, second = array[..., :size], array[..., size:]
        grow = [(0, 0)] * (array.ndim - 1)
        first = jnp.pad(first, grow + [(0, padded_size - size)])
        second = jnp.pad(second, grow + [(0, padded_size - second.shape[-1])])
        return jnp.where(is_first, first, second)

    flights = Flights(chain)
    staged = shards == 8 and seq_count == 4
    y, z, zz = 1, 2, 4
    top = bits_of(seq_count)[0]

    inputs = patches.reshape(flat, width)
    incoming = cotangent.reshape(flat, width)
    vectors = [
        first_gain,
        first_shift,
        query_bias,
        value_bias,
        output_bias,
        second_gain,
        second_shift,
        down_bias,
    ]
    shard_qkv, shard_out = chain.done(
        *attention_shards(
            core_flag, [query_weight, key_weight, value_weight, output_weight], vectors, half, padded
        )
    )
    place_flag = place[None].astype(jnp.int32)

    def over(box_from, bits):
        return flights.send(box_from[0], "fsdp", bits)

    if staged:
        q = {0: [shard_qkv]}
        q[y] = over(q[0], y)
        q[z], q[zz] = over(q[0], z), over(q[0], zz)
        incoming_pair = flights.send(incoming, "seq", 1)
        shard_ho, shard_down = chain.done(
            *mlp_shards(core_flag, shard_out, hidden_weight, down_weight, ff_half)
        )
        h, d = {0: [shard_ho]}, {0: [shard_down]}
        need, seg_rows, seg_cols, seg_near_row, seg_near_col = chain.done(
            *masks(chain(lengths), place_flag, seq_count, tokens)
        )
        core_flag, raw_own = flights.land(core_flag, inputs)
        q[zz | z], q[z | y], q[zz | y] = over(q[zz], z), over(q[z], y), over(q[zz], y)
        far_raw = [flights.send(raw_own, "seq", 2)]
        raw_pair = flights.send(raw_own, "seq", 1)
        core_flag, incoming_pair[0] = flights.land(core_flag, incoming_pair[0], only=[q[zz | z]])
        q[zz | z | y] = over(q[zz | z], y)
        incoming_near = chain.done(jnp.concatenate([incoming, incoming_pair[0]], axis=0))
        core_flag, shard_ho = flights.land(core_flag, shard_ho, only=[q[z | y], q[zz | y], raw_pair])
        h[0] = [shard_ho]
        h[z], h[y] = over(h[0], z), over(h[0], y)
        core_flag, shard_ho, shard_down = flights.land(
            core_flag, shard_ho, shard_down, only=[q[zz | z | y], far_raw[0]]
        )
        h[0], d[0] = [shard_ho], [shard_down]
        far_pair = [flights.send(far_raw[0][0], "seq", 1)]
        h[zz] = over(h[0], zz)
        w_q, w_kv = chain.done(*assemble({k: box[0] for k, box in q.items()}, me, padded))
        stacked, bias_q, bias_kv = chain.done(
            *lay_vectors(chain(core_flag), w_q, len(vectors), half, padded)
        )
        gain_one, shift_one = stacked[0:1], stacked[1:2]
        gain_one = chain(gain_one)
        normed_near = chain.done(norm([inputs, raw_pair[0]], gain_one, shift_one))
        bias_hidden = my_half(after(hidden_bias, gain_one).astype(F32)[None], ff_half, ff_half)
    else:
        parts = gather_all(shard_qkv)
        shard_ho, shard_down = mlp_shards(core_flag, shard_out, hidden_weight, down_weight, ff_half)
        raw = {0: inputs}
        for bit in bits_of(seq_count):
            raw.update({j | bit: swap(part, "seq", bit) for j, part in list(raw.items())})
        need, seg_rows, seg_cols, seg_near_row, seg_near_col = masks(lengths, place_flag, seq_count, tokens)
        w_q, w_kv = chain.done(*assemble(parts, me, padded))
        stacked, bias_q, bias_kv = lay_vectors(core_flag, w_q, len(vectors), half, padded)
        gain_one, shift_one = stacked[0:1], stacked[1:2]
        normed_near = norm([raw[0], raw[1]], gain_one, shift_one)
        far_raw, far_pair = [[raw[j]] for j in range(2, seq_count)], []
        incoming_near = jnp.concatenate([incoming, swap(incoming, "seq", 1)], axis=0)
        bias_hidden = my_half(hidden_bias.astype(F32)[None], ff_half, ff_half)
    _, _, bias_query, bias_value, bias_output, gain_two, shift_two, bias_down = [
        stacked[i : i + 1] for i in range(8)
    ]

    near_in, w_q, w_kv = chain(normed_near, w_q, w_kv)
    (query,) = rows_matmul("query", [near_in], [w_q], with_bias, [bias_q], [like(2 * flat, padded)])
    near_in = after(near_in, query)
    (near,) = rows_matmul("near", [near_in], [w_kv], with_bias, [bias_kv], [like(2 * flat, 2 * padded)])
    chain.done(query, near)
    if staged:
        gain_one = flights.land(gain_one, only=[h[z], far_pair[0]])
        h[z | y] = over(h[z], y)
    gain_one, w_kv = chain(gain_one, w_kv)
    normed_far = chain.done(norm([box[0] for box in far_raw + far_pair], gain_one, shift_one))
    if staged:
        w_kv = flights.land(w_kv, only=[h[y], h[zz]])
        h[zz | y], h[zz | z] = over(h[zz], y), over(h[zz], z)
    far_in, w_kv = chain(normed_far, w_kv)
    (far,) = rows_matmul(
        "far", [far_in], [w_kv], with_bias, [bias_kv], [like(normed_far.shape[0], 2 * padded)]
    )
    chain.done(far)
    query = query.reshape(2, rows, tokens, padded)
    near = near.reshape(2, rows, tokens, 2 * padded)
    far = far.reshape(seq_count - 2, rows, tokens, 2 * padded)
    found = ()
    for row in range(rows):
        query, near, far = chain(query, near, far)
        if staged and row == 1:
            query = flights.land(query, only=[h[z | y], h[zz | z]])
            h[zz | z | y] = over(h[zz | z], y)
            d[y], d[z], d[zz] = over(d[0], y), over(d[0], z), over(d[0], zz)
        found = chain.done(*attend(row, query, near, far, need, seg_near_col, seg_rows, heads, found))
    out_own, out_pair, lse = found
    if staged:
        out_own, out_pair = flights.land(out_own, out_pair, only=list(h.values()))
        h_parts = {k: box[0] for k, box in h.items()}
    else:
        out_own, out_pair = flights.land(out_own, out_pair)
        h_parts = gather_all(chain(shard_ho))
    w_out_mine, w_hidden = chain.done(*assemble(h_parts, me, out_cols))
    if staged:
        out_pair, w_out_mine = flights.land(out_pair, w_out_mine, only=[d[y], d[z], d[zz]])
    else:
        out_pair, w_out_mine = chain(out_pair, w_out_mine)
    other_half = flights.send(out_pair, "seq", 1)
    w_out_other = flights.send(w_out_mine, "seq", 1)
    if staged:
        d[zz | z], d[z | y] = over(d[zz], z), over(d[z], y)
    w_out_mine, w_hidden = flights.land(w_out_mine, w_hidden, only=[other_half, w_out_other])
    w_out = chain.done(both_cores(core_flag, w_out_mine, w_out_other[0], out_cut, width))
    own_half, w_out = chain(out_own.reshape(flat, padded), w_out)
    attended, middle, second = chain.done(
        *join(
            core_flag,
            own_half,
            other_half[0].reshape(flat, padded),
            inputs,
            w_out,
            bias_output,
            gain_two,
            shift_two,
            half,
        )
    )
    if staged:
        second = flights.land(second, only=[d[zz | z], d[z | y]])
    second_pair = flights.send(second, "seq", 1)
    if staged:
        d[zz | y], d[zz | z | y] = over(d[zz], y), over(d[zz | z], y)
    second, w_hidden = flights.land(second, w_hidden, only=[second_pair])
    act, slope, second_near = chain.done(*hidden([second, second_pair[0]], w_hidden, bias_hidden))

    incoming_near, act = chain(incoming_near, act)
    grad_down = chain.done(token_dot(incoming_near, act))
    if staged:
        slope, grad_down = flights.land(slope, grad_down)
        d_parts = {k: box[0] for k, box in d.items()}
    else:
        d_parts = gather_all(chain(shard_down))
    part_down = lax.psum_scatter(grad_down, "fsdp", scatter_dimension=0, tiled=True)
    w_down = chain.done(assemble(d_parts, me))
    incoming_near, slope, w_down = chain(incoming_near, slope, w_down)
    grad_pre, hidden_line = chain.done(
        *rows_matmul(
            "grad_pre",
            [incoming_near],
            [w_down],
            with_slope,
            [slope],
            [like(2 * flat, ff_half), like(1, ff_half, F32)],
        )
    )
    grad_pre = chain(grad_pre)
    back, back_pair = chain.done(
        *rows_matmul("back", [grad_pre], [w_hidden], plain, [], [like(2 * flat, width)], NT, True)
    )
    back_other = flights.send(back_pair, "seq", 1)
    second_near, grad_pre = chain(second_near, grad_pre)
    grad_hidden = chain.done(token_dot(second_near, grad_pre, out_cols))
    back = flights.land(back)
    grad_middle, branch, grad_mine, grad_send, lines = second_back(
        core_flag, middle, [back, back_other[0]], gain_two, incoming, w_out, hidden_line, half, padded
    )
    chain.done(branch, grad_send)
    grad_pair = flights.send(grad_send, "seq", 1)
    attended, branch = chain(attended, branch)
    partial_out = flights.land(chain.done(token_dot(attended, branch)))
    out_mine, out_other = chain.done(*core_columns(core_flag, [partial_out], out_cols))
    query = flights.land(query)

    links = {"x": ("seq", top), "core": ("seq", 1)} | {bit: ("fsdp", bit) for bit in bits_of(shards)}
    out_back = flights.send(out_other, "seq", 1)
    shape = (rows, tokens, padded)
    grads = [grad_mine.reshape(shape), grad_pair[0].reshape(shape)]
    found = ()
    far_bits = [2 << k for k in range(shards.bit_length() - 2)]
    def next_step(keep, box, bits):
        keep, send = scatter_step(keep, box[0], shard_rows)
        chain.done(keep)
        return keep, flights.send(send, "fsdp", bits.pop(0)) if bits else None

    def seq_rest(mine, arrived):
        for bit in bits_of(seq_count)[1:-1]:
            (mine,) = add_rows(mine, arrived)
            arrived = swap(mine, "seq", bit)
        return chain.done(*add_rows(mine, arrived, F32))

    for row in range(rows):
        query, near, far, *grads = chain(query, near, far, *grads)
        found = attend_back(
            row, query, near, far, grads, [out_own, out_pair], lse, need, seg_cols, seg_near_row, heads, found
        )
        chain.done(*found)
        query = flights.land(query)
        if row == 0:
            grad_ho = chain.done(add_into(grad_hidden, out_mine, out_back[0], ff_half))
            part_hidden = lax.psum_scatter(grad_ho, "fsdp", scatter_dimension=0, tiled=True)
        if row == 1:
            part_down = chain(part_down)
            down_seq = flights.send(part_down, "seq", top)
    dq, dnear, dfar = [g.reshape(-1, g.shape[-1]) for g in found]
    dfar, w_kv, down_seq[0] = chain(dfar, w_kv, down_seq[0])
    two = seq_count == 4
    back_far = rows_matmul("back_far", [dfar], [w_kv], plain, [], [like(dfar.shape[0], width)], NT, two)
    chain.done(*back_far)
    dnear = chain(dnear)
    if two:
        far_parts = {2 + i: part for i, part in enumerate(back_far)}
    else:
        far_parts = {j: back_far[0][(j - 2) * flat : (j - 1) * flat] for j in range(2, seq_count)}
    far_sent = {j: flights.send(part, "seq", 1) for j, part in far_parts.items() if j & 1}
    normed_near, dnear, dfar = chain(normed_near, dnear, dfar)
    kv_keep, kv_send, kv_sums = chain.done(
        *weight_grad([normed_near, normed_far], [dnear, dfar], me, shards)
    )
    dq = flights.land(dq)
    kv_box = flights.send(kv_send, "fsdp", y)
    far_sums = {j: add_rows(far_parts[j], far_sent[j | 1][0])[0] for j in far_parts if not j & 1}
    chain.done(*far_sums.values())
    arrived = []
    for bit in bits_of(seq_count)[:-1]:
        for j in [j for j in far_sums if j & bit]:
            part = far_sums.pop(j)
            if j == bit:
                arrived.append(flights.send(part, "seq", bit))
            else:
                (far_sums[j ^ bit],) = add_rows(far_sums[j ^ bit], swap(part, "seq", bit))
    dq, dnear = chain(dq, dnear)
    back_own, back_pair = chain.done(
        *rows_matmul("back_near", [dq, dnear], [w_q, w_kv], plain, [], [like(2 * flat, width)], NT, True)
    )
    pair_back = flights.send(back_pair, "seq", 1)
    act, middle = chain(act, middle)
    (down_pair,) = rows_matmul(
        "down_pair", [act], [w_down], plain, [], [like(flat, width)], NT, first_row=flat
    )
    chain.done(down_pair)
    down_back = flights.send(down_pair, "seq", 1)
    normed_near, dq = chain(normed_near, dq)
    q_keep, q_send, q_sums = chain.done(*weight_grad([normed_near], [dq], me, shards))
    q_box = flights.send(q_send, "fsdp", y)
    kv_bits, q_bits = list(far_bits), list(far_bits)
    act, late_in = flights.land(act, inputs, only=[kv_box] + arrived)
    kv_keep, kv_box = next_step(kv_keep, kv_box, kv_bits)
    late_in = flights.land(late_in, only=[pair_back])
    grad_patches, late = chain.done(
        *first_back(
            core_flag,
            late_in,
            [back_own, pair_back[0]] + [box[0] for box in arrived],
            gain_one,
            grad_middle,
            q_sums,
            kv_sums,
            half,
        )
    )
    small = jnp.concatenate([lines, late], axis=0)
    if staged:
        small_todo = [("fsdp", zz), ("fsdp", y), ("seq", top), ("fsdp", z), ("seq", 1)]
    else:
        small_todo = [("fsdp", bit) for bit in bits_of(shards)] + [("seq", bit) for bit in bits_of(seq_count)]

    def small_send():
        return flights.send(small, *small_todo.pop(0)) if small_todo else None

    def small_step(small, box):
        return chain.done(*add_rows(small, box[0], F32))

    act, middle, small = flights.land(act, middle, small, only=[q_box, down_back])
    q_keep, q_box = next_step(q_keep, q_box, q_bits)
    small_box = small_send()
    act, middle = chain(act, middle)
    (layer_output,) = rows_matmul(
        "down_own", [act], [w_down], layer_end, [middle, down_back[0], bias_down], [like(flat, width)], NT
    )
    layer_output = chain.done(layer_output).reshape(rows, tokens, width)

    def move_on(*also):
        nonlocal small, small_box, kv_keep, kv_box, q_keep, q_box
        flights.land(only=[box for box in (kv_box, q_box, small_box, *also) if box is not None])
        if kv_box is not None:
            kv_keep, kv_box = next_step(kv_keep, kv_box, kv_bits)
        if q_box is not None:
            q_keep, q_box = next_step(q_keep, q_box, q_bits)
        if small_box is not None:
            small = small_step(small, small_box)
            small_box = small_send()

    move_on()
    part_hidden = chain(part_hidden)
    hidden_seq = flights.send(part_hidden, "seq", top)
    while kv_box is not None or q_box is not None:
        move_on()
    kv_seq = flights.send(kv_keep, "seq", top)
    q_seq = flights.send(q_keep, "seq", top)
    flights.land(only=[hidden_seq])
    hidden_total = seq_rest(part_hidden, hidden_seq[0])
    hidden_other = flights.send(hidden_total, "seq", 1)
    move_on(kv_seq, q_seq)
    kv_total = seq_rest(kv_keep, kv_seq[0])
    kv_other = flights.send(kv_total, "seq", 1)
    q_total = seq_rest(q_keep, q_seq[0])
    q_other = flights.send(q_total, "seq", 1)
    flights.land(only=[hidden_other])
    down_total = seq_rest(part_down, down_seq[0])
    down_other = flights.send(down_total, "seq", 1)
    while small_box is not None:
        move_on()
    flights.land()

    own_lines = lax.dynamic_slice_in_dim(small[:8], me * shard_rows, shard_rows, 1)
    late_lines = lax.dynamic_slice_in_dim(small[8:], me * shard_rows, shard_rows, 1)
    cuts = [width, ff_half - width, width, ff - ff_half - width]
    full_bias = jnp.concatenate([small[4 + i, :size] for i, size in enumerate(cuts)])
    full_down = both_columns(is_first, down_total, down_other[0], ff_half, ff).T
    full_hidden = both_columns(is_first, hidden_total, hidden_other[0], ff_half, ff)
    full_out = both_columns(is_first, hidden_total, hidden_other[0], out_cut, width, ff_half)
    full_query = both_columns(is_first, q_total, q_other[0], half, width)
    full_key = both_columns(is_first, kv_total, kv_other[0], half, width)
    full_value = both_columns(is_first, kv_total, kv_other[0], half, width, padded)
    return (
        layer_output,
        grad_patches.reshape(rows, tokens, width),
        late_lines[0],
        late_lines[1],
        full_query,
        late_lines[2],
        full_key,
        full_value,
        late_lines[3],
        full_out,
        own_lines[2],
        own_lines[0],
        own_lines[1],
        full_hidden,
        full_bias,
        full_down,
        own_lines[3],
    )


def solution(mesh):
    shard, line, tokens = P("fsdp", None), P("fsdp"), P("fsdp", "seq", None)
    in_specs = (
        tokens,
        shard,
        line,
        line,
        shard,
        line,
        shard,
        shard,
        line,
        shard,
        line,
        line,
        line,
        shard,
        P(),
        P(None, "fsdp"),
        line,
        tokens,
    )
    out_specs = (
        tokens,
        tokens,
        line,
        line,
        shard,
        line,
        shard,
        shard,
        line,
        shard,
        line,
        line,
        line,
        shard,
        P(),
        P(None, "fsdp"),
        line,
    )
    return jax.shard_map(local, mesh=mesh, in_specs=in_specs, out_specs=out_specs, check_vma=False)
```
